32 devices in a mesh: ctx: 4 (over x, core), fsdp: 8 (over z, y).
Axes of the slice: x: 2, y: 2, z: 4, core: 2. Of those that a mesh axis runs over, the one named last changes fastest.
Arguments:
- inputs: bfloat16 [2, 8, 512, 1024], P(None, 'fsdp', 'ctx'), may hold values from -6 to 6
- cotangent: bfloat16 [2, 8, 512, 1024], P(None, 'fsdp', 'ctx'), may hold values from -6 to 6
- lengths: int32 [2, 8], P(None, 'fsdp'), may hold values from 128 to 512, as said below
- query_weight: bfloat16 [1024, 1024], P('fsdp'), may hold values from -0.1875 to 0.1875
- key_weight: bfloat16 [1024, 1024], P('fsdp'), may hold values from -0.1875 to 0.1875
- value_weight: bfloat16 [1024, 1024], P('fsdp'), may hold values from -0.1875 to 0.1875
- output_weight: bfloat16 [1024, 1024], P('fsdp'), may hold values from -0.75 to 0.75
- query_bias: bfloat16 [1024], P('fsdp'), may hold values from -3 to 3
- value_bias: bfloat16 [1024], P('fsdp'), may hold values from -3 to 3
- output_bias: bfloat16 [1024], P('fsdp'), may hold values from -2 to 2
- first_gain: bfloat16 [1024], P('fsdp'), may hold values from 0.099609375 to 1.8984375
- first_shift: bfloat16 [1024], P('fsdp'), may hold values from -2 to 2
- inner_weight: bfloat16 [1024, 4096], P('fsdp'), may hold values from -0.1875 to 0.1875
- inner_bias: bfloat16 [4096], P('fsdp'), may hold values from -3 to 3
- outer_weight: bfloat16 [4096, 1024], P('fsdp'), may hold values from -0.09375 to 0.09375
- outer_bias: bfloat16 [1024], P('fsdp'), may hold values from -2 to 2
- second_gain: bfloat16 [1024], P('fsdp'), may hold values from 0.099609375 to 1.8984375
- second_shift: bfloat16 [1024], P('fsdp'), may hold values from -2 to 2
Outputs:
- layer_output: bfloat16 [2, 8, 512, 1024], P(None, 'fsdp', 'ctx')
- input_gradient: float32 [2, 8, 512, 1024], P(None, 'fsdp', 'ctx')
- query_weight_gradient: float32 [1024, 1024], P('fsdp')
- key_weight_gradient: float32 [1024, 1024], P('fsdp')
- value_weight_gradient: float32 [1024, 1024], P('fsdp')
- output_weight_gradient: float32 [1024, 1024], P('fsdp')
- query_bias_gradient: float32 [1024], P('fsdp')
- value_bias_gradient: float32 [1024], P('fsdp')
- output_bias_gradient: float32 [1024], P('fsdp')
- first_gain_gradient: float32 [1024], P('fsdp')
- first_shift_gradient: float32 [1024], P('fsdp')
- inner_weight_gradient: float32 [1024, 4096], P('fsdp')
- inner_bias_gradient: float32 [4096], P('fsdp')
- outer_weight_gradient: float32 [4096, 1024], P('fsdp')
- outer_bias_gradient: float32 [1024], P('fsdp')
- second_gain_gradient: float32 [1024], P('fsdp')
- second_shift_gradient: float32 [1024], P('fsdp')
The draws below stay inside these ranges and needn't reach their ends.
Inputs may be any that keep to these rules, and one draw needn't show every extreme that they name: The valid slots of a sequence are its first lengths entries; in every micro-batch some sequence fills all 512 slots.
All inputs are finite; a program needn't handle non-finite values.
Results may differ from the reference program's by a relative error of at most 0.018.
Values may be sent and summed in bfloat16 or wider, within the bound.
A program may use at most 256 MiB of HBM per device.

```python
import math
import jax
import jax.numpy as jnp
from jax import lax

D = 1024
HEADS = 16
HEAD_DIM = 64
FF = 4096
SLOTS = 512
MICRO = 2
SEQS = 8


def draw_lengths(key, part):
    first_key, second_key = jax.random.split(jax.random.fold_in(key, 11))
    base_lengths = jax.random.randint(first_key, (MICRO, SEQS), SLOTS // 4, SLOTS + 1)
    chosen = jax.random.randint(second_key, (MICRO, 1), 0, SEQS)
    columns = jnp.arange(SEQS, dtype=jnp.int32)[None, :]
    return jnp.where(columns == chosen, SLOTS, base_lengths).astype(jnp.int32)


def strengthened(array, stream_key, source, target, parts, factor):
    def block_of(position):
        return (jnp.arange(array.shape[position]) // (array.shape[position] // parts)).reshape((-1,) + (1,) * (array.ndim - 1 - position))

    one_side = jax.random.permutation(stream_key, parts)[block_of(target)]
    other_side = (block_of(target) + parts // 2) % parts
    return jnp.where((block_of(source) == one_side) | (block_of(source) == other_side), factor * array, array)


def block_levels(key, shape, cuts, low, top_value):
    level, own = 1.0, jax.random.fold_in(key, 6)
    for position, shards_of in cuts:
        steps = jnp.exp(jax.random.uniform(jax.random.fold_in(own, position), (shards_of,), jnp.float32, low / len(cuts), top_value / len(cuts)))
        level = level * jnp.repeat(steps, shape[position] // shards_of).reshape([-1 if axis == position else 1 for axis in range(len(shape))])
    return level


def noise(own_key, extent, width, limit, cuts=(), kind=jnp.bfloat16):
    entries = jax.random.normal(own_key, extent, jnp.float32) * width
    if len(cuts) > 0:
        entries = block_levels(own_key, extent, cuts, -0.22, 0.18) * entries
    return jnp.clip(entries, min=-limit, max=limit).astype(kind)


def bell_draw_with(key, shape, deviation, bound, cuts, heavy, kind=jnp.bfloat16):
    drawn = deviation * jax.random.normal(key, shape, jnp.float32)
    if cuts:
        drawn = drawn * block_levels(key, shape, cuts, -0.22, 0.18)
    return jnp.clip(strengthened(drawn, jax.random.fold_in(key, 3), *heavy), -bound, bound).astype(kind)


def setup_inputs(seed: int = 0) -> dict:
    keys = jax.random.split(jax.random.key(seed), 19)
    return {
        "inputs": bell_draw_with(keys[0], (MICRO, SEQS, SLOTS, D), 1.0, 6.0, ((1, 8), (2, 4)), (1, 3, 8, 2.0)),
        "cotangent": noise(keys[1], (MICRO, SEQS, SLOTS, D), 1.0, 6.0, ((1, 8), (2, 4))),
        "lengths": draw_lengths(jax.random.fold_in(keys[18], 71), 0),
        "query_weight": noise(keys[3], (D, D), D ** -0.5, 0.1875, ((0, 8),)),
        "key_weight": noise(keys[4], (D, D), D ** -0.5, 0.1875, ((0, 8),)),
        "value_weight": noise(keys[5], (D, D), D ** -0.5, 0.1875, ((0, 8),)),
        "output_weight": noise(keys[6], (D, D), (D // 16) ** -0.5, 0.75, ((0, 8),)),
        "query_bias": noise(keys[7], (D,), 0.5, 3.0, ((0, 8),)),
        "value_bias": noise(keys[8], (D,), 0.5, 3.0, ((0, 8),)),
        "output_bias": noise(keys[9], (D,), 0.3, 2.0, ((0, 8),)),
        "first_gain": jnp.clip(1.0 + 0.18 * jax.random.normal(keys[10], (D,), jnp.float32), 0.099609375, 1.8984375).astype(jnp.bfloat16),
        "first_shift": noise(keys[11], (D,), 0.3, 2.0, ((0, 8),)),
        "inner_weight": noise(keys[12], (D, FF), D ** -0.5, 0.1875, ((0, 8),)),
        "inner_bias": noise(keys[13], (FF,), 0.5, 3.0, ((0, 8),)),
        "outer_weight": noise(keys[14], (FF, D), FF ** -0.5, 0.09375, ((0, 8),)),
        "outer_bias": noise(keys[15], (D,), 0.3, 2.0, ((0, 8),)),
        "second_gain": jnp.clip(1.0 + 0.18 * jax.random.normal(keys[16], (D,), jnp.float32), 0.099609375, 1.8984375).astype(jnp.bfloat16),
        "second_shift": noise(keys[17], (D,), 0.3, 2.0, ((0, 8),)),
    }


@jax.custom_vjp
def low(v):
    return lax.optimization_barrier(v.astype(jnp.bfloat16)).astype(jnp.float32)

@jax.custom_vjp
def low_back(v):
    return v

def low_keep(v):
    return (low(v), None)

def low_pass(kept, grad):
    return (grad,)

def back_keep(v):
    return (v, None)

def back_low(kept, grad):
    return (low(grad),)
low.defvjp(low_keep, low_pass)
low_back.defvjp(back_keep, back_low)

def layer_norm(hidden, gain, shift):
    average = lax.optimization_barrier(jnp.mean(hidden, axis=-1, keepdims=True))
    centered = hidden - average
    variance = lax.optimization_barrier(jnp.mean(centered * centered, axis=-1, keepdims=True))
    return centered * lax.rsqrt(variance + 1e-06) * gain + shift

def dense(left, right):
    return jnp.dot(left, right, precision=lax.Precision.HIGHEST)

def forward(params, block_in, valid_mask):
    query_weight, key_weight, value_weight, output_weight, query_bias, value_bias, output_bias, first_gain, first_shift, inner_weight, inner_bias, outer_weight, outer_bias, second_gain, second_shift = params
    group_size = block_in.shape[0]
    flat_rows = block_in.reshape(group_size * SLOTS, D)
    queries = low_back(low(dense(flat_rows, query_weight) + query_bias))
    keys_all = low_back(low(dense(flat_rows, key_weight)))
    values_all = low_back(low(dense(flat_rows, value_weight) + value_bias))
    shaped = (group_size, SLOTS, HEADS, HEAD_DIM)
    scores = jnp.einsum('sqhd,skhd->shqk', queries.reshape(shaped), keys_all.reshape(shaped), precision=lax.Precision.HIGHEST)
    scores = low_back(scores * HEAD_DIM ** (-0.5))
    scores = jnp.where(valid_mask[:, None, None, :], scores, -1e+30)
    probs = low(jax.nn.softmax(scores, axis=-1))
    context = jnp.einsum('shqk,skhd->sqhd', probs, values_all.reshape(shaped), precision=lax.Precision.HIGHEST)
    context = low_back(low(context.reshape(group_size * SLOTS, D)))
    branch = low_back(dense(context, output_weight) + output_bias)
    normed = layer_norm(flat_rows + branch, first_gain, first_shift)
    hidden = low_back(dense(low(normed), inner_weight) + inner_bias)
    active = low(jax.nn.gelu(hidden, approximate=False))
    second = low_back(dense(active, outer_weight) + outer_bias)
    result = layer_norm(normed + second, second_gain, second_shift)
    row_mask = valid_mask.astype(result.dtype).reshape(group_size * SLOTS, 1)
    return (result * row_mask).reshape(group_size, SLOTS, D)

def reference(inputs, cotangent, lengths, query_weight, key_weight, value_weight, output_weight, query_bias, value_bias, output_bias, first_gain, first_shift, inner_weight, inner_bias, outer_weight, outer_bias, second_gain, second_shift):
    params = tuple((item_value.astype(jnp.float32) for item_value in (query_weight, key_weight, value_weight, output_weight, query_bias, value_bias, output_bias, first_gain, first_shift, inner_weight, inner_bias, outer_weight, outer_bias, second_gain, second_shift)))
    total_seqs = MICRO * SEQS
    group_size = math.gcd(total_seqs, max(1, 4096 // SLOTS))
    batches = total_seqs // group_size
    flat_in = inputs.astype(jnp.float32).reshape(batches, group_size, SLOTS, D)
    flat_ct = cotangent.astype(jnp.float32).reshape(batches, group_size, SLOTS, D)
    flat_len = lengths.reshape(batches, group_size).astype(jnp.int32)
    positions = jnp.arange(SLOTS, dtype=jnp.int32)

    def advance(totals, pieces):
        block_in, block_ct, block_len = pieces
        valid_mask = positions[None, :] < block_len[:, None]

        def layer_apply(param_set, data_rows):
            return forward(param_set, data_rows, valid_mask)
        result, pullback = jax.vjp(layer_apply, params, block_in)
        param_grads, input_grads = pullback(block_ct)
        totals = jax.tree.map(jnp.add, totals, param_grads)
        return (totals, (result, input_grads))
    zero_grads = jax.tree.map(jnp.zeros_like, params)
    totals, (results, input_grads) = lax.scan(advance, zero_grads, (flat_in, flat_ct, flat_len))
    layer_output = results.reshape(MICRO, SEQS, SLOTS, D).astype(jnp.bfloat16)
    input_gradient = input_grads.reshape(MICRO, SEQS, SLOTS, D).astype(jnp.float32)
    return (layer_output, input_gradient, totals[0], totals[1], totals[2], totals[3], totals[4], totals[5], totals[6], totals[7], totals[8], totals[9], totals[10], totals[11], totals[12], totals[13], totals[14])
```

```python
import jax
import jax.numpy as jnp
from jax import lax
from jax.sharding import PartitionSpec as P

HEAD_DIM = 64
EPSILON = 1e-06
F32 = jnp.float32
BF16 = jnp.bfloat16


def exact_gelu(hidden):
    return jax.nn.gelu(hidden, approximate=False)


def plain_product(left, right):
    return jnp.dot(left, right, preferred_element_type=F32)


def left_product(left, right):
    return lax.dot_general(left, right, (((0,), (0,)), ((), ())), preferred_element_type=F32)


def right_product(left, right):
    return lax.dot_general(left, right, (((1,), (1,)), ((), ())), preferred_element_type=F32)


def column_sums(rows):
    return jnp.sum(rows.astype(F32), axis=0)


def norm_parts(total):
    average = jnp.mean(total, axis=-1, keepdims=True)
    centered = total - average
    variance = jnp.mean(centered * centered, axis=-1, keepdims=True)
    rate = lax.rsqrt(variance + EPSILON)
    return centered * rate, rate


def norm_back(unit, rate, grad):
    return rate * (
        grad
        - jnp.mean(grad, axis=-1, keepdims=True)
        - unit * jnp.mean(grad * unit, axis=-1, keepdims=True)
    )


def split_columns(packed, widths):
    pieces = []
    start = 0
    for width in widths:
        pieces.append(packed[..., start : start + width])
        start += width
    return pieces


def attention_forward(queries, keys_all, values_all, key_valid, heads):
    shape = queries.shape[:2] + (heads, HEAD_DIM)
    key_shape = keys_all.shape[:2] + (heads, HEAD_DIM)
    scores = jnp.einsum(
        "sqhd,skhd->shqk",
        queries.reshape(shape),
        keys_all.reshape(key_shape),
        preferred_element_type=F32,
    ) * (HEAD_DIM**-0.5)
    scores = jnp.where(key_valid[:, None, None, :], scores, -1e30)
    top = jnp.max(scores, axis=-1, keepdims=True)
    weights = jnp.exp(scores - top)
    probs = (weights / jnp.sum(weights, axis=-1, keepdims=True)).astype(BF16)
    context = jnp.einsum(
        "shqk,skhd->sqhd", probs, values_all.reshape(key_shape), preferred_element_type=F32
    )
    return context.reshape(queries.shape).astype(BF16), probs


def attention_backward(queries, keys_all, values_all, probs, context_grad, heads):
    shape = queries.shape[:2] + (heads, HEAD_DIM)
    key_shape = keys_all.shape[:2] + (heads, HEAD_DIM)
    scale = HEAD_DIM**-0.5
    grad_heads = context_grad.reshape(shape)
    wide = probs.astype(F32)
    probs_grad = jnp.einsum(
        "sqhd,skhd->shqk", grad_heads, values_all.reshape(key_shape), preferred_element_type=F32
    )
    inner_total = jnp.sum(wide * probs_grad, axis=-1, keepdims=True)
    scores_grad = (wide * (probs_grad - inner_total)).astype(BF16)
    query_grad = jnp.einsum(
        "shqk,skhd->sqhd", scores_grad, keys_all.reshape(key_shape), preferred_element_type=F32
    )
    key_part = jnp.einsum(
        "shqk,sqhd->skhd", scores_grad, queries.reshape(shape), preferred_element_type=F32
    )
    value_part = jnp.einsum("shqk,sqhd->skhd", probs, grad_heads, preferred_element_type=F32)
    return (
        (query_grad * scale).astype(BF16).reshape(queries.shape),
        (key_part * scale).astype(BF16).reshape(keys_all.shape),
        value_part.astype(BF16).reshape(values_all.shape),
    )


def gather_rows(part):
    return lax.all_gather(part, "fsdp", axis=0, tiled=True)


def reduce_rows(part):
    share = lax.psum_scatter(part.astype(BF16), "fsdp", scatter_dimension=0, tiled=True)
    return lax.psum(share, "ctx").astype(F32)


def body(
    inputs,
    cotangent,
    lengths,
    query_weight,
    key_weight,
    value_weight,
    output_weight,
    query_bias,
    value_bias,
    output_bias,
    first_gain,
    first_shift,
    inner_weight,
    inner_bias,
    outer_weight,
    outer_bias,
    second_gain,
    second_shift,
):
    vectors = (
        query_bias,
        value_bias,
        output_bias,
        first_gain,
        first_shift,
        inner_bias,
        outer_bias,
        second_gain,
        second_shift,
    )
    widths = [member.shape[0] for member in vectors]
    packed = lax.all_gather(jnp.concatenate(vectors), "fsdp", axis=0, tiled=False)
    (
        bias_query,
        bias_value,
        bias_output,
        gain_first,
        shift_first,
        bias_inner,
        bias_outer,
        gain_second,
        shift_second,
    ) = [piece.reshape(-1).astype(F32) for piece in split_columns(packed, widths)]
    full_qkv = gather_rows(jnp.concatenate((query_weight, key_weight, value_weight), axis=1))
    full_output = gather_rows(output_weight)
    full_inner = gather_rows(inner_weight)
    full_outer = gather_rows(outer_weight)

    micro, seqs, block_len, width = inputs.shape
    heads = width // HEAD_DIM
    ctx_size = lax.axis_size("ctx")
    total_slots = block_len * ctx_size
    group = micro * seqs
    rows = group * block_len
    flat_len = lengths.reshape(group)
    local_pos = lax.axis_index("ctx") * block_len + jnp.arange(block_len, dtype=jnp.int32)
    row_mask = (local_pos[None, :] < flat_len[:, None]).astype(F32).reshape(rows, 1)
    key_valid = jnp.arange(total_slots, dtype=jnp.int32)[None, :] < flat_len[:, None]

    flat_rows = inputs.reshape(rows, width)
    qkv = plain_product(flat_rows, full_qkv)
    queries = (qkv[:, :width] + bias_query).astype(BF16)
    keys_values = jnp.concatenate(
        (qkv[:, width : 2 * width], qkv[:, 2 * width :] + bias_value), axis=1
    ).astype(BF16)
    keys_values_all = lax.all_gather(
        keys_values.reshape(group, block_len, 2 * width), "ctx", axis=1, tiled=True
    )
    keys_all = keys_values_all[:, :, :width]
    values_all = keys_values_all[:, :, width:]
    queries3 = queries.reshape(group, block_len, width)
    context, probs = attention_forward(queries3, keys_all, values_all, key_valid, heads)
    context = context.reshape(rows, width)

    first_sum = flat_rows.astype(F32) + plain_product(context, full_output) + bias_output
    first_unit, first_rate = norm_parts(first_sum)
    normed = first_unit * gain_first + shift_first
    normed_low = normed.astype(BF16)
    hidden = plain_product(normed_low, full_inner) + bias_inner
    active, gelu_back = jax.vjp(exact_gelu, hidden)
    active_low = active.astype(BF16)
    second_sum = normed + plain_product(active_low, full_outer) + bias_outer
    second_unit, second_rate = norm_parts(second_sum)
    output = ((second_unit * gain_second + shift_second) * row_mask).astype(BF16)

    out_grad = cotangent.reshape(rows, width).astype(F32) * row_mask
    second_gain_part = jnp.sum(out_grad * second_unit, axis=0)
    second_shift_part = jnp.sum(out_grad, axis=0)
    second_grad = norm_back(second_unit, second_rate, out_grad * gain_second)
    second_low = second_grad.astype(BF16)
    outer_weight_part = left_product(active_low, second_low).astype(BF16)
    outer_bias_part = column_sums(second_low)
    (hidden_grad,) = gelu_back(right_product(second_low, full_outer))
    hidden_low = hidden_grad.astype(BF16)
    inner_weight_part = left_product(normed_low, hidden_low).astype(BF16)
    inner_bias_part = column_sums(hidden_low)
    normed_grad = second_grad + right_product(hidden_low, full_inner)
    first_gain_part = jnp.sum(normed_grad * first_unit, axis=0)
    first_shift_part = jnp.sum(normed_grad, axis=0)
    first_grad = norm_back(first_unit, first_rate, normed_grad * gain_first)
    branch_low = first_grad.astype(BF16)
    output_weight_part = left_product(context, branch_low).astype(BF16)
    output_bias_part = column_sums(branch_low)
    context_grad = right_product(branch_low, full_output).astype(BF16)
    query_grad, key_part, value_part = attention_backward(
        queries3, keys_all, values_all, probs, context_grad.reshape(queries3.shape), heads
    )
    keys_values_grad = lax.psum_scatter(
        jnp.concatenate((key_part, value_part), axis=2), "ctx", scatter_dimension=1, tiled=True
    ).reshape(rows, 2 * width)
    qkv_grad = jnp.concatenate((query_grad.reshape(rows, width), keys_values_grad), axis=1)
    qkv_weight_part = left_product(flat_rows, qkv_grad).astype(BF16)
    query_bias_part = column_sums(qkv_grad[:, :width])
    value_bias_part = column_sums(qkv_grad[:, 2 * width :])
    input_grad = first_grad + right_product(qkv_grad, full_qkv)

    qkv_share = reduce_rows(qkv_weight_part)
    output_share = reduce_rows(output_weight_part)
    inner_share = reduce_rows(inner_weight_part)
    outer_share = reduce_rows(outer_weight_part)
    vector_parts = (
        query_bias_part,
        value_bias_part,
        output_bias_part,
        first_gain_part,
        first_shift_part,
        inner_bias_part,
        outer_bias_part,
        second_gain_part,
        second_shift_part,
    )
    fsdp_size = lax.axis_size("fsdp")
    packed_parts = jnp.concatenate(
        [part.reshape(fsdp_size, -1) for part in vector_parts], axis=1
    )
    vector_share = lax.psum(
        lax.psum_scatter(packed_parts, "fsdp", scatter_dimension=0, tiled=True), "ctx"
    )[0]
    shares = split_columns(vector_share, widths)
    query_share, key_share, value_share = split_columns(qkv_share, [width] * 3)
    return (
        output.reshape(inputs.shape),
        input_grad.reshape(inputs.shape),
        query_share,
        key_share,
        value_share,
        output_share,
        shares[0],
        shares[1],
        shares[2],
        shares[3],
        shares[4],
        inner_share,
        shares[5],
        outer_share,
        shares[6],
        shares[7],
        shares[8],
    )


def solution(mesh):
    data = P(None, "fsdp", "ctx", None)
    matrix = P("fsdp", None)
    vector = P("fsdp")
    return jax.shard_map(
        body,
        mesh=mesh,
        in_specs=(data, data, P(None, "fsdp"))
        + (matrix,) * 4
        + (vector,) * 5
        + (matrix, vector, matrix, vector, vector, vector),
        out_specs=(data, data)
        + (matrix,) * 4
        + (vector,) * 5
        + (matrix, vector, matrix, vector, vector, vector),
        check_vma=False,
    )
```

```python
import functools

import jax
import jax.numpy as jnp
from jax import lax
from jax.experimental import pallas as pl
from jax.experimental.pallas import tpu as pltpu
from jax.sharding import PartitionSpec as P

HEAD_DIM = 64
EPSILON = 1e-06
F32 = jnp.float32
BF16 = jnp.bfloat16
MESH = pl.DeviceIdType.MESH
LINE = 4
PAIR = 2


class Place:
    def __init__(self):
        self.ctx = lax.axis_index("ctx")
        self.shard = lax.axis_index("fsdp")
        self.side = lax.div(self.ctx, 2)
        self.core = lax.rem(self.ctx, 2)
        self.line = lax.div(self.shard, PAIR)
        self.pair = lax.rem(self.shard, PAIR)

    def ahead(self, way):
        return (self.ctx, self.shard + way * PAIR)

    def across(self):
        return (self.ctx, self.shard + 1 - 2 * self.pair)

    def beside(self):
        return (self.ctx + 2 - 4 * self.side, self.shard)

    def twin(self):
        return (self.ctx + 1 - 2 * self.core, self.shard)

    def has(self, way, steps):
        if steps == 0:
            return None
        return self.line >= steps if way > 0 else self.line <= LINE - 1 - steps

    def can(self, way):
        return self.line <= LINE - 2 if way > 0 else self.line >= 1

    def shard_of(self, way, steps, other):
        pair = 1 - self.pair if other else self.pair
        return (self.line - way * steps) * PAIR + pair


def when(conditions, action):
    held = [c for c in conditions if c is not None]
    if not held:
        action()
        return
    both = held[0]
    for c in held[1:]:
        both = jnp.logical_and(both, c)
    pl.when(both)(action)


def greet(place):
    barrier = pltpu.get_barrier_semaphore()
    for peer in (place.across(), place.beside(), place.twin()):
        pl.semaphore_signal(barrier, inc=1, device_id=peer, device_id_type=MESH)
    for way in (1, -1):
        when(
            [place.can(way)],
            lambda way=way: pl.semaphore_signal(
                barrier, inc=1, device_id=place.ahead(way), device_id_type=MESH
            ),
        )
    lines = jnp.minimum(place.line, 1) + jnp.minimum(LINE - 1 - place.line, 1)
    pl.semaphore_wait(barrier, 3 + lines)


class Flow:
    def __init__(self, array, shard_rows, region, order="line", sides=False, cores=True):
        self.array = array
        self.shard_rows = shard_rows
        self.region = region
        self.order = order
        self.sides = sides
        self.cores = cores

    def view(self, ref, shard, core, side):
        row, rows, column, columns = self.region(core, side)
        start = row if shard is None else shard * self.shard_rows + row
        if not isinstance(start, int):
            start = pl.multiple_of(start, 16)
        if not isinstance(column, int):
            column = pl.multiple_of(column, 128)
        return ref.at[pl.ds(start, rows), pl.ds(column, columns)]


def positions(order):
    found = []
    if order == "line":
        found.append(("P", 1, 0, True))
        for steps in range(1, LINE):
            for way in (1, -1):
                found.append(("L", way, steps, False))
                found.append(("P", way, steps, True))
    else:
        found.append(("P", 1, 0, True))
        for steps in range(1, LINE):
            for way in (1, -1):
                found.append(("L", way, steps, False))
                found.append(("L", way, steps, True))
    return found


class Labels:
    def __init__(self):
        self.numbers = {}

    def __call__(self, key):
        return self.numbers.setdefault(key, len(self.numbers))


def gather_labels(flows):
    labels = Labels()
    for number, flow in enumerate(flows):
        for spot in positions(flow.order):
            labels((number, "in") + spot)
            if flow.sides:
                labels((number, "side") + spot)
            if flow.cores:
                labels((number, "twin") + spot)
                if flow.sides:
                    labels((number, "twinside") + spot)
    return labels


class Gather:
    def __init__(self, place, flows, owns, fulls, send, recv):
        self.place, self.flows, self.owns, self.fulls = place, flows, owns, fulls
        self.send, self.recv = send, recv
        self.labels = gather_labels(flows)
        self.sent = []

    def copy(self, number, key, spot, peer, core, side, own=False):
        flow = self.flows[number]
        place = self.place
        if own:
            shard = place.shard
            source = flow.view(self.owns[flow.array], None, core, side)
        else:
            shard = place.shard_of(*spot[1:])
            source = flow.view(self.fulls[flow.array], shard, core, side)
        target = flow.view(self.fulls[flow.array], shard, core, side)
        label = self.labels((number,) + key)
        return pltpu.make_async_remote_copy(
            source,
            target,
            self.send.at[label],
            self.recv.at[label],
            device_id=peer,
            device_id_type=MESH,
        )

    def start(self, conditions, copy):
        when(conditions, copy.start)
        self.sent.append((conditions, copy))

    def begin(self, number):
        flow, place = self.flows[number], self.place
        core, side = place.core, place.side
        here = (None, 1, 0, False)
        for way in (1, -1):
            self.start(
                [place.can(way)],
                self.copy(
                    number, ("in", "L", way, 1, False), here, place.ahead(way), core, side, True
                ),
            )
        self.start(
            [],
            self.copy(number, ("in", "P", 1, 0, True), here, place.across(), core, side, True),
        )

    def arrive(self, number, spot):
        flow, place = self.flows[number], self.place
        kind, way, steps, other = spot
        core, side = place.core, place.side
        there = place.has(way, steps)

        def take():
            self.copy(number, ("in",) + spot, spot, place.across(), core, side).wait_recv()

        when([there], take)

        def onward(extra, key, peer):
            self.start(
                [c for c in (there, extra) if c is not None],
                self.copy(number, key, spot, peer, core, side),
            )

        if kind == "L" and steps + 1 < LINE:
            onward(place.can(way), ("in", "L", way, steps + 1, other), place.ahead(way))
        if kind == "L" and flow.order == "line":
            onward(None, ("in", "P", way, steps, True), place.across())
        if kind == "P" and flow.order == "pair":
            for direction in (1, -1):
                onward(
                    place.can(direction), ("in", "L", direction, 1, True), place.ahead(direction)
                )
        if flow.sides:
            onward(None, ("side",) + spot, place.beside())
        if flow.cores:
            onward(None, ("twin",) + spot, place.twin())

    def arrive_side(self, number, spot):
        flow, place = self.flows[number], self.place
        there = place.has(*spot[1:3])
        core, side = place.core, 1 - place.side
        when(
            [there],
            lambda: self.copy(
                number, ("side",) + spot, spot, place.beside(), core, side
            ).wait_recv(),
        )
        if flow.cores:
            self.start(
                [there] if there is not None else [],
                self.copy(number, ("twinside",) + spot, spot, place.twin(), core, side),
            )

    def arrive_twin(self, number, spot):
        flow, place = self.flows[number], self.place
        there = place.has(*spot[1:3])
        core = 1 - place.core
        if flow.cores:
            when(
                [there],
                lambda: self.copy(
                    number, ("twin",) + spot, spot, place.twin(), core, place.side
                ).wait_recv(),
            )
            if flow.sides:
                when(
                    [there],
                    lambda: self.copy(
                        number, ("twinside",) + spot, spot, place.twin(), core, 1 - place.side
                    ).wait_recv(),
                )

    def steps(self, flow_order=None):
        order = list(range(len(self.flows)))
        todo = [lambda n=n: self.begin(n) for n in order]
        late = []
        spots = {n: positions(self.flows[n].order) for n in order}
        for index in range(len(positions("line"))):
            for n in order:
                spot = spots[n][index]
                todo.append(lambda n=n, spot=spot: self.arrive(n, spot))
                if self.flows[n].sides:
                    late.append((index, n, spot))
            ready = [entry for entry in late if entry[0] < index - 1]
            late = [entry for entry in late if entry[0] >= index - 1]
            for _, n, spot in ready:
                todo.append(lambda n=n, spot=spot: self.arrive_side(n, spot))
        for _, n, spot in late:
            todo.append(lambda n=n, spot=spot: self.arrive_side(n, spot))
        return todo

    def finish(self):
        for number, flow in enumerate(self.flows):
            for spot in positions(flow.order):
                self.arrive_twin(number, spot)
        for conditions, copy in self.sent:
            when(conditions, copy.wait_send)


def gather_kernel(flows, count, *refs):
    owns, fulls = refs[:count], refs[count : 2 * count]
    send, recv, local = refs[2 * count :]
    place = Place()
    keep = [
        pltpu.make_async_copy(
            owns[k], fulls[k].at[pl.ds(place.shard * owns[k].shape[0], owns[k].shape[0]), :], local.at[k]
        )
        for k in range(count)
    ]
    greet(place)
    work = Gather(place, flows, owns, fulls, send, recv)
    for copy in keep:
        copy.start()
    for step in work.steps():
        step()
    work.finish()
    for copy in keep:
        copy.wait()


def gather_call(arrays, flows, shards, collective_id):
    labels = gather_labels(flows)
    count = len(arrays)
    return pl.pallas_call(
        functools.partial(gather_kernel, flows, count),
        out_shape=[
            jax.ShapeDtypeStruct((shards * a.shape[0], a.shape[1]), a.dtype) for a in arrays
        ],
        in_specs=[pl.BlockSpec(memory_space=pltpu.VMEM)] * count,
        out_specs=[pl.BlockSpec(memory_space=pl.ANY)] * count,
        scratch_shapes=[
            pltpu.SemaphoreType.DMA((len(labels.numbers),)),
            pltpu.SemaphoreType.DMA((len(labels.numbers),)),
            pltpu.SemaphoreType.DMA((count,)),
        ],
        compiler_params=pltpu.CompilerParams(collective_id=collective_id, has_side_effects=True),
        name="gather_weights",
    )(*arrays)


def column_flows(array, shard_rows, columns, shared, early):
    half = columns // 2
    part = (half - shared) // 2
    flows = []
    if shared:
        flows.append(
            Flow(array, shard_rows, lambda core, side: (0, shard_rows, core * half, shared))
        )
    if early:
        flows.append(
            Flow(
                array,
                shard_rows,
                lambda core, side: (0, shard_rows, core * half + shared + side * part, early),
                sides=True,
            )
        )
    if part > early:
        flows.append(
            Flow(
                array,
                shard_rows,
                lambda core, side: (
                    0,
                    shard_rows,
                    core * half + shared + side * part + early,
                    part - early,
                ),
                order="pair",
                sides=True,
            )
        )
    return flows


def row_flows(array, shard_rows, columns, shared, early):
    half = shard_rows // 2
    part = (half - shared) // 2
    return [
        Flow(array, shard_rows, lambda core, side: (core * half, shared, 0, columns)),
        Flow(
            array,
            shard_rows,
            lambda core, side: (core * half + shared + side * part, early, 0, columns),
            sides=True,
        ),
        Flow(
            array,
            shard_rows,
            lambda core, side: (core * half + shared + side * part + early, part - early, 0, columns),
            order="pair",
            sides=True,
        ),
    ]


class Part:
    def __init__(self, rows, columns, along, flows, dtype=BF16):
        self.rows, self.columns, self.along, self.dtype = rows, columns, along, dtype
        self.flows = flows
        self.half_rows = rows // 2 if along == "rows" else rows
        self.half_columns = columns // 2 if along == "columns" else columns

    def half(self, ref, shard, core):
        base = 0 if shard is None else pl.multiple_of(shard * self.rows, 16)
        if self.along == "rows":
            row = core * self.half_rows + (0 if shard is None else shard * self.rows)
            return ref.at[pl.ds(pl.multiple_of(row, 16), self.half_rows), :]
        if self.along == "columns":
            column = pl.multiple_of(core * self.half_columns, 128)
            return ref.at[pl.ds(base, self.rows), pl.ds(column, self.half_columns)]
        return ref.at[pl.ds(base, self.rows), :]

    def inner(self, flow, side):
        first, extent = flow[0](side), flow[1]
        if self.along == "rows":
            start = first if isinstance(first, int) else pl.multiple_of(first, 16)
            return pl.ds(start, extent), slice(None)
        start = first if isinstance(first, int) else pl.multiple_of(first, 128)
        return slice(None), pl.ds(start, extent)

    def outer(self, flow, core, side):
        first, extent = flow[0](side), flow[1]
        if self.along == "rows":
            return pl.ds(pl.multiple_of(core * self.half_rows + first, 16), extent), slice(None)
        if self.along == "columns":
            return slice(None), pl.ds(
                pl.multiple_of(core * self.half_columns + first, 128), extent
            )
        return slice(None), slice(None)

    def extent(self, flow):
        if self.along == "rows":
            return flow[1], self.half_columns
        return self.half_rows, flow[1]


SPOTS = [(1, 3), (-1, 3), (1, 2), (-1, 2), (1, 1), (-1, 1), (1, 0)]


def reduce_scratch(parts):
    shapes = []
    for part in parts:
        half = (LINE * PAIR, part.half_rows, part.half_columns)
        shapes.append(pltpu.VMEM(half, part.dtype))
        shapes.append(pltpu.VMEM(half if part.along else half[1:], part.dtype))
        for flow in part.flows:
            rows, columns = part.extent(flow)
            shapes.append(
                pltpu.VMEM((LINE * PAIR if flow[3] else 1, rows, columns), part.dtype)
            )
            shapes.append(
                pltpu.VMEM((LINE if flow[2] == "line" else 1, rows, columns), part.dtype)
            )
            shapes.append(
                pltpu.VMEM(
                    ((LINE + 1) * (1 if flow[2] == "line" else PAIR), rows, columns), part.dtype
                )
            )
    return shapes


def reduce_labels(parts):
    labels = Labels()
    for n, part in enumerate(parts):
        for way, steps in SPOTS:
            for other in (False, True):
                labels((n, "twin", way, steps, other))
        labels((n, "twinend"))
        for k, flow in enumerate(part.flows):
            for way, steps in SPOTS:
                for other in (False, True):
                    if flow[3]:
                        labels((n, k, "side", way, steps, other))
                    if flow[2] == "pair" or not other:
                        labels((n, k, "line", way, steps, other))
                        if steps == 0:
                            labels((n, k, "line", -way, steps, other))
                if flow[2] == "line" or steps == 0:
                    labels((n, k, "pair", way, steps))
            labels((n, k, "sideend"))
            labels((n, k, "twinend"))
            labels((n, k, "twinsideend"))
    return labels


class Reduce:
    def __init__(self, place, parts, grads, outs, scratch, send, recv, load):
        self.place, self.parts, self.grads, self.outs = place, parts, grads, outs
        self.send, self.recv, self.load = send, recv, load
        self.labels = reduce_labels(parts)
        self.sent = []
        self.own, self.other, self.lanes = [], [], []
        at = 0
        for part in parts:
            self.own.append(scratch[at])
            self.other.append(scratch[at + 1])
            at += 2
            lanes = []
            for _ in part.flows:
                lanes.append(scratch[at : at + 3])
                at += 3
            self.lanes.append(lanes)

    def copy(self, source, target, key, peer):
        label = self.labels(key)
        return pltpu.make_async_remote_copy(
            source,
            target,
            self.send.at[label],
            self.recv.at[label],
            device_id=peer,
            device_id_type=MESH,
        )

    def start(self, conditions, copy):
        when(conditions, copy.start)
        self.sent.append((conditions, copy))

    def there(self, spot):
        return self.place.has(-spot[0], spot[1])

    def shard(self, spot, other):
        return self.place.shard_of(-spot[0], spot[1], other)

    def keep(self, n, spot, other):
        shard = self.shard(spot, other)
        label = SPOTS.index(spot) * 2 + int(other)
        return pltpu.make_async_copy(
            self.parts[n].half(self.grads[n], shard, self.place.core),
            self.own[n].at[shard],
            self.load.at[n * 2 * len(SPOTS) + label],
        )

    def twin(self, n, spot, other, core):
        shard = self.shard(spot, other)
        return self.copy(
            self.parts[n].half(self.grads[n], shard, core),
            self.other[n].at[shard],
            (n, "twin") + spot + (other,),
            self.place.twin(),
        )

    def begin(self, n):
        for spot in SPOTS:
            for other in (True, False):
                there = self.there(spot)
                when([there], self.keep(n, spot, other).start)
                if self.parts[n].along:
                    self.start([there], self.twin(n, spot, other, 1 - self.place.core))

    def piece(self, n, k, shard, side):
        part = self.parts[n]
        rows, columns = part.inner(part.flows[k], side)
        return self.own[n].at[shard, rows, columns]

    def side_copy(self, n, k, spot, other, side):
        shard = self.shard(spot, other)
        return self.copy(
            self.piece(n, k, shard, side),
            self.lanes[n][k][0].at[shard],
            (n, k, "side") + spot + (other,),
            self.place.beside(),
        )

    def stage_cores(self, spot):
        there = self.there(spot)
        for n, part in enumerate(self.parts):
            for other in (True, False):
                shard = self.shard(spot, other)

                def add(n=n, part=part, other=other, shard=shard):
                    self.keep(n, spot, other).wait()
                    if part.along:
                        self.twin(n, spot, other, self.place.core).wait_recv()
                        self.own[n][shard] = self.own[n][shard] + self.other[n][shard]

                when([there], add)
        for n, part in enumerate(self.parts):
            for other in (True, False):
                for k, flow in enumerate(part.flows):
                    if flow[3]:
                        self.start(
                            [there], self.side_copy(n, k, spot, other, 1 - self.place.side)
                        )

    def pair_copy(self, n, k, spot, shard):
        flow = self.parts[n].flows[k]
        slot = self.place.line + spot[0] * spot[1] if flow[2] == "line" else 0
        return self.copy(
            self.piece(n, k, shard, self.place.side),
            self.lanes[n][k][1].at[slot],
            (n, k, "pair") + spot,
            self.place.across(),
        )

    def stage_sides(self, spot):
        there = self.there(spot)
        side = self.place.side
        for n, part in enumerate(self.parts):
            for k, flow in enumerate(part.flows):
                if not flow[3]:
                    continue
                for other in (True, False):
                    shard = self.shard(spot, other)

                    def add(n=n, k=k, other=other, shard=shard):
                        self.side_copy(n, k, spot, other, side).wait_recv()
                        piece = self.piece(n, k, shard, side)
                        piece[...] = piece[...] + self.lanes[n][k][0][shard]

                    when([there], add)
        for n, part in enumerate(self.parts):
            for k, flow in enumerate(part.flows):
                if flow[2] == "line":
                    self.start([there], self.pair_copy(n, k, spot, self.shard(spot, True)))

    def line_slot(self, flow, way, steps, other, line):
        slot = line if (steps > 0 or way > 0) else LINE
        return slot + (LINE + 1) * int(other) if flow[2] == "pair" else slot

    def line_copy(self, n, k, spot, other, arriving):
        flow = self.parts[n].flows[k]
        way, steps = spot
        shard = self.shard(spot, other)
        line = self.place.line + way * steps
        left = steps if arriving else steps - 1
        return self.copy(
            self.piece(n, k, shard, self.place.side),
            self.lanes[n][k][2].at[self.line_slot(flow, way, left, other, line)],
            (n, k, "line", way, left, other),
            self.place.ahead(way),
        )

    def stage_line(self, spot):
        place = self.place
        there = self.there(spot)
        way, steps = spot
        side = place.side
        todo = []
        for n, part in enumerate(self.parts):
            for k, flow in enumerate(part.flows):
                if flow[2] == "line":
                    shard = self.shard(spot, False)

                    def add(n=n, k=k, shard=shard):
                        self.pair_copy(n, k, spot, shard).wait_recv()
                        slot = place.line + way * steps
                        piece = self.piece(n, k, shard, side)
                        piece[...] = piece[...] + self.lanes[n][k][1][slot]

                    when([there], add)
                for other in (True, False) if flow[2] == "pair" else (False,):
                    for direction in (1, -1) if steps == 0 else (way,):
                        here = (direction, steps)

                        def add_line(n=n, k=k, other=other, here=here, flow=flow):
                            self.line_copy(n, k, here, other, True).wait_recv()
                            shard = self.shard(here, other)
                            piece = self.piece(n, k, shard, side)
                            slot = self.line_slot(
                                flow, here[0], here[1], other, place.line + here[0] * here[1]
                            )
                            piece[...] = piece[...] + self.lanes[n][k][2][slot]

                        when([there, place.can(-direction)], add_line)
                    if steps > 0:
                        todo.append(
                            lambda n=n, k=k, other=other: self.start(
                                [there], self.line_copy(n, k, spot, other, False)
                            )
                        )
        for action in todo:
            action()

    def out_view(self, n, k, core, side):
        part = self.parts[n]
        rows, columns = part.outer(part.flows[k], core, side)
        return self.outs[n].at[rows, columns]

    def out_copy(self, n, k, key, peer, core, side):
        view = self.out_view(n, k, core, side)
        return self.copy(view, view, (n, k, key), peer)

    def last(self):
        place = self.place
        core, side = place.core, place.side
        spot = (1, 0)
        here = place.shard
        everything = [(n, k) for n, part in enumerate(self.parts) for k in range(len(part.flows))]
        for n, k in everything:
            if self.parts[n].flows[k][2] == "pair":
                self.start([], self.pair_copy(n, k, spot, self.shard(spot, True)))
        for n, k in everything:
            if self.parts[n].flows[k][2] == "pair":
                self.pair_copy(n, k, spot, here).wait_recv()
                piece = self.piece(n, k, here, side)
                piece[...] = piece[...] + self.lanes[n][k][1][0]

        def swap(n, k):
            return self.copy(
                self.piece(n, k, here, side),
                self.lanes[n][k][0].at[0],
                (n, k, "sideend"),
                place.beside(),
            )

        for n, k in everything:
            if not self.parts[n].flows[k][3]:
                self.start([], swap(n, k))
        for n, k in everything:
            if self.parts[n].flows[k][3]:
                self.out_view(n, k, core, side)[...] = self.piece(n, k, here, side)[...]
        for n, k in everything:
            if self.parts[n].flows[k][3]:
                self.start([], self.out_copy(n, k, "sideend", place.beside(), core, side))
                self.start([], self.out_copy(n, k, "twinend", place.twin(), core, side))
        for n, k in everything:
            if not self.parts[n].flows[k][3]:
                swap(n, k).wait_recv()
                self.out_view(n, k, core, side)[...] = (
                    self.piece(n, k, here, side)[...] + self.lanes[n][k][0][0]
                )
        for n, k in everything:
            if not self.parts[n].flows[k][3] and self.parts[n].along:
                self.start([], self.out_copy(n, k, "twinend", place.twin(), core, side))
        for n, k in everything:
            if not self.parts[n].along:
                self.start([], self.whole(n, k))
        for n, k in everything:
            if self.parts[n].flows[k][3]:
                self.out_copy(n, k, "sideend", place.beside(), core, 1 - side).wait_recv()
                self.start([], self.out_copy(n, k, "twinsideend", place.twin(), core, 1 - side))
        for n, k in everything:
            if self.parts[n].along:
                self.out_copy(n, k, "twinend", place.twin(), 1 - core, side).wait_recv()
                if self.parts[n].flows[k][3]:
                    self.out_copy(
                        n, k, "twinsideend", place.twin(), 1 - core, 1 - side
                    ).wait_recv()
            else:
                self.whole(n, k).wait_recv()
        for conditions, copy in self.sent:
            when(conditions, copy.wait_send)
        for n, k in everything:
            if not self.parts[n].along:
                view = self.out_view(n, k, core, side)
                view[...] = view[...] + self.other[n][...]

    def whole(self, n, k):
        return self.copy(
            self.out_view(n, k, self.place.core, self.place.side),
            self.other[n],
            (n, k, "twinend"),
            self.place.twin(),
        )

    def steps(self):
        todo = [lambda n=n: self.begin(n) for n in range(len(self.parts))]
        for tick in range(len(SPOTS) + 2):
            if tick < len(SPOTS):
                todo.append(lambda spot=SPOTS[tick]: self.stage_cores(spot))
            if 0 <= tick - 1 < len(SPOTS):
                todo.append(lambda spot=SPOTS[tick - 1]: self.stage_sides(spot))
            if 0 <= tick - 2 < len(SPOTS):
                todo.append(lambda spot=SPOTS[tick - 2]: self.stage_line(spot))
        todo.append(self.last)
        return todo


def reduce_kernel(parts, *refs):
    count = len(parts)
    grads, outs = refs[:count], refs[count : 2 * count]
    scratch, (send, recv, load) = refs[2 * count : -3], refs[-3:]
    place = Place()
    greet(place)
    work = Reduce(place, parts, grads, outs, scratch, send, recv, load)
    for step in work.steps():
        step()


def reduce_call(arrays, parts, collective_id):
    labels = reduce_labels(parts)
    count = len(arrays)
    return pl.pallas_call(
        functools.partial(reduce_kernel, parts),
        out_shape=[jax.ShapeDtypeStruct((p.rows, p.columns), p.dtype) for p in parts],
        in_specs=[pl.BlockSpec(memory_space=pl.ANY)] * count,
        out_specs=[pl.BlockSpec(memory_space=pltpu.VMEM)] * count,
        scratch_shapes=reduce_scratch(parts)
        + [
            pltpu.SemaphoreType.DMA((len(labels.numbers),)),
            pltpu.SemaphoreType.DMA((len(labels.numbers),)),
            pltpu.SemaphoreType.DMA((count * 2 * len(SPOTS),)),
        ],
        compiler_params=pltpu.CompilerParams(
            collective_id=collective_id, has_side_effects=True, vmem_limit_bytes=63 << 20
        ),
        name="reduce_gradients",
    )(*arrays)


def column_part(rows, columns, shared, early):
    half = columns // 2
    part = (half - shared) // 2
    flows = []
    if shared:
        flows.append((lambda side: 0, shared, "line", False))
    if early:
        flows.append((lambda side: shared + side * part, early, "line", True))
    if part > early:
        flows.append((lambda side: shared + side * part + early, part - early, "pair", True))
    return Part(rows, columns, "columns", flows)


def row_part(rows, columns, shared, early):
    half = rows // 2
    part = (half - shared) // 2
    return Part(
        rows,
        columns,
        "rows",
        [
            (lambda side: 0, shared, "line", False),
            (lambda side: shared + side * part, early, "line", True),
            (lambda side: shared + side * part + early, part - early, "pair", True),
        ],
    )


def vector_part(rows, columns):
    return Part(rows, columns, None, [(lambda side: 0, columns, "line", False)], F32)


def exact_gelu(hidden):
    return jax.nn.gelu(hidden, approximate=False)


def plain_product(left, right):
    return jnp.dot(left, right, preferred_element_type=F32)


def left_product(left, right):
    return lax.dot_general(left, right, (((0,), (0,)), ((), ())), preferred_element_type=F32)


def right_product(left, right):
    return lax.dot_general(left, right, (((1,), (1,)), ((), ())), preferred_element_type=F32)


def column_sums(rows):
    return jnp.sum(rows.astype(F32), axis=0)


def norm_parts(total):
    average = jnp.mean(total, axis=-1, keepdims=True)
    centered = total - average
    variance = jnp.mean(centered * centered, axis=-1, keepdims=True)
    rate = lax.rsqrt(variance + EPSILON)
    return centered * rate, rate


def norm_back(unit, rate, grad):
    return rate * (
        grad
        - jnp.mean(grad, axis=-1, keepdims=True)
        - unit * jnp.mean(grad * unit, axis=-1, keepdims=True)
    )


def split_columns(packed, widths):
    pieces = []
    start = 0
    for width in widths:
        pieces.append(packed[..., start : start + width])
        start += width
    return pieces


def attention_forward(queries, keys_all, values_all, key_valid, heads):
    shape = queries.shape[:2] + (heads, HEAD_DIM)
    key_shape = keys_all.shape[:2] + (heads, HEAD_DIM)
    scores = jnp.einsum(
        "sqhd,skhd->shqk",
        queries.reshape(shape),
        keys_all.reshape(key_shape),
        preferred_element_type=F32,
    ) * (HEAD_DIM**-0.5)
    scores = jnp.where(key_valid[:, None, None, :], scores, -1e30)
    top = jnp.max(scores, axis=-1, keepdims=True)
    weights = jnp.exp(scores - top)
    probs = (weights / jnp.sum(weights, axis=-1, keepdims=True)).astype(BF16)
    context = jnp.einsum(
        "shqk,skhd->sqhd", probs, values_all.reshape(key_shape), preferred_element_type=F32
    )
    return context.reshape(queries.shape).astype(BF16), probs


def attention_backward(queries, keys_all, values_all, probs, context_grad, heads):
    shape = queries.shape[:2] + (heads, HEAD_DIM)
    key_shape = keys_all.shape[:2] + (heads, HEAD_DIM)
    scale = HEAD_DIM**-0.5
    grad_heads = context_grad.reshape(shape)
    wide = probs.astype(F32)
    probs_grad = jnp.einsum(
        "sqhd,skhd->shqk", grad_heads, values_all.reshape(key_shape), preferred_element_type=F32
    )
    inner_total = jnp.sum(wide * probs_grad, axis=-1, keepdims=True)
    scores_grad = (wide * (probs_grad - inner_total)).astype(BF16)
    query_grad = jnp.einsum(
        "shqk,skhd->sqhd", scores_grad, keys_all.reshape(key_shape), preferred_element_type=F32
    )
    key_part = jnp.einsum(
        "shqk,sqhd->skhd", scores_grad, queries.reshape(shape), preferred_element_type=F32
    )
    value_part = jnp.einsum("shqk,sqhd->skhd", probs, grad_heads, preferred_element_type=F32)
    return (
        (query_grad * scale).astype(BF16).reshape(queries.shape),
        (key_part * scale).astype(BF16).reshape(keys_all.shape),
        value_part.astype(BF16).reshape(values_all.shape),
    )


def direct(width):
    return lax.axis_size("fsdp") == LINE * PAIR and lax.axis_size("ctx") == 4 and width % 1024 == 0


def gather_all(vectors, qkv, output, inner, outer):
    arrays = (qkv, output, inner, outer)
    if not direct(output.shape[1]):
        return (lax.all_gather(vectors, "fsdp", axis=0, tiled=False),) + tuple(
            gather_rows(part) for part in arrays
        )
    shards = lax.axis_size("fsdp")
    lanes = 128
    rows = -(-vectors.shape[0] // (16 * lanes)) * 16
    table = jnp.pad(vectors, (0, rows * lanes - vectors.shape[0])).reshape(rows, lanes)
    flows = [Flow(0, rows, lambda core, side: (0, rows, 0, lanes), cores=False)]
    flows += gather_columns(1, qkv)
    flows += gather_columns(2, output)
    flows += gather_columns(3, inner)
    flows += gather_lines(4, outer)
    full = gather_call((table,) + arrays, flows, shards, 1)
    packed = full[0].reshape(shards, rows * lanes)[:, : vectors.shape[0]]
    return (packed,) + tuple(full[1:])


def near(value, share, unit):
    return int(round(value * share / unit)) * unit


def gather_columns(number, shard):
    rows, columns = shard.shape
    half = columns // 2
    shared = half - 2 * near(half, 0.32, 128)
    return column_flows(number, rows, columns, shared, max(128, near(half - shared, 0.3, 128)))


def gather_lines(number, shard):
    rows, columns = shard.shape
    half = rows // 2
    shared = half - 2 * near(half, 0.32, 16)
    return row_flows(number, rows, columns, shared, near(half - shared, 0.3, 16))


def reduce_columns(rows, columns):
    half = columns // 2
    shared = half - 2 * near(half, 0.25, 128)
    return column_part(rows, columns, shared, near(half - shared, 0.25, 128))


def reduce_lines(rows, columns):
    half = rows // 2
    shared = half - 2 * near(half, 0.25, 16)
    return row_part(rows, columns, shared, near(half - shared, 0.25, 16))


def reduce_all(vectors, qkv, output, inner, outer):
    shards, count = vectors.shape
    if not direct(output.shape[1]):
        share = lax.psum_scatter(vectors, "fsdp", scatter_dimension=0, tiled=True)
        return (lax.psum(share, "ctx")[0],) + tuple(
            reduce_rows(part) for part in (qkv, output, inner, outer)
        )
    lanes = 128
    rows = -(-count // (16 * lanes)) * 16
    table = jnp.pad(vectors, ((0, 0), (0, rows * lanes - count))).reshape(shards * rows, lanes)
    parts = [
        reduce_columns(inner.shape[0] // shards, inner.shape[1]),
        reduce_lines(outer.shape[0] // shards, outer.shape[1]),
        reduce_columns(output.shape[0] // shards, output.shape[1]),
        reduce_columns(qkv.shape[0] // shards, qkv.shape[1]),
        vector_part(rows, lanes),
    ]
    sums = reduce_call((inner, outer, output, qkv, table), parts, 2)
    share = sums[4].reshape(-1)[:count]
    return (share, sums[3].astype(F32), sums[2].astype(F32), sums[0].astype(F32), sums[1].astype(F32))


def gather_rows(part):
    return lax.all_gather(part, "fsdp", axis=0, tiled=True)


def reduce_rows(part):
    share = lax.psum_scatter(part.astype(BF16), "fsdp", scatter_dimension=0, tiled=True)
    return lax.psum(share, "ctx").astype(F32)


def body(
    inputs,
    cotangent,
    lengths,
    query_weight,
    key_weight,
    value_weight,
    output_weight,
    query_bias,
    value_bias,
    output_bias,
    first_gain,
    first_shift,
    inner_weight,
    inner_bias,
    outer_weight,
    outer_bias,
    second_gain,
    second_shift,
):
    vectors = (
        query_bias,
        value_bias,
        output_bias,
        first_gain,
        first_shift,
        inner_bias,
        outer_bias,
        second_gain,
        second_shift,
    )
    widths = [member.shape[0] for member in vectors]
    packed, full_qkv, full_output, full_inner, full_outer = gather_all(
        jnp.concatenate(vectors),
        jnp.concatenate((query_weight, key_weight, value_weight), axis=1),
        output_weight,
        inner_weight,
        outer_weight,
    )
    (
        bias_query,
        bias_value,
        bias_output,
        gain_first,
        shift_first,
        bias_inner,
        bias_outer,
        gain_second,
        shift_second,
    ) = [piece.reshape(-1).astype(F32) for piece in split_columns(packed, widths)]
    micro, seqs, block_len, width = inputs.shape
    heads = width // HEAD_DIM
    ctx_size = lax.axis_size("ctx")
    total_slots = block_len * ctx_size
    group = micro * seqs
    rows = group * block_len
    flat_len = lengths.reshape(group)
    local_pos = lax.axis_index("ctx") * block_len + jnp.arange(block_len, dtype=jnp.int32)
    row_mask = (local_pos[None, :] < flat_len[:, None]).astype(F32).reshape(rows, 1)
    key_valid = jnp.arange(total_slots, dtype=jnp.int32)[None, :] < flat_len[:, None]

    flat_rows = inputs.reshape(rows, width)
    qkv = plain_product(flat_rows, full_qkv)
    queries = (qkv[:, :width] + bias_query).astype(BF16)
    keys_values = jnp.concatenate(
        (qkv[:, width : 2 * width], qkv[:, 2 * width :] + bias_value), axis=1
    ).astype(BF16)
    keys_values_all = lax.all_gather(
        keys_values.reshape(group, block_len, 2 * width), "ctx", axis=1, tiled=True
    )
    keys_all = keys_values_all[:, :, :width]
    values_all = keys_values_all[:, :, width:]
    queries3 = queries.reshape(group, block_len, width)
    context, probs = attention_forward(queries3, keys_all, values_all, key_valid, heads)
    context = context.reshape(rows, width)

    first_sum = flat_rows.astype(F32) + plain_product(context, full_output) + bias_output
    first_unit, first_rate = norm_parts(first_sum)
    normed = first_unit * gain_first + shift_first
    normed_low = normed.astype(BF16)
    hidden = plain_product(normed_low, full_inner) + bias_inner
    active, gelu_back = jax.vjp(exact_gelu, hidden)
    active_low = active.astype(BF16)
    second_sum = normed + plain_product(active_low, full_outer) + bias_outer
    second_unit, second_rate = norm_parts(second_sum)
    output = ((second_unit * gain_second + shift_second) * row_mask).astype(BF16)

    out_grad = cotangent.reshape(rows, width).astype(F32) * row_mask
    second_gain_part = jnp.sum(out_grad * second_unit, axis=0)
    second_shift_part = jnp.sum(out_grad, axis=0)
    second_grad = norm_back(second_unit, second_rate, out_grad * gain_second)
    second_low = second_grad.astype(BF16)
    outer_weight_part = left_product(active_low, second_low).astype(BF16)
    outer_bias_part = column_sums(second_low)
    (hidden_grad,) = gelu_back(right_product(second_low, full_outer))
    hidden_low = hidden_grad.astype(BF16)
    inner_weight_part = left_product(normed_low, hidden_low).astype(BF16)
    inner_bias_part = column_sums(hidden_low)
    normed_grad = second_grad + right_product(hidden_low, full_inner)
    first_gain_part = jnp.sum(normed_grad * first_unit, axis=0)
    first_shift_part = jnp.sum(normed_grad, axis=0)
    first_grad = norm_back(first_unit, first_rate, normed_grad * gain_first)
    branch_low = first_grad.astype(BF16)
    output_weight_part = left_product(context, branch_low).astype(BF16)
    output_bias_part = column_sums(branch_low)
    context_grad = right_product(branch_low, full_output).astype(BF16)
    query_grad, key_part, value_part = attention_backward(
        queries3, keys_all, values_all, probs, context_grad.reshape(queries3.shape), heads
    )
    keys_values_grad = lax.psum_scatter(
        jnp.concatenate((key_part, value_part), axis=2), "ctx", scatter_dimension=1, tiled=True
    ).reshape(rows, 2 * width)
    qkv_grad = jnp.concatenate((query_grad.reshape(rows, width), keys_values_grad), axis=1)
    qkv_weight_part = left_product(flat_rows, qkv_grad).astype(BF16)
    query_bias_part = column_sums(qkv_grad[:, :width])
    value_bias_part = column_sums(qkv_grad[:, 2 * width :])
    input_grad = first_grad + right_product(qkv_grad, full_qkv)

    vector_parts = (
        query_bias_part,
        value_bias_part,
        output_bias_part,
        first_gain_part,
        first_shift_part,
        inner_bias_part,
        outer_bias_part,
        second_gain_part,
        second_shift_part,
    )
    fsdp_size = lax.axis_size("fsdp")
    packed_parts = jnp.concatenate(
        [part.reshape(fsdp_size, -1) for part in vector_parts], axis=1
    )
    vector_share, qkv_share, output_share, inner_share, outer_share = reduce_all(
        packed_parts, qkv_weight_part, output_weight_part, inner_weight_part, outer_weight_part
    )
    shares = split_columns(vector_share, widths)
    query_share, key_share, value_share = split_columns(qkv_share, [width] * 3)
    return (
        output.reshape(inputs.shape),
        input_grad.reshape(inputs.shape),
        query_share,
        key_share,
        value_share,
        output_share,
        shares[0],
        shares[1],
        shares[2],
        shares[3],
        shares[4],
        inner_share,
        shares[5],
        outer_share,
        shares[6],
        shares[7],
        shares[8],
    )


def solution(mesh):
    data = P(None, "fsdp", "ctx", None)
    matrix = P("fsdp", None)
    vector = P("fsdp")
    return jax.shard_map(
        body,
        mesh=mesh,
        in_specs=(data, data, P(None, "fsdp"))
        + (matrix,) * 4
        + (vector,) * 5
        + (matrix, vector, matrix, vector, vector, vector),
        out_specs=(data, data)
        + (matrix,) * 4
        + (vector,) * 5
        + (matrix, vector, matrix, vector, vector, vector),
        check_vma=False,
    )
```

```python
import functools

import jax
import jax.numpy as jnp
from jax import lax
from jax.experimental import pallas as pl
from jax.experimental.pallas import tpu as pltpu
from jax.sharding import PartitionSpec as P

HEAD_DIM = 64
EPSILON = 1e-06
F32 = jnp.float32
BF16 = jnp.bfloat16

GATHER_SPLIT = ((512, 256), (256, 128), (512, 512), (128, 48))
REDUCE_SPLIT = ((768, 256), (128, 32), (256, 128), (1024, 128))
GATHER_ORDER = (
    5, 11, 7, 2, 22, 1, 3, 19, 4, 6, 33, 16, 70, 14, 0, 13, 8, 71, 75, 9, 10, 37, 69, 35, 78, 36,
    31, 18, 43, 79, 86, 41, 81, 82, 73, 32, 76, 24, 38, 26, 74, 40, 17, 34, 46, 29, 72, 12, 21,
    15, 42, 83, 147, 109, 88, 146, 50, 44, 80, 56, 89, 77, 45, 52, 145, 48, 90, 84, 108, 20, 92,
    27, 54, 62, 149, 47, 51, 39, 28, 23, 100, 152, 95, 30, 111, 60, 107, 114, 97, 117, 91, 116,
    98, 49, 151, 110, 57, 148, 119, 154, 113, 155, 124, 85, 102, 59, 58, 63, 126, 150, 157, 93,
    64, 223, 67, 65, 121, 122, 222, 25, 94, 96, 156, 53, 105, 55, 221, 128, 153, 120, 112, 160,
    118, 103, 183, 115, 99, 187, 61, 101, 159, 68, 135, 184, 164, 162, 166, 130, 133, 228, 225,
    158, 106, 190, 193, 127, 138, 176, 185, 123, 230, 132, 170, 143, 171, 202, 227, 194, 168, 163,
    231, 224, 87, 247, 125, 209, 140, 165, 189, 131, 242, 104, 161, 232, 66, 191, 195, 204, 139,
    240, 208, 167, 192, 212, 236, 233, 173, 174, 197, 250, 249, 186, 246, 181, 169, 226, 136, 179,
    248, 144, 257, 211, 141, 252, 172, 219, 235, 229, 258, 196, 198, 205, 200, 206, 217, 244, 251,
    203, 214, 243, 210, 238, 201, 129, 241, 178, 177, 180, 207, 254, 175, 188, 134, 255, 253, 216,
    245, 218, 137, 237, 234, 142, 213, 199, 239, 182, 215, 256, 220, 259,
)
REDUCE_ORDER = (
    1, 28, 0, 2, 17, 4, 14, 3, 5, 8, 6, 214, 7, 18, 9, 30, 34, 220, 10, 13, 16, 12, 23, 15, 21,
    22, 11, 19, 31, 217, 20, 32, 218, 29, 215, 36, 25, 33, 216, 24, 26, 219, 222, 35, 224, 221,
    223, 37, 39, 27, 225, 42, 38, 226, 227, 53, 43, 40, 69, 84, 45, 67, 68, 228, 41, 51, 55, 70,
    44, 57, 87, 85, 73, 74, 71, 135, 46, 72, 88, 86, 47, 59, 136, 138, 139, 89, 133, 52, 137, 77,
    58, 134, 91, 75, 76, 166, 90, 229, 54, 167, 61, 165, 168, 170, 56, 171, 78, 48, 94, 122, 92,
    169, 118, 119, 116, 63, 117, 60, 79, 102, 80, 123, 93, 95, 100, 49, 96, 120, 121, 141, 173,
    81, 126, 127, 140, 149, 143, 142, 161, 151, 199, 110, 106, 97, 108, 124, 125, 98, 172, 185,
    197, 183, 128, 187, 144, 104, 157, 198, 181, 145, 159, 62, 175, 200, 191, 203, 193, 209, 201,
    174, 202, 177, 176, 64, 146, 65, 147, 155, 101, 204, 153, 103, 129, 205, 184, 206, 130, 152,
    150, 50, 82, 207, 66, 99, 182, 178, 208, 107, 179, 188, 189, 105, 154, 210, 211, 112, 186,
    156, 131, 109, 111, 148, 160, 158, 192, 83, 190, 212, 162, 163, 113, 114, 132, 194, 164, 195,
    180, 115, 213, 196, 230,
)

MESH = pl.DeviceIdType.MESH
LINE = 4
PAIR = 2


class Place:
    def __init__(self):
        self.ctx = lax.axis_index("ctx")
        self.shard = lax.axis_index("fsdp")
        self.side = lax.div(self.ctx, 2)
        self.core = lax.rem(self.ctx, 2)
        self.line = lax.div(self.shard, PAIR)
        self.pair = lax.rem(self.shard, PAIR)

    def ahead(self, way):
        return (self.ctx, self.shard + way * PAIR)

    def across(self):
        return (self.ctx, self.shard + 1 - 2 * self.pair)

    def beside(self):
        return (self.ctx + 2 - 4 * self.side, self.shard)

    def twin(self):
        return (self.ctx + 1 - 2 * self.core, self.shard)

    def has(self, way, steps):
        if steps == 0:
            return None
        return self.line >= steps if way > 0 else self.line <= LINE - 1 - steps

    def can(self, way):
        return self.line <= LINE - 2 if way > 0 else self.line >= 1

    def shard_of(self, way, steps, other):
        pair = 1 - self.pair if other else self.pair
        return (self.line - way * steps) * PAIR + pair


def when(conditions, action):
    held = [c for c in conditions if c is not None]
    if not held:
        action()
        return
    both = held[0]
    for c in held[1:]:
        both = jnp.logical_and(both, c)
    pl.when(both)(action)


def greet(place):
    barrier = pltpu.get_barrier_semaphore()
    for peer in (place.across(), place.beside(), place.twin()):
        pl.semaphore_signal(barrier, inc=1, device_id=peer, device_id_type=MESH)
    for way in (1, -1):
        when(
            [place.can(way)],
            lambda way=way: pl.semaphore_signal(
                barrier, inc=1, device_id=place.ahead(way), device_id_type=MESH
            ),
        )
    lines = jnp.minimum(place.line, 1) + jnp.minimum(LINE - 1 - place.line, 1)
    pl.semaphore_wait(barrier, 3 + lines)


class Flow:
    def __init__(self, array, shard_rows, region, order="line", sides=False, cores=True):
        self.array = array
        self.shard_rows = shard_rows
        self.region = region
        self.order = order
        self.sides = sides
        self.cores = cores

    def view(self, ref, shard, core, side):
        row, rows, column, columns = self.region(core, side)
        start = row if shard is None else shard * self.shard_rows + row
        if not isinstance(start, int):
            start = pl.multiple_of(start, 16)
        if not isinstance(column, int):
            column = pl.multiple_of(column, 128)
        return ref.at[pl.ds(start, rows), pl.ds(column, columns)]


def positions(order):
    found = []
    if order == "line":
        found.append(("P", 1, 0, True))
        for steps in range(1, LINE):
            for way in (1, -1):
                found.append(("L", way, steps, False))
                found.append(("P", way, steps, True))
    else:
        found.append(("P", 1, 0, True))
        for steps in range(1, LINE):
            for way in (1, -1):
                found.append(("L", way, steps, False))
                found.append(("L", way, steps, True))
    return found


class Labels:
    def __init__(self):
        self.numbers = {}

    def __call__(self, key):
        return self.numbers.setdefault(key, len(self.numbers))


def gather_labels(flows):
    labels = Labels()
    for number, flow in enumerate(flows):
        for spot in positions(flow.order):
            labels((number, "in") + spot)
            if flow.sides:
                labels((number, "side") + spot)
            if flow.cores:
                labels((number, "twin") + spot)
                if flow.sides:
                    labels((number, "twinside") + spot)
    return labels


class Gather:
    def __init__(self, place, flows, owns, fulls, send, recv):
        self.place, self.flows, self.owns, self.fulls = place, flows, owns, fulls
        self.send, self.recv = send, recv
        self.labels = gather_labels(flows)
        self.sent = []

    def copy(self, number, key, spot, peer, core, side, own=False):
        flow = self.flows[number]
        place = self.place
        if own:
            shard = place.shard
            source = flow.view(self.owns[flow.array], None, core, side)
        else:
            shard = place.shard_of(*spot[1:])
            source = flow.view(self.fulls[flow.array], shard, core, side)
        target = flow.view(self.fulls[flow.array], shard, core, side)
        label = self.labels((number,) + key)
        return pltpu.make_async_remote_copy(
            source,
            target,
            self.send.at[label],
            self.recv.at[label],
            device_id=peer,
            device_id_type=MESH,
        )

    def start(self, conditions, copy):
        when(conditions, copy.start)
        self.sent.append((conditions, copy))

    def begin(self, number):
        flow, place = self.flows[number], self.place
        core, side = place.core, place.side
        here = (None, 1, 0, False)
        for way in (1, -1):
            self.start(
                [place.can(way)],
                self.copy(
                    number, ("in", "L", way, 1, False), here, place.ahead(way), core, side, True
                ),
            )
        self.start(
            [],
            self.copy(number, ("in", "P", 1, 0, True), here, place.across(), core, side, True),
        )

    def arrive(self, number, spot):
        flow, place = self.flows[number], self.place
        kind, way, steps, other = spot
        core, side = place.core, place.side
        there = place.has(way, steps)

        def take():
            self.copy(number, ("in",) + spot, spot, place.across(), core, side).wait_recv()

        when([there], take)

        def onward(extra, key, peer):
            self.start(
                [c for c in (there, extra) if c is not None],
                self.copy(number, key, spot, peer, core, side),
            )

        if kind == "L" and steps + 1 < LINE:
            onward(place.can(way), ("in", "L", way, steps + 1, other), place.ahead(way))
        if kind == "L" and flow.order == "line":
            onward(None, ("in", "P", way, steps, True), place.across())
        if kind == "P" and flow.order == "pair":
            for direction in (1, -1):
                onward(
                    place.can(direction), ("in", "L", direction, 1, True), place.ahead(direction)
                )
        if flow.sides:
            onward(None, ("side",) + spot, place.beside())
        if flow.cores:
            onward(None, ("twin",) + spot, place.twin())

    def arrive_side(self, number, spot):
        flow, place = self.flows[number], self.place
        there = place.has(*spot[1:3])
        core, side = place.core, 1 - place.side
        when(
            [there],
            lambda: self.copy(
                number, ("side",) + spot, spot, place.beside(), core, side
            ).wait_recv(),
        )
        if flow.cores:
            self.start(
                [there] if there is not None else [],
                self.copy(number, ("twinside",) + spot, spot, place.twin(), core, side),
            )

    def arrive_twin(self, number, spot):
        flow, place = self.flows[number], self.place
        there = place.has(*spot[1:3])
        core = 1 - place.core
        if flow.cores:
            when(
                [there],
                lambda: self.copy(
                    number, ("twin",) + spot, spot, place.twin(), core, place.side
                ).wait_recv(),
            )
            if flow.sides:
                when(
                    [there],
                    lambda: self.copy(
                        number, ("twinside",) + spot, spot, place.twin(), core, 1 - place.side
                    ).wait_recv(),
                )

    def actions(self):
        found = []
        for n, flow in enumerate(self.flows):
            found.append((("begin", n), lambda n=n: self.begin(n)))
        for index in range(len(positions("line"))):
            for n, flow in enumerate(self.flows):
                spot = positions(flow.order)[index]
                found.append((("in", n, spot), lambda n=n, spot=spot: self.arrive(n, spot)))
                if flow.sides:
                    found.append(
                        (("side", n, spot), lambda n=n, spot=spot: self.arrive_side(n, spot))
                    )
        found.append((("last",), self.finish))
        return found

    def finish(self):
        for number, flow in enumerate(self.flows):
            for spot in positions(flow.order):
                self.arrive_twin(number, spot)
        for conditions, copy in self.sent:
            when(conditions, copy.wait_send)


class Swap:
    def __init__(self, place, ins, outs, send, recv, local):
        side = place.side
        self.away = [
            pltpu.make_async_remote_copy(
                here.at[1 - side],
                there.at[side],
                send.at[k],
                recv.at[k],
                device_id=place.beside(),
                device_id_type=MESH,
            )
            for k, (here, there) in enumerate(zip(ins, outs))
        ]
        self.stay = [
            pltpu.make_async_copy(here.at[side], there.at[side], local.at[k])
            for k, (here, there) in enumerate(zip(ins, outs))
        ]

    def start(self):
        for copy in self.away + self.stay:
            copy.start()

    def finish(self):
        for copy in self.away + self.stay:
            copy.wait()


def swap_scratch(count):
    return [pltpu.SemaphoreType.DMA((count,))] * 3


def gather_kernel(flows, count, blocks, order, *refs):
    owns, refs = refs[:count], refs[count:]
    ins, refs = refs[:blocks], refs[blocks:]
    fulls, refs = refs[:count], refs[count:]
    outs, refs = refs[:blocks], refs[blocks:]
    send, recv, local = refs[:3]
    place = Place()
    keep = [
        pltpu.make_async_copy(
            owns[k], fulls[k].at[pl.ds(place.shard * owns[k].shape[0], owns[k].shape[0]), :], local.at[k]
        )
        for k in range(count)
    ]
    greet(place)
    swap = Swap(place, ins, outs, *refs[3:])
    swap.start()
    work = Gather(place, flows, owns, fulls, send, recv)
    for copy in keep:
        copy.start()
    for step in in_order(work.actions(), order):
        step()
    for copy in keep:
        copy.wait()
    swap.finish()


def gather_call(arrays, blocks, flows, shards, collective_id, order=None):
    labels = gather_labels(flows)
    count = len(arrays)
    return pl.pallas_call(
        functools.partial(gather_kernel, flows, count, len(blocks), order),
        out_shape=[
            jax.ShapeDtypeStruct((shards * a.shape[0], a.shape[1]), a.dtype) for a in arrays
        ]
        + [jax.ShapeDtypeStruct(b.shape, b.dtype) for b in blocks],
        in_specs=[pl.BlockSpec(memory_space=pltpu.VMEM)] * (count + len(blocks)),
        out_specs=[pl.BlockSpec(memory_space=pl.ANY)] * (count + len(blocks)),
        scratch_shapes=[
            pltpu.SemaphoreType.DMA((len(labels.numbers),)),
            pltpu.SemaphoreType.DMA((len(labels.numbers),)),
            pltpu.SemaphoreType.DMA((count,)),
        ]
        + swap_scratch(len(blocks)),
        compiler_params=pltpu.CompilerParams(collective_id=collective_id, has_side_effects=True),
        name="gather_weights",
    )(*arrays, *blocks)


def column_flows(array, shard_rows, columns, shared, early):
    half = columns // 2
    part = (half - shared) // 2
    flows = []
    if shared:
        flows.append(
            Flow(array, shard_rows, lambda core, side: (0, shard_rows, core * half, shared))
        )
    if early:
        flows.append(
            Flow(
                array,
                shard_rows,
                lambda core, side: (0, shard_rows, core * half + shared + side * part, early),
                sides=True,
            )
        )
    if part > early:
        flows.append(
            Flow(
                array,
                shard_rows,
                lambda core, side: (
                    0,
                    shard_rows,
                    core * half + shared + side * part + early,
                    part - early,
                ),
                order="pair",
                sides=True,
            )
        )
    return flows


def row_flows(array, shard_rows, columns, shared, early):
    half = shard_rows // 2
    part = (half - shared) // 2
    return [
        Flow(array, shard_rows, lambda core, side: (core * half, shared, 0, columns)),
        Flow(
            array,
            shard_rows,
            lambda core, side: (core * half + shared + side * part, early, 0, columns),
            sides=True,
        ),
        Flow(
            array,
            shard_rows,
            lambda core, side: (core * half + shared + side * part + early, part - early, 0, columns),
            order="pair",
            sides=True,
        ),
    ]


class Part:
    def __init__(self, rows, columns, along, flows, dtype=BF16):
        self.rows, self.columns, self.along, self.dtype = rows, columns, along, dtype
        self.flows = flows
        self.half_rows = rows // 2 if along == "rows" else rows
        self.half_columns = columns // 2 if along == "columns" else columns

    def half(self, ref, shard, core):
        base = 0 if shard is None else pl.multiple_of(shard * self.rows, 16)
        if self.along == "rows":
            row = core * self.half_rows + (0 if shard is None else shard * self.rows)
            return ref.at[pl.ds(pl.multiple_of(row, 16), self.half_rows), :]
        if self.along == "columns":
            column = pl.multiple_of(core * self.half_columns, 128)
            return ref.at[pl.ds(base, self.rows), pl.ds(column, self.half_columns)]
        return ref.at[pl.ds(base, self.rows), :]

    def inner(self, flow, side):
        first, extent = flow[0](side), flow[1]
        if self.along == "rows":
            start = first if isinstance(first, int) else pl.multiple_of(first, 16)
            return pl.ds(start, extent), slice(None)
        start = first if isinstance(first, int) else pl.multiple_of(first, 128)
        return slice(None), pl.ds(start, extent)

    def outer(self, flow, core, side):
        first, extent = flow[0](side), flow[1]
        if self.along == "rows":
            return pl.ds(pl.multiple_of(core * self.half_rows + first, 16), extent), slice(None)
        if self.along == "columns":
            return slice(None), pl.ds(
                pl.multiple_of(core * self.half_columns + first, 128), extent
            )
        return slice(None), slice(None)

    def extent(self, flow):
        if self.along == "rows":
            return flow[1], self.half_columns
        return self.half_rows, flow[1]


SPOTS = [(1, 3), (-1, 3), (1, 2), (-1, 2), (1, 1), (-1, 1), (1, 0)]


def reduce_scratch(parts):
    shapes = []
    for part in parts:
        half = (LINE * PAIR, part.half_rows, part.half_columns)
        shapes.append(pltpu.VMEM(half, part.dtype))
        shapes.append(pltpu.VMEM(half if part.along else half[1:], part.dtype))
        for flow in part.flows:
            rows, columns = part.extent(flow)
            shapes.append(
                pltpu.VMEM((LINE * PAIR if flow[3] else 1, rows, columns), part.dtype)
            )
            shapes.append(
                pltpu.VMEM((LINE if flow[2] == "line" else 1, rows, columns), part.dtype)
            )
            shapes.append(
                pltpu.VMEM(
                    ((LINE + 1) * (1 if flow[2] == "line" else PAIR), rows, columns), part.dtype
                )
            )
    return shapes


def reduce_labels(parts):
    labels = Labels()
    for n, part in enumerate(parts):
        for way, steps in SPOTS:
            for other in (False, True):
                labels((n, "twin", way, steps, other))
        labels((n, "twinend"))
        for k, flow in enumerate(part.flows):
            for way, steps in SPOTS:
                for other in (False, True):
                    if flow[3]:
                        labels((n, k, "side", way, steps, other))
                    if flow[2] == "pair" or not other:
                        labels((n, k, "line", way, steps, other))
                        if steps == 0:
                            labels((n, k, "line", -way, steps, other))
                if flow[2] == "line" or steps == 0:
                    labels((n, k, "pair", way, steps))
            labels((n, k, "sideend"))
            labels((n, k, "twinend"))
            labels((n, k, "twinsideend"))
    return labels


class Reduce:
    def __init__(self, place, parts, grads, outs, scratch, send, recv, load):
        self.place, self.parts, self.grads, self.outs = place, parts, grads, outs
        self.send, self.recv, self.load = send, recv, load
        self.labels = reduce_labels(parts)
        self.sent = []
        self.own, self.other, self.lanes = [], [], []
        at = 0
        for part in parts:
            self.own.append(scratch[at])
            self.other.append(scratch[at + 1])
            at += 2
            lanes = []
            for _ in part.flows:
                lanes.append(scratch[at : at + 3])
                at += 3
            self.lanes.append(lanes)

    def copy(self, source, target, key, peer):
        label = self.labels(key)
        return pltpu.make_async_remote_copy(
            source,
            target,
            self.send.at[label],
            self.recv.at[label],
            device_id=peer,
            device_id_type=MESH,
        )

    def start(self, conditions, copy):
        when(conditions, copy.start)
        self.sent.append((conditions, copy))

    def there(self, spot):
        return self.place.has(-spot[0], spot[1])

    def shard(self, spot, other):
        return self.place.shard_of(-spot[0], spot[1], other)

    def keep(self, n, spot, other):
        shard = self.shard(spot, other)
        label = SPOTS.index(spot) * 2 + int(other)
        return pltpu.make_async_copy(
            self.parts[n].half(self.grads[n], shard, self.place.core),
            self.own[n].at[shard],
            self.load.at[n * 2 * len(SPOTS) + label],
        )

    def twin(self, n, spot, other, core):
        shard = self.shard(spot, other)
        return self.copy(
            self.parts[n].half(self.grads[n], shard, core),
            self.other[n].at[shard],
            (n, "twin") + spot + (other,),
            self.place.twin(),
        )

    def begin(self, n, spot):
        there = self.there(spot)
        for other in (True, False):
            when([there], self.keep(n, spot, other).start)
            if self.parts[n].along:
                self.start([there], self.twin(n, spot, other, 1 - self.place.core))

    def piece(self, n, k, shard, side):
        part = self.parts[n]
        rows, columns = part.inner(part.flows[k], side)
        return self.own[n].at[shard, rows, columns]

    def side_copy(self, n, k, spot, other, side):
        shard = self.shard(spot, other)
        return self.copy(
            self.piece(n, k, shard, side),
            self.lanes[n][k][0].at[shard],
            (n, k, "side") + spot + (other,),
            self.place.beside(),
        )

    def add_cores(self, n, spot):
        there = self.there(spot)
        part = self.parts[n]
        for other in (True, False):

            def add(other=other):
                shard = self.shard(spot, other)
                self.keep(n, spot, other).wait()
                if part.along:
                    self.twin(n, spot, other, self.place.core).wait_recv()
                    self.own[n][shard] = self.own[n][shard] + self.other[n][shard]

            when([there], add)
        for other in (True, False):
            for k, flow in enumerate(part.flows):
                if flow[3]:
                    self.start([there], self.side_copy(n, k, spot, other, 1 - self.place.side))
                elif other:
                    self.start([there], self.pair_copy(n, k, spot, self.shard(spot, True)))

    def pair_copy(self, n, k, spot, shard):
        flow = self.parts[n].flows[k]
        slot = self.place.line + spot[0] * spot[1] if flow[2] == "line" else 0
        return self.copy(
            self.piece(n, k, shard, self.place.side),
            self.lanes[n][k][1].at[slot],
            (n, k, "pair") + spot,
            self.place.across(),
        )

    def add_sides(self, n, k, spot):
        there = self.there(spot)
        side = self.place.side
        for other in (True, False):

            def add(other=other):
                shard = self.shard(spot, other)
                self.side_copy(n, k, spot, other, side).wait_recv()
                piece = self.piece(n, k, shard, side)
                piece[...] = piece[...] + self.lanes[n][k][0][shard]

            when([there], add)
        if self.parts[n].flows[k][2] == "line":
            self.start([there], self.pair_copy(n, k, spot, self.shard(spot, True)))

    def line_slot(self, flow, way, steps, other, line):
        slot = line if (steps > 0 or way > 0) else LINE
        return slot + (LINE + 1) * int(other) if flow[2] == "pair" else slot

    def line_copy(self, n, k, spot, other, arriving):
        flow = self.parts[n].flows[k]
        way, steps = spot
        shard = self.shard(spot, other)
        line = self.place.line + way * steps
        left = steps if arriving else steps - 1
        return self.copy(
            self.piece(n, k, shard, self.place.side),
            self.lanes[n][k][2].at[self.line_slot(flow, way, left, other, line)],
            (n, k, "line", way, left, other),
            self.place.ahead(way),
        )

    def add_line(self, n, k, spot):
        place = self.place
        there = self.there(spot)
        way, steps = spot
        side = place.side
        flow = self.parts[n].flows[k]
        if flow[2] == "line":

            def add():
                shard = self.shard(spot, False)
                self.pair_copy(n, k, spot, shard).wait_recv()
                piece = self.piece(n, k, shard, side)
                piece[...] = piece[...] + self.lanes[n][k][1][place.line + way * steps]

            when([there], add)
        for other in (True, False) if flow[2] == "pair" else (False,):
            for direction in (1, -1) if steps == 0 else (way,):

                def add_line(other=other, here=(direction, steps)):
                    self.line_copy(n, k, here, other, True).wait_recv()
                    piece = self.piece(n, k, self.shard(here, other), side)
                    line = place.line + here[0] * here[1]
                    slot = self.line_slot(flow, here[0], here[1], other, line)
                    piece[...] = piece[...] + self.lanes[n][k][2][slot]

                when([there, place.can(-direction)], add_line)
            if steps > 0:
                self.start([there], self.line_copy(n, k, spot, other, False))

    def send_pair(self, n, k):
        self.start([], self.pair_copy(n, k, (1, 0), self.shard((1, 0), True)))

    def send_swap(self, n, k):
        self.start([], self.swap(n, k))

    def settle(self, n, k):
        place = self.place
        core, side, here = place.core, place.side, place.shard
        part = self.parts[n]
        flow = part.flows[k]
        piece = self.piece(n, k, here, side)
        out = self.out_view(n, k, core, side)
        if flow[3]:
            if flow[2] == "pair":
                self.pair_copy(n, k, (1, 0), here).wait_recv()
                out[...] = piece[...] + self.lanes[n][k][1][0]
            else:
                out[...] = piece[...]
            self.start([], self.out_copy(n, k, "sideend", place.beside(), core, side))
        else:
            self.swap(n, k).wait_recv()
            out[...] = piece[...] + self.lanes[n][k][0][0]
        if part.along:
            self.start([], self.out_copy(n, k, "twinend", place.twin(), core, side))
        else:
            self.start([], self.whole(n, k))

    def settle_side(self, n, k):
        place = self.place
        core, side = place.core, 1 - place.side
        self.out_copy(n, k, "sideend", place.beside(), core, side).wait_recv()
        self.start([], self.out_copy(n, k, "twinsideend", place.twin(), core, side))

    def swap(self, n, k):
        return self.copy(
            self.piece(n, k, self.place.shard, self.place.side),
            self.lanes[n][k][0].at[0],
            (n, k, "sideend"),
            self.place.beside(),
        )

    def out_view(self, n, k, core, side):
        part = self.parts[n]
        rows, columns = part.outer(part.flows[k], core, side)
        return self.outs[n].at[rows, columns]

    def out_copy(self, n, k, key, peer, core, side):
        view = self.out_view(n, k, core, side)
        return self.copy(view, view, (n, k, key), peer)

    def last(self):
        place = self.place
        core, side = place.core, place.side
        everything = [(n, k) for n, part in enumerate(self.parts) for k in range(len(part.flows))]
        for n, k in everything:
            if self.parts[n].along:
                self.out_copy(n, k, "twinend", place.twin(), 1 - core, side).wait_recv()
                if self.parts[n].flows[k][3]:
                    self.out_copy(
                        n, k, "twinsideend", place.twin(), 1 - core, 1 - side
                    ).wait_recv()
            else:
                self.whole(n, k).wait_recv()
        for conditions, copy in self.sent:
            when(conditions, copy.wait_send)
        for n, k in everything:
            if not self.parts[n].along:
                view = self.out_view(n, k, core, side)
                view[...] = view[...] + self.other[n][...]

    def whole(self, n, k):
        return self.copy(
            self.out_view(n, k, self.place.core, self.place.side),
            self.other[n],
            (n, k, "twinend"),
            self.place.twin(),
        )

    def actions(self):
        found = []
        for n, part in enumerate(self.parts):
            for spot in SPOTS:
                found.append((("begin", n, spot), lambda n=n, s=spot: self.begin(n, s)))
        for n, part in enumerate(self.parts):
            for spot in SPOTS:
                found.append((("cores", n, spot), lambda n=n, s=spot: self.add_cores(n, s)))
            for k, flow in enumerate(part.flows):
                at = (n, k)
                for spot in SPOTS:
                    if flow[3]:
                        found.append(
                            (("sides", n, k, spot), lambda at=at, s=spot: self.add_sides(*at, s))
                        )
                    found.append(
                        (("line", n, k, spot), lambda at=at, s=spot: self.add_line(*at, s))
                    )
                if flow[2] == "pair":
                    found.append((("pair", n, k), lambda at=at: self.send_pair(*at)))
                if not flow[3]:
                    found.append((("swap", n, k), lambda at=at: self.send_swap(*at)))
                found.append((("settle", n, k), lambda at=at: self.settle(*at)))
                if flow[3]:
                    found.append((("after", n, k), lambda at=at: self.settle_side(*at)))
        found.append((("last",), self.last))
        return found


def in_order(actions, order):
    if order is None:
        return [action for _, action in actions]
    assert sorted(order) == list(range(len(actions)))
    return [actions[i][1] for i in order]


def reduce_kernel(parts, blocks, order, *refs):
    count = len(parts)
    grads, refs = refs[:count], refs[count:]
    ins, refs = refs[:blocks], refs[blocks:]
    outs, refs = refs[:count], refs[count:]
    swapped, refs = refs[:blocks], refs[blocks:]
    scratch, (send, recv, load), sems = refs[:-6], refs[-6:-3], refs[-3:]
    place = Place()
    greet(place)
    swap = Swap(place, ins, swapped, *sems)
    swap.start()
    work = Reduce(place, parts, grads, outs, scratch, send, recv, load)
    for step in in_order(work.actions(), order):
        step()
    swap.finish()


def reduce_call(arrays, blocks, parts, collective_id, order=None):
    labels = reduce_labels(parts)
    count = len(arrays)
    return pl.pallas_call(
        functools.partial(reduce_kernel, parts, len(blocks), order),
        out_shape=[jax.ShapeDtypeStruct((p.rows, p.columns), p.dtype) for p in parts]
        + [jax.ShapeDtypeStruct(b.shape, b.dtype) for b in blocks],
        in_specs=[pl.BlockSpec(memory_space=pl.ANY)] * (count + len(blocks)),
        out_specs=[pl.BlockSpec(memory_space=pltpu.VMEM)] * count
        + [pl.BlockSpec(memory_space=pl.ANY)] * len(blocks),
        scratch_shapes=reduce_scratch(parts)
        + [
            pltpu.SemaphoreType.DMA((len(labels.numbers),)),
            pltpu.SemaphoreType.DMA((len(labels.numbers),)),
            pltpu.SemaphoreType.DMA((count * 2 * len(SPOTS),)),
        ]
        + swap_scratch(len(blocks)),
        compiler_params=pltpu.CompilerParams(
            collective_id=collective_id, has_side_effects=True, vmem_limit_bytes=63 << 20
        ),
        name="reduce_gradients",
    )(*arrays, *blocks)


def column_part(rows, columns, shared, early):
    half = columns // 2
    part = (half - shared) // 2
    flows = []
    if shared:
        flows.append((lambda side: 0, shared, "line", False))
    if early:
        flows.append((lambda side: shared + side * part, early, "line", True))
    if part > early:
        flows.append((lambda side: shared + side * part + early, part - early, "pair", True))
    return Part(rows, columns, "columns", flows)


def row_part(rows, columns, shared, early):
    half = rows // 2
    part = (half - shared) // 2
    return Part(
        rows,
        columns,
        "rows",
        [
            (lambda side: 0, shared, "line", False),
            (lambda side: shared + side * part, early, "line", True),
            (lambda side: shared + side * part + early, part - early, "pair", True),
        ],
    )


def vector_part(rows, columns):
    return Part(rows, columns, None, [(lambda side: 0, columns, "line", False)], F32)


def attend_kernel(qkv_ref, bias_ref, context_ref, probs_ref, away_ref, send, recv):
    place = Place()
    rows, width = context_ref.shape
    pairs = width // (2 * HEAD_DIM)
    span = 2 * HEAD_DIM
    greet_twin(place)

    def columns(section, pair):
        return pl.ds(pl.multiple_of(section * width + pair * span, span), span)

    def fetch(which, pair):
        return pltpu.make_async_remote_copy(
            qkv_ref.at[:, columns(which + 1, pair)],
            away_ref.at[:, columns(which, pair)],
            send.at[which, pair],
            recv.at[which, pair],
            device_id=place.twin(),
            device_id_type=MESH,
        )

    for pair in range(pairs):
        for which in range(2):
            fetch(which, pair).start()
    lower = lax.broadcasted_iota(jnp.int32, (rows, span), 1) < HEAD_DIM
    bias = bias_ref[...]

    def step(pair, carry):
        for which in range(2):
            fetch(which, pair).wait_recv()
        query = qkv_ref[:, columns(0, pair)] * HEAD_DIM**-0.5
        stacked = stack_heads(query, lower)
        keys = jnp.concatenate((qkv_ref[:, columns(1, pair)], away_ref[:, columns(0, pair)]), axis=0)
        values = jnp.concatenate(
            (qkv_ref[:, columns(2, pair)], away_ref[:, columns(1, pair)]), axis=0
        )
        scores = right_product(stacked, keys) + bias
        top = jnp.max(scores, axis=1, keepdims=True)
        weights = jnp.exp(scores - top)
        total = jnp.sum(weights, axis=1, keepdims=True)
        probs = (weights * (1.0 / total)).astype(BF16)
        probs_ref[pair] = probs
        mixed = plain_product(probs, values)
        context_ref[:, columns(0, pair)] = jnp.where(lower, mixed[:rows], mixed[rows:]).astype(BF16)
        return carry

    lax.fori_loop(0, pairs, step, 0)
    for pair in range(pairs):
        for which in range(2):
            fetch(which, pair).wait_send()


def stack_heads(block, lower):
    zero = jnp.zeros_like(block)
    return jnp.concatenate((jnp.where(lower, block, zero), jnp.where(lower, zero, block)), axis=0)


def greet_twin(place):
    barrier = pltpu.get_barrier_semaphore()
    pl.semaphore_signal(barrier, inc=1, device_id=place.twin(), device_id_type=MESH)
    pl.semaphore_wait(barrier, 1)


def attend_back_kernel(
    qkv_ref, away_ref, probs_ref, grad_ref, out_ref, keep, leave, come, send, recv
):
    place = Place()
    rows, width = grad_ref.shape
    span = 2 * HEAD_DIM
    pairs = width // span
    greet_twin(place)

    def columns(section, pair):
        return pl.ds(pl.multiple_of(section * width + pair * span, span), span)

    def give(which, pair):
        return pltpu.make_async_remote_copy(
            leave.at[:, columns(which, pair)],
            come.at[:, columns(which, pair)],
            send.at[which, pair],
            recv.at[which, pair],
            device_id=place.twin(),
            device_id_type=MESH,
        )

    lower = lax.broadcasted_iota(jnp.int32, (rows, span), 1) < HEAD_DIM
    scale = HEAD_DIM**-0.5

    def step(pair, carry):
        stacked = stack_heads(qkv_ref[:, columns(0, pair)] * scale, lower)
        keys = jnp.concatenate((qkv_ref[:, columns(1, pair)], away_ref[:, columns(0, pair)]), axis=0)
        values = jnp.concatenate(
            (qkv_ref[:, columns(2, pair)], away_ref[:, columns(1, pair)]), axis=0
        )
        grad = stack_heads(grad_ref[:, columns(0, pair)], lower)
        probs = probs_ref[pair]
        value_part = left_product(probs, grad)
        probs_grad = right_product(grad, values)
        wide = probs.astype(F32)
        inner = jnp.sum(wide * probs_grad, axis=1, keepdims=True)
        scores_grad = (wide * (probs_grad - inner)).astype(BF16)
        key_part = left_product(scores_grad, stacked)
        leave[:, columns(0, pair)] = key_part[rows:].astype(BF16)
        leave[:, columns(1, pair)] = value_part[rows:].astype(BF16)
        keep[:, columns(0, pair)] = key_part[:rows]
        keep[:, columns(1, pair)] = value_part[:rows]
        mixed = plain_product(scores_grad, keys) * scale
        out_ref[:, columns(0, pair)] = jnp.where(lower, mixed[:rows], mixed[rows:]).astype(BF16)
        for which in range(2):
            give(which, pair).start()
        return carry

    lax.fori_loop(0, pairs, step, 0)

    def gather(pair, carry):
        for which in range(2):
            give(which, pair).wait_recv()
            here = columns(which, pair)
            out_ref[:, columns(which + 1, pair)] = (
                keep[:, here] + come[:, here].astype(F32)
            ).astype(BF16)
        return carry

    lax.fori_loop(0, pairs, gather, 0)
    for pair in range(pairs):
        for which in range(2):
            give(which, pair).wait_send()


def attend(qkv, bias, collective_id):
    rows, width = qkv.shape[0], qkv.shape[1] // 3
    pairs = width // (2 * HEAD_DIM)
    return pl.pallas_call(
        attend_kernel,
        out_shape=[
            jax.ShapeDtypeStruct((rows, width), BF16),
            jax.ShapeDtypeStruct((pairs, 2 * rows, 2 * rows), BF16),
            jax.ShapeDtypeStruct((rows, 2 * width), BF16),
        ],
        in_specs=[pl.BlockSpec(memory_space=pltpu.VMEM)] * 2,
        out_specs=[pl.BlockSpec(memory_space=pltpu.VMEM)] * 3,
        scratch_shapes=[pltpu.SemaphoreType.DMA((2, pairs)), pltpu.SemaphoreType.DMA((2, pairs))],
        compiler_params=pltpu.CompilerParams(
            collective_id=collective_id, has_side_effects=True, vmem_limit_bytes=40 << 20
        ),
        name="attention_forward",
    )(qkv, bias)


def attend_back(qkv, away, probs, grad, collective_id):
    rows, width = grad.shape
    pairs = width // (2 * HEAD_DIM)
    return pl.pallas_call(
        attend_back_kernel,
        out_shape=jax.ShapeDtypeStruct((rows, 3 * width), BF16),
        in_specs=[pl.BlockSpec(memory_space=pltpu.VMEM)] * 4,
        out_specs=pl.BlockSpec(memory_space=pltpu.VMEM),
        scratch_shapes=[
            pltpu.VMEM((rows, 2 * width), F32),
            pltpu.VMEM((rows, 2 * width), BF16),
            pltpu.VMEM((rows, 2 * width), BF16),
            pltpu.SemaphoreType.DMA((2, pairs)),
            pltpu.SemaphoreType.DMA((2, pairs)),
        ],
        compiler_params=pltpu.CompilerParams(
            collective_id=collective_id, has_side_effects=True, vmem_limit_bytes=40 << 20
        ),
        name="attention_backward",
    )(qkv, away, probs, grad)


def exact_gelu(hidden):
    return jax.nn.gelu(hidden, approximate=False)


def plain_product(left, right):
    return jnp.dot(left, right, preferred_element_type=F32)


def left_product(left, right):
    return lax.dot_general(left, right, (((0,), (0,)), ((), ())), preferred_element_type=F32)


def right_product(left, right):
    return lax.dot_general(left, right, (((1,), (1,)), ((), ())), preferred_element_type=F32)


def column_sums(rows):
    return jnp.sum(rows.astype(F32), axis=0)


def norm_parts(total):
    average = jnp.mean(total, axis=-1, keepdims=True)
    centered = total - average
    variance = jnp.mean(centered * centered, axis=-1, keepdims=True)
    rate = lax.rsqrt(variance + EPSILON)
    return centered * rate, rate


def norm_back(unit, rate, grad):
    return rate * (
        grad
        - jnp.mean(grad, axis=-1, keepdims=True)
        - unit * jnp.mean(grad * unit, axis=-1, keepdims=True)
    )


def split_columns(packed, widths):
    pieces = []
    start = 0
    for width in widths:
        pieces.append(packed[..., start : start + width])
        start += width
    return pieces


def native_forward(queries, keys_all, values_all, key_valid, heads):
    shape = queries.shape[:2] + (heads, HEAD_DIM)
    key_shape = keys_all.shape[:2] + (heads, HEAD_DIM)
    scores = jnp.einsum(
        "sqhd,skhd->shqk",
        queries.reshape(shape),
        keys_all.reshape(key_shape),
        preferred_element_type=F32,
    ) * (HEAD_DIM**-0.5)
    scores = jnp.where(key_valid[:, None, None, :], scores, -1e30)
    top = jnp.max(scores, axis=-1, keepdims=True)
    weights = jnp.exp(scores - top)
    probs = (weights / jnp.sum(weights, axis=-1, keepdims=True)).astype(BF16)
    context = jnp.einsum(
        "shqk,skhd->sqhd", probs, values_all.reshape(key_shape), preferred_element_type=F32
    )
    return context.reshape(queries.shape).astype(BF16), probs


def native_backward(queries, keys_all, values_all, probs, context_grad, heads):
    shape = queries.shape[:2] + (heads, HEAD_DIM)
    key_shape = keys_all.shape[:2] + (heads, HEAD_DIM)
    scale = HEAD_DIM**-0.5
    grad_heads = context_grad.reshape(shape)
    wide = probs.astype(F32)
    probs_grad = jnp.einsum(
        "sqhd,skhd->shqk", grad_heads, values_all.reshape(key_shape), preferred_element_type=F32
    )
    inner_total = jnp.sum(wide * probs_grad, axis=-1, keepdims=True)
    scores_grad = (wide * (probs_grad - inner_total)).astype(BF16)
    query_grad = jnp.einsum(
        "shqk,skhd->sqhd", scores_grad, keys_all.reshape(key_shape), preferred_element_type=F32
    )
    key_part = jnp.einsum(
        "shqk,sqhd->skhd", scores_grad, queries.reshape(shape), preferred_element_type=F32
    )
    value_part = jnp.einsum("shqk,sqhd->skhd", probs, grad_heads, preferred_element_type=F32)
    return (
        (query_grad * scale).astype(BF16).reshape(queries.shape),
        (key_part * scale).astype(BF16).reshape(keys_all.shape),
        value_part.astype(BF16).reshape(values_all.shape),
    )


def gather_rows(part):
    return lax.all_gather(part, "fsdp", axis=0, tiled=True)


def reduce_rows(part):
    share = lax.psum_scatter(part.astype(BF16), "fsdp", scatter_dimension=0, tiled=True)
    return lax.psum(share, "ctx").astype(F32)


def layer(flat_rows, cot_rows, row_mask, packed, widths, weights, forward, backward):
    full_qkv, full_output, full_inner, full_outer = weights
    rows, width = flat_rows.shape
    shards = packed.shape[0]
    (
        bias_query,
        bias_value,
        bias_output,
        gain_first,
        shift_first,
        bias_inner,
        bias_outer,
        gain_second,
        shift_second,
    ) = [piece.reshape(-1).astype(F32) for piece in split_columns(packed, widths)]
    bias_qkv = jnp.concatenate((bias_query, jnp.zeros_like(bias_query), bias_value))
    qkv = (plain_product(flat_rows, full_qkv) + bias_qkv).astype(BF16)
    context, saved = forward(qkv)

    first_sum = flat_rows.astype(F32) + plain_product(context, full_output) + bias_output
    first_unit, first_rate = norm_parts(first_sum)
    normed = first_unit * gain_first + shift_first
    normed_low = normed.astype(BF16)
    hidden = plain_product(normed_low, full_inner) + bias_inner
    active, gelu_back = jax.vjp(exact_gelu, hidden)
    active_low = active.astype(BF16)
    second_sum = normed + plain_product(active_low, full_outer) + bias_outer
    second_unit, second_rate = norm_parts(second_sum)
    output = ((second_unit * gain_second + shift_second) * row_mask).astype(BF16)

    out_grad = cot_rows.astype(F32) * row_mask
    second_gain_part = jnp.sum(out_grad * second_unit, axis=0)
    second_shift_part = jnp.sum(out_grad, axis=0)
    second_grad = norm_back(second_unit, second_rate, out_grad * gain_second)
    second_low = second_grad.astype(BF16)
    outer_weight_part = left_product(active_low, second_low).astype(BF16)
    outer_bias_part = column_sums(second_low)
    (hidden_grad,) = gelu_back(right_product(second_low, full_outer))
    hidden_low = hidden_grad.astype(BF16)
    inner_weight_part = left_product(normed_low, hidden_low).astype(BF16)
    inner_bias_part = column_sums(hidden_low)
    normed_grad = second_grad + right_product(hidden_low, full_inner)
    first_gain_part = jnp.sum(normed_grad * first_unit, axis=0)
    first_shift_part = jnp.sum(normed_grad, axis=0)
    first_grad = norm_back(first_unit, first_rate, normed_grad * gain_first)
    branch_low = first_grad.astype(BF16)
    output_weight_part = left_product(context, branch_low).astype(BF16)
    output_bias_part = column_sums(branch_low)
    context_grad = right_product(branch_low, full_output).astype(BF16)
    qkv_grad = backward(saved, context_grad)
    qkv_weight_part = left_product(flat_rows, qkv_grad).astype(BF16)
    query_bias_part = column_sums(qkv_grad[:, :width])
    value_bias_part = column_sums(qkv_grad[:, 2 * width :])
    input_grad = first_grad + right_product(qkv_grad, full_qkv)
    vector_parts = (
        query_bias_part,
        value_bias_part,
        output_bias_part,
        first_gain_part,
        first_shift_part,
        inner_bias_part,
        outer_bias_part,
        second_gain_part,
        second_shift_part,
    )
    packed_parts = jnp.concatenate([part.reshape(shards, -1) for part in vector_parts], axis=1)
    return (
        output,
        input_grad,
        packed_parts,
        (qkv_weight_part, output_weight_part, inner_weight_part, outer_weight_part),
    )


def native_body(inputs, cotangent, lengths, vectors, widths, weights):
    packed = lax.all_gather(vectors, "fsdp", axis=0, tiled=False)
    full = tuple(gather_rows(part) for part in weights)
    micro, seqs, block_len, width = inputs.shape
    heads = width // HEAD_DIM
    total_slots = block_len * lax.axis_size("ctx")
    group = micro * seqs
    rows = group * block_len
    flat_len = lengths.reshape(group)
    local_pos = lax.axis_index("ctx") * block_len + jnp.arange(block_len, dtype=jnp.int32)
    row_mask = (local_pos[None, :] < flat_len[:, None]).astype(F32).reshape(rows, 1)
    key_valid = jnp.arange(total_slots, dtype=jnp.int32)[None, :] < flat_len[:, None]

    def forward(qkv):
        queries = qkv[:, :width].reshape(group, block_len, width)
        keys_values = lax.all_gather(
            qkv[:, width:].reshape(group, block_len, 2 * width), "ctx", axis=1, tiled=True
        )
        keys, values = keys_values[:, :, :width], keys_values[:, :, width:]
        context, probs = native_forward(queries, keys, values, key_valid, heads)
        return context.reshape(rows, width), (queries, keys, values, probs)

    def backward(saved, context_grad):
        query_grad, key_part, value_part = native_backward(
            *saved, context_grad.reshape(group, block_len, width), heads
        )
        keys_values_grad = lax.psum_scatter(
            jnp.concatenate((key_part, value_part), axis=2), "ctx", scatter_dimension=1, tiled=True
        )
        return jnp.concatenate(
            (query_grad.reshape(rows, width), keys_values_grad.reshape(rows, 2 * width)), axis=1
        )

    output, input_grad, packed_parts, parts = layer(
        inputs.reshape(rows, width),
        cotangent.reshape(rows, width),
        row_mask,
        packed,
        widths,
        full,
        forward,
        backward,
    )
    share = lax.psum_scatter(packed_parts, "fsdp", scatter_dimension=0, tiled=True)
    return (
        output.reshape(inputs.shape),
        input_grad.reshape(inputs.shape),
        lax.psum(share, "ctx")[0],
        tuple(reduce_rows(part) for part in parts),
    )


def direct_body(inputs, cotangent, lengths, vectors, widths, weights):
    micro, seqs, block_len, width = inputs.shape
    shards = LINE * PAIR
    lanes = 128
    count = vectors.shape[0]
    rows = 2 * block_len
    table_rows = -(-count // (16 * lanes)) * 16
    table = jnp.pad(vectors, (0, table_rows * lanes - count)).reshape(table_rows, lanes)
    blocks = (inputs.reshape(micro, block_len, width), cotangent.reshape(micro, block_len, width))
    flows = [Flow(0, table_rows, lambda core, side: (0, table_rows, 0, lanes), cores=False)]
    flows += column_flows(1, *weights[0].shape, *GATHER_SPLIT[0])
    flows += column_flows(2, *weights[1].shape, *GATHER_SPLIT[1])
    flows += column_flows(3, *weights[2].shape, *GATHER_SPLIT[2])
    flows += row_flows(4, *weights[3].shape, *GATHER_SPLIT[3])
    full = gather_call((table,) + weights, blocks, flows, shards, 1, GATHER_ORDER)
    packed = full[0].reshape(shards, table_rows * lanes)[:, :count]
    ctx = lax.axis_index("ctx")
    side, core = ctx // 2, ctx % 2
    length = lax.dynamic_index_in_dim(lengths[:, 0], side, keepdims=False)

    def places(which):
        halves = jnp.arange(2, dtype=jnp.int32)[:, None] * rows
        return (halves + which * block_len + jnp.arange(block_len, dtype=jnp.int32)).reshape(rows)

    row_mask = (places(core) < length).astype(F32).reshape(rows, 1)
    key_places = jnp.concatenate((places(core), places(1 - core)))
    key_bias = jnp.where(key_places < length, 0.0, -1e30).astype(F32).reshape(1, 2 * rows)

    def forward(qkv):
        context, probs, away = attend(qkv, key_bias, 3)
        return context, (qkv, away, probs)

    def backward(saved, context_grad):
        return attend_back(*saved, context_grad, 4)

    output, input_grad, packed_parts, parts = layer(
        full[-2].reshape(rows, width),
        full[-1].reshape(rows, width),
        row_mask,
        packed,
        widths,
        full[1:5],
        forward,
        backward,
    )
    grad_table = jnp.pad(packed_parts, ((0, 0), (0, table_rows * lanes - count)))
    part_qkv, part_output, part_inner, part_outer = parts
    sums = reduce_call(
        (
            part_inner,
            part_outer,
            part_output,
            part_qkv,
            grad_table.reshape(shards * table_rows, lanes),
        ),
        (
            output.reshape(micro, block_len, width),
            input_grad.astype(BF16).reshape(micro, block_len, width),
        ),
        [
            column_part(part_inner.shape[0] // shards, part_inner.shape[1], *REDUCE_SPLIT[0]),
            row_part(part_outer.shape[0] // shards, part_outer.shape[1], *REDUCE_SPLIT[1]),
            column_part(part_output.shape[0] // shards, part_output.shape[1], *REDUCE_SPLIT[2]),
            column_part(part_qkv.shape[0] // shards, part_qkv.shape[1], *REDUCE_SPLIT[3]),
            vector_part(table_rows, lanes),
        ],
        2,
        REDUCE_ORDER,
    )
    return (
        sums[-2].reshape(inputs.shape),
        sums[-1].astype(F32).reshape(inputs.shape),
        sums[4].reshape(-1)[:count],
        tuple(sums[k].astype(F32) for k in (3, 2, 0, 1)),
    )


def body(
    inputs,
    cotangent,
    lengths,
    query_weight,
    key_weight,
    value_weight,
    output_weight,
    query_bias,
    value_bias,
    output_bias,
    first_gain,
    first_shift,
    inner_weight,
    inner_bias,
    outer_weight,
    outer_bias,
    second_gain,
    second_shift,
):
    vectors = (
        query_bias,
        value_bias,
        output_bias,
        first_gain,
        first_shift,
        inner_bias,
        outer_bias,
        second_gain,
        second_shift,
    )
    widths = [member.shape[0] for member in vectors]
    weights = (
        jnp.concatenate((query_weight, key_weight, value_weight), axis=1),
        output_weight,
        inner_weight,
        outer_weight,
    )
    width = inputs.shape[-1]
    laid_out = lax.axis_size("fsdp") == LINE * PAIR and lax.axis_size("ctx") == 4
    direct = laid_out and inputs.shape[:2] == (2, 1)
    run = direct_body if direct else native_body
    output, input_grad, vector_share, weight_shares = run(
        inputs, cotangent, lengths, jnp.concatenate(vectors), widths, weights
    )
    shares = split_columns(vector_share, widths)
    qkv_share, output_share, inner_share, outer_share = weight_shares
    query_share, key_share, value_share = split_columns(qkv_share, [width] * 3)
    return (
        output,
        input_grad,
        query_share,
        key_share,
        value_share,
        output_share,
        shares[0],
        shares[1],
        shares[2],
        shares[3],
        shares[4],
        inner_share,
        shares[5],
        outer_share,
        shares[6],
        shares[7],
        shares[8],
    )


def solution(mesh):
    data = P(None, "fsdp", "ctx", None)
    matrix = P("fsdp", None)
    vector = P("fsdp")
    return jax.shard_map(
        body,
        mesh=mesh,
        in_specs=(data, data, P(None, "fsdp"))
        + (matrix,) * 4
        + (vector,) * 5
        + (matrix, vector, matrix, vector, vector, vector),
        out_specs=(data, data)
        + (matrix,) * 4
        + (vector,) * 5
        + (matrix, vector, matrix, vector, vector, vector),
        check_vma=False,
    )
```

```python
import functools

import jax
import jax.numpy as jnp
from jax import lax
from jax.experimental import pallas as pl
from jax.experimental.pallas import tpu as pltpu
from jax.sharding import PartitionSpec as P

HEAD_DIM = 64
EPSILON = 1e-06
F32 = jnp.float32
BF16 = jnp.bfloat16

GATHER_SPLIT = ((256, 384), (256, 128), (512, 384), (160, 32))
REDUCE_SPLIT = ((768, 256), (128, 48), (256, 128), (1024, 128))
GATHER_ORDER = (
    0, 1, 9, 2, 3, 4, 13, 5, 6, 7, 10, 8, 11, 70, 32, 71, 69, 18, 35, 75, 33, 31, 76, 14, 16, 38,
    34, 41, 48, 37, 40, 12, 73, 22, 21, 17, 46, 78, 74, 24, 89, 43, 19, 81, 79, 107, 15, 27, 20,
    39, 45, 83, 72, 50, 23, 77, 86, 88, 36, 42, 29, 145, 108, 57, 146, 26, 84, 109, 147, 92, 54,
    111, 94, 30, 44, 80, 25, 55, 149, 114, 60, 62, 51, 113, 90, 95, 82, 152, 151, 116, 52, 110,
    47, 154, 97, 56, 87, 100, 117, 96, 155, 119, 49, 157, 150, 105, 59, 148, 85, 67, 121, 124,
    221, 93, 126, 28, 98, 159, 222, 112, 115, 53, 160, 102, 153, 162, 156, 183, 122, 184, 223, 63,
    165, 185, 58, 168, 130, 225, 187, 120, 158, 91, 127, 65, 164, 101, 103, 132, 227, 190, 128,
    228, 138, 166, 171, 189, 61, 186, 224, 133, 240, 99, 64, 241, 176, 230, 191, 188, 170, 231,
    118, 226, 229, 106, 202, 242, 204, 131, 161, 136, 247, 192, 66, 169, 193, 232, 141, 181, 123,
    172, 143, 174, 173, 209, 129, 68, 194, 163, 125, 246, 212, 233, 167, 135, 211, 248, 250, 178,
    205, 203, 195, 210, 235, 140, 249, 104, 200, 198, 179, 134, 234, 208, 182, 238, 244, 213, 137,
    206, 139, 177, 197, 243, 144, 180, 252, 257, 142, 236, 219, 239, 217, 201, 196, 254, 207, 214,
    199, 245, 251, 215, 255, 258, 175, 237, 253, 216, 256, 218, 220, 259,
)
REDUCE_ORDER = (
    0, 1, 9, 2, 3, 4, 5, 6, 7, 8, 10, 11, 32, 34, 220, 30, 218, 12, 14, 216, 13, 18, 28, 25, 15,
    17, 214, 16, 19, 20, 23, 21, 22, 31, 217, 24, 221, 29, 215, 33, 219, 222, 35, 36, 37, 27, 38,
    42, 223, 224, 226, 40, 43, 39, 225, 227, 85, 228, 41, 87, 84, 45, 86, 51, 44, 47, 88, 53, 89,
    90, 69, 70, 67, 68, 133, 46, 137, 26, 135, 136, 73, 74, 138, 57, 55, 165, 134, 71, 72, 166,
    168, 167, 139, 170, 171, 169, 59, 92, 91, 118, 119, 48, 94, 77, 49, 93, 75, 76, 63, 78, 54,
    79, 80, 81, 229, 61, 100, 116, 117, 95, 102, 96, 141, 140, 52, 122, 110, 123, 58, 120, 121,
    106, 126, 97, 143, 56, 142, 124, 125, 112, 173, 104, 172, 108, 128, 98, 127, 145, 144, 174,
    151, 157, 153, 199, 175, 129, 155, 161, 130, 197, 159, 203, 146, 183, 147, 198, 60, 149, 177,
    181, 185, 201, 189, 200, 202, 193, 176, 187, 62, 204, 101, 50, 64, 207, 208, 65, 205, 82, 103,
    178, 179, 206, 105, 152, 148, 150, 209, 107, 210, 211, 109, 131, 191, 156, 111, 154, 182, 83,
    184, 160, 158, 188, 113, 114, 99, 186, 192, 180, 190, 212, 162, 163, 194, 195, 66, 213, 115,
    164, 132, 196, 230,
)

MESH = pl.DeviceIdType.MESH
LINE = 4
PAIR = 2


class Place:
    def __init__(self):
        self.ctx = lax.axis_index("ctx")
        self.shard = lax.axis_index("fsdp")
        self.side = lax.div(self.ctx, 2)
        self.core = lax.rem(self.ctx, 2)
        self.line = lax.div(self.shard, PAIR)
        self.pair = lax.rem(self.shard, PAIR)

    def ahead(self, way):
        return (self.ctx, self.shard + way * PAIR)

    def across(self):
        return (self.ctx, self.shard + 1 - 2 * self.pair)

    def beside(self):
        return (self.ctx + 2 - 4 * self.side, self.shard)

    def twin(self):
        return (self.ctx + 1 - 2 * self.core, self.shard)

    def has(self, way, steps):
        if steps == 0:
            return None
        return self.line >= steps if way > 0 else self.line <= LINE - 1 - steps

    def can(self, way):
        return self.line <= LINE - 2 if way > 0 else self.line >= 1

    def shard_of(self, way, steps, other):
        pair = 1 - self.pair if other else self.pair
        return (self.line - way * steps) * PAIR + pair


def when(conditions, action):
    held = [c for c in conditions if c is not None]
    if not held:
        action()
        return
    both = held[0]
    for c in held[1:]:
        both = jnp.logical_and(both, c)
    pl.when(both)(action)


def greet(place):
    barrier = pltpu.get_barrier_semaphore()
    for peer in (place.across(), place.beside(), place.twin()):
        pl.semaphore_signal(barrier, inc=1, device_id=peer, device_id_type=MESH)
    for way in (1, -1):
        when(
            [place.can(way)],
            lambda way=way: pl.semaphore_signal(
                barrier, inc=1, device_id=place.ahead(way), device_id_type=MESH
            ),
        )
    lines = jnp.minimum(place.line, 1) + jnp.minimum(LINE - 1 - place.line, 1)
    pl.semaphore_wait(barrier, 3 + lines)


class Flow:
    def __init__(self, array, shard_rows, region, order="line", sides=False, cores=True):
        self.array = array
        self.shard_rows = shard_rows
        self.region = region
        self.order = order
        self.sides = sides
        self.cores = cores

    def view(self, ref, shard, core, side):
        row, rows, column, columns = self.region(core, side)
        start = row if shard is None else shard * self.shard_rows + row
        if not isinstance(start, int):
            start = pl.multiple_of(start, 16)
        if not isinstance(column, int):
            column = pl.multiple_of(column, 128)
        return ref.at[pl.ds(start, rows), pl.ds(column, columns)]


def positions(order):
    found = []
    if order == "line":
        found.append(("P", 1, 0, True))
        for steps in range(1, LINE):
            for way in (1, -1):
                found.append(("L", way, steps, False))
                found.append(("P", way, steps, True))
    else:
        found.append(("P", 1, 0, True))
        for steps in range(1, LINE):
            for way in (1, -1):
                found.append(("L", way, steps, False))
                found.append(("L", way, steps, True))
    return found


class Labels:
    def __init__(self):
        self.numbers = {}

    def __call__(self, key):
        return self.numbers.setdefault(key, len(self.numbers))


def gather_labels(flows):
    labels = Labels()
    for number, flow in enumerate(flows):
        for spot in positions(flow.order):
            labels((number, "in") + spot)
            if flow.sides:
                labels((number, "side") + spot)
            if flow.cores:
                labels((number, "twin") + spot)
                if flow.sides:
                    labels((number, "twinside") + spot)
    return labels


class Gather:
    def __init__(self, place, flows, owns, fulls, send, recv):
        self.place, self.flows, self.owns, self.fulls = place, flows, owns, fulls
        self.send, self.recv = send, recv
        self.labels = gather_labels(flows)
        self.sent = []

    def copy(self, number, key, spot, peer, core, side, own=False):
        flow = self.flows[number]
        place = self.place
        if own:
            shard = place.shard
            source = flow.view(self.owns[flow.array], None, core, side)
        else:
            shard = place.shard_of(*spot[1:])
            source = flow.view(self.fulls[flow.array], shard, core, side)
        target = flow.view(self.fulls[flow.array], shard, core, side)
        label = self.labels((number,) + key)
        return pltpu.make_async_remote_copy(
            source,
            target,
            self.send.at[label],
            self.recv.at[label],
            device_id=peer,
            device_id_type=MESH,
        )

    def start(self, conditions, copy):
        when(conditions, copy.start)
        self.sent.append((conditions, copy))

    def begin(self, number):
        flow, place = self.flows[number], self.place
        core, side = place.core, place.side
        here = (None, 1, 0, False)
        for way in (1, -1):
            self.start(
                [place.can(way)],
                self.copy(
                    number, ("in", "L", way, 1, False), here, place.ahead(way), core, side, True
                ),
            )
        self.start(
            [],
            self.copy(number, ("in", "P", 1, 0, True), here, place.across(), core, side, True),
        )

    def arrive(self, number, spot):
        flow, place = self.flows[number], self.place
        kind, way, steps, other = spot
        core, side = place.core, place.side
        there = place.has(way, steps)

        def take():
            self.copy(number, ("in",) + spot, spot, place.across(), core, side).wait_recv()

        when([there], take)

        def onward(extra, key, peer):
            self.start(
                [c for c in (there, extra) if c is not None],
                self.copy(number, key, spot, peer, core, side),
            )

        if kind == "L" and steps + 1 < LINE:
            onward(place.can(way), ("in", "L", way, steps + 1, other), place.ahead(way))
        if kind == "L" and flow.order == "line":
            onward(None, ("in", "P", way, steps, True), place.across())
        if kind == "P" and flow.order == "pair":
            for direction in (1, -1):
                onward(
                    place.can(direction), ("in", "L", direction, 1, True), place.ahead(direction)
                )
        if flow.sides:
            onward(None, ("side",) + spot, place.beside())
        if flow.cores:
            onward(None, ("twin",) + spot, place.twin())

    def arrive_side(self, number, spot):
        flow, place = self.flows[number], self.place
        there = place.has(*spot[1:3])
        core, side = place.core, 1 - place.side
        when(
            [there],
            lambda: self.copy(
                number, ("side",) + spot, spot, place.beside(), core, side
            ).wait_recv(),
        )
        if flow.cores:
            self.start(
                [there] if there is not None else [],
                self.copy(number, ("twinside",) + spot, spot, place.twin(), core, side),
            )

    def arrive_twin(self, number, spot):
        flow, place = self.flows[number], self.place
        there = place.has(*spot[1:3])
        core = 1 - place.core
        if flow.cores:
            when(
                [there],
                lambda: self.copy(
                    number, ("twin",) + spot, spot, place.twin(), core, place.side
                ).wait_recv(),
            )
            if flow.sides:
                when(
                    [there],
                    lambda: self.copy(
                        number, ("twinside",) + spot, spot, place.twin(), core, 1 - place.side
                    ).wait_recv(),
                )

    def actions(self):
        found = []
        for n, flow in enumerate(self.flows):
            found.append((("begin", n), lambda n=n: self.begin(n)))
        for index in range(len(positions("line"))):
            for n, flow in enumerate(self.flows):
                spot = positions(flow.order)[index]
                found.append((("in", n, spot), lambda n=n, spot=spot: self.arrive(n, spot)))
                if flow.sides:
                    found.append(
                        (("side", n, spot), lambda n=n, spot=spot: self.arrive_side(n, spot))
                    )
        found.append((("last",), self.finish))
        return found

    def finish(self):
        for number, flow in enumerate(self.flows):
            for spot in positions(flow.order):
                self.arrive_twin(number, spot)
        for conditions, copy in self.sent:
            when(conditions, copy.wait_send)


class Swap:
    def __init__(self, place, ins, outs, send, recv, local):
        side = place.side
        self.away = [
            pltpu.make_async_remote_copy(
                here.at[1 - side],
                there.at[side],
                send.at[k],
                recv.at[k],
                device_id=place.beside(),
                device_id_type=MESH,
            )
            for k, (here, there) in enumerate(zip(ins, outs))
        ]
        self.stay = [
            pltpu.make_async_copy(here.at[side], there.at[side], local.at[k])
            for k, (here, there) in enumerate(zip(ins, outs))
        ]

    def start(self):
        for copy in self.away + self.stay:
            copy.start()

    def finish(self):
        for copy in self.away + self.stay:
            copy.wait()


def swap_scratch(count):
    return [pltpu.SemaphoreType.DMA((count,))] * 3


def gather_kernel(flows, spots, blocks, order, *refs):
    count = max(array for array, _ in spots) + 1
    shares, refs = refs[: len(spots)], refs[len(spots) :]
    ins, refs = refs[:blocks], refs[blocks:]
    fulls, refs = refs[:count], refs[count:]
    outs, refs = refs[:blocks], refs[blocks:]
    owns, refs = refs[:count], refs[count:]
    send, recv, local, load = refs[:4]
    place = Place()
    loads = [
        pltpu.make_async_copy(
            share, owns[array].at[:, pl.ds(column, share.shape[1])], load.at[k]
        )
        for k, (share, (array, column)) in enumerate(zip(shares, spots))
    ]
    for copy in loads:
        copy.start()
    keep = [
        pltpu.make_async_copy(
            own, full.at[pl.ds(place.shard * own.shape[0], own.shape[0]), :], local.at[k]
        )
        for k, (own, full) in enumerate(zip(owns, fulls))
    ]
    greet(place)
    for copy in loads:
        copy.wait()
    swap = Swap(place, ins, outs, *refs[4:])
    swap.start()
    work = Gather(place, flows, owns, fulls, send, recv)
    for copy in keep:
        copy.start()
    for step in in_order(work.actions(), order):
        step()
    for copy in keep:
        copy.wait()
    swap.finish()


def gather_call(shares, spots, blocks, flows, shards, collective_id, order=None):
    labels = gather_labels(flows)
    count = max(array for array, _ in spots) + 1
    shapes = []
    for array in range(count):
        members = [share for share, spot in zip(shares, spots) if spot[0] == array]
        shapes.append((members[0].shape[0], sum(m.shape[1] for m in members)))
    far = pl.BlockSpec(memory_space=pl.ANY)
    return pl.pallas_call(
        functools.partial(gather_kernel, flows, spots, len(blocks), order),
        out_shape=[jax.ShapeDtypeStruct((shards * r, c), BF16) for r, c in shapes]
        + [jax.ShapeDtypeStruct(b.shape, b.dtype) for b in blocks],
        in_specs=[far] * (len(shares) + len(blocks)),
        out_specs=[far] * (count + len(blocks)),
        scratch_shapes=[pltpu.VMEM(shape, BF16) for shape in shapes]
        + [
            pltpu.SemaphoreType.DMA((len(labels.numbers),)),
            pltpu.SemaphoreType.DMA((len(labels.numbers),)),
            pltpu.SemaphoreType.DMA((count,)),
            pltpu.SemaphoreType.DMA((len(shares),)),
        ]
        + swap_scratch(len(blocks)),
        compiler_params=pltpu.CompilerParams(collective_id=collective_id, has_side_effects=True),
        name="gather_weights",
    )(*shares, *blocks)


def column_flows(array, shard_rows, columns, shared, early):
    half = columns // 2
    part = (half - shared) // 2
    flows = []
    if shared:
        flows.append(
            Flow(array, shard_rows, lambda core, side: (0, shard_rows, core * half, shared))
        )
    if early:
        flows.append(
            Flow(
                array,
                shard_rows,
                lambda core, side: (0, shard_rows, core * half + shared + side * part, early),
                sides=True,
            )
        )
    if part > early:
        flows.append(
            Flow(
                array,
                shard_rows,
                lambda core, side: (
                    0,
                    shard_rows,
                    core * half + shared + side * part + early,
                    part - early,
                ),
                order="pair",
                sides=True,
            )
        )
    return flows


def row_flows(array, shard_rows, columns, shared, early):
    half = shard_rows // 2
    part = (half - shared) // 2
    return [
        Flow(array, shard_rows, lambda core, side: (core * half, shared, 0, columns)),
        Flow(
            array,
            shard_rows,
            lambda core, side: (core * half + shared + side * part, early, 0, columns),
            sides=True,
        ),
        Flow(
            array,
            shard_rows,
            lambda core, side: (core * half + shared + side * part + early, part - early, 0, columns),
            order="pair",
            sides=True,
        ),
    ]


class Part:
    def __init__(self, rows, columns, along, flows, dtype=BF16):
        self.rows, self.columns, self.along, self.dtype = rows, columns, along, dtype
        self.flows = flows
        self.half_rows = rows // 2 if along == "rows" else rows
        self.half_columns = columns // 2 if along == "columns" else columns

    def half(self, ref, shard, core):
        base = 0 if shard is None else pl.multiple_of(shard * self.rows, 16)
        if self.along == "rows":
            row = core * self.half_rows + (0 if shard is None else shard * self.rows)
            return ref.at[pl.ds(pl.multiple_of(row, 16), self.half_rows), :]
        if self.along == "columns":
            column = pl.multiple_of(core * self.half_columns, 128)
            return ref.at[pl.ds(base, self.rows), pl.ds(column, self.half_columns)]
        return ref.at[pl.ds(base, self.rows), :]

    def inner(self, flow, side):
        first, extent = flow[0](side), flow[1]
        if self.along == "rows":
            start = first if isinstance(first, int) else pl.multiple_of(first, 16)
            return pl.ds(start, extent), slice(None)
        start = first if isinstance(first, int) else pl.multiple_of(first, 128)
        return slice(None), pl.ds(start, extent)

    def outer(self, flow, core, side):
        first, extent = flow[0](side), flow[1]
        if self.along == "rows":
            return pl.ds(pl.multiple_of(core * self.half_rows + first, 16), extent), slice(None)
        if self.along == "columns":
            return slice(None), pl.ds(
                pl.multiple_of(core * self.half_columns + first, 128), extent
            )
        return slice(None), slice(None)

    def extent(self, flow):
        if self.along == "rows":
            return flow[1], self.half_columns
        return self.half_rows, flow[1]


SPOTS = [(1, 3), (-1, 3), (1, 2), (-1, 2), (1, 1), (-1, 1), (1, 0)]


def reduce_scratch(parts):
    shapes = []
    for part in parts:
        half = (LINE * PAIR, part.half_rows, part.half_columns)
        shapes.append(pltpu.VMEM(half, part.dtype))
        shapes.append(pltpu.VMEM(half if part.along else half[1:], part.dtype))
        for flow in part.flows:
            rows, columns = part.extent(flow)
            shapes.append(
                pltpu.VMEM((LINE * PAIR if flow[3] else 1, rows, columns), part.dtype)
            )
            shapes.append(
                pltpu.VMEM((LINE if flow[2] == "line" else 1, rows, columns), part.dtype)
            )
            shapes.append(
                pltpu.VMEM(
                    ((LINE + 1) * (1 if flow[2] == "line" else PAIR), rows, columns), part.dtype
                )
            )
    return shapes


def reduce_labels(parts):
    labels = Labels()
    for n, part in enumerate(parts):
        for way, steps in SPOTS:
            for other in (False, True):
                labels((n, "twin", way, steps, other))
        labels((n, "twinend"))
        for k, flow in enumerate(part.flows):
            for way, steps in SPOTS:
                for other in (False, True):
                    if flow[3]:
                        labels((n, k, "side", way, steps, other))
                    if flow[2] == "pair" or not other:
                        labels((n, k, "line", way, steps, other))
                        if steps == 0:
                            labels((n, k, "line", -way, steps, other))
                if flow[2] == "line" or steps == 0:
                    labels((n, k, "pair", way, steps))
            labels((n, k, "sideend"))
            labels((n, k, "twinend"))
            labels((n, k, "twinsideend"))
    return labels


class Reduce:
    def __init__(self, place, parts, grads, outs, scratch, send, recv, load):
        self.place, self.parts, self.grads, self.outs = place, parts, grads, outs
        self.send, self.recv, self.load = send, recv, load
        self.labels = reduce_labels(parts)
        self.sent = []
        self.own, self.other, self.lanes = [], [], []
        at = 0
        for part in parts:
            self.own.append(scratch[at])
            self.other.append(scratch[at + 1])
            at += 2
            lanes = []
            for _ in part.flows:
                lanes.append(scratch[at : at + 3])
                at += 3
            self.lanes.append(lanes)

    def copy(self, source, target, key, peer):
        label = self.labels(key)
        return pltpu.make_async_remote_copy(
            source,
            target,
            self.send.at[label],
            self.recv.at[label],
            device_id=peer,
            device_id_type=MESH,
        )

    def start(self, conditions, copy):
        when(conditions, copy.start)
        self.sent.append((conditions, copy))

    def there(self, spot):
        return self.place.has(-spot[0], spot[1])

    def shard(self, spot, other):
        return self.place.shard_of(-spot[0], spot[1], other)

    def keep(self, n, spot, other):
        shard = self.shard(spot, other)
        label = SPOTS.index(spot) * 2 + int(other)
        return pltpu.make_async_copy(
            self.parts[n].half(self.grads[n], shard, self.place.core),
            self.own[n].at[shard],
            self.load.at[n * 2 * len(SPOTS) + label],
        )

    def twin(self, n, spot, other, core):
        shard = self.shard(spot, other)
        return self.copy(
            self.parts[n].half(self.grads[n], shard, core),
            self.other[n].at[shard],
            (n, "twin") + spot + (other,),
            self.place.twin(),
        )

    def begin(self, n, spot):
        there = self.there(spot)
        for other in (True, False):
            when([there], self.keep(n, spot, other).start)
            if self.parts[n].along:
                self.start([there], self.twin(n, spot, other, 1 - self.place.core))

    def piece(self, n, k, shard, side):
        part = self.parts[n]
        rows, columns = part.inner(part.flows[k], side)
        return self.own[n].at[shard, rows, columns]

    def side_copy(self, n, k, spot, other, side):
        shard = self.shard(spot, other)
        return self.copy(
            self.piece(n, k, shard, side),
            self.lanes[n][k][0].at[shard],
            (n, k, "side") + spot + (other,),
            self.place.beside(),
        )

    def add_cores(self, n, spot):
        there = self.there(spot)
        part = self.parts[n]
        for other in (True, False):

            def add(other=other):
                shard = self.shard(spot, other)
                self.keep(n, spot, other).wait()
                if part.along:
                    self.twin(n, spot, other, self.place.core).wait_recv()
                    self.own[n][shard] = self.own[n][shard] + self.other[n][shard]

            when([there], add)
        for other in (True, False):
            for k, flow in enumerate(part.flows):
                if flow[3]:
                    self.start([there], self.side_copy(n, k, spot, other, 1 - self.place.side))
                elif other:
                    self.start([there], self.pair_copy(n, k, spot, self.shard(spot, True)))

    def pair_copy(self, n, k, spot, shard):
        flow = self.parts[n].flows[k]
        slot = self.place.line + spot[0] * spot[1] if flow[2] == "line" else 0
        return self.copy(
            self.piece(n, k, shard, self.place.side),
            self.lanes[n][k][1].at[slot],
            (n, k, "pair") + spot,
            self.place.across(),
        )

    def add_sides(self, n, k, spot):
        there = self.there(spot)
        side = self.place.side
        for other in (True, False):

            def add(other=other):
                shard = self.shard(spot, other)
                self.side_copy(n, k, spot, other, side).wait_recv()
                piece = self.piece(n, k, shard, side)
                piece[...] = piece[...] + self.lanes[n][k][0][shard]

            when([there], add)
        if self.parts[n].flows[k][2] == "line":
            self.start([there], self.pair_copy(n, k, spot, self.shard(spot, True)))

    def line_slot(self, flow, way, steps, other, line):
        slot = line if (steps > 0 or way > 0) else LINE
        return slot + (LINE + 1) * int(other) if flow[2] == "pair" else slot

    def line_copy(self, n, k, spot, other, arriving):
        flow = self.parts[n].flows[k]
        way, steps = spot
        shard = self.shard(spot, other)
        line = self.place.line + way * steps
        left = steps if arriving else steps - 1
        return self.copy(
            self.piece(n, k, shard, self.place.side),
            self.lanes[n][k][2].at[self.line_slot(flow, way, left, other, line)],
            (n, k, "line", way, left, other),
            self.place.ahead(way),
        )

    def add_line(self, n, k, spot):
        place = self.place
        there = self.there(spot)
        way, steps = spot
        side = place.side
        flow = self.parts[n].flows[k]
        if flow[2] == "line":

            def add():
                shard = self.shard(spot, False)
                self.pair_copy(n, k, spot, shard).wait_recv()
                piece = self.piece(n, k, shard, side)
                piece[...] = piece[...] + self.lanes[n][k][1][place.line + way * steps]

            when([there], add)
        for other in (True, False) if flow[2] == "pair" else (False,):
            for direction in (1, -1) if steps == 0 else (way,):

                def add_line(other=other, here=(direction, steps)):
                    self.line_copy(n, k, here, other, True).wait_recv()
                    piece = self.piece(n, k, self.shard(here, other), side)
                    line = place.line + here[0] * here[1]
                    slot = self.line_slot(flow, here[0], here[1], other, line)
                    piece[...] = piece[...] + self.lanes[n][k][2][slot]

                when([there, place.can(-direction)], add_line)
            if steps > 0:
                self.start([there], self.line_copy(n, k, spot, other, False))

    def send_pair(self, n, k):
        self.start([], self.pair_copy(n, k, (1, 0), self.shard((1, 0), True)))

    def send_swap(self, n, k):
        self.start([], self.swap(n, k))

    def settle(self, n, k):
        place = self.place
        core, side, here = place.core, place.side, place.shard
        part = self.parts[n]
        flow = part.flows[k]
        piece = self.piece(n, k, here, side)
        out = self.out_view(n, k, core, side)
        if flow[3]:
            if flow[2] == "pair":
                self.pair_copy(n, k, (1, 0), here).wait_recv()
                out[...] = piece[...] + self.lanes[n][k][1][0]
            else:
                out[...] = piece[...]
            self.start([], self.out_copy(n, k, "sideend", place.beside(), core, side))
        else:
            self.swap(n, k).wait_recv()
            out[...] = piece[...] + self.lanes[n][k][0][0]
        if part.along:
            self.start([], self.out_copy(n, k, "twinend", place.twin(), core, side))
        else:
            self.start([], self.whole(n, k))

    def settle_side(self, n, k):
        place = self.place
        core, side = place.core, 1 - place.side
        self.out_copy(n, k, "sideend", place.beside(), core, side).wait_recv()
        self.start([], self.out_copy(n, k, "twinsideend", place.twin(), core, side))

    def swap(self, n, k):
        return self.copy(
            self.piece(n, k, self.place.shard, self.place.side),
            self.lanes[n][k][0].at[0],
            (n, k, "sideend"),
            self.place.beside(),
        )

    def out_view(self, n, k, core, side):
        part = self.parts[n]
        rows, columns = part.outer(part.flows[k], core, side)
        return self.outs[n].at[rows, columns]

    def out_copy(self, n, k, key, peer, core, side):
        view = self.out_view(n, k, core, side)
        return self.copy(view, view, (n, k, key), peer)

    def last(self):
        place = self.place
        core, side = place.core, place.side
        everything = [(n, k) for n, part in enumerate(self.parts) for k in range(len(part.flows))]
        for n, k in everything:
            if self.parts[n].along:
                self.out_copy(n, k, "twinend", place.twin(), 1 - core, side).wait_recv()
                if self.parts[n].flows[k][3]:
                    self.out_copy(
                        n, k, "twinsideend", place.twin(), 1 - core, 1 - side
                    ).wait_recv()
            else:
                self.whole(n, k).wait_recv()
        for conditions, copy in self.sent:
            when(conditions, copy.wait_send)
        for n, k in everything:
            if not self.parts[n].along:
                view = self.out_view(n, k, core, side)
                view[...] = view[...] + self.other[n][...]

    def whole(self, n, k):
        return self.copy(
            self.out_view(n, k, self.place.core, self.place.side),
            self.other[n],
            (n, k, "twinend"),
            self.place.twin(),
        )

    def actions(self):
        found = []
        for n, part in enumerate(self.parts):
            for spot in SPOTS:
                found.append((("begin", n, spot), lambda n=n, s=spot: self.begin(n, s)))
        for n, part in enumerate(self.parts):
            for spot in SPOTS:
                found.append((("cores", n, spot), lambda n=n, s=spot: self.add_cores(n, s)))
            for k, flow in enumerate(part.flows):
                at = (n, k)
                for spot in SPOTS:
                    if flow[3]:
                        found.append(
                            (("sides", n, k, spot), lambda at=at, s=spot: self.add_sides(*at, s))
                        )
                    found.append(
                        (("line", n, k, spot), lambda at=at, s=spot: self.add_line(*at, s))
                    )
                if flow[2] == "pair":
                    found.append((("pair", n, k), lambda at=at: self.send_pair(*at)))
                if not flow[3]:
                    found.append((("swap", n, k), lambda at=at: self.send_swap(*at)))
                found.append((("settle", n, k), lambda at=at: self.settle(*at)))
                if flow[3]:
                    found.append((("after", n, k), lambda at=at: self.settle_side(*at)))
        found.append((("last",), self.last))
        return found


def in_order(actions, order):
    if order is None:
        return [action for _, action in actions]
    assert sorted(order) == list(range(len(actions)))
    return [actions[i][1] for i in order]


def reduce_kernel(parts, blocks, order, *refs):
    count = len(parts)
    grads, refs = refs[:count], refs[count:]
    ins, refs = refs[:blocks], refs[blocks:]
    outs, refs = refs[:count], refs[count:]
    swapped, refs = refs[:blocks], refs[blocks:]
    scratch, (send, recv, load), sems = refs[:-6], refs[-6:-3], refs[-3:]
    place = Place()
    greet(place)
    swap = Swap(place, ins, swapped, *sems)
    swap.start()
    work = Reduce(place, parts, grads, outs, scratch, send, recv, load)
    for step in in_order(work.actions(), order):
        step()
    swap.finish()


def reduce_call(arrays, blocks, parts, collective_id, order=None):
    labels = reduce_labels(parts)
    count = len(arrays)
    return pl.pallas_call(
        functools.partial(reduce_kernel, parts, len(blocks), order),
        out_shape=[jax.ShapeDtypeStruct((p.rows, p.columns), p.dtype) for p in parts]
        + [jax.ShapeDtypeStruct(b.shape, b.dtype) for b in blocks],
        in_specs=[pl.BlockSpec(memory_space=pl.ANY)] * (count + len(blocks)),
        out_specs=[pl.BlockSpec(memory_space=pltpu.VMEM)] * count
        + [pl.BlockSpec(memory_space=pl.ANY)] * len(blocks),
        scratch_shapes=reduce_scratch(parts)
        + [
            pltpu.SemaphoreType.DMA((len(labels.numbers),)),
            pltpu.SemaphoreType.DMA((len(labels.numbers),)),
            pltpu.SemaphoreType.DMA((count * 2 * len(SPOTS),)),
        ]
        + swap_scratch(len(blocks)),
        compiler_params=pltpu.CompilerParams(
            collective_id=collective_id, has_side_effects=True, vmem_limit_bytes=63 << 20
        ),
        name="reduce_gradients",
    )(*arrays, *blocks)


def column_part(rows, columns, shared, early):
    half = columns // 2
    part = (half - shared) // 2
    flows = []
    if shared:
        flows.append((lambda side: 0, shared, "line", False))
    if early:
        flows.append((lambda side: shared + side * part, early, "line", True))
    if part > early:
        flows.append((lambda side: shared + side * part + early, part - early, "pair", True))
    return Part(rows, columns, "columns", flows)


def row_part(rows, columns, shared, early):
    half = rows // 2
    part = (half - shared) // 2
    return Part(
        rows,
        columns,
        "rows",
        [
            (lambda side: 0, shared, "line", False),
            (lambda side: shared + side * part, early, "line", True),
            (lambda side: shared + side * part + early, part - early, "pair", True),
        ],
    )


def vector_part(rows, columns):
    return Part(rows, columns, None, [(lambda side: 0, columns, "line", False)], F32)


ROW_QUERY, ROW_VALUE, ROW_OUTPUT, ROW_GAIN1, ROW_SHIFT1, ROW_INNER, INNER = 0, 1, 2, 3, 4, 5, 4
ROW_OUTER, ROW_GAIN2, ROW_SHIFT2 = 9, 10, 11
TABLE_ROWS = 16
LANES = 128
BAND = 32


def spread_table(table_ref, vec):
    for shard in range(table_ref.shape[0] // TABLE_ROWS):
        vec[:, pl.ds(shard * LANES, LANES)] = table_ref[
            pl.ds(shard * TABLE_ROWS, TABLE_ROWS), :
        ].astype(F32)


def fold_table(vec, table_ref, first, count):
    for shard in range(table_ref.shape[0] // TABLE_ROWS):
        table_ref[pl.ds(shard * TABLE_ROWS + first, count), :] = vec[
            pl.ds(first, count), pl.ds(shard * LANES, LANES)
        ]


def row_place(row, core, rows):
    half = rows // 2
    return jnp.where(row < half, row, row + half) + core * half


def total_rows(block):
    return jnp.sum(block.astype(F32), axis=0, keepdims=True)


def middle_kernel(
    rows_ref,
    context_ref,
    cot_ref,
    lengths_ref,
    table_ref,
    output_w,
    inner_w,
    outer_w,
    out_ref,
    first_grad_ref,
    context_grad_ref,
    sums_ref,
    output_g,
    inner_g,
    outer_g,
    output_v,
    inner_v,
    outer_v,
    vec,
    sums,
    active,
    slope,
    unit1,
    unit2,
    rate1,
    total,
    low,
    low_t,
    second,
    second_low,
    inner_b,
    outer_b,
    load,
    save,
):
    rows, width = rows_ref.shape
    tiles, _, tile = inner_v.shape
    ctx = lax.axis_index("ctx")
    side, core = lax.div(ctx, 2), lax.rem(ctx, 2)
    length = lengths_ref[side, 0]
    bands = rows // BAND

    def inner_load(t):
        return pltpu.make_async_copy(
            inner_w.at[:, pl.ds(pl.multiple_of(t * tile, tile), tile)], inner_v.at[t], load.at[0, t]
        )

    def outer_load(t):
        return pltpu.make_async_copy(
            outer_w.at[pl.ds(pl.multiple_of(t * tile, tile), tile), :], outer_v.at[t], load.at[1, t]
        )

    output_load = pltpu.make_async_copy(output_w, output_v, load.at[2, 0])
    output_load.start()
    for t in range(tiles):
        inner_load(t).start()
        outer_load(t).start()
    spread_table(table_ref, vec)
    sums[...] = jnp.zeros_like(sums)
    output_load.wait()
    total[...] = plain_product(context_ref[...], output_v[...])

    def band_of(b):
        return pl.ds(pl.multiple_of(b * BAND, BAND), BAND)

    def first_norm(b, carry):
        here = band_of(b)
        first_sum = (
            rows_ref[here, :].astype(F32) + total[here, :] + vec[pl.ds(ROW_OUTPUT, 1), :]
        )
        unit, rate = norm_parts(first_sum)
        unit1[here, :] = unit
        rate1[here, :] = jnp.broadcast_to(rate, (BAND, LANES))
        normed = unit * vec[pl.ds(ROW_GAIN1, 1), :] + vec[pl.ds(ROW_SHIFT1, 1), :]
        low[here, :] = normed.astype(BF16)
        total[here, :] = normed + vec[pl.ds(ROW_OUTER, 1), :]
        return carry

    lax.fori_loop(0, bands, first_norm, 0)
    low_t[...] = low[...].T

    def forward(t, carry):
        inner_load(t).wait()
        bias = jnp.concatenate(
            [
                vec[pl.ds(ROW_INNER + k, 1), pl.ds(pl.multiple_of(t * LANES, LANES), LANES)]
                for k in range(INNER)
            ],
            axis=1,
        )
        hidden = plain_product(low[...], inner_v[t]) + bias
        share = 0.5 + 0.5 * lax.erf(hidden * 0.7071067811865476)
        active[t] = (hidden * share).astype(BF16)
        slope[t] = share + hidden * (jnp.exp(-0.5 * hidden * hidden) * 0.3989422804014327)
        outer_load(t).wait()
        total[...] += plain_product(active[t], outer_v[t])
        return carry

    lax.fori_loop(0, tiles, forward, 0)

    def second_norm(b, carry):
        here = band_of(b)
        unit, rate = norm_parts(total[here, :])
        row = b * BAND + lax.broadcasted_iota(jnp.int32, (BAND, width), 0)
        mask = (row_place(row, core, rows) < length).astype(F32)
        gain = vec[pl.ds(ROW_GAIN2, 1), :]
        out_ref[here, :] = ((unit * gain + vec[pl.ds(ROW_SHIFT2, 1), :]) * mask).astype(BF16)
        out_grad = cot_ref[here, :].astype(F32) * mask
        grad = norm_back(unit, rate, out_grad * gain)
        second[here, :] = grad
        grad_low = grad.astype(BF16)
        second_low[here, :] = grad_low
        sums[pl.ds(ROW_GAIN2, 1), :] += total_rows(out_grad * unit)
        sums[pl.ds(ROW_SHIFT2, 1), :] += total_rows(out_grad)
        sums[pl.ds(ROW_OUTER, 1), :] += total_rows(grad_low)
        return carry

    lax.fori_loop(0, bands, second_norm, 0)

    def inner_save(t):
        slot = lax.rem(t, 2)
        return pltpu.make_async_copy(
            inner_b.at[slot],
            inner_g.at[:, pl.ds(pl.multiple_of(t * tile, tile), tile)],
            save.at[0, slot],
        )

    def outer_save(t):
        slot = lax.rem(t, 2)
        return pltpu.make_async_copy(
            outer_b.at[slot],
            outer_g.at[pl.ds(pl.multiple_of(t * tile, tile), tile), :],
            save.at[1, slot],
        )

    def backward(t, carry):
        slot = lax.rem(t, 2)
        hidden_grad = (right_product(second_low[...], outer_v[t]) * slope[t]).astype(BF16)
        summed = total_rows(hidden_grad)
        for k in range(INNER):
            sums[
                pl.ds(ROW_INNER + k, 1), pl.ds(pl.multiple_of(t * LANES, LANES), LANES)
            ] = summed[:, k * LANES : (k + 1) * LANES]

        @pl.when(t >= 2)
        def _():
            outer_save(t - 2).wait()
            inner_save(t - 2).wait()

        outer_b[slot] = left_product(active[t], second_low[...]).astype(BF16)
        inner_b[slot] = plain_product(low_t[...], hidden_grad).astype(BF16)
        outer_save(t).start()
        second[...] += right_product(hidden_grad, inner_v[t])
        inner_save(t).start()
        return carry

    lax.fori_loop(0, tiles, backward, 0)

    def first_back(b, carry):
        here = band_of(b)
        grad = second[here, :]
        unit = unit1[here, :]
        sums[pl.ds(ROW_GAIN1, 1), :] += total_rows(grad * unit)
        sums[pl.ds(ROW_SHIFT1, 1), :] += total_rows(grad)
        back = norm_back(unit, rate1[here, :1], grad * vec[pl.ds(ROW_GAIN1, 1), :])
        first_grad_ref[here, :] = back
        back_low = back.astype(BF16)
        second_low[here, :] = back_low
        sums[pl.ds(ROW_OUTPUT, 1), :] += total_rows(back_low)
        return carry

    lax.fori_loop(0, bands, first_back, 0)
    context_grad_ref[...] = right_product(second_low[...], output_v[...]).astype(BF16)
    output_g[...] = left_product(context_ref[...], second_low[...]).astype(BF16)
    fold_table(sums, sums_ref, 0, TABLE_ROWS)
    for t in range(tiles - 2, tiles):
        outer_save(t).wait()
        inner_save(t).wait()


def middle(rows, context, cot, lengths, table, output_w, inner_w, outer_w):
    count, width = rows.shape
    hidden = inner_w.shape[1]
    tile = INNER * LANES
    tiles = hidden // tile
    whole = pl.BlockSpec(memory_space=pltpu.VMEM)
    far = pl.BlockSpec(memory_space=pl.ANY)

    def space(dtype):
        return pltpu.VMEM((count, width), dtype)

    return pl.pallas_call(
        middle_kernel,
        out_shape=[
            jax.ShapeDtypeStruct((count, width), BF16),
            jax.ShapeDtypeStruct((count, width), F32),
            jax.ShapeDtypeStruct((count, width), BF16),
            jax.ShapeDtypeStruct(table.shape, F32),
            jax.ShapeDtypeStruct(output_w.shape, BF16),
            jax.ShapeDtypeStruct(inner_w.shape, BF16),
            jax.ShapeDtypeStruct(outer_w.shape, BF16),
        ],
        in_specs=[whole] * 3 + [pl.BlockSpec(memory_space=pltpu.SMEM), whole] + [far] * 3,
        out_specs=[whole] * 5 + [far] * 2,
        scratch_shapes=[
            pltpu.VMEM(output_w.shape, BF16),
            pltpu.VMEM((tiles, width, tile), BF16),
            pltpu.VMEM((tiles, tile, width), BF16),
            pltpu.VMEM((TABLE_ROWS, width), F32),
            pltpu.VMEM((TABLE_ROWS, width), F32),
            pltpu.VMEM((tiles, count, tile), BF16),
            pltpu.VMEM((tiles, count, tile), F32),
            space(F32),
            pltpu.VMEM((8, LANES), F32),
            pltpu.VMEM((count, LANES), F32),
            space(F32),
            space(BF16),
            pltpu.VMEM((width, count), BF16),
            space(F32),
            space(BF16),
            pltpu.VMEM((2, width, tile), BF16),
            pltpu.VMEM((2, tile, width), BF16),
            pltpu.SemaphoreType.DMA((3, tiles)),
            pltpu.SemaphoreType.DMA((2, 2)),
        ],
        compiler_params=pltpu.CompilerParams(vmem_limit_bytes=60 << 20),
        name="feed_forward",
    )(rows, context, cot, lengths, table, output_w, inner_w, outer_w)


def widen_kernel(splits, *refs):
    count = len(splits)
    ins, refs = refs[:count], refs[count:]
    outs = refs[: sum(splits)]
    wides, sems = refs[sum(splits) : -1], refs[-1]
    copies = []
    at = 0
    for source, parts in zip(ins, splits):
        columns = source.shape[-1] // parts
        for part in range(parts):
            wides[at][...] = source[..., part * columns : (part + 1) * columns].astype(F32)
            copies.append(pltpu.make_async_copy(wides[at], outs[at], sems.at[at]))
            copies[-1].start()
            at += 1
    for copy in copies:
        copy.wait()


def widen(arrays, splits):
    shapes = []
    for array, parts in zip(arrays, splits):
        shapes += [array.shape[:-1] + (array.shape[-1] // parts,)] * parts
    return pl.pallas_call(
        functools.partial(widen_kernel, splits),
        out_shape=[jax.ShapeDtypeStruct(shape, F32) for shape in shapes],
        in_specs=[pl.BlockSpec(memory_space=pltpu.VMEM)] * len(arrays),
        out_specs=[pl.BlockSpec(memory_space=pl.ANY)] * len(shapes),
        scratch_shapes=[pltpu.VMEM(shape, F32) for shape in shapes]
        + [pltpu.SemaphoreType.DMA((len(shapes),))],
        compiler_params=pltpu.CompilerParams(vmem_limit_bytes=40 << 20),
        name="widen_results",
    )(*arrays)


def greet_twin(place):
    barrier = pltpu.get_barrier_semaphore()
    pl.semaphore_signal(barrier, inc=1, device_id=place.twin(), device_id_type=MESH)
    pl.semaphore_wait(barrier, 1)


def stack_heads(block, lower):
    zero = jnp.zeros_like(block)
    return jnp.concatenate((jnp.where(lower, block, zero), jnp.where(lower, zero, block)), axis=0)


SPAN = 2 * HEAD_DIM


def span_of(section, pair, width):
    return pl.ds(pl.multiple_of(section * width + pair * SPAN, SPAN), SPAN)


class AttentionForward:
    def __init__(self, place, rows, weight, vec, bias, qkv, context, probs, away, tiles, send, recv, load):
        self.place, self.rows, self.weight, self.vec, self.bias = place, rows, weight, vec, bias
        self.qkv, self.context, self.probs, self.away = qkv, context, probs, away
        self.tiles, self.send, self.recv, self.load = tiles, send, recv, load
        self.count, self.width = context.shape
        self.pairs = self.width // SPAN
        self.tile = tiles.shape[2]

    def fetch_weight(self, t):
        return pltpu.make_async_copy(
            self.weight.at[:, pl.ds(t * self.tile, self.tile)], self.tiles.at[t], self.load.at[t]
        )

    def fetch(self, which, pair):
        return pltpu.make_async_remote_copy(
            self.qkv.at[:, span_of(which + 1, pair, self.width)],
            self.away.at[:, span_of(which, pair, self.width)],
            self.send.at[which, pair],
            self.recv.at[which, pair],
            device_id=self.place.twin(),
            device_id_type=MESH,
        )

    def project(self, t):
        columns = pl.ds(t * self.tile, self.tile)
        per = self.width // self.tile
        section = t // per
        self.fetch_weight(t).wait()
        product = plain_product(self.rows[...], self.tiles[t])
        if section != 1:
            row = ROW_QUERY if section == 0 else ROW_VALUE
            product = product + self.vec[pl.ds(row, 1), pl.ds((t % per) * self.tile, self.tile)]
        self.qkv[:, columns] = product.astype(BF16)

    def give(self, t):
        per = self.width // self.tile
        section = t // per
        if section:
            share = self.tile // SPAN
            for pair in range((t % per) * share, (t % per + 1) * share):
                self.fetch(section - 1, pair).start()

    def attend(self, pair):
        for which in range(2):
            self.fetch(which, pair).wait_recv()
        count = self.count
        lower = lax.broadcasted_iota(jnp.int32, (count, SPAN), 1) < HEAD_DIM

        def here(section):
            return self.qkv[:, span_of(section, pair, self.width)]

        def there(section):
            return self.away[:, span_of(section - 1, pair, self.width)]

        stacked = stack_heads(here(0) * HEAD_DIM**-0.5, lower)
        keys = jnp.concatenate((here(1), there(1)), axis=0)
        values = jnp.concatenate((here(2), there(2)), axis=0)
        scores = right_product(stacked, keys) + self.bias[:1, :]
        top = jnp.max(scores, axis=1, keepdims=True)
        weights = jnp.exp(scores - top)
        total = jnp.sum(weights, axis=1, keepdims=True)
        probs = (weights * (1.0 / total)).astype(BF16)
        self.probs[pair] = probs
        mixed = plain_product(probs, values)
        self.context[:, span_of(0, pair, self.width)] = jnp.where(
            lower, mixed[:count], mixed[count:]
        ).astype(BF16)

    def finish(self):
        for pair in range(self.pairs):
            for which in range(2):
                self.fetch(which, pair).wait_send()


def attend_kernel(
    rows_ref, lengths_ref, table_ref, weight, qkv, context, probs, away, bias_ref, tiles, vec, send, recv, load
):
    place = Place()
    rows = rows_ref.shape[0]
    length = lengths_ref[place.side, 0]
    row = lax.broadcasted_iota(jnp.int32, (8, rows), 1)
    for k, core in enumerate((place.core, 1 - place.core)):
        bias_ref[:, pl.ds(k * rows, rows)] = jnp.where(
            row_place(row, core, rows) < length, 0.0, -1e30
        )
    work = AttentionForward(
        place, rows_ref, weight, vec, bias_ref, qkv, context, probs, away, tiles, send, recv, load
    )
    count = tiles.shape[0]
    order = list(range(count // 3, count)) + list(range(count // 3))
    for t in order:
        work.fetch_weight(t).start()
    greet_twin(place)
    spread_table(table_ref, vec)
    for before, t in zip([None] + order, order):
        work.project(t)
        if before is not None:
            work.give(before)

    def step(pair, carry):
        work.attend(pair)
        return carry

    lax.fori_loop(0, work.pairs, step, 0)
    work.finish()


def attend(rows, lengths, table, weight, collective_id):
    count, width = rows.shape
    pairs = width // SPAN
    tile = 512
    tiles = weight.shape[1] // tile
    whole = pl.BlockSpec(memory_space=pltpu.VMEM)
    return pl.pallas_call(
        attend_kernel,
        out_shape=[
            jax.ShapeDtypeStruct((count, 3 * width), BF16),
            jax.ShapeDtypeStruct((count, width), BF16),
            jax.ShapeDtypeStruct((pairs, 2 * count, 2 * count), BF16),
            jax.ShapeDtypeStruct((count, 2 * width), BF16),
        ],
        in_specs=[
            whole,
            pl.BlockSpec(memory_space=pltpu.SMEM),
            whole,
            pl.BlockSpec(memory_space=pl.ANY),
        ],
        out_specs=[whole] * 4,
        scratch_shapes=[
            pltpu.VMEM((8, 2 * count), F32),
            pltpu.VMEM((tiles, width, tile), BF16),
            pltpu.VMEM((TABLE_ROWS, width), F32),
            pltpu.SemaphoreType.DMA((2, pairs)),
            pltpu.SemaphoreType.DMA((2, pairs)),
            pltpu.SemaphoreType.DMA((tiles,)),
        ],
        compiler_params=pltpu.CompilerParams(
            collective_id=collective_id, has_side_effects=True, vmem_limit_bytes=40 << 20
        ),
        name="attention_forward",
    )(rows, lengths, table, weight)


class AttentionBackward:
    def __init__(
        self, place, rows, qkv, away, probs, grad, weight, out, weight_grad, tiles, blocks, keep, leave, come, send, recv, load, save
    ):
        self.place, self.rows, self.qkv, self.away, self.probs = place, rows, qkv, away, probs
        self.grad, self.weight, self.out, self.weight_grad = grad, weight, out, weight_grad
        self.tiles, self.blocks, self.keep, self.leave, self.come = tiles, blocks, keep, leave, come
        self.send, self.recv, self.load, self.save = send, recv, load, save
        self.count, self.width = grad.shape
        self.pairs = self.width // SPAN
        self.tile = tiles.shape[2]

    def fetch_weight(self, t):
        return pltpu.make_async_copy(
            self.weight.at[:, pl.ds(t * self.tile, self.tile)], self.tiles.at[t], self.load.at[t]
        )

    def give(self, which, pair):
        return pltpu.make_async_remote_copy(
            self.leave.at[:, span_of(which, pair, self.width)],
            self.come.at[:, span_of(which, pair, self.width)],
            self.send.at[which, pair],
            self.recv.at[which, pair],
            device_id=self.place.twin(),
            device_id_type=MESH,
        )

    def attend(self, pair):
        count = self.count
        lower = lax.broadcasted_iota(jnp.int32, (count, SPAN), 1) < HEAD_DIM
        scale = HEAD_DIM**-0.5

        def here(section):
            return self.qkv[:, span_of(section, pair, self.width)]

        def there(section):
            return self.away[:, span_of(section - 1, pair, self.width)]

        first = span_of(0, pair, self.width)
        second = span_of(1, pair, self.width)
        stacked = stack_heads(here(0) * scale, lower)
        keys = jnp.concatenate((here(1), there(1)), axis=0)
        values = jnp.concatenate((here(2), there(2)), axis=0)
        grad = stack_heads(self.grad[:, first], lower)
        probs = self.probs[pair]
        value_part = left_product(probs, grad)
        probs_grad = right_product(grad, values)
        wide = probs.astype(F32)
        inner = jnp.sum(wide * probs_grad, axis=1, keepdims=True)
        scores_grad = (wide * (probs_grad - inner)).astype(BF16)
        key_part = left_product(scores_grad, stacked)
        self.leave[:, first] = key_part[count:].astype(BF16)
        self.leave[:, second] = value_part[count:].astype(BF16)
        self.keep[:, first] = key_part[:count]
        self.keep[:, second] = value_part[:count]
        mixed = plain_product(scores_grad, keys) * scale
        self.out[:, first] = jnp.where(lower, mixed[:count], mixed[count:]).astype(BF16)
        for which in range(2):
            self.give(which, pair).start()

    def settle(self, pair):
        for which in range(2):
            self.give(which, pair).wait_recv()
            here = span_of(which, pair, self.width)
            self.out[:, span_of(which + 1, pair, self.width)] = (
                self.keep[:, here] + self.come[:, here].astype(F32)
            ).astype(BF16)

    def weigh(self, t, rows_t):
        columns = pl.ds(t * self.tile, self.tile)
        self.blocks[t] = plain_product(rows_t, self.out[:, columns]).astype(BF16)

    def save_weight(self, t):
        return pltpu.make_async_copy(
            self.blocks.at[t], self.weight_grad.at[:, pl.ds(t * self.tile, self.tile)], self.save.at[t]
        )

    def spread(self, t):
        columns = pl.ds(t * self.tile, self.tile)
        self.fetch_weight(t).wait()
        return right_product(self.out[:, columns], self.tiles[t])

    def bias_sums(self, sums):
        sums[pl.ds(ROW_QUERY, 1), :] = total_rows(self.out[:, : self.width])
        sums[pl.ds(ROW_VALUE, 1), :] = total_rows(self.out[:, 2 * self.width :])

    def finish(self):
        for pair in range(self.pairs):
            for which in range(2):
                self.give(which, pair).wait_send()


def attend_back_kernel(
    rows_ref, qkv, away, probs, grad, first_grad, table_ref, weight,
    weight_grad, input_grad, sums_ref,
    out, tiles, blocks, keep, leave, come, total, sums, rows_t, send, recv, load, save,
):
    place = Place()
    work = AttentionBackward(
        place, rows_ref, qkv, away, probs, grad, weight, out, weight_grad, tiles, blocks,
        keep, leave, come, send, recv, load, save,
    )
    count = tiles.shape[0]
    for t in range(count):
        work.fetch_weight(t).start()
    greet_twin(place)

    def step(pair, carry):
        work.attend(pair)
        return carry

    lax.fori_loop(0, work.pairs, step, 0)
    rows_t[...] = rows_ref[...].T
    total[...] = first_grad[...]
    for t in range(count):
        if t == count // 3:

            def settle(pair, carry):
                work.settle(pair)
                return carry

            lax.fori_loop(0, work.pairs, settle, 0)
        work.weigh(t, rows_t[...])
        if t:
            work.save_weight(t - 1).start()
        total[...] += work.spread(t)
    work.save_weight(count - 1).start()
    input_grad[...] = total[...].astype(BF16)
    work.bias_sums(sums)
    sums_ref[...] = table_ref[...]
    fold_table(sums, sums_ref, ROW_QUERY, 2)
    for t in range(count):
        work.save_weight(t).wait()
    work.finish()


def attend_back(rows, saved, grad, first_grad, table, weight, collective_id):
    qkv, away, probs = saved
    count, width = rows.shape
    pairs = width // SPAN
    tile = 512
    tiles = weight.shape[1] // tile
    whole = pl.BlockSpec(memory_space=pltpu.VMEM)
    far = pl.BlockSpec(memory_space=pl.ANY)
    return pl.pallas_call(
        attend_back_kernel,
        out_shape=[
            jax.ShapeDtypeStruct(weight.shape, BF16),
            jax.ShapeDtypeStruct((count, width), BF16),
            jax.ShapeDtypeStruct(table.shape, F32),
        ],
        in_specs=[whole] * 7 + [far],
        out_specs=[far, whole, whole],
        scratch_shapes=[
            pltpu.VMEM((count, 3 * width), BF16),
            pltpu.VMEM((tiles, width, tile), BF16),
            pltpu.VMEM((tiles, width, tile), BF16),
            pltpu.VMEM((count, 2 * width), F32),
            pltpu.VMEM((count, 2 * width), BF16),
            pltpu.VMEM((count, 2 * width), BF16),
            pltpu.VMEM((count, width), F32),
            pltpu.VMEM((TABLE_ROWS, width), F32),
            pltpu.VMEM((width, count), BF16),
            pltpu.SemaphoreType.DMA((2, pairs)),
            pltpu.SemaphoreType.DMA((2, pairs)),
            pltpu.SemaphoreType.DMA((tiles,)),
            pltpu.SemaphoreType.DMA((tiles,)),
        ],
        compiler_params=pltpu.CompilerParams(
            collective_id=collective_id, has_side_effects=True, vmem_limit_bytes=60 << 20
        ),
        name="attention_backward",
    )(rows, qkv, away, probs, grad, first_grad, table, weight)


def exact_gelu(hidden):
    return jax.nn.gelu(hidden, approximate=False)


def plain_product(left, right):
    return jnp.dot(left, right, preferred_element_type=F32)


def left_product(left, right):
    return lax.dot_general(left, right, (((0,), (0,)), ((), ())), preferred_element_type=F32)


def right_product(left, right):
    return lax.dot_general(left, right, (((1,), (1,)), ((), ())), preferred_element_type=F32)


def column_sums(rows):
    return jnp.sum(rows.astype(F32), axis=0)


def norm_parts(total):
    average = jnp.mean(total, axis=-1, keepdims=True)
    centered = total - average
    variance = jnp.mean(centered * centered, axis=-1, keepdims=True)
    rate = lax.rsqrt(variance + EPSILON)
    return centered * rate, rate


def norm_back(unit, rate, grad):
    return rate * (
        grad
        - jnp.mean(grad, axis=-1, keepdims=True)
        - unit * jnp.mean(grad * unit, axis=-1, keepdims=True)
    )


def split_columns(packed, widths):
    pieces = []
    start = 0
    for width in widths:
        pieces.append(packed[..., start : start + width])
        start += width
    return pieces


def native_forward(queries, keys_all, values_all, key_valid, heads):
    shape = queries.shape[:2] + (heads, HEAD_DIM)
    key_shape = keys_all.shape[:2] + (heads, HEAD_DIM)
    scores = jnp.einsum(
        "sqhd,skhd->shqk",
        queries.reshape(shape),
        keys_all.reshape(key_shape),
        preferred_element_type=F32,
    ) * (HEAD_DIM**-0.5)
    scores = jnp.where(key_valid[:, None, None, :], scores, -1e30)
    top = jnp.max(scores, axis=-1, keepdims=True)
    weights = jnp.exp(scores - top)
    probs = (weights / jnp.sum(weights, axis=-1, keepdims=True)).astype(BF16)
    context = jnp.einsum(
        "shqk,skhd->sqhd", probs, values_all.reshape(key_shape), preferred_element_type=F32
    )
    return context.reshape(queries.shape).astype(BF16), probs


def native_backward(queries, keys_all, values_all, probs, context_grad, heads):
    shape = queries.shape[:2] + (heads, HEAD_DIM)
    key_shape = keys_all.shape[:2] + (heads, HEAD_DIM)
    scale = HEAD_DIM**-0.5
    grad_heads = context_grad.reshape(shape)
    wide = probs.astype(F32)
    probs_grad = jnp.einsum(
        "sqhd,skhd->shqk", grad_heads, values_all.reshape(key_shape), preferred_element_type=F32
    )
    inner_total = jnp.sum(wide * probs_grad, axis=-1, keepdims=True)
    scores_grad = (wide * (probs_grad - inner_total)).astype(BF16)
    query_grad = jnp.einsum(
        "shqk,skhd->sqhd", scores_grad, keys_all.reshape(key_shape), preferred_element_type=F32
    )
    key_part = jnp.einsum(
        "shqk,sqhd->skhd", scores_grad, queries.reshape(shape), preferred_element_type=F32
    )
    value_part = jnp.einsum("shqk,sqhd->skhd", probs, grad_heads, preferred_element_type=F32)
    return (
        (query_grad * scale).astype(BF16).reshape(queries.shape),
        (key_part * scale).astype(BF16).reshape(keys_all.shape),
        value_part.astype(BF16).reshape(values_all.shape),
    )


def gather_rows(part):
    return lax.all_gather(part, "fsdp", axis=0, tiled=True)


def reduce_rows(part):
    share = lax.psum_scatter(part.astype(BF16), "fsdp", scatter_dimension=0, tiled=True)
    return lax.psum(share, "ctx").astype(F32)


def layer(flat_rows, cot_rows, row_mask, packed, widths, weights, forward, backward):
    full_qkv, full_output, full_inner, full_outer = weights
    rows, width = flat_rows.shape
    shards = packed.shape[0]
    (
        bias_query,
        bias_value,
        bias_output,
        gain_first,
        shift_first,
        bias_inner,
        bias_outer,
        gain_second,
        shift_second,
    ) = [piece.reshape(-1).astype(F32) for piece in split_columns(packed, widths)]
    bias_qkv = jnp.concatenate((bias_query, jnp.zeros_like(bias_query), bias_value))
    qkv = (plain_product(flat_rows, full_qkv) + bias_qkv).astype(BF16)
    context, saved = forward(qkv)

    first_sum = flat_rows.astype(F32) + plain_product(context, full_output) + bias_output
    first_unit, first_rate = norm_parts(first_sum)
    normed = first_unit * gain_first + shift_first
    normed_low = normed.astype(BF16)
    hidden = plain_product(normed_low, full_inner) + bias_inner
    active, gelu_back = jax.vjp(exact_gelu, hidden)
    active_low = active.astype(BF16)
    second_sum = normed + plain_product(active_low, full_outer) + bias_outer
    second_unit, second_rate = norm_parts(second_sum)
    output = ((second_unit * gain_second + shift_second) * row_mask).astype(BF16)

    out_grad = cot_rows.astype(F32) * row_mask
    second_gain_part = jnp.sum(out_grad * second_unit, axis=0)
    second_shift_part = jnp.sum(out_grad, axis=0)
    second_grad = norm_back(second_unit, second_rate, out_grad * gain_second)
    second_low = second_grad.astype(BF16)
    outer_weight_part = left_product(active_low, second_low).astype(BF16)
    outer_bias_part = column_sums(second_low)
    (hidden_grad,) = gelu_back(right_product(second_low, full_outer))
    hidden_low = hidden_grad.astype(BF16)
    inner_weight_part = left_product(normed_low, hidden_low).astype(BF16)
    inner_bias_part = column_sums(hidden_low)
    normed_grad = second_grad + right_product(hidden_low, full_inner)
    first_gain_part = jnp.sum(normed_grad * first_unit, axis=0)
    first_shift_part = jnp.sum(normed_grad, axis=0)
    first_grad = norm_back(first_unit, first_rate, normed_grad * gain_first)
    branch_low = first_grad.astype(BF16)
    output_weight_part = left_product(context, branch_low).astype(BF16)
    output_bias_part = column_sums(branch_low)
    context_grad = right_product(branch_low, full_output).astype(BF16)
    qkv_grad = backward(saved, context_grad)
    qkv_weight_part = left_product(flat_rows, qkv_grad).astype(BF16)
    query_bias_part = column_sums(qkv_grad[:, :width])
    value_bias_part = column_sums(qkv_grad[:, 2 * width :])
    input_grad = first_grad + right_product(qkv_grad, full_qkv)
    vector_parts = (
        query_bias_part,
        value_bias_part,
        output_bias_part,
        first_gain_part,
        first_shift_part,
        inner_bias_part,
        outer_bias_part,
        second_gain_part,
        second_shift_part,
    )
    packed_parts = jnp.concatenate([part.reshape(shards, -1) for part in vector_parts], axis=1)
    return (
        output,
        input_grad,
        packed_parts,
        (qkv_weight_part, output_weight_part, inner_weight_part, outer_weight_part),
    )


def native_body(inputs, cotangent, lengths, vectors, weights):
    widths = [member.shape[0] for member in vectors]
    packed = lax.all_gather(jnp.concatenate(vectors), "fsdp", axis=0, tiled=False)
    joined = (jnp.concatenate(weights[:3], axis=1),) + weights[3:]
    full = tuple(gather_rows(part) for part in joined)
    micro, seqs, block_len, width = inputs.shape
    heads = width // HEAD_DIM
    total_slots = block_len * lax.axis_size("ctx")
    group = micro * seqs
    rows = group * block_len
    flat_len = lengths.reshape(group)
    local_pos = lax.axis_index("ctx") * block_len + jnp.arange(block_len, dtype=jnp.int32)
    row_mask = (local_pos[None, :] < flat_len[:, None]).astype(F32).reshape(rows, 1)
    key_valid = jnp.arange(total_slots, dtype=jnp.int32)[None, :] < flat_len[:, None]

    def forward(qkv):
        queries = qkv[:, :width].reshape(group, block_len, width)
        keys_values = lax.all_gather(
            qkv[:, width:].reshape(group, block_len, 2 * width), "ctx", axis=1, tiled=True
        )
        keys, values = keys_values[:, :, :width], keys_values[:, :, width:]
        context, probs = native_forward(queries, keys, values, key_valid, heads)
        return context.reshape(rows, width), (queries, keys, values, probs)

    def backward(saved, context_grad):
        query_grad, key_part, value_part = native_backward(
            *saved, context_grad.reshape(group, block_len, width), heads
        )
        keys_values_grad = lax.psum_scatter(
            jnp.concatenate((key_part, value_part), axis=2), "ctx", scatter_dimension=1, tiled=True
        )
        return jnp.concatenate(
            (query_grad.reshape(rows, width), keys_values_grad.reshape(rows, 2 * width)), axis=1
        )

    output, input_grad, packed_parts, parts = layer(
        inputs.reshape(rows, width),
        cotangent.reshape(rows, width),
        row_mask,
        packed,
        widths,
        full,
        forward,
        backward,
    )
    share = lax.psum_scatter(packed_parts, "fsdp", scatter_dimension=0, tiled=True)
    return (
        output.reshape(inputs.shape),
        input_grad.reshape(inputs.shape),
        lax.psum(share, "ctx")[0],
        tuple(split_columns(reduce_rows(parts[0]), [width] * 3))
        + tuple(reduce_rows(part) for part in parts[1:]),
    )


def direct_body(inputs, cotangent, lengths, vectors, weights):
    micro, seqs, block_len, width = inputs.shape
    shards = LINE * PAIR
    rows = 2 * block_len
    table = jnp.zeros((TABLE_ROWS, LANES), F32)
    row = 0
    for vector in vectors:
        lines = vector.shape[0] // LANES
        filled = ((row, TABLE_ROWS - row - lines), (0, 0))
        table += jnp.pad(vector.astype(F32).reshape(lines, LANES), filled)
        row += lines
    query_weight, key_weight, value_weight, output_weight, inner_weight, outer_weight = weights
    blocks = (inputs.reshape(micro, block_len, width), cotangent.reshape(micro, block_len, width))
    shard_rows, hidden = inner_weight.shape
    flows = [Flow(0, TABLE_ROWS, lambda core, side: (0, TABLE_ROWS, 0, LANES), cores=False)]
    flows += column_flows(1, shard_rows, 3 * width, *GATHER_SPLIT[0])
    flows += column_flows(2, shard_rows, width, *GATHER_SPLIT[1])
    flows += column_flows(3, shard_rows, hidden, *GATHER_SPLIT[2])
    flows += row_flows(4, hidden // shards, width, *GATHER_SPLIT[3])
    tables, full_qkv, full_output, full_inner, full_outer, in_rows, cot_rows = gather_call(
        (table.astype(BF16),) + weights,
        ((0, 0), (1, 0), (1, width), (1, 2 * width), (2, 0), (3, 0), (4, 0)),
        blocks,
        flows,
        shards,
        1,
        GATHER_ORDER,
    )
    in_rows = in_rows.reshape(rows, width)
    cot_rows = cot_rows.reshape(rows, width)
    qkv, context, probs, away = attend(in_rows, lengths, tables, full_qkv, 3)
    output, first_grad, context_grad, table_grad, output_part, inner_part, outer_part = middle(
        in_rows, context, cot_rows, lengths, tables, full_output, full_inner, full_outer
    )
    qkv_part, input_grad, table_grad = attend_back(
        in_rows, (qkv, away, probs), context_grad, first_grad, table_grad, full_qkv, 4
    )
    sums = reduce_call(
        (inner_part, outer_part, output_part, qkv_part, table_grad),
        (
            output.reshape(micro, block_len, width),
            input_grad.reshape(micro, block_len, width),
        ),
        [
            column_part(shard_rows, hidden, *REDUCE_SPLIT[0]),
            row_part(hidden // shards, width, *REDUCE_SPLIT[1]),
            column_part(shard_rows, width, *REDUCE_SPLIT[2]),
            column_part(shard_rows, 3 * width, *REDUCE_SPLIT[3]),
            vector_part(TABLE_ROWS, LANES),
        ],
        2,
        REDUCE_ORDER,
    )
    inner_share, outer_share, output_share, qkv_share, table_share, outs, grads = sums
    wide = widen((qkv_share, output_share, inner_share, outer_share, grads), (3, 1, 1, 1, 1))
    return (
        outs.reshape(inputs.shape),
        wide[6].reshape(inputs.shape),
        table_share.reshape(-1),
        tuple(wide[:6]),
    )


def body(
    inputs,
    cotangent,
    lengths,
    query_weight,
    key_weight,
    value_weight,
    output_weight,
    query_bias,
    value_bias,
    output_bias,
    first_gain,
    first_shift,
    inner_weight,
    inner_bias,
    outer_weight,
    outer_bias,
    second_gain,
    second_shift,
):
    vectors = (
        query_bias,
        value_bias,
        output_bias,
        first_gain,
        first_shift,
        inner_bias,
        outer_bias,
        second_gain,
        second_shift,
    )
    widths = [member.shape[0] for member in vectors]
    weights = (
        query_weight,
        key_weight,
        value_weight,
        output_weight,
        inner_weight,
        outer_weight,
    )
    laid_out = lax.axis_size("fsdp") == LINE * PAIR and lax.axis_size("ctx") == 4
    whole_lines = all(extent % LANES == 0 for extent in widths)
    direct = laid_out and inputs.shape[:2] == (2, 1) and whole_lines
    run = direct_body if direct else native_body
    output, input_grad, vector_share, weight_shares = run(
        inputs, cotangent, lengths, vectors, weights
    )
    shares = split_columns(vector_share, widths)
    query_share, key_share, value_share, output_share, inner_share, outer_share = weight_shares
    return (
        output,
        input_grad,
        query_share,
        key_share,
        value_share,
        output_share,
        shares[0],
        shares[1],
        shares[2],
        shares[3],
        shares[4],
        inner_share,
        shares[5],
        outer_share,
        shares[6],
        shares[7],
        shares[8],
    )


def solution(mesh):
    data = P(None, "fsdp", "ctx", None)
    matrix = P("fsdp", None)
    vector = P("fsdp")
    return jax.shard_map(
        body,
        mesh=mesh,
        in_specs=(data, data, P(None, "fsdp"))
        + (matrix,) * 4
        + (vector,) * 5
        + (matrix, vector, matrix, vector, vector, vector),
        out_specs=(data, data)
        + (matrix,) * 4
        + (vector,) * 5
        + (matrix, vector, matrix, vector, vector, vector),
        check_vma=False,
    )
```

```python
import functools

import jax
import jax.numpy as jnp
from jax import lax
from jax.experimental import pallas as pl
from jax.experimental.pallas import tpu as pltpu
from jax.sharding import PartitionSpec as P

HEAD_DIM = 64
EPSILON = 1e-06
F32 = jnp.float32
BF16 = jnp.bfloat16

GATHER_SPLIT = ((512, 0), (256, 0), (256, 384), (128, 32))
REDUCE_SPLIT = ((768, 512), (128, 32), (256, 128), (768, 256))
GATHER_ORDER = (
    5, 6, 2, 0, 1, 3, 9, 13, 64, 29, 10, 4, 81, 30, 26, 62, 36, 7, 47, 149, 75, 70, 53, 94, 14,
    104, 11, 32, 82, 27, 79, 217, 143, 46, 33, 218, 35, 24, 49, 28, 162, 16, 160, 63, 71, 38, 132,
    131, 67, 34, 115, 200, 60, 172, 41, 8, 98, 21, 96, 201, 101, 58, 84, 66, 138, 68, 189, 100,
    69, 109, 50, 103, 135, 113, 80, 106, 97, 164, 163, 130, 40, 211, 54, 120, 45, 22, 152, 169,
    166, 126, 23, 31, 74, 116, 72, 83, 144, 89, 61, 212, 148, 183, 198, 76, 171, 174, 139, 147,
    114, 12, 153, 137, 177, 118, 77, 168, 161, 206, 203, 173, 136, 199, 154, 55, 215, 65, 121,
    155, 91, 110, 230, 99, 142, 134, 228, 216, 39, 181, 95, 105, 78, 184, 48, 37, 165, 73, 150,
    223, 178, 188, 229, 19, 102, 167, 17, 182, 85, 128, 140, 87, 186, 15, 51, 25, 170, 156, 108,
    133, 205, 207, 145, 119, 175, 220, 59, 57, 194, 86, 52, 204, 43, 157, 56, 151, 232, 122, 233,
    234, 90, 210, 129, 185, 20, 123, 42, 127, 141, 196, 125, 190, 235, 18, 159, 221, 44, 202, 117,
    176, 92, 224, 236, 107, 111, 208, 237, 222, 213, 88, 179, 197, 158, 231, 191, 225, 238, 193,
    214, 209, 112, 124, 219, 187, 180, 239, 226, 195, 192, 146, 93, 227, 240,
)
REDUCE_ORDER = (
    30, 232, 8, 29, 7, 84, 33, 15, 0, 6, 231, 9, 10, 18, 85, 14, 233, 1, 35, 2, 41, 134, 234, 235,
    118, 87, 86, 91, 92, 119, 12, 236, 51, 137, 42, 34, 36, 89, 28, 237, 31, 11, 19, 133, 3, 240,
    215, 52, 37, 238, 27, 21, 93, 88, 141, 122, 214, 94, 140, 22, 20, 106, 219, 23, 43, 100, 53,
    38, 239, 166, 44, 17, 69, 4, 165, 116, 13, 120, 138, 167, 95, 26, 39, 110, 104, 101, 123, 221,
    217, 149, 25, 157, 222, 108, 45, 67, 173, 68, 90, 32, 172, 96, 136, 16, 135, 117, 54, 24, 71,
    46, 183, 124, 126, 197, 5, 220, 199, 200, 169, 224, 102, 241, 40, 103, 57, 121, 216, 170, 198,
    184, 151, 143, 242, 75, 72, 70, 105, 174, 55, 47, 63, 168, 243, 58, 73, 187, 74, 153, 223,
    139, 127, 61, 125, 181, 185, 150, 48, 218, 76, 49, 109, 175, 128, 59, 154, 159, 205, 171, 56,
    226, 97, 107, 145, 225, 201, 177, 202, 176, 142, 152, 182, 98, 50, 62, 227, 189, 155, 111, 77,
    203, 60, 191, 207, 193, 178, 206, 179, 129, 158, 130, 79, 161, 204, 78, 228, 112, 156, 144,
    188, 131, 209, 186, 64, 99, 65, 160, 180, 113, 208, 114, 132, 192, 190, 162, 163, 80, 81, 146,
    147, 210, 66, 211, 229, 194, 82, 164, 195, 148, 212, 115, 83, 196, 213, 230,
)

MESH = pl.DeviceIdType.MESH
LINE = 4
PAIR = 2


class Place:
    def __init__(self):
        self.ctx = lax.axis_index("ctx")
        self.shard = lax.axis_index("fsdp")
        self.side = lax.div(self.ctx, 2)
        self.core = lax.rem(self.ctx, 2)
        self.line = lax.div(self.shard, PAIR)
        self.pair = lax.rem(self.shard, PAIR)

    def ahead(self, way):
        return (self.ctx, self.shard + way * PAIR)

    def across(self):
        return (self.ctx, self.shard + 1 - 2 * self.pair)

    def beside(self):
        return (self.ctx + 2 - 4 * self.side, self.shard)

    def twin(self):
        return (self.ctx + 1 - 2 * self.core, self.shard)

    def has(self, way, steps):
        if steps == 0:
            return None
        return self.line >= steps if way > 0 else self.line <= LINE - 1 - steps

    def can(self, way):
        return self.line <= LINE - 2 if way > 0 else self.line >= 1

    def shard_of(self, way, steps, other):
        pair = 1 - self.pair if other else self.pair
        return (self.line - way * steps) * PAIR + pair


def when(conditions, action):
    held = [c for c in conditions if c is not None]
    if not held:
        action()
        return
    both = held[0]
    for c in held[1:]:
        both = jnp.logical_and(both, c)
    pl.when(both)(action)


def greet(place):
    barrier = pltpu.get_barrier_semaphore()
    for peer in (place.across(), place.beside(), place.twin()):
        pl.semaphore_signal(barrier, inc=1, device_id=peer, device_id_type=MESH)
    for way in (1, -1):
        when(
            [place.can(way)],
            lambda way=way: pl.semaphore_signal(
                barrier, inc=1, device_id=place.ahead(way), device_id_type=MESH
            ),
        )
    lines = jnp.minimum(place.line, 1) + jnp.minimum(LINE - 1 - place.line, 1)
    pl.semaphore_wait(barrier, 3 + lines)


class Flow:
    def __init__(self, array, shard_rows, region, order="line", sides=False, cores=True):
        self.array = array
        self.shard_rows = shard_rows
        self.region = region
        self.order = order
        self.sides = sides
        self.cores = cores

    def view(self, ref, shard, core, side):
        row, rows, column, columns = self.region(core, side)
        start = row if shard is None else shard * self.shard_rows + row
        if not isinstance(start, int):
            start = pl.multiple_of(start, 16)
        if not isinstance(column, int):
            column = pl.multiple_of(column, 128)
        return ref.at[pl.ds(start, rows), pl.ds(column, columns)]


def positions(order):
    found = []
    if order == "line":
        found.append(("P", 1, 0, True))
        for steps in range(1, LINE):
            for way in (1, -1):
                found.append(("L", way, steps, False))
                found.append(("P", way, steps, True))
    else:
        found.append(("P", 1, 0, True))
        for steps in range(1, LINE):
            for way in (1, -1):
                found.append(("L", way, steps, False))
                found.append(("L", way, steps, True))
    return found


class Labels:
    def __init__(self):
        self.numbers = {}

    def __call__(self, key):
        return self.numbers.setdefault(key, len(self.numbers))


def gather_labels(flows):
    labels = Labels()
    for number, flow in enumerate(flows):
        for spot in positions(flow.order):
            labels((number, "in") + spot)
            if flow.sides:
                labels((number, "side") + spot)
            if flow.cores:
                labels((number, "twin") + spot)
                if flow.sides:
                    labels((number, "twinside") + spot)
    return labels


class Gather:
    def __init__(self, place, flows, owns, fulls, send, recv):
        self.place, self.flows, self.owns, self.fulls = place, flows, owns, fulls
        self.send, self.recv = send, recv
        self.labels = gather_labels(flows)
        self.sent = []

    def copy(self, number, key, spot, peer, core, side, own=False):
        flow = self.flows[number]
        place = self.place
        if own:
            shard = place.shard
            source = flow.view(self.owns[flow.array], None, core, side)
        else:
            shard = place.shard_of(*spot[1:])
            source = flow.view(self.fulls[flow.array], shard, core, side)
        target = flow.view(self.fulls[flow.array], shard, core, side)
        label = self.labels((number,) + key)
        return pltpu.make_async_remote_copy(
            source,
            target,
            self.send.at[label],
            self.recv.at[label],
            device_id=peer,
            device_id_type=MESH,
        )

    def start(self, conditions, copy):
        when(conditions, copy.start)
        self.sent.append((conditions, copy))

    def begin(self, number):
        flow, place = self.flows[number], self.place
        core, side = place.core, place.side
        here = (None, 1, 0, False)
        for way in (1, -1):
            self.start(
                [place.can(way)],
                self.copy(
                    number, ("in", "L", way, 1, False), here, place.ahead(way), core, side, True
                ),
            )
        self.start(
            [],
            self.copy(number, ("in", "P", 1, 0, True), here, place.across(), core, side, True),
        )

    def arrive(self, number, spot):
        flow, place = self.flows[number], self.place
        kind, way, steps, other = spot
        core, side = place.core, place.side
        there = place.has(way, steps)

        def take():
            self.copy(number, ("in",) + spot, spot, place.across(), core, side).wait_recv()

        when([there], take)

        def onward(extra, key, peer):
            self.start(
                [c for c in (there, extra) if c is not None],
                self.copy(number, key, spot, peer, core, side),
            )

        if kind == "L" and steps + 1 < LINE:
            onward(place.can(way), ("in", "L", way, steps + 1, other), place.ahead(way))
        if kind == "L" and flow.order == "line":
            onward(None, ("in", "P", way, steps, True), place.across())
        if kind == "P" and flow.order == "pair":
            for direction in (1, -1):
                onward(
                    place.can(direction), ("in", "L", direction, 1, True), place.ahead(direction)
                )
        if flow.sides:
            onward(None, ("side",) + spot, place.beside())
        if flow.cores:
            onward(None, ("twin",) + spot, place.twin())

    def arrive_side(self, number, spot):
        flow, place = self.flows[number], self.place
        there = place.has(*spot[1:3])
        core, side = place.core, 1 - place.side
        when(
            [there],
            lambda: self.copy(
                number, ("side",) + spot, spot, place.beside(), core, side
            ).wait_recv(),
        )
        if flow.cores:
            self.start(
                [there] if there is not None else [],
                self.copy(number, ("twinside",) + spot, spot, place.twin(), core, side),
            )

    def arrive_twin(self, number, spot):
        flow, place = self.flows[number], self.place
        there = place.has(*spot[1:3])
        core = 1 - place.core
        if flow.cores:
            when(
                [there],
                lambda: self.copy(
                    number, ("twin",) + spot, spot, place.twin(), core, place.side
                ).wait_recv(),
            )
            if flow.sides:
                when(
                    [there],
                    lambda: self.copy(
                        number, ("twinside",) + spot, spot, place.twin(), core, 1 - place.side
                    ).wait_recv(),
                )

    def actions(self):
        found = []
        for n, flow in enumerate(self.flows):
            found.append((("begin", n), lambda n=n: self.begin(n)))
        for index in range(len(positions("line"))):
            for n, flow in enumerate(self.flows):
                spot = positions(flow.order)[index]
                found.append((("in", n, spot), lambda n=n, spot=spot: self.arrive(n, spot)))
                if flow.sides:
                    found.append(
                        (("side", n, spot), lambda n=n, spot=spot: self.arrive_side(n, spot))
                    )
        return found

    def wait_twins(self, arrays):
        for number, flow in enumerate(self.flows):
            if flow.array in arrays:
                for spot in positions(flow.order):
                    self.arrive_twin(number, spot)

    def finish(self, arrays):
        self.wait_twins(arrays)
        for conditions, copy in self.sent:
            when(conditions, copy.wait_send)


class Swap:
    def __init__(self, place, ins, outs, send, recv, local):
        side = place.side
        self.away = [
            pltpu.make_async_remote_copy(
                here.at[1 - side],
                there.at[side],
                send.at[k],
                recv.at[k],
                device_id=place.beside(),
                device_id_type=MESH,
            )
            for k, (here, there) in enumerate(zip(ins, outs))
        ]
        self.stay = [
            pltpu.make_async_copy(here.at[side], there.at[side], local.at[k])
            for k, (here, there) in enumerate(zip(ins, outs))
        ]

    def start(self):
        for copy in self.away + self.stay:
            copy.start()

    def finish(self):
        for copy in self.away + self.stay:
            copy.wait()


def swap_scratch(count):
    return [pltpu.SemaphoreType.DMA((count,))] * 3


def column_flows(array, shard_rows, columns, shared, early):
    half = columns // 2
    part = (half - shared) // 2
    flows = []
    if shared:
        flows.append(
            Flow(array, shard_rows, lambda core, side: (0, shard_rows, core * half, shared))
        )
    if early:
        flows.append(
            Flow(
                array,
                shard_rows,
                lambda core, side: (0, shard_rows, core * half + shared + side * part, early),
                sides=True,
            )
        )
    if part > early:
        flows.append(
            Flow(
                array,
                shard_rows,
                lambda core, side: (
                    0,
                    shard_rows,
                    core * half + shared + side * part + early,
                    part - early,
                ),
                order="pair",
                sides=True,
            )
        )
    return flows


def row_flows(array, shard_rows, columns, shared, early):
    half = shard_rows // 2
    part = (half - shared) // 2
    return [
        Flow(array, shard_rows, lambda core, side: (core * half, shared, 0, columns)),
        Flow(
            array,
            shard_rows,
            lambda core, side: (core * half + shared + side * part, early, 0, columns),
            sides=True,
        ),
        Flow(
            array,
            shard_rows,
            lambda core, side: (core * half + shared + side * part + early, part - early, 0, columns),
            order="pair",
            sides=True,
        ),
    ]


class Part:
    def __init__(self, rows, columns, along, flows, dtype=BF16, inside=False):
        self.rows, self.columns, self.along, self.dtype = rows, columns, along, dtype
        self.inside = inside
        self.flows = flows
        self.half_rows = rows // 2 if along == "rows" else rows
        self.half_columns = columns // 2 if along == "columns" else columns

    def half(self, ref, shard, core):
        base = 0 if shard is None else pl.multiple_of(shard * self.rows, 16)
        if self.along == "rows":
            row = core * self.half_rows + (0 if shard is None else shard * self.rows)
            return ref.at[pl.ds(pl.multiple_of(row, 16), self.half_rows), :]
        if self.along == "columns":
            column = pl.multiple_of(core * self.half_columns, 128)
            return ref.at[pl.ds(base, self.rows), pl.ds(column, self.half_columns)]
        return ref.at[pl.ds(base, self.rows), :]

    def inner(self, flow, side):
        first, extent = flow[0](side), flow[1]
        if self.along == "rows":
            start = first if isinstance(first, int) else pl.multiple_of(first, 16)
            return pl.ds(start, extent), slice(None)
        start = first if isinstance(first, int) else pl.multiple_of(first, 128)
        return slice(None), pl.ds(start, extent)

    def outer(self, flow, core, side):
        first, extent = flow[0](side), flow[1]
        if self.along == "rows":
            return pl.ds(pl.multiple_of(core * self.half_rows + first, 16), extent), slice(None)
        if self.along == "columns":
            return slice(None), pl.ds(
                pl.multiple_of(core * self.half_columns + first, 128), extent
            )
        return slice(None), slice(None)

    def extent(self, flow):
        if self.along == "rows":
            return flow[1], self.half_columns
        return self.half_rows, flow[1]


SPOTS = [(1, 3), (-1, 3), (1, 2), (-1, 2), (1, 1), (-1, 1), (1, 0)]


def reduce_scratch(parts):
    shapes = []
    for part in parts:
        half = (LINE * PAIR, part.half_rows, part.half_columns)
        shapes.append(pltpu.VMEM(half, part.dtype))
        shapes.append(pltpu.VMEM(half if part.along else half[1:], part.dtype))
        for flow in part.flows:
            rows, columns = part.extent(flow)
            shapes.append(
                pltpu.VMEM((LINE * PAIR if flow[3] else 1, rows, columns), part.dtype)
            )
            shapes.append(
                pltpu.VMEM((LINE if flow[2] == "line" else 1, rows, columns), part.dtype)
            )
            shapes.append(
                pltpu.VMEM(
                    ((LINE + 1) * (1 if flow[2] == "line" else PAIR), rows, columns), part.dtype
                )
            )
    return shapes


def reduce_labels(parts):
    labels = Labels()
    for n, part in enumerate(parts):
        for way, steps in SPOTS:
            for other in (False, True):
                labels((n, "twin", way, steps, other))
        labels((n, "twinend"))
        for k, flow in enumerate(part.flows):
            for way, steps in SPOTS:
                for other in (False, True):
                    if flow[3]:
                        labels((n, k, "side", way, steps, other))
                    if flow[2] == "pair" or not other:
                        labels((n, k, "line", way, steps, other))
                        if steps == 0:
                            labels((n, k, "line", -way, steps, other))
                if flow[2] == "line" or steps == 0:
                    labels((n, k, "pair", way, steps))
            labels((n, k, "sideend"))
            labels((n, k, "twinend"))
            labels((n, k, "twinsideend"))
    return labels


class Reduce:
    def __init__(self, place, parts, grads, outs, scratch, send, recv, load):
        self.place, self.parts, self.grads, self.outs = place, parts, grads, outs
        self.send, self.recv, self.load = send, recv, load
        self.labels = reduce_labels(parts)
        self.sent = []
        self.own, self.other, self.lanes = [], [], []
        at = 0
        for part in parts:
            self.own.append(scratch[at])
            self.other.append(scratch[at + 1])
            at += 2
            lanes = []
            for _ in part.flows:
                lanes.append(scratch[at : at + 3])
                at += 3
            self.lanes.append(lanes)

    def copy(self, source, target, key, peer):
        label = self.labels(key)
        return pltpu.make_async_remote_copy(
            source,
            target,
            self.send.at[label],
            self.recv.at[label],
            device_id=peer,
            device_id_type=MESH,
        )

    def start(self, conditions, copy):
        when(conditions, copy.start)
        self.sent.append((conditions, copy))

    def there(self, spot):
        return self.place.has(-spot[0], spot[1])

    def shard(self, spot, other):
        return self.place.shard_of(-spot[0], spot[1], other)

    def keep(self, n, spot, other):
        shard = self.shard(spot, other)
        label = SPOTS.index(spot) * 2 + int(other)
        return pltpu.make_async_copy(
            self.parts[n].half(self.grads[n], shard, self.place.core),
            self.own[n].at[shard],
            self.load.at[n * 2 * len(SPOTS) + label],
        )

    def twin(self, n, spot, other, core):
        shard = self.shard(spot, other)
        part = self.parts[n]
        return self.copy(
            self.grads[n].at[shard] if part.inside else part.half(self.grads[n], shard, core),
            self.other[n].at[shard],
            (n, "twin") + spot + (other,),
            self.place.twin(),
        )

    def begin(self, n, spot):
        there = self.there(spot)
        for other in (True, False):
            if not self.parts[n].inside:
                when([there], self.keep(n, spot, other).start)
            if self.parts[n].along:
                self.start([there], self.twin(n, spot, other, 1 - self.place.core))

    def piece(self, n, k, shard, side):
        part = self.parts[n]
        rows, columns = part.inner(part.flows[k], side)
        return self.own[n].at[shard, rows, columns]

    def side_copy(self, n, k, spot, other, side):
        shard = self.shard(spot, other)
        return self.copy(
            self.piece(n, k, shard, side),
            self.lanes[n][k][0].at[shard],
            (n, k, "side") + spot + (other,),
            self.place.beside(),
        )

    def add_cores(self, n, spot):
        there = self.there(spot)
        part = self.parts[n]
        for other in (True, False):

            def add(other=other):
                shard = self.shard(spot, other)
                if not part.inside:
                    self.keep(n, spot, other).wait()
                if part.along:
                    self.twin(n, spot, other, self.place.core).wait_recv()
                    self.own[n][shard] = self.own[n][shard] + self.other[n][shard]

            when([there], add)
        for other in (True, False):
            for k, flow in enumerate(part.flows):
                if flow[3]:
                    self.start([there], self.side_copy(n, k, spot, other, 1 - self.place.side))
                elif other:
                    self.start([there], self.pair_copy(n, k, spot, self.shard(spot, True)))

    def pair_copy(self, n, k, spot, shard):
        flow = self.parts[n].flows[k]
        slot = self.place.line + spot[0] * spot[1] if flow[2] == "line" else 0
        return self.copy(
            self.piece(n, k, shard, self.place.side),
            self.lanes[n][k][1].at[slot],
            (n, k, "pair") + spot,
            self.place.across(),
        )

    def add_sides(self, n, k, spot):
        there = self.there(spot)
        side = self.place.side
        for other in (True, False):

            def add(other=other):
                shard = self.shard(spot, other)
                self.side_copy(n, k, spot, other, side).wait_recv()
                piece = self.piece(n, k, shard, side)
                piece[...] = piece[...] + self.lanes[n][k][0][shard]

            when([there], add)
        if self.parts[n].flows[k][2] == "line":
            self.start([there], self.pair_copy(n, k, spot, self.shard(spot, True)))

    def line_slot(self, flow, way, steps, other, line):
        slot = line if (steps > 0 or way > 0) else LINE
        return slot + (LINE + 1) * int(other) if flow[2] == "pair" else slot

    def line_copy(self, n, k, spot, other, arriving):
        flow = self.parts[n].flows[k]
        way, steps = spot
        shard = self.shard(spot, other)
        line = self.place.line + way * steps
        left = steps if arriving else steps - 1
        return self.copy(
            self.piece(n, k, shard, self.place.side),
            self.lanes[n][k][2].at[self.line_slot(flow, way, left, other, line)],
            (n, k, "line", way, left, other),
            self.place.ahead(way),
        )

    def add_line(self, n, k, spot):
        place = self.place
        there = self.there(spot)
        way, steps = spot
        side = place.side
        flow = self.parts[n].flows[k]
        if flow[2] == "line":

            def add():
                shard = self.shard(spot, False)
                self.pair_copy(n, k, spot, shard).wait_recv()
                piece = self.piece(n, k, shard, side)
                piece[...] = piece[...] + self.lanes[n][k][1][place.line + way * steps]

            when([there], add)
        for other in (True, False) if flow[2] == "pair" else (False,):
            for direction in (1, -1) if steps == 0 else (way,):

                def add_line(other=other, here=(direction, steps)):
                    self.line_copy(n, k, here, other, True).wait_recv()
                    piece = self.piece(n, k, self.shard(here, other), side)
                    line = place.line + here[0] * here[1]
                    slot = self.line_slot(flow, here[0], here[1], other, line)
                    piece[...] = piece[...] + self.lanes[n][k][2][slot]

                when([there, place.can(-direction)], add_line)
            if steps > 0:
                self.start([there], self.line_copy(n, k, spot, other, False))

    def send_pair(self, n, k):
        self.start([], self.pair_copy(n, k, (1, 0), self.shard((1, 0), True)))

    def send_swap(self, n, k):
        self.start([], self.swap(n, k))

    def settle(self, n, k):
        place = self.place
        core, side, here = place.core, place.side, place.shard
        part = self.parts[n]
        flow = part.flows[k]
        piece = self.piece(n, k, here, side)
        out = self.out_view(n, k, core, side)
        if flow[3]:
            if flow[2] == "pair":
                self.pair_copy(n, k, (1, 0), here).wait_recv()
                out[...] = piece[...] + self.lanes[n][k][1][0]
            else:
                out[...] = piece[...]
            self.start([], self.out_copy(n, k, "sideend", place.beside(), core, side))
        else:
            self.swap(n, k).wait_recv()
            out[...] = piece[...] + self.lanes[n][k][0][0]
        if part.along:
            self.start([], self.out_copy(n, k, "twinend", place.twin(), core, side))
        else:
            self.start([], self.whole(n, k))

    def settle_side(self, n, k):
        place = self.place
        core, side = place.core, 1 - place.side
        self.out_copy(n, k, "sideend", place.beside(), core, side).wait_recv()
        self.start([], self.out_copy(n, k, "twinsideend", place.twin(), core, side))

    def swap(self, n, k):
        return self.copy(
            self.piece(n, k, self.place.shard, self.place.side),
            self.lanes[n][k][0].at[0],
            (n, k, "sideend"),
            self.place.beside(),
        )

    def out_view(self, n, k, core, side):
        part = self.parts[n]
        rows, columns = part.outer(part.flows[k], core, side)
        return self.outs[n].at[rows, columns]

    def out_copy(self, n, k, key, peer, core, side):
        view = self.out_view(n, k, core, side)
        return self.copy(view, view, (n, k, key), peer)

    def last(self):
        place = self.place
        core, side = place.core, place.side
        everything = [(n, k) for n, part in enumerate(self.parts) for k in range(len(part.flows))]
        for n, k in everything:
            if self.parts[n].along:
                self.out_copy(n, k, "twinend", place.twin(), 1 - core, side).wait_recv()
                if self.parts[n].flows[k][3]:
                    self.out_copy(
                        n, k, "twinsideend", place.twin(), 1 - core, 1 - side
                    ).wait_recv()
            else:
                self.whole(n, k).wait_recv()
        for conditions, copy in self.sent:
            when(conditions, copy.wait_send)
        for n, k in everything:
            if not self.parts[n].along:
                view = self.out_view(n, k, core, side)
                view[...] = view[...] + self.other[n][...]

    def whole(self, n, k):
        return self.copy(
            self.out_view(n, k, self.place.core, self.place.side),
            self.other[n],
            (n, k, "twinend"),
            self.place.twin(),
        )

    def actions(self):
        found = []
        for n, part in enumerate(self.parts):
            for spot in SPOTS:
                found.append((("begin", n, spot), lambda n=n, s=spot: self.begin(n, s)))
        for n, part in enumerate(self.parts):
            for spot in SPOTS:
                found.append((("cores", n, spot), lambda n=n, s=spot: self.add_cores(n, s)))
            for k, flow in enumerate(part.flows):
                at = (n, k)
                for spot in SPOTS:
                    if flow[3]:
                        found.append(
                            (("sides", n, k, spot), lambda at=at, s=spot: self.add_sides(*at, s))
                        )
                    found.append(
                        (("line", n, k, spot), lambda at=at, s=spot: self.add_line(*at, s))
                    )
                if flow[2] == "pair":
                    found.append((("pair", n, k), lambda at=at: self.send_pair(*at)))
                if not flow[3]:
                    found.append((("swap", n, k), lambda at=at: self.send_swap(*at)))
                found.append((("settle", n, k), lambda at=at: self.settle(*at)))
                if flow[3]:
                    found.append((("after", n, k), lambda at=at: self.settle_side(*at)))
        found.append((("last",), self.last))
        return found


def in_order(actions, order):
    if order is None:
        return [action for _, action in actions]
    assert sorted(order) == list(range(len(actions)))
    return [actions[i][1] for i in order]


def reduce_kernel(parts, blocks, order, *refs):
    count = len(parts)
    grads, refs = refs[:count], refs[count:]
    ins, refs = refs[:blocks], refs[blocks:]
    outs, refs = refs[:count], refs[count:]
    swapped, refs = refs[:blocks], refs[blocks:]
    scratch, (send, recv, load), sems = refs[:-6], refs[-6:-3], refs[-3:]
    place = Place()
    greet(place)
    swap = Swap(place, ins, swapped, *sems)
    swap.start()
    work = Reduce(place, parts, grads, outs, scratch, send, recv, load)
    for step in in_order(work.actions(), order):
        step()
    swap.finish()


def reduce_call(arrays, blocks, parts, collective_id, order=None):
    labels = reduce_labels(parts)
    count = len(arrays)
    return pl.pallas_call(
        functools.partial(reduce_kernel, parts, len(blocks), order),
        out_shape=[jax.ShapeDtypeStruct((p.rows, p.columns), p.dtype) for p in parts]
        + [jax.ShapeDtypeStruct(b.shape, b.dtype) for b in blocks],
        in_specs=[pl.BlockSpec(memory_space=pltpu.HBM)] * (count + len(blocks)),
        out_specs=[pl.BlockSpec(memory_space=pltpu.VMEM)] * count
        + [pl.BlockSpec(memory_space=pltpu.HBM)] * len(blocks),
        scratch_shapes=reduce_scratch(parts)
        + [
            pltpu.SemaphoreType.DMA((len(labels.numbers),)),
            pltpu.SemaphoreType.DMA((len(labels.numbers),)),
            pltpu.SemaphoreType.DMA((count * 2 * len(SPOTS),)),
        ]
        + swap_scratch(len(blocks)),
        compiler_params=pltpu.CompilerParams(
            collective_id=collective_id, has_side_effects=True, vmem_limit_bytes=63 << 20
        ),
        name="reduce_gradients",
    )(*arrays, *blocks)


def column_part(rows, columns, shared, early, inside=False):
    half = columns // 2
    part = (half - shared) // 2
    flows = []
    if shared:
        flows.append((lambda side: 0, shared, "line", False))
    if early:
        flows.append((lambda side: shared + side * part, early, "line", True))
    if part > early:
        flows.append((lambda side: shared + side * part + early, part - early, "pair", True))
    return Part(rows, columns, "columns", flows, inside=inside)


def row_part(rows, columns, shared, early):
    half = rows // 2
    part = (half - shared) // 2
    return Part(
        rows,
        columns,
        "rows",
        [
            (lambda side: 0, shared, "line", False),
            (lambda side: shared + side * part, early, "line", True),
            (lambda side: shared + side * part + early, part - early, "pair", True),
        ],
    )


def vector_part(rows, columns, inside=False):
    return Part(rows, columns, None, [(lambda side: 0, columns, "line", False)], F32, inside)


ROW_QUERY, ROW_VALUE, ROW_OUTPUT, ROW_GAIN1, ROW_SHIFT1, ROW_INNER, INNER = 0, 1, 2, 3, 4, 5, 4
ROW_OUTER, ROW_GAIN2, ROW_SHIFT2 = 9, 10, 11
TABLE_ROWS = 16
LANES = 128
BAND = 32


def spread_table(table_ref, vec):
    for shard in range(table_ref.shape[0] // TABLE_ROWS):
        vec[:, pl.ds(shard * LANES, LANES)] = table_ref[
            pl.ds(shard * TABLE_ROWS, TABLE_ROWS), :
        ].astype(F32)


def fold_table(vec, table_ref, first, count):
    for shard in range(table_ref.shape[0] // TABLE_ROWS):
        table_ref[pl.ds(shard * TABLE_ROWS + first, count), :] = vec[
            pl.ds(first, count), pl.ds(shard * LANES, LANES)
        ]


def row_place(row, core, rows):
    half = rows // 2
    return jnp.where(row < half, row, row + half) + core * half


def total_rows(block):
    return jnp.sum(block.astype(F32), axis=0, keepdims=True)


def middle_kernel(
    rows_ref,
    context_ref,
    cot_ref,
    lengths_ref,
    table_ref,
    output_w,
    inner_w,
    outer_w,
    out_ref,
    first_grad_ref,
    context_grad_ref,
    sums_ref,
    output_g,
    inner_g,
    outer_g,
    output_v,
    inner_v,
    outer_v,
    vec,
    sums,
    active,
    slope,
    unit1,
    unit2,
    rate1,
    total,
    low,
    low_t,
    second,
    second_low,
    inner_b,
    outer_b,
    load,
    save,
):
    rows, width = rows_ref.shape
    tiles, _, tile = inner_v.shape
    ctx = lax.axis_index("ctx")
    side, core = lax.div(ctx, 2), lax.rem(ctx, 2)
    length = lengths_ref[side, 0]
    bands = rows // BAND

    def inner_load(t):
        return pltpu.make_async_copy(
            inner_w.at[:, pl.ds(pl.multiple_of(t * tile, tile), tile)], inner_v.at[t], load.at[0, t]
        )

    def outer_load(t):
        return pltpu.make_async_copy(
            outer_w.at[pl.ds(pl.multiple_of(t * tile, tile), tile), :], outer_v.at[t], load.at[1, t]
        )

    output_load = pltpu.make_async_copy(output_w, output_v, load.at[2, 0])
    output_load.start()
    for t in range(tiles):
        inner_load(t).start()
        outer_load(t).start()
    spread_table(table_ref, vec)
    sums[...] = jnp.zeros_like(sums)
    output_load.wait()
    total[...] = plain_product(context_ref[...], output_v[...])

    def band_of(b):
        return pl.ds(pl.multiple_of(b * BAND, BAND), BAND)

    def first_norm(b, carry):
        here = band_of(b)
        first_sum = (
            rows_ref[here, :].astype(F32) + total[here, :] + vec[pl.ds(ROW_OUTPUT, 1), :]
        )
        unit, rate = norm_parts(first_sum)
        unit1[here, :] = unit
        rate1[here, :] = jnp.broadcast_to(rate, (BAND, LANES))
        normed = unit * vec[pl.ds(ROW_GAIN1, 1), :] + vec[pl.ds(ROW_SHIFT1, 1), :]
        low[here, :] = normed.astype(BF16)
        total[here, :] = normed + vec[pl.ds(ROW_OUTER, 1), :]
        return carry

    lax.fori_loop(0, bands, first_norm, 0)
    low_t[...] = low[...].T

    def forward(t, carry):
        inner_load(t).wait()
        bias = jnp.concatenate(
            [
                vec[pl.ds(ROW_INNER + k, 1), pl.ds(pl.multiple_of(t * LANES, LANES), LANES)]
                for k in range(INNER)
            ],
            axis=1,
        )
        hidden = plain_product(low[...], inner_v[t]) + bias
        share = 0.5 + 0.5 * lax.erf(hidden * 0.7071067811865476)
        active[t] = (hidden * share).astype(BF16)
        slope[t] = share + hidden * (jnp.exp(-0.5 * hidden * hidden) * 0.3989422804014327)
        outer_load(t).wait()
        total[...] += plain_product(active[t], outer_v[t])
        return carry

    lax.fori_loop(0, tiles, forward, 0)

    def second_norm(b, carry):
        here = band_of(b)
        unit, rate = norm_parts(total[here, :])
        row = b * BAND + lax.broadcasted_iota(jnp.int32, (BAND, width), 0)
        mask = (row_place(row, core, rows) < length).astype(F32)
        gain = vec[pl.ds(ROW_GAIN2, 1), :]
        out_ref[here, :] = ((unit * gain + vec[pl.ds(ROW_SHIFT2, 1), :]) * mask).astype(BF16)
        out_grad = cot_ref[here, :].astype(F32) * mask
        grad = norm_back(unit, rate, out_grad * gain)
        second[here, :] = grad
        grad_low = grad.astype(BF16)
        second_low[here, :] = grad_low
        sums[pl.ds(ROW_GAIN2, 1), :] += total_rows(out_grad * unit)
        sums[pl.ds(ROW_SHIFT2, 1), :] += total_rows(out_grad)
        sums[pl.ds(ROW_OUTER, 1), :] += total_rows(grad_low)
        return carry

    lax.fori_loop(0, bands, second_norm, 0)

    def inner_save(t):
        slot = lax.rem(t, 2)
        return pltpu.make_async_copy(
            inner_b.at[slot],
            inner_g.at[:, pl.ds(pl.multiple_of(t * tile, tile), tile)],
            save.at[0, slot],
        )

    def outer_save(t):
        slot = lax.rem(t, 2)
        return pltpu.make_async_copy(
            outer_b.at[slot],
            outer_g.at[pl.ds(pl.multiple_of(t * tile, tile), tile), :],
            save.at[1, slot],
        )

    def backward(t, carry):
        slot = lax.rem(t, 2)
        hidden_grad = (right_product(second_low[...], outer_v[t]) * slope[t]).astype(BF16)
        summed = total_rows(hidden_grad)
        for k in range(INNER):
            sums[
                pl.ds(ROW_INNER + k, 1), pl.ds(pl.multiple_of(t * LANES, LANES), LANES)
            ] = summed[:, k * LANES : (k + 1) * LANES]

        @pl.when(t >= 2)
        def _():
            outer_save(t - 2).wait()
            inner_save(t - 2).wait()

        outer_b[slot] = left_product(active[t], second_low[...]).astype(BF16)
        inner_b[slot] = plain_product(low_t[...], hidden_grad).astype(BF16)
        outer_save(t).start()
        second[...] += right_product(hidden_grad, inner_v[t])
        inner_save(t).start()
        return carry

    lax.fori_loop(0, tiles, backward, 0)

    def first_back(b, carry):
        here = band_of(b)
        grad = second[here, :]
        unit = unit1[here, :]
        sums[pl.ds(ROW_GAIN1, 1), :] += total_rows(grad * unit)
        sums[pl.ds(ROW_SHIFT1, 1), :] += total_rows(grad)
        back = norm_back(unit, rate1[here, :1], grad * vec[pl.ds(ROW_GAIN1, 1), :])
        first_grad_ref[here, :] = back
        back_low = back.astype(BF16)
        second_low[here, :] = back_low
        sums[pl.ds(ROW_OUTPUT, 1), :] += total_rows(back_low)
        return carry

    lax.fori_loop(0, bands, first_back, 0)
    context_grad_ref[...] = right_product(second_low[...], output_v[...]).astype(BF16)
    output_g[...] = left_product(context_ref[...], second_low[...]).astype(BF16)
    fold_table(sums, sums_ref, 0, TABLE_ROWS)
    for t in range(tiles - 2, tiles):
        outer_save(t).wait()
        inner_save(t).wait()


def middle(rows, context, cot, lengths, table, output_w, inner_w, outer_w):
    count, width = rows.shape
    hidden = inner_w.shape[1]
    tile = INNER * LANES
    tiles = hidden // tile
    whole = pl.BlockSpec(memory_space=pltpu.VMEM)
    far = pl.BlockSpec(memory_space=pltpu.HBM)

    def space(dtype):
        return pltpu.VMEM((count, width), dtype)

    return pl.pallas_call(
        middle_kernel,
        out_shape=[
            jax.ShapeDtypeStruct((count, width), BF16),
            jax.ShapeDtypeStruct((count, width), F32),
            jax.ShapeDtypeStruct((count, width), BF16),
            jax.ShapeDtypeStruct(table.shape, F32),
            jax.ShapeDtypeStruct(output_w.shape, BF16),
            jax.ShapeDtypeStruct(inner_w.shape, BF16),
            jax.ShapeDtypeStruct(outer_w.shape, BF16),
        ],
        in_specs=[whole] * 3 + [pl.BlockSpec(memory_space=pltpu.SMEM), whole] + [far] * 3,
        out_specs=[whole] * 5 + [far] * 2,
        scratch_shapes=[
            pltpu.VMEM(output_w.shape, BF16),
            pltpu.VMEM((tiles, width, tile), BF16),
            pltpu.VMEM((tiles, tile, width), BF16),
            pltpu.VMEM((TABLE_ROWS, width), F32),
            pltpu.VMEM((TABLE_ROWS, width), F32),
            pltpu.VMEM((tiles, count, tile), BF16),
            pltpu.VMEM((tiles, count, tile), F32),
            space(F32),
            pltpu.VMEM((8, LANES), F32),
            pltpu.VMEM((count, LANES), F32),
            space(F32),
            space(BF16),
            pltpu.VMEM((width, count), BF16),
            space(F32),
            space(BF16),
            pltpu.VMEM((2, width, tile), BF16),
            pltpu.VMEM((2, tile, width), BF16),
            pltpu.SemaphoreType.DMA((3, tiles)),
            pltpu.SemaphoreType.DMA((2, 2)),
        ],
        compiler_params=pltpu.CompilerParams(vmem_limit_bytes=60 << 20),
        name="feed_forward",
    )(rows, context, cot, lengths, table, output_w, inner_w, outer_w)


def widen_kernel(splits, lines, *refs):
    count = len(splits)
    many = sum(splits)
    ins, table, outs = refs[:count], refs[count], refs[count + 1 : count + 1 + many]
    vectors = refs[count + 1 + many : count + 1 + many + len(lines)]
    rest = refs[count + 1 + many + len(lines) :]
    narrow, held, wides = rest[:count], rest[count], rest[count + 1 : count + 1 + many]
    load, save = rest[-2:]
    loads = [
        pltpu.make_async_copy(here, there, load.at[k])
        for k, (here, there) in enumerate(zip(ins + (table,), narrow + (held,)))
    ]
    for copy in loads:
        copy.start()
    copies = []
    at = 0
    for k, parts in enumerate(splits):
        loads[k].wait()
        columns = narrow[k].shape[-1] // parts
        for part in range(parts):
            wides[at][...] = narrow[k][..., part * columns : (part + 1) * columns].astype(
                wides[at].dtype
            )
            copies.append(pltpu.make_async_copy(wides[at], outs[at], save.at[at]))
            copies[-1].start()
            at += 1
    loads[count].wait()
    row = 0
    for vector, extent in zip(vectors, lines):
        for line in range(extent):
            copies.append(
                pltpu.make_async_copy(
                    held.at[row], vector.at[pl.ds(line * LANES, LANES)], save.at[many + row]
                )
            )
            copies[-1].start()
            row += 1
    for copy in copies:
        copy.wait()


def widen(arrays, splits, types, table, lines):
    shapes = []
    for array, parts, kind in zip(arrays, splits, types):
        shape = array.shape[:-1] + (array.shape[-1] // parts,)
        shapes += [jax.ShapeDtypeStruct(shape, kind)] * parts
    far = pl.BlockSpec(memory_space=pltpu.HBM)
    return pl.pallas_call(
        functools.partial(widen_kernel, splits, lines),
        out_shape=shapes + [jax.ShapeDtypeStruct((k * LANES,), F32) for k in lines],
        in_specs=[far] * (len(arrays) + 1),
        out_specs=[far] * (len(shapes) + len(lines)),
        scratch_shapes=[pltpu.VMEM(array.shape, array.dtype) for array in arrays + (table,)]
        + [pltpu.VMEM(shape.shape, shape.dtype) for shape in shapes]
        + [
            pltpu.SemaphoreType.DMA((len(arrays) + 1,)),
            pltpu.SemaphoreType.DMA((len(shapes) + sum(lines),)),
        ],
        compiler_params=pltpu.CompilerParams(vmem_limit_bytes=40 << 20),
        name="widen_results",
    )(*arrays, table)


def stack_heads(block, lower):
    zero = jnp.zeros_like(block)
    return jnp.concatenate((jnp.where(lower, block, zero), jnp.where(lower, zero, block)), axis=0)


def repeat(first, stop, action):
    def step(i, carry):
        action(i)
        return carry

    lax.fori_loop(first, stop, step, 0)


GROUPS = 4
HALVES = 2


SPAN = 2 * HEAD_DIM


def span_of(section, pair, width):
    return pl.ds(pl.multiple_of(section * width + pair * SPAN, SPAN), SPAN)


class AttentionForward:
    def __init__(self, place, rows, weight, vec, bias, qkv, context, probs, held, away, send, recv, save):
        self.place, self.rows, self.weight, self.vec, self.bias = place, rows, weight, vec, bias
        self.qkv, self.context, self.probs, self.held, self.away = qkv, context, probs, held, away
        self.send, self.recv, self.save = send, recv, save
        self.count, self.width = context.shape
        self.pairs = self.width // SPAN

    def save_probs(self, pair):
        return pltpu.make_async_copy(self.held.at[pair], self.probs.at[pair], self.save.at[pair])

    def fetch(self, which, pair):
        return pltpu.make_async_remote_copy(
            self.qkv.at[:, span_of(which + 1, pair, self.width)],
            self.away.at[:, span_of(which, pair, self.width)],
            self.send.at[which, pair],
            self.recv.at[which, pair],
            device_id=self.place.twin(),
            device_id_type=MESH,
        )

    def project(self, section):
        tile = 512
        rows = self.rows[...].reshape(self.count, self.width)

        def one(t):
            columns = pl.ds(pl.multiple_of(section * self.width + t * tile, tile), tile)
            product = plain_product(rows, self.weight[:, columns])
            if section != 1:
                row = ROW_QUERY if section == 0 else ROW_VALUE
                product = product + self.vec[
                    pl.ds(row, 1), pl.ds(pl.multiple_of(t * tile, tile), tile)
                ]
            self.qkv[:, columns] = product.astype(BF16)

        repeat(0, self.width // tile, one)

    def give(self, which):
        for pair in range(self.pairs):
            self.fetch(which, pair).start()

    def attend(self, pair):
        for which in range(2):
            self.fetch(which, pair).wait_recv()
        count = self.count
        lower = lax.broadcasted_iota(jnp.int32, (count, SPAN), 1) < HEAD_DIM

        def here(section):
            return self.qkv[:, span_of(section, pair, self.width)]

        def there(section):
            return self.away[:, span_of(section - 1, pair, self.width)]

        stacked = stack_heads(here(0) * HEAD_DIM**-0.5, lower)
        keys = jnp.concatenate((here(1), there(1)), axis=0)
        values = jnp.concatenate((here(2), there(2)), axis=0)
        scores = right_product(stacked, keys) + self.bias[:1, :]
        top = jnp.max(scores, axis=1, keepdims=True)
        weights = jnp.exp(scores - top)
        total = jnp.sum(weights, axis=1, keepdims=True)
        probs = (weights * (1.0 / total)).astype(BF16)
        self.held[pair] = probs
        self.save_probs(pair).start()
        mixed = plain_product(probs, values)
        self.context[:, span_of(0, pair, self.width)] = jnp.where(
            lower, mixed[:count], mixed[count:]
        ).astype(BF16)

    def attend_group(self, group):
        each = self.pairs // GROUPS
        repeat(group * each, (group + 1) * each, self.attend)

    def finish(self):
        for pair in range(self.pairs):
            for which in range(2):
                self.fetch(which, pair).wait_send()
            self.save_probs(pair).wait()


TABLE, QUERIES = 0, 1


def start_actions(gather, work, keep, swaps, save, table_ref):
    found = gather.actions()
    others = [k for k in range(len(keep)) if k not in (TABLE, QUERIES)]

    def ready():
        gather.wait_twins((TABLE, QUERIES))
        for k in (TABLE, QUERIES):
            keep[k].wait()
        swaps[0].finish()
        spread_table(table_ref, work.vec)
        save.start()

    def values():
        work.project(2)
        work.give(0)

    def queries():
        work.give(1)
        work.project(0)

    found.append((("ready",), ready))
    found.append((("project", 0), lambda: work.project(1)))
    found.append((("project", 1), values))
    found.append((("project", 2), queries))
    for group in range(GROUPS):
        found.append((("pa", group), lambda group=group: work.attend_group(group)))

    def last():
        gather.finish(others)
        work.finish()
        for k in others:
            keep[k].wait()
        swaps[1].finish()
        save.wait()

    found.append((("last",), last))
    return found


def start_kernel(flows, spots, order, *refs):
    count = max(array for array, _ in spots) + 1
    shares, refs = refs[: len(spots)], refs[len(spots) :]
    (in_block, cot_block, lengths_ref), refs = refs[:3], refs[3:]
    table_ref, refs = refs[0], refs[1:]
    far, refs = refs[: count - 1], refs[count - 1 :]
    rows, cots, qkv, context, probs, away = refs[:6]
    owns, refs = refs[6 : 6 + count], refs[6 + count :]
    weight, held, vec, bias = refs[:4]
    send, recv, local, load, send2, recv2, save2, saveq = refs[4:12]
    fulls = (table_ref, weight) + tuple(far[1:])
    place = Place()
    loads = [
        pltpu.make_async_copy(
            share, owns[array].at[:, pl.ds(column, share.shape[1])], load.at[k]
        )
        for k, (share, (array, column)) in enumerate(zip(shares, spots))
    ]
    for copy in loads:
        copy.start()
    keep = [
        pltpu.make_async_copy(
            own, full.at[pl.ds(pl.multiple_of(place.shard * own.shape[0], 16), own.shape[0]), :], local.at[k]
        )
        for k, (own, full) in enumerate(zip(owns, fulls))
    ]
    greet(place)
    rows_count = context.shape[0]
    length = lengths_ref[place.side, 0]
    row = lax.broadcasted_iota(jnp.int32, (8, rows_count), 1)
    for k, core in enumerate((place.core, 1 - place.core)):
        bias[:, pl.ds(k * rows_count, rows_count)] = jnp.where(
            row_place(row, core, rows_count) < length, 0.0, -1e30
        )
    for copy in loads:
        copy.wait()
    swaps = [
        Swap(place, [in_block], [rows], *refs[12:15]),
        Swap(place, [cot_block], [cots], *refs[15:18]),
    ]
    for swap in swaps:
        swap.start()
    gather = Gather(place, flows, owns, fulls, send, recv)
    for copy in keep:
        copy.start()
    work = AttentionForward(
        place, rows, weight, vec, bias, qkv, context, probs, held, away, send2, recv2, save2
    )
    save = pltpu.make_async_copy(weight, far[0], saveq.at[0])
    for step in in_order(start_actions(gather, work, keep, swaps, save, table_ref), order):
        step()


def start(shares, spots, blocks, lengths, flows, shards, collective_id, order):
    labels = gather_labels(flows)
    count = max(array for array, _ in spots) + 1
    shapes = []
    for array in range(count):
        members = [share for share, spot in zip(shares, spots) if spot[0] == array]
        shapes.append((members[0].shape[0], sum(m.shape[1] for m in members)))
    _, block_len, width = blocks[0].shape
    rows = 2 * block_len
    pairs = width // SPAN
    far = pl.BlockSpec(memory_space=pltpu.HBM)
    whole = pl.BlockSpec(memory_space=pltpu.VMEM)
    probs_shape = (pairs, 2 * rows, 2 * rows)
    return pl.pallas_call(
        functools.partial(start_kernel, flows, spots, order),
        out_shape=[jax.ShapeDtypeStruct((shards * r, c), BF16) for r, c in shapes]
        + [jax.ShapeDtypeStruct(block.shape, BF16) for block in blocks]
        + [
            jax.ShapeDtypeStruct((rows, 3 * width), BF16),
            jax.ShapeDtypeStruct((rows, width), BF16),
            jax.ShapeDtypeStruct(probs_shape, BF16),
            jax.ShapeDtypeStruct((rows, 2 * width), BF16),
        ],
        in_specs=[far] * (len(shares) + 2) + [pl.BlockSpec(memory_space=pltpu.SMEM)],
        out_specs=[whole] + [far] * (count - 1) + [whole, far] + [whole, whole, far, whole],
        scratch_shapes=[pltpu.VMEM(shape, BF16) for shape in shapes]
        + [
            pltpu.VMEM((shards * shapes[QUERIES][0], shapes[QUERIES][1]), BF16),
            pltpu.VMEM(probs_shape, BF16),
            pltpu.VMEM((TABLE_ROWS, width), F32),
            pltpu.VMEM((8, 2 * rows), F32),
            pltpu.SemaphoreType.DMA((len(labels.numbers),)),
            pltpu.SemaphoreType.DMA((len(labels.numbers),)),
            pltpu.SemaphoreType.DMA((count,)),
            pltpu.SemaphoreType.DMA((len(shares),)),
            pltpu.SemaphoreType.DMA((2, pairs)),
            pltpu.SemaphoreType.DMA((2, pairs)),
            pltpu.SemaphoreType.DMA((pairs,)),
            pltpu.SemaphoreType.DMA((1,)),
        ]
        + swap_scratch(1) * 2,
        compiler_params=pltpu.CompilerParams(
            collective_id=collective_id, has_side_effects=True, vmem_limit_bytes=48 << 20
        ),
        name="gather_attention_forward",
    )(*shares, *blocks, lengths)


class AttentionBackward:
    def __init__(self, place, qkv, away, grad, out, keep, leave, come, send, recv):
        self.place, self.qkv, self.away, self.grad = place, qkv, away, grad
        self.out, self.keep, self.leave, self.come = out, keep, leave, come
        self.send, self.recv = send, recv
        self.count, self.width = grad.shape
        self.pairs = self.width // SPAN

    def give(self, which, pair):
        return pltpu.make_async_remote_copy(
            self.leave.at[:, span_of(which, pair, self.width)],
            self.come.at[:, span_of(which, pair, self.width)],
            self.send.at[which, pair],
            self.recv.at[which, pair],
            device_id=self.place.twin(),
            device_id_type=MESH,
        )

    def attend(self, pair, probs):
        count = self.count
        lower = lax.broadcasted_iota(jnp.int32, (count, SPAN), 1) < HEAD_DIM
        scale = HEAD_DIM**-0.5

        def here(section):
            return self.qkv[:, span_of(section, pair, self.width)]

        def there(section):
            return self.away[:, span_of(section - 1, pair, self.width)]

        first = span_of(0, pair, self.width)
        second = span_of(1, pair, self.width)
        stacked = stack_heads(here(0) * scale, lower)
        keys = jnp.concatenate((here(1), there(1)), axis=0)
        values = jnp.concatenate((here(2), there(2)), axis=0)
        grad = stack_heads(self.grad[:, first], lower)
        value_part = left_product(probs, grad)
        probs_grad = right_product(grad, values)
        wide = probs.astype(F32)
        inner = jnp.sum(wide * probs_grad, axis=1, keepdims=True)
        scores_grad = (wide * (probs_grad - inner)).astype(BF16)
        key_part = left_product(scores_grad, stacked)
        self.leave[:, first] = key_part[count:].astype(BF16)
        self.leave[:, second] = value_part[count:].astype(BF16)
        self.keep[:, first] = key_part[:count]
        self.keep[:, second] = value_part[:count]
        mixed = plain_product(scores_grad, keys) * scale
        self.out[:, first] = jnp.where(lower, mixed[:count], mixed[count:]).astype(BF16)
        for which in range(2):
            self.give(which, pair).start()

    def settle(self, pair):
        for which in range(2):
            self.give(which, pair).wait_recv()
            here = span_of(which, pair, self.width)
            self.out[:, span_of(which + 1, pair, self.width)] = (
                self.keep[:, here] + self.come[:, here].astype(F32)
            ).astype(BF16)

    def finish(self):
        for pair in range(self.pairs):
            for which in range(2):
                self.give(which, pair).wait_send()


class Finish:
    def __init__(self, work, tiles, weight, rows_ref, rows_t, first_grad, total, block, sums, held, probs, load, sems):
        self.work, self.tiles, self.weight, self.rows_ref, self.rows_t = work, tiles, weight, rows_ref, rows_t
        self.total, self.block, self.sums = total, block, sums
        self.held, self.probs, self.load, self.sems = held, probs, load, sems
        self.grad_load = pltpu.make_async_copy(first_grad, total, sems.at[held.shape[0]])
        self.count, self.width = total.shape
        self.tile = tiles.shape[2]

    def weight_load(self, t):
        columns = pl.ds(pl.multiple_of(t * self.tile, self.tile), self.tile)
        slot = lax.rem(t, self.tiles.shape[0])
        return pltpu.make_async_copy(
            self.weight.at[:, columns], self.tiles.at[slot], self.load.at[slot]
        )

    def probs_load(self, pair):
        slot = lax.rem(pair, self.held.shape[0])
        return pltpu.make_async_copy(
            self.probs.at[pair], self.held.at[slot], self.sems.at[slot]
        )

    def begin(self):
        for pair in range(self.held.shape[0]):
            self.probs_load(pair).start()
        for t in range(self.tiles.shape[0]):
            self.weight_load(t).start()
        self.grad_load.start()

    def attend(self, group):
        each = self.work.pairs // GROUPS

        slots = self.held.shape[0]

        def one(pair):
            self.probs_load(pair).wait()
            self.work.attend(pair, self.held[lax.rem(pair, slots)])
            pl.when(pair + slots < self.work.pairs)(self.probs_load(pair + slots).start)

        repeat(group * each, (group + 1) * each, one)

    def settle(self):
        repeat(0, self.work.pairs, self.work.settle)

    def weigh(self, core, target):
        shards, rows, columns = target.shape
        tile = self.tile

        def one(j):
            start = pl.multiple_of(core * columns + j * tile, tile)
            product = plain_product(self.rows_t[...], self.work.out[:, pl.ds(start, tile)])
            low = product.astype(BF16)
            for shard in range(shards):
                target[shard, :, pl.ds(pl.multiple_of(j * tile, tile), tile)] = low[
                    shard * rows : (shard + 1) * rows
                ]

        repeat(0, columns // tile, one)

    def turn(self):
        self.rows_t[...] = self.rows_ref[...].T

    def bias_sums(self, target):
        self.sums[pl.ds(0, 1), :] = total_rows(self.work.out[:, : self.width])
        self.sums[pl.ds(1, 1), :] = total_rows(self.work.out[:, 2 * self.width :])
        for shard in range(target.shape[0]):
            target[shard, pl.ds(ROW_QUERY, 2), :] = self.sums[
                pl.ds(0, 2), pl.ds(shard * LANES, LANES)
            ]

    def spread(self, half):
        count = self.weight.shape[1] // self.tile
        each = count // HALVES
        slots = self.tiles.shape[0]
        if half == 0:
            self.grad_load.wait()

        def one(t):
            self.weight_load(t).wait()
            columns = pl.ds(pl.multiple_of(t * self.tile, self.tile), self.tile)
            tile = self.tiles[lax.rem(t, slots)]
            self.total[...] += right_product(self.work.out[:, columns], tile)
            pl.when(t + slots < count)(self.weight_load(t + slots).start)

        repeat(half * each, (half + 1) * each, one)
        if half == HALVES - 1:
            rows = self.block.shape[1]
            for part in range(2):
                self.block[part] = self.total[pl.ds(part * rows, rows), :].astype(BF16)


def finish_actions(reduce, finish, swaps):
    queries, vectors = 3, 4
    place = reduce.place
    found = reduce.actions()

    def load():
        finish.begin()
        finish.turn()

    found.append((("load",), load))
    found.append((("swapout",), swaps[0].start))
    for group in range(GROUPS):
        found.append((("att", group), lambda group=group: finish.attend(group)))
    found.append((("settleatt",), finish.settle))
    found.append((("leave",), lambda: finish.weigh(1 - place.core, reduce.grads[queries])))
    found.append((("own",), lambda: finish.weigh(place.core, reduce.own[queries])))
    found.append((("sums",), lambda: finish.bias_sums(reduce.own[vectors])))
    for half in range(HALVES):
        found.append((("dx", half), lambda half=half: finish.spread(half)))
    found.append((("swapin",), swaps[1].start))
    return found


def finish_kernel(parts, order, *refs):
    rows_ref, qkv, away, grad, table_ref, first_grad, probs, weight = refs[:8]
    grads, out_block = list(refs[8:11]), refs[11]
    outs, swapped, refs = refs[12:17], refs[17:19], refs[19:]
    leave_q, tiles, held, out, keep, leave, come, total, sums, rows_t, block = refs[:11]
    send2, recv2, load2, sems = refs[11:15]
    scratch, rest = refs[15:-9], refs[-9:]
    place = Place()
    work = AttentionBackward(place, qkv, away, grad, out, keep, leave, come, send2, recv2)
    finish = Finish(
        work, tiles, weight, rows_ref, rows_t, first_grad, total, block, sums, held, probs, load2, sems
    )
    reduce = Reduce(place, parts, grads + [leave_q, None], outs, scratch, *rest[:3])
    swaps = [
        Swap(place, [out_block], [swapped[0]], *rest[3:6]),
        Swap(place, [block], [swapped[1]], *rest[6:9]),
    ]
    for shard in range(LINE * PAIR):
        reduce.own[4][shard] = table_ref[pl.ds(shard * TABLE_ROWS, TABLE_ROWS), :]
    greet(place)
    for step in in_order(finish_actions(reduce, finish, swaps), order):
        step()
    work.finish()
    for swap in swaps:
        swap.finish()


def finish(rows, saved, grad, first_grad, table, weight, grads, block, parts, collective_id, order):
    qkv, away, probs = saved
    count, width = rows.shape
    pairs = width // SPAN
    tile = 512
    labels = reduce_labels(parts)
    whole = pl.BlockSpec(memory_space=pltpu.VMEM)
    far = pl.BlockSpec(memory_space=pltpu.HBM)
    queries = parts[3]
    return pl.pallas_call(
        functools.partial(finish_kernel, parts, order),
        out_shape=[jax.ShapeDtypeStruct((p.rows, p.columns), p.dtype) for p in parts]
        + [jax.ShapeDtypeStruct(block.shape, BF16)] * 2,
        in_specs=[whole] * 5 + [far] * 7,
        out_specs=[whole] * len(parts) + [far] * 2,
        scratch_shapes=[
            pltpu.VMEM((LINE * PAIR, queries.half_rows, queries.half_columns), BF16),
            pltpu.VMEM((2, width, tile), BF16),
            pltpu.VMEM((pairs // 2,) + probs.shape[1:], BF16),
            pltpu.VMEM((count, 3 * width), BF16),
            pltpu.VMEM((count, 2 * width), F32),
            pltpu.VMEM((count, 2 * width), BF16),
            pltpu.VMEM((count, 2 * width), BF16),
            pltpu.VMEM((count, width), F32),
            pltpu.VMEM((8, width), F32),
            pltpu.VMEM((width, count), BF16),
            pltpu.VMEM(block.shape, BF16),
            pltpu.SemaphoreType.DMA((2, pairs)),
            pltpu.SemaphoreType.DMA((2, pairs)),
            pltpu.SemaphoreType.DMA((2,)),
            pltpu.SemaphoreType.DMA((pairs // 2 + 1,)),
        ]
        + reduce_scratch(parts)
        + [
            pltpu.SemaphoreType.DMA((len(labels.numbers),)),
            pltpu.SemaphoreType.DMA((len(labels.numbers),)),
            pltpu.SemaphoreType.DMA((len(parts) * 2 * len(SPOTS),)),
        ]
        + swap_scratch(1) * 2,
        compiler_params=pltpu.CompilerParams(
            collective_id=collective_id, has_side_effects=True, vmem_limit_bytes=63 << 20
        ),
        name="attention_backward_reduce",
    )(rows, qkv, away, grad, table, first_grad, probs, weight, *grads, block)


def exact_gelu(hidden):
    return jax.nn.gelu(hidden, approximate=False)


def plain_product(left, right):
    return jnp.dot(left, right, preferred_element_type=F32)


def left_product(left, right):
    return lax.dot_general(left, right, (((0,), (0,)), ((), ())), preferred_element_type=F32)


def right_product(left, right):
    return lax.dot_general(left, right, (((1,), (1,)), ((), ())), preferred_element_type=F32)


def column_sums(rows):
    return jnp.sum(rows.astype(F32), axis=0)


def norm_parts(total):
    average = jnp.mean(total, axis=-1, keepdims=True)
    centered = total - average
    variance = jnp.mean(centered * centered, axis=-1, keepdims=True)
    rate = lax.rsqrt(variance + EPSILON)
    return centered * rate, rate


def norm_back(unit, rate, grad):
    return rate * (
        grad
        - jnp.mean(grad, axis=-1, keepdims=True)
        - unit * jnp.mean(grad * unit, axis=-1, keepdims=True)
    )


def split_columns(packed, widths):
    pieces = []
    start = 0
    for width in widths:
        pieces.append(packed[..., start : start + width])
        start += width
    return pieces


def native_forward(queries, keys_all, values_all, key_valid, heads):
    shape = queries.shape[:2] + (heads, HEAD_DIM)
    key_shape = keys_all.shape[:2] + (heads, HEAD_DIM)
    scores = jnp.einsum(
        "sqhd,skhd->shqk",
        queries.reshape(shape),
        keys_all.reshape(key_shape),
        preferred_element_type=F32,
    ) * (HEAD_DIM**-0.5)
    scores = jnp.where(key_valid[:, None, None, :], scores, -1e30)
    top = jnp.max(scores, axis=-1, keepdims=True)
    weights = jnp.exp(scores - top)
    probs = (weights / jnp.sum(weights, axis=-1, keepdims=True)).astype(BF16)
    context = jnp.einsum(
        "shqk,skhd->sqhd", probs, values_all.reshape(key_shape), preferred_element_type=F32
    )
    return context.reshape(queries.shape).astype(BF16), probs


def native_backward(queries, keys_all, values_all, probs, context_grad, heads):
    shape = queries.shape[:2] + (heads, HEAD_DIM)
    key_shape = keys_all.shape[:2] + (heads, HEAD_DIM)
    scale = HEAD_DIM**-0.5
    grad_heads = context_grad.reshape(shape)
    wide = probs.astype(F32)
    probs_grad = jnp.einsum(
        "sqhd,skhd->shqk", grad_heads, values_all.reshape(key_shape), preferred_element_type=F32
    )
    inner_total = jnp.sum(wide * probs_grad, axis=-1, keepdims=True)
    scores_grad = (wide * (probs_grad - inner_total)).astype(BF16)
    query_grad = jnp.einsum(
        "shqk,skhd->sqhd", scores_grad, keys_all.reshape(key_shape), preferred_element_type=F32
    )
    key_part = jnp.einsum(
        "shqk,sqhd->skhd", scores_grad, queries.reshape(shape), preferred_element_type=F32
    )
    value_part = jnp.einsum("shqk,sqhd->skhd", probs, grad_heads, preferred_element_type=F32)
    return (
        (query_grad * scale).astype(BF16).reshape(queries.shape),
        (key_part * scale).astype(BF16).reshape(keys_all.shape),
        value_part.astype(BF16).reshape(values_all.shape),
    )


def gather_rows(part):
    return lax.all_gather(part, "fsdp", axis=0, tiled=True)


def reduce_rows(part):
    share = lax.psum_scatter(part.astype(BF16), "fsdp", scatter_dimension=0, tiled=True)
    return lax.psum(share, "ctx").astype(F32)


def layer(flat_rows, cot_rows, row_mask, packed, widths, weights, forward, backward):
    full_qkv, full_output, full_inner, full_outer = weights
    rows, width = flat_rows.shape
    shards = packed.shape[0]
    (
        bias_query,
        bias_value,
        bias_output,
        gain_first,
        shift_first,
        bias_inner,
        bias_outer,
        gain_second,
        shift_second,
    ) = [piece.reshape(-1).astype(F32) for piece in split_columns(packed, widths)]
    bias_qkv = jnp.concatenate((bias_query, jnp.zeros_like(bias_query), bias_value))
    qkv = (plain_product(flat_rows, full_qkv) + bias_qkv).astype(BF16)
    context, saved = forward(qkv)

    first_sum = flat_rows.astype(F32) + plain_product(context, full_output) + bias_output
    first_unit, first_rate = norm_parts(first_sum)
    normed = first_unit * gain_first + shift_first
    normed_low = normed.astype(BF16)
    hidden = plain_product(normed_low, full_inner) + bias_inner
    active, gelu_back = jax.vjp(exact_gelu, hidden)
    active_low = active.astype(BF16)
    second_sum = normed + plain_product(active_low, full_outer) + bias_outer
    second_unit, second_rate = norm_parts(second_sum)
    output = ((second_unit * gain_second + shift_second) * row_mask).astype(BF16)

    out_grad = cot_rows.astype(F32) * row_mask
    second_gain_part = jnp.sum(out_grad * second_unit, axis=0)
    second_shift_part = jnp.sum(out_grad, axis=0)
    second_grad = norm_back(second_unit, second_rate, out_grad * gain_second)
    second_low = second_grad.astype(BF16)
    outer_weight_part = left_product(active_low, second_low).astype(BF16)
    outer_bias_part = column_sums(second_low)
    (hidden_grad,) = gelu_back(right_product(second_low, full_outer))
    hidden_low = hidden_grad.astype(BF16)
    inner_weight_part = left_product(normed_low, hidden_low).astype(BF16)
    inner_bias_part = column_sums(hidden_low)
    normed_grad = second_grad + right_product(hidden_low, full_inner)
    first_gain_part = jnp.sum(normed_grad * first_unit, axis=0)
    first_shift_part = jnp.sum(normed_grad, axis=0)
    first_grad = norm_back(first_unit, first_rate, normed_grad * gain_first)
    branch_low = first_grad.astype(BF16)
    output_weight_part = left_product(context, branch_low).astype(BF16)
    output_bias_part = column_sums(branch_low)
    context_grad = right_product(branch_low, full_output).astype(BF16)
    qkv_grad = backward(saved, context_grad)
    qkv_weight_part = left_product(flat_rows, qkv_grad).astype(BF16)
    query_bias_part = column_sums(qkv_grad[:, :width])
    value_bias_part = column_sums(qkv_grad[:, 2 * width :])
    input_grad = first_grad + right_product(qkv_grad, full_qkv)
    vector_parts = (
        query_bias_part,
        value_bias_part,
        output_bias_part,
        first_gain_part,
        first_shift_part,
        inner_bias_part,
        outer_bias_part,
        second_gain_part,
        second_shift_part,
    )
    packed_parts = jnp.concatenate([part.reshape(shards, -1) for part in vector_parts], axis=1)
    return (
        output,
        input_grad,
        packed_parts,
        (qkv_weight_part, output_weight_part, inner_weight_part, outer_weight_part),
    )


def native_body(inputs, cotangent, lengths, vectors, weights):
    widths = [member.shape[0] for member in vectors]
    packed = lax.all_gather(jnp.concatenate(vectors), "fsdp", axis=0, tiled=False)
    joined = (jnp.concatenate(weights[:3], axis=1),) + weights[3:]
    full = tuple(gather_rows(part) for part in joined)
    micro, seqs, block_len, width = inputs.shape
    heads = width // HEAD_DIM
    total_slots = block_len * lax.axis_size("ctx")
    group = micro * seqs
    rows = group * block_len
    flat_len = lengths.reshape(group)
    local_pos = lax.axis_index("ctx") * block_len + jnp.arange(block_len, dtype=jnp.int32)
    row_mask = (local_pos[None, :] < flat_len[:, None]).astype(F32).reshape(rows, 1)
    key_valid = jnp.arange(total_slots, dtype=jnp.int32)[None, :] < flat_len[:, None]

    def forward(qkv):
        queries = qkv[:, :width].reshape(group, block_len, width)
        keys_values = lax.all_gather(
            qkv[:, width:].reshape(group, block_len, 2 * width), "ctx", axis=1, tiled=True
        )
        keys, values = keys_values[:, :, :width], keys_values[:, :, width:]
        context, probs = native_forward(queries, keys, values, key_valid, heads)
        return context.reshape(rows, width), (queries, keys, values, probs)

    def backward(saved, context_grad):
        query_grad, key_part, value_part = native_backward(
            *saved, context_grad.reshape(group, block_len, width), heads
        )
        keys_values_grad = lax.psum_scatter(
            jnp.concatenate((key_part, value_part), axis=2), "ctx", scatter_dimension=1, tiled=True
        )
        return jnp.concatenate(
            (query_grad.reshape(rows, width), keys_values_grad.reshape(rows, 2 * width)), axis=1
        )

    output, input_grad, packed_parts, parts = layer(
        inputs.reshape(rows, width),
        cotangent.reshape(rows, width),
        row_mask,
        packed,
        widths,
        full,
        forward,
        backward,
    )
    share = lax.psum_scatter(packed_parts, "fsdp", scatter_dimension=0, tiled=True)
    return (
        output.reshape(inputs.shape),
        input_grad.reshape(inputs.shape),
        split_columns(lax.psum(share, "ctx")[0], widths),
        tuple(split_columns(reduce_rows(parts[0]), [width] * 3))
        + tuple(reduce_rows(part) for part in parts[1:]),
    )


def direct_body(inputs, cotangent, lengths, vectors, weights):
    micro, seqs, block_len, width = inputs.shape
    shards = LINE * PAIR
    rows = 2 * block_len
    table = jnp.zeros((TABLE_ROWS, LANES), F32)
    row = 0
    for vector in vectors:
        lines = vector.shape[0] // LANES
        filled = ((row, TABLE_ROWS - row - lines), (0, 0))
        table += jnp.pad(vector.astype(F32).reshape(lines, LANES), filled)
        row += lines
    query_weight, key_weight, value_weight, output_weight, inner_weight, outer_weight = weights
    blocks = (inputs.reshape(micro, block_len, width), cotangent.reshape(micro, block_len, width))
    shard_rows, hidden = inner_weight.shape
    flows = [Flow(0, TABLE_ROWS, lambda core, side: (0, TABLE_ROWS, 0, LANES), cores=False)]
    flows += column_flows(1, shard_rows, 3 * width, *GATHER_SPLIT[0])
    flows += column_flows(2, shard_rows, width, *GATHER_SPLIT[1])
    flows += column_flows(3, shard_rows, hidden, *GATHER_SPLIT[2])
    flows += row_flows(4, hidden // shards, width, *GATHER_SPLIT[3])
    (
        tables,
        full_qkv,
        full_output,
        full_inner,
        full_outer,
        in_rows,
        cot_rows,
        qkv,
        context,
        probs,
        away,
    ) = start(
        (table.astype(BF16),) + weights,
        ((0, 0), (1, 0), (1, width), (1, 2 * width), (2, 0), (3, 0), (4, 0)),
        blocks,
        lengths,
        flows,
        shards,
        1,
        GATHER_ORDER,
    )
    in_rows = in_rows.reshape(rows, width)
    cot_rows = cot_rows.reshape(rows, width)
    output, first_grad, context_grad, table_grad, output_part, inner_part, outer_part = middle(
        in_rows, context, cot_rows, lengths, tables, full_output, full_inner, full_outer
    )
    sums = finish(
        in_rows,
        (qkv, away, probs),
        context_grad,
        first_grad,
        table_grad,
        full_qkv,
        (inner_part, outer_part, output_part),
        output.reshape(micro, block_len, width),
        [
            column_part(shard_rows, hidden, *REDUCE_SPLIT[0]),
            row_part(hidden // shards, width, *REDUCE_SPLIT[1]),
            column_part(shard_rows, width, *REDUCE_SPLIT[2]),
            column_part(shard_rows, 3 * width, *REDUCE_SPLIT[3], inside=True),
            vector_part(TABLE_ROWS, LANES, inside=True),
        ],
        2,
        REDUCE_ORDER,
    )
    inner_share, outer_share, output_share, qkv_share, table_share, outs, grads = sums
    lines = tuple(vector.shape[0] // LANES for vector in vectors)
    wide = widen(
        (qkv_share, output_share, inner_share, outer_share, grads, outs),
        (3, 1, 1, 1, 1, 1),
        (F32,) * 5 + (BF16,),
        table_share,
        lines,
    )
    return (
        wide[7].reshape(inputs.shape),
        wide[6].reshape(inputs.shape),
        tuple(wide[8:]),
        tuple(wide[:6]),
    )


def body(
    inputs,
    cotangent,
    lengths,
    query_weight,
    key_weight,
    value_weight,
    output_weight,
    query_bias,
    value_bias,
    output_bias,
    first_gain,
    first_shift,
    inner_weight,
    inner_bias,
    outer_weight,
    outer_bias,
    second_gain,
    second_shift,
):
    vectors = (
        query_bias,
        value_bias,
        output_bias,
        first_gain,
        first_shift,
        inner_bias,
        outer_bias,
        second_gain,
        second_shift,
    )
    widths = [member.shape[0] for member in vectors]
    weights = (
        query_weight,
        key_weight,
        value_weight,
        output_weight,
        inner_weight,
        outer_weight,
    )
    laid_out = lax.axis_size("fsdp") == LINE * PAIR and lax.axis_size("ctx") == 4
    whole_lines = all(extent % LANES == 0 for extent in widths)
    direct = laid_out and inputs.shape[:2] == (2, 1) and whole_lines
    run = direct_body if direct else native_body
    output, input_grad, shares, weight_shares = run(inputs, cotangent, lengths, vectors, weights)
    query_share, key_share, value_share, output_share, inner_share, outer_share = weight_shares
    return (
        output,
        input_grad,
        query_share,
        key_share,
        value_share,
        output_share,
        shares[0],
        shares[1],
        shares[2],
        shares[3],
        shares[4],
        inner_share,
        shares[5],
        outer_share,
        shares[6],
        shares[7],
        shares[8],
    )


def solution(mesh):
    data = P(None, "fsdp", "ctx", None)
    matrix = P("fsdp", None)
    vector = P("fsdp")
    return jax.shard_map(
        body,
        mesh=mesh,
        in_specs=(data, data, P(None, "fsdp"))
        + (matrix,) * 4
        + (vector,) * 5
        + (matrix, vector, matrix, vector, vector, vector),
        out_specs=(data, data)
        + (matrix,) * 4
        + (vector,) * 5
        + (matrix, vector, matrix, vector, vector, vector),
        check_vma=False,
    )
```

```python
import functools

import jax
import jax.numpy as jnp
from jax import lax
from jax.experimental import pallas as pl
from jax.experimental.pallas import tpu as pltpu
from jax.sharding import PartitionSpec as P

HEAD_DIM = 64
EPSILON = 1e-06
F32 = jnp.float32
BF16 = jnp.bfloat16

GATHER_SPLIT = ((256, 384), (256, 128), (1024, 128), (128, 64))
REDUCE_SPLIT = ((512, 512), (128, 48), (256, 128), (1024, 256))
GATHER_ORDER = (
    7, 3, 5, 0, 1, 2, 10, 73, 71, 33, 8, 16, 27, 32, 69, 11, 14, 81, 147, 12, 70, 6, 185, 31, 86,
    35, 223, 109, 40, 76, 79, 34, 9, 48, 19, 41, 111, 15, 4, 29, 128, 38, 92, 152, 110, 54, 43,
    74, 145, 108, 93, 24, 242, 67, 107, 90, 37, 204, 84, 60, 130, 168, 75, 59, 52, 46, 146, 224,
    13, 129, 100, 17, 21, 155, 143, 83, 116, 62, 187, 36, 114, 117, 222, 26, 22, 112, 113, 206,
    157, 105, 184, 82, 53, 88, 151, 166, 228, 25, 124, 65, 57, 94, 169, 45, 244, 85, 63, 207, 205,
    78, 20, 42, 119, 87, 149, 219, 164, 160, 50, 153, 68, 23, 122, 138, 91, 183, 101, 51, 231,
    102, 221, 135, 193, 47, 132, 18, 192, 133, 120, 233, 106, 171, 131, 243, 55, 49, 126, 176,
    121, 227, 127, 154, 170, 250, 150, 165, 159, 186, 28, 95, 172, 162, 203, 188, 39, 136, 245,
    202, 89, 115, 167, 161, 66, 123, 58, 225, 189, 240, 226, 174, 139, 64, 148, 72, 195, 125, 247,
    30, 96, 56, 200, 241, 179, 259, 260, 261, 181, 196, 252, 97, 236, 180, 175, 194, 198, 80, 158,
    44, 251, 163, 214, 98, 156, 230, 103, 220, 182, 173, 262, 263, 141, 255, 264, 215, 257, 199,
    190, 208, 235, 212, 232, 177, 197, 77, 246, 140, 217, 229, 178, 265, 237, 248, 249, 256, 211,
    201, 209, 134, 238, 258, 104, 137, 142, 118, 191, 213, 234, 61, 266, 218, 239, 144, 254, 210,
    216, 253, 99, 267,
)
REDUCE_ORDER = (
    215, 14, 3, 7, 2, 0, 8, 214, 216, 38, 1, 10, 84, 133, 85, 37, 9, 33, 11, 217, 36, 218, 28, 86,
    87, 35, 29, 12, 219, 4, 5, 92, 17, 89, 57, 91, 220, 221, 21, 88, 24, 26, 34, 40, 42, 94, 222,
    16, 23, 22, 136, 44, 165, 223, 168, 93, 15, 197, 39, 20, 43, 202, 51, 134, 135, 166, 53, 167,
    45, 67, 6, 19, 68, 102, 170, 204, 47, 141, 126, 198, 143, 96, 18, 25, 172, 173, 95, 71, 54,
    116, 52, 30, 103, 118, 119, 151, 41, 55, 46, 149, 117, 138, 106, 174, 59, 199, 181, 175, 27,
    75, 31, 200, 13, 169, 61, 205, 69, 58, 139, 70, 150, 206, 185, 108, 140, 224, 90, 77, 183,
    120, 121, 48, 203, 137, 49, 72, 189, 100, 225, 226, 56, 63, 177, 191, 171, 124, 76, 142, 122,
    60, 104, 187, 97, 123, 32, 201, 73, 98, 145, 74, 144, 155, 110, 153, 79, 182, 128, 176, 127,
    146, 62, 125, 152, 78, 159, 184, 101, 107, 157, 147, 186, 207, 64, 65, 80, 178, 179, 105, 148,
    193, 188, 208, 99, 154, 66, 190, 81, 129, 130, 109, 112, 156, 209, 111, 161, 82, 192, 158,
    210, 160, 211, 131, 180, 113, 114, 162, 163, 50, 194, 195, 83, 212, 132, 164, 115, 196, 213,
)

MESH = pl.DeviceIdType.MESH
LINE = 4
PAIR = 2


class Place:
    def __init__(self):
        self.ctx = lax.axis_index("ctx")
        self.shard = lax.axis_index("fsdp")
        self.side = lax.div(self.ctx, 2)
        self.core = lax.rem(self.ctx, 2)
        self.line = lax.div(self.shard, PAIR)
        self.pair = lax.rem(self.shard, PAIR)

    def ahead(self, way):
        return (self.ctx, self.shard + way * PAIR)

    def across(self):
        return (self.ctx, self.shard + 1 - 2 * self.pair)

    def beside(self):
        return (self.ctx + 2 - 4 * self.side, self.shard)

    def twin(self):
        return (self.ctx + 1 - 2 * self.core, self.shard)

    def has(self, way, steps):
        if steps == 0:
            return None
        return self.line >= steps if way > 0 else self.line <= LINE - 1 - steps

    def can(self, way):
        return self.line <= LINE - 2 if way > 0 else self.line >= 1

    def shard_of(self, way, steps, other):
        pair = 1 - self.pair if other else self.pair
        return (self.line - way * steps) * PAIR + pair


def when(conditions, action):
    held = [c for c in conditions if c is not None]
    if not held:
        action()
        return
    both = held[0]
    for c in held[1:]:
        both = jnp.logical_and(both, c)
    pl.when(both)(action)


def greet(place):
    barrier = pltpu.get_barrier_semaphore()
    for peer in (place.across(), place.beside(), place.twin()):
        pl.semaphore_signal(barrier, inc=1, device_id=peer, device_id_type=MESH)
    for way in (1, -1):
        when(
            [place.can(way)],
            lambda way=way: pl.semaphore_signal(
                barrier, inc=1, device_id=place.ahead(way), device_id_type=MESH
            ),
        )
    lines = jnp.minimum(place.line, 1) + jnp.minimum(LINE - 1 - place.line, 1)
    pl.semaphore_wait(barrier, 3 + lines)


class Flow:
    def __init__(self, array, shard_rows, region, order="line", sides=False, cores=True):
        self.array = array
        self.shard_rows = shard_rows
        self.region = region
        self.order = order
        self.sides = sides
        self.cores = cores

    def view(self, ref, shard, core, side):
        row, rows, column, columns = self.region(core, side)
        start = row if shard is None else shard * self.shard_rows + row
        if not isinstance(start, int):
            start = pl.multiple_of(start, 16)
        if not isinstance(column, int):
            column = pl.multiple_of(column, 128)
        return ref.at[pl.ds(start, rows), pl.ds(column, columns)]


def positions(order):
    found = []
    if order == "line":
        found.append(("P", 1, 0, True))
        for steps in range(1, LINE):
            for way in (1, -1):
                found.append(("L", way, steps, False))
                found.append(("P", way, steps, True))
    else:
        found.append(("P", 1, 0, True))
        for steps in range(1, LINE):
            for way in (1, -1):
                found.append(("L", way, steps, False))
                found.append(("L", way, steps, True))
    return found


class Labels:
    def __init__(self):
        self.numbers = {}

    def __call__(self, key):
        return self.numbers.setdefault(key, len(self.numbers))


def gather_labels(flows):
    labels = Labels()
    for number, flow in enumerate(flows):
        for spot in positions(flow.order):
            labels((number, "in") + spot)
            if flow.sides:
                labels((number, "side") + spot)
            if flow.cores:
                labels((number, "twin") + spot)
                if flow.sides:
                    labels((number, "twinside") + spot)
    return labels


class Gather:
    def __init__(self, place, flows, owns, fulls, send, recv):
        self.place, self.flows, self.owns, self.fulls = place, flows, owns, fulls
        self.send, self.recv = send, recv
        self.labels = gather_labels(flows)
        self.sent = []

    def copy(self, number, key, spot, peer, core, side, own=False):
        flow = self.flows[number]
        place = self.place
        if own:
            shard = place.shard
            source = flow.view(self.owns[flow.array], None, core, side)
        else:
            shard = place.shard_of(*spot[1:])
            source = flow.view(self.fulls[flow.array], shard, core, side)
        target = flow.view(self.fulls[flow.array], shard, core, side)
        label = self.labels((number,) + key)
        return pltpu.make_async_remote_copy(
            source,
            target,
            self.send.at[label],
            self.recv.at[label],
            device_id=peer,
            device_id_type=MESH,
        )

    def start(self, conditions, copy):
        when(conditions, copy.start)
        self.sent.append((conditions, copy))

    def begin(self, number):
        flow, place = self.flows[number], self.place
        core, side = place.core, place.side
        here = (None, 1, 0, False)
        for way in (1, -1):
            self.start(
                [place.can(way)],
                self.copy(
                    number, ("in", "L", way, 1, False), here, place.ahead(way), core, side, True
                ),
            )
        self.start(
            [],
            self.copy(number, ("in", "P", 1, 0, True), here, place.across(), core, side, True),
        )

    def arrive(self, number, spot):
        flow, place = self.flows[number], self.place
        kind, way, steps, other = spot
        core, side = place.core, place.side
        there = place.has(way, steps)

        def take():
            self.copy(number, ("in",) + spot, spot, place.across(), core, side).wait_recv()

        when([there], take)

        def onward(extra, key, peer):
            self.start(
                [c for c in (there, extra) if c is not None],
                self.copy(number, key, spot, peer, core, side),
            )

        if kind == "L" and steps + 1 < LINE:
            onward(place.can(way), ("in", "L", way, steps + 1, other), place.ahead(way))
        if kind == "L" and flow.order == "line":
            onward(None, ("in", "P", way, steps, True), place.across())
        if kind == "P" and flow.order == "pair":
            for direction in (1, -1):
                onward(
                    place.can(direction), ("in", "L", direction, 1, True), place.ahead(direction)
                )
        if flow.sides:
            onward(None, ("side",) + spot, place.beside())
        if flow.cores:
            onward(None, ("twin",) + spot, place.twin())

    def arrive_side(self, number, spot):
        flow, place = self.flows[number], self.place
        there = place.has(*spot[1:3])
        core, side = place.core, 1 - place.side
        when(
            [there],
            lambda: self.copy(
                number, ("side",) + spot, spot, place.beside(), core, side
            ).wait_recv(),
        )
        if flow.cores:
            self.start(
                [there] if there is not None else [],
                self.copy(number, ("twinside",) + spot, spot, place.twin(), core, side),
            )

    def arrive_twin(self, number, spot):
        flow, place = self.flows[number], self.place
        there = place.has(*spot[1:3])
        core = 1 - place.core
        if flow.cores:
            when(
                [there],
                lambda: self.copy(
                    number, ("twin",) + spot, spot, place.twin(), core, place.side
                ).wait_recv(),
            )
            if flow.sides:
                when(
                    [there],
                    lambda: self.copy(
                        number, ("twinside",) + spot, spot, place.twin(), core, 1 - place.side
                    ).wait_recv(),
                )

    def actions(self):
        found = []
        for n, flow in enumerate(self.flows):
            found.append((("begin", n), lambda n=n: self.begin(n)))
        for index in range(len(positions("line"))):
            for n, flow in enumerate(self.flows):
                spot = positions(flow.order)[index]
                found.append((("in", n, spot), lambda n=n, spot=spot: self.arrive(n, spot)))
                if flow.sides:
                    found.append(
                        (("side", n, spot), lambda n=n, spot=spot: self.arrive_side(n, spot))
                    )
        return found

    def wait_twins(self, arrays):
        for number, flow in enumerate(self.flows):
            if flow.array in arrays:
                for spot in positions(flow.order):
                    self.arrive_twin(number, spot)

    def finish(self, arrays):
        self.wait_twins(arrays)
        for conditions, copy in self.sent:
            when(conditions, copy.wait_send)


class Swap:
    def __init__(self, place, ins, outs, send, recv, local):
        side = place.side
        self.away = [
            pltpu.make_async_remote_copy(
                here.at[1 - side],
                there.at[side],
                send.at[k],
                recv.at[k],
                device_id=place.beside(),
                device_id_type=MESH,
            )
            for k, (here, there) in enumerate(zip(ins, outs))
        ]
        self.stay = [
            pltpu.make_async_copy(here.at[side], there.at[side], local.at[k])
            for k, (here, there) in enumerate(zip(ins, outs))
        ]

    def start(self):
        for copy in self.away + self.stay:
            copy.start()

    def finish(self):
        for copy in self.away + self.stay:
            copy.wait()


def swap_scratch(count):
    return [pltpu.SemaphoreType.DMA((count,))] * 3


def column_flows(array, shard_rows, columns, shared, early):
    half = columns // 2
    part = (half - shared) // 2
    flows = []
    if shared:
        flows.append(
            Flow(array, shard_rows, lambda core, side: (0, shard_rows, core * half, shared))
        )
    if early:
        flows.append(
            Flow(
                array,
                shard_rows,
                lambda core, side: (0, shard_rows, core * half + shared + side * part, early),
                sides=True,
            )
        )
    if part > early:
        flows.append(
            Flow(
                array,
                shard_rows,
                lambda core, side: (
                    0,
                    shard_rows,
                    core * half + shared + side * part + early,
                    part - early,
                ),
                order="pair",
                sides=True,
            )
        )
    return flows


def row_flows(array, shard_rows, columns, shared, early):
    half = shard_rows // 2
    part = (half - shared) // 2
    return [
        Flow(array, shard_rows, lambda core, side: (core * half, shared, 0, columns)),
        Flow(
            array,
            shard_rows,
            lambda core, side: (core * half + shared + side * part, early, 0, columns),
            sides=True,
        ),
        Flow(
            array,
            shard_rows,
            lambda core, side: (core * half + shared + side * part + early, part - early, 0, columns),
            order="pair",
            sides=True,
        ),
    ]


class Part:
    def __init__(self, rows, columns, along, flows, dtype=BF16, inside=False):
        self.rows, self.columns, self.along, self.dtype = rows, columns, along, dtype
        self.inside = inside
        self.flows = flows
        self.half_rows = rows // 2 if along == "rows" else rows
        self.half_columns = columns // 2 if along == "columns" else columns

    def half(self, ref, shard, core):
        base = 0 if shard is None else pl.multiple_of(shard * self.rows, 16)
        if self.along == "rows":
            row = core * self.half_rows + (0 if shard is None else shard * self.rows)
            return ref.at[pl.ds(pl.multiple_of(row, 16), self.half_rows), :]
        if self.along == "columns":
            column = pl.multiple_of(core * self.half_columns, 128)
            return ref.at[pl.ds(base, self.rows), pl.ds(column, self.half_columns)]
        return ref.at[pl.ds(base, self.rows), :]

    def inner(self, flow, side):
        first, extent = flow[0](side), flow[1]
        if self.along == "rows":
            start = first if isinstance(first, int) else pl.multiple_of(first, 16)
            return pl.ds(start, extent), slice(None)
        start = first if isinstance(first, int) else pl.multiple_of(first, 128)
        return slice(None), pl.ds(start, extent)

    def outer(self, flow, core, side):
        first, extent = flow[0](side), flow[1]
        if self.along == "rows":
            return pl.ds(pl.multiple_of(core * self.half_rows + first, 16), extent), slice(None)
        if self.along == "columns":
            return slice(None), pl.ds(
                pl.multiple_of(core * self.half_columns + first, 128), extent
            )
        return slice(None), slice(None)

    def extent(self, flow):
        if self.along == "rows":
            return flow[1], self.half_columns
        return self.half_rows, flow[1]


SPOTS = [(1, 3), (-1, 3), (1, 2), (-1, 2), (1, 1), (-1, 1), (1, 0)]


def reduce_scratch(parts):
    shapes = []
    for part in parts:
        half = (LINE * PAIR, part.half_rows, part.half_columns)
        shapes.append(pltpu.VMEM(half, part.dtype))
        shapes.append(pltpu.VMEM(half if part.along else half[1:], part.dtype))
        for flow in part.flows:
            rows, columns = part.extent(flow)
            shapes.append(
                pltpu.VMEM((LINE * PAIR if flow[3] else 1, rows, columns), part.dtype)
            )
            shapes.append(
                pltpu.VMEM((LINE if flow[2] == "line" else 1, rows, columns), part.dtype)
            )
            shapes.append(
                pltpu.VMEM(
                    ((LINE + 1) * (1 if flow[2] == "line" else PAIR), rows, columns), part.dtype
                )
            )
    return shapes


def reduce_labels(parts):
    labels = Labels()
    for n, part in enumerate(parts):
        for way, steps in SPOTS:
            for other in (False, True):
                labels((n, "twin", way, steps, other))
        labels((n, "twinend"))
        for k, flow in enumerate(part.flows):
            for way, steps in SPOTS:
                for other in (False, True):
                    if flow[3]:
                        labels((n, k, "side", way, steps, other))
                    if flow[2] == "pair" or not other:
                        labels((n, k, "line", way, steps, other))
                        if steps == 0:
                            labels((n, k, "line", -way, steps, other))
                if flow[2] == "line" or steps == 0:
                    labels((n, k, "pair", way, steps))
            labels((n, k, "sideend"))
            labels((n, k, "twinend"))
            labels((n, k, "twinsideend"))
    return labels


class Reduce:
    def __init__(self, place, parts, grads, outs, scratch, send, recv, load):
        self.place, self.parts, self.grads, self.outs = place, parts, grads, outs
        self.send, self.recv, self.load = send, recv, load
        self.labels = reduce_labels(parts)
        self.sent = []
        self.own, self.other, self.lanes = [], [], []
        at = 0
        for part in parts:
            self.own.append(scratch[at])
            self.other.append(scratch[at + 1])
            at += 2
            lanes = []
            for _ in part.flows:
                lanes.append(scratch[at : at + 3])
                at += 3
            self.lanes.append(lanes)

    def copy(self, source, target, key, peer):
        label = self.labels(key)
        return pltpu.make_async_remote_copy(
            source,
            target,
            self.send.at[label],
            self.recv.at[label],
            device_id=peer,
            device_id_type=MESH,
        )

    def start(self, conditions, copy):
        when(conditions, copy.start)
        self.sent.append((conditions, copy))

    def there(self, spot):
        return self.place.has(-spot[0], spot[1])

    def shard(self, spot, other):
        return self.place.shard_of(-spot[0], spot[1], other)

    def keep(self, n, spot, other):
        shard = self.shard(spot, other)
        label = SPOTS.index(spot) * 2 + int(other)
        return pltpu.make_async_copy(
            self.parts[n].half(self.grads[n], shard, self.place.core),
            self.own[n].at[shard],
            self.load.at[n * 2 * len(SPOTS) + label],
        )

    def twin(self, n, spot, other, core):
        shard = self.shard(spot, other)
        part = self.parts[n]
        return self.copy(
            self.grads[n].at[shard] if part.inside else part.half(self.grads[n], shard, core),
            self.other[n].at[shard],
            (n, "twin") + spot + (other,),
            self.place.twin(),
        )

    def begin(self, n, spot):
        there = self.there(spot)
        for other in (True, False):
            if not self.parts[n].inside:
                when([there], self.keep(n, spot, other).start)
            if self.parts[n].along:
                self.start([there], self.twin(n, spot, other, 1 - self.place.core))

    def piece(self, n, k, shard, side):
        part = self.parts[n]
        rows, columns = part.inner(part.flows[k], side)
        return self.own[n].at[shard, rows, columns]

    def side_copy(self, n, k, spot, other, side):
        shard = self.shard(spot, other)
        return self.copy(
            self.piece(n, k, shard, side),
            self.lanes[n][k][0].at[shard],
            (n, k, "side") + spot + (other,),
            self.place.beside(),
        )

    def add_cores(self, n, spot):
        there = self.there(spot)
        part = self.parts[n]
        for other in (True, False):

            def add(other=other):
                shard = self.shard(spot, other)
                if not part.inside:
                    self.keep(n, spot, other).wait()
                if part.along:
                    self.twin(n, spot, other, self.place.core).wait_recv()
                    self.own[n][shard] = self.own[n][shard] + self.other[n][shard]

            when([there], add)
        for other in (True, False):
            for k, flow in enumerate(part.flows):
                if flow[3]:
                    self.start([there], self.side_copy(n, k, spot, other, 1 - self.place.side))
                elif other:
                    self.start([there], self.pair_copy(n, k, spot, self.shard(spot, True)))

    def pair_copy(self, n, k, spot, shard):
        flow = self.parts[n].flows[k]
        slot = self.place.line + spot[0] * spot[1] if flow[2] == "line" else 0
        return self.copy(
            self.piece(n, k, shard, self.place.side),
            self.lanes[n][k][1].at[slot],
            (n, k, "pair") + spot,
            self.place.across(),
        )

    def add_sides(self, n, k, spot):
        there = self.there(spot)
        side = self.place.side
        for other in (True, False):

            def add(other=other):
                shard = self.shard(spot, other)
                self.side_copy(n, k, spot, other, side).wait_recv()
                piece = self.piece(n, k, shard, side)
                piece[...] = piece[...] + self.lanes[n][k][0][shard]

            when([there], add)
        if self.parts[n].flows[k][2] == "line":
            self.start([there], self.pair_copy(n, k, spot, self.shard(spot, True)))

    def line_slot(self, flow, way, steps, other, line):
        slot = line if (steps > 0 or way > 0) else LINE
        return slot + (LINE + 1) * int(other) if flow[2] == "pair" else slot

    def line_copy(self, n, k, spot, other, arriving):
        flow = self.parts[n].flows[k]
        way, steps = spot
        shard = self.shard(spot, other)
        line = self.place.line + way * steps
        left = steps if arriving else steps - 1
        return self.copy(
            self.piece(n, k, shard, self.place.side),
            self.lanes[n][k][2].at[self.line_slot(flow, way, left, other, line)],
            (n, k, "line", way, left, other),
            self.place.ahead(way),
        )

    def add_line(self, n, k, spot):
        place = self.place
        there = self.there(spot)
        way, steps = spot
        side = place.side
        flow = self.parts[n].flows[k]
        if flow[2] == "line":

            def add():
                shard = self.shard(spot, False)
                self.pair_copy(n, k, spot, shard).wait_recv()
                piece = self.piece(n, k, shard, side)
                piece[...] = piece[...] + self.lanes[n][k][1][place.line + way * steps]

            when([there], add)
        for other in (True, False) if flow[2] == "pair" else (False,):
            for direction in (1, -1) if steps == 0 else (way,):

                def add_line(other=other, here=(direction, steps)):
                    self.line_copy(n, k, here, other, True).wait_recv()
                    piece = self.piece(n, k, self.shard(here, other), side)
                    line = place.line + here[0] * here[1]
                    slot = self.line_slot(flow, here[0], here[1], other, line)
                    piece[...] = piece[...] + self.lanes[n][k][2][slot]

                when([there, place.can(-direction)], add_line)
            if steps > 0:
                self.start([there], self.line_copy(n, k, spot, other, False))

    def send_pair(self, n, k):
        self.start([], self.pair_copy(n, k, (1, 0), self.shard((1, 0), True)))

    def send_swap(self, n, k):
        self.start([], self.swap(n, k))

    def settle(self, n, k):
        place = self.place
        core, side, here = place.core, place.side, place.shard
        part = self.parts[n]
        flow = part.flows[k]
        piece = self.piece(n, k, here, side)
        out = self.out_view(n, k, core, side)
        if flow[3]:
            if flow[2] == "pair":
                self.pair_copy(n, k, (1, 0), here).wait_recv()
                out[...] = piece[...] + self.lanes[n][k][1][0]
            else:
                out[...] = piece[...]
            self.start([], self.out_copy(n, k, "sideend", place.beside(), core, side))
        else:
            self.swap(n, k).wait_recv()
            out[...] = piece[...] + self.lanes[n][k][0][0]
        if part.along:
            self.start([], self.out_copy(n, k, "twinend", place.twin(), core, side))
        else:
            self.start([], self.whole(n, k))

    def settle_side(self, n, k):
        place = self.place
        core, side = place.core, 1 - place.side
        self.out_copy(n, k, "sideend", place.beside(), core, side).wait_recv()
        self.start([], self.out_copy(n, k, "twinsideend", place.twin(), core, side))

    def swap(self, n, k):
        return self.copy(
            self.piece(n, k, self.place.shard, self.place.side),
            self.lanes[n][k][0].at[0],
            (n, k, "sideend"),
            self.place.beside(),
        )

    def out_view(self, n, k, core, side):
        part = self.parts[n]
        rows, columns = part.outer(part.flows[k], core, side)
        return self.outs[n].at[rows, columns]

    def out_copy(self, n, k, key, peer, core, side):
        view = self.out_view(n, k, core, side)
        return self.copy(view, view, (n, k, key), peer)

    def last(self):
        place = self.place
        core, side = place.core, place.side
        everything = [(n, k) for n, part in enumerate(self.parts) for k in range(len(part.flows))]
        for n, k in everything:
            if self.parts[n].along:
                self.out_copy(n, k, "twinend", place.twin(), 1 - core, side).wait_recv()
                if self.parts[n].flows[k][3]:
                    self.out_copy(
                        n, k, "twinsideend", place.twin(), 1 - core, 1 - side
                    ).wait_recv()
            else:
                self.whole(n, k).wait_recv()
        for conditions, copy in self.sent:
            when(conditions, copy.wait_send)
        for n, k in everything:
            if not self.parts[n].along:
                view = self.out_view(n, k, core, side)
                view[...] = view[...] + self.other[n][...]

    def whole(self, n, k):
        return self.copy(
            self.out_view(n, k, self.place.core, self.place.side),
            self.other[n],
            (n, k, "twinend"),
            self.place.twin(),
        )

    def actions(self):
        found = []
        for n, part in enumerate(self.parts):
            for spot in SPOTS:
                found.append((("begin", n, spot), lambda n=n, s=spot: self.begin(n, s)))
        for n, part in enumerate(self.parts):
            for spot in SPOTS:
                found.append((("cores", n, spot), lambda n=n, s=spot: self.add_cores(n, s)))
            for k, flow in enumerate(part.flows):
                at = (n, k)
                for spot in SPOTS:
                    if flow[3]:
                        found.append(
                            (("sides", n, k, spot), lambda at=at, s=spot: self.add_sides(*at, s))
                        )
                    found.append(
                        (("line", n, k, spot), lambda at=at, s=spot: self.add_line(*at, s))
                    )
                if flow[2] == "pair":
                    found.append((("pair", n, k), lambda at=at: self.send_pair(*at)))
                if not flow[3]:
                    found.append((("swap", n, k), lambda at=at: self.send_swap(*at)))
                found.append((("settle", n, k), lambda at=at: self.settle(*at)))
                if flow[3]:
                    found.append((("after", n, k), lambda at=at: self.settle_side(*at)))
        found.append((("last",), self.last))
        return found


def in_order(actions, order):
    if order is None:
        return [action for _, action in actions]
    assert sorted(order) == list(range(len(actions)))
    return [actions[i][1] for i in order]


def column_part(rows, columns, shared, early, inside=False):
    half = columns // 2
    part = (half - shared) // 2
    flows = []
    if shared:
        flows.append((lambda side: 0, shared, "line", False))
    if early:
        flows.append((lambda side: shared + side * part, early, "line", True))
    if part > early:
        flows.append((lambda side: shared + side * part + early, part - early, "pair", True))
    return Part(rows, columns, "columns", flows, inside=inside)


def row_part(rows, columns, shared, early):
    half = rows // 2
    part = (half - shared) // 2
    return Part(
        rows,
        columns,
        "rows",
        [
            (lambda side: 0, shared, "line", False),
            (lambda side: shared + side * part, early, "line", True),
            (lambda side: shared + side * part + early, part - early, "pair", True),
        ],
    )


def vector_part(rows, columns, inside=False):
    return Part(rows, columns, None, [(lambda side: 0, columns, "line", False)], F32, inside)


ROW_QUERY, ROW_VALUE, ROW_OUTPUT, ROW_GAIN1, ROW_SHIFT1, ROW_INNER, INNER = 0, 1, 2, 3, 4, 5, 4
ROW_OUTER, ROW_GAIN2, ROW_SHIFT2 = 9, 10, 11
TABLE_ROWS = 16
VMEM = 67043328
LANES = 128
BAND = 128


def spread_table(table_ref, vec):
    for shard in range(table_ref.shape[0] // TABLE_ROWS):
        vec[:, pl.ds(shard * LANES, LANES)] = table_ref[
            pl.ds(shard * TABLE_ROWS, TABLE_ROWS), :
        ].astype(F32)


def fold_table(vec, table_ref, first, count):
    for shard in range(table_ref.shape[0] // TABLE_ROWS):
        table_ref[pl.ds(shard * TABLE_ROWS + first, count), :] = vec[
            pl.ds(first, count), pl.ds(shard * LANES, LANES)
        ]


def row_place(row, core, rows):
    half = rows // 2
    return jnp.where(row < half, row, row + half) + core * half


def total_rows(block):
    return jnp.sum(block.astype(F32), axis=0, keepdims=True)


def middle_kernel(
    rows_ref,
    context_ref,
    cot_ref,
    lengths_ref,
    table_ref,
    output_w,
    inner_w,
    outer_w,
    out_ref,
    first_grad_ref,
    context_grad_ref,
    sums_ref,
    output_g,
    inner_g,
    outer_g,
    output_v,
    inner_v,
    outer_v,
    vec,
    sums,
    active,
    slope,
    unit1,
    unit2,
    rate1,
    total,
    low,
    low_t,
    second,
    second_low,
    inner_b,
    outer_b,
    load,
    save,
):
    rows, width = rows_ref.shape
    tiles, _, tile = inner_v.shape
    ctx = lax.axis_index("ctx")
    side, core = lax.div(ctx, 2), lax.rem(ctx, 2)
    length = lengths_ref[side, 0]
    bands = rows // BAND

    def inner_load(t):
        return pltpu.make_async_copy(
            inner_w.at[:, pl.ds(pl.multiple_of(t * tile, tile), tile)], inner_v.at[t], load.at[0, t]
        )

    def outer_load(t):
        return pltpu.make_async_copy(
            outer_w.at[pl.ds(pl.multiple_of(t * tile, tile), tile), :], outer_v.at[t], load.at[1, t]
        )

    output_load = pltpu.make_async_copy(output_w, output_v, load.at[2, 0])
    output_load.start()
    for t in range(tiles):
        inner_load(t).start()
        outer_load(t).start()
    spread_table(table_ref, vec)
    sums[...] = jnp.zeros_like(sums)
    output_load.wait()
    total[...] = plain_product(context_ref[...], output_v[...])

    def band_of(b):
        return pl.ds(pl.multiple_of(b * BAND, BAND), BAND)

    def first_norm(b, carry):
        here = band_of(b)
        first_sum = (
            rows_ref[here, :].astype(F32) + total[here, :] + vec[pl.ds(ROW_OUTPUT, 1), :]
        )
        unit, rate = norm_parts(first_sum)
        unit1[here, :] = unit
        rate1[here, :] = jnp.broadcast_to(rate, (BAND, LANES))
        normed = unit * vec[pl.ds(ROW_GAIN1, 1), :] + vec[pl.ds(ROW_SHIFT1, 1), :]
        low[here, :] = normed.astype(BF16)
        total[here, :] = normed + vec[pl.ds(ROW_OUTER, 1), :]
        return carry

    lax.fori_loop(0, bands, first_norm, 0)
    low_t[...] = low[...].T

    def forward(t, carry):
        inner_load(t).wait()
        bias = jnp.concatenate(
            [
                vec[pl.ds(ROW_INNER + k, 1), pl.ds(pl.multiple_of(t * LANES, LANES), LANES)]
                for k in range(INNER)
            ],
            axis=1,
        )
        hidden = plain_product(low[...], inner_v[t]) + bias
        share = 0.5 + 0.5 * lax.erf(hidden * 0.7071067811865476)
        active[t] = (hidden * share).astype(BF16)
        slope[t] = share + hidden * (jnp.exp(-0.5 * hidden * hidden) * 0.3989422804014327)
        outer_load(t).wait()
        total[...] += plain_product(active[t], outer_v[t])
        return carry

    lax.fori_loop(0, tiles, forward, 0)

    def second_norm(b, carry):
        here = band_of(b)
        unit, rate = norm_parts(total[here, :])
        row = b * BAND + lax.broadcasted_iota(jnp.int32, (BAND, width), 0)
        mask = (row_place(row, core, rows) < length).astype(F32)
        gain = vec[pl.ds(ROW_GAIN2, 1), :]
        out_ref[here, :] = ((unit * gain + vec[pl.ds(ROW_SHIFT2, 1), :]) * mask).astype(BF16)
        out_grad = cot_ref[here, :].astype(F32) * mask
        grad = norm_back(unit, rate, out_grad * gain)
        second[here, :] = grad
        grad_low = grad.astype(BF16)
        second_low[here, :] = grad_low
        sums[pl.ds(ROW_GAIN2, 1), :] += total_rows(out_grad * unit)
        sums[pl.ds(ROW_SHIFT2, 1), :] += total_rows(out_grad)
        sums[pl.ds(ROW_OUTER, 1), :] += total_rows(grad_low)
        return carry

    lax.fori_loop(0, bands, second_norm, 0)

    def inner_save(t):
        slot = lax.rem(t, 2)
        return pltpu.make_async_copy(
            inner_b.at[slot],
            inner_g.at[:, pl.ds(pl.multiple_of(t * tile, tile), tile)],
            save.at[0, slot],
        )

    def outer_save(t):
        slot = lax.rem(t, 2)
        return pltpu.make_async_copy(
            outer_b.at[slot],
            outer_g.at[pl.ds(pl.multiple_of(t * tile, tile), tile), :],
            save.at[1, slot],
        )

    def backward(t, carry):
        slot = lax.rem(t, 2)
        hidden_grad = (right_product(second_low[...], outer_v[t]) * slope[t]).astype(BF16)
        summed = total_rows(hidden_grad)
        for k in range(INNER):
            sums[
                pl.ds(ROW_INNER + k, 1), pl.ds(pl.multiple_of(t * LANES, LANES), LANES)
            ] = summed[:, k * LANES : (k + 1) * LANES]

        @pl.when(t >= 2)
        def _():
            outer_save(t - 2).wait()
            inner_save(t - 2).wait()

        outer_b[slot] = left_product(active[t], second_low[...]).astype(BF16)
        inner_b[slot] = plain_product(low_t[...], hidden_grad).astype(BF16)
        outer_save(t).start()
        second[...] += right_product(hidden_grad, inner_v[t])
        inner_save(t).start()
        return carry

    lax.fori_loop(0, tiles, backward, 0)

    def first_back(b, carry):
        here = band_of(b)
        grad = second[here, :]
        unit = unit1[here, :]
        sums[pl.ds(ROW_GAIN1, 1), :] += total_rows(grad * unit)
        sums[pl.ds(ROW_SHIFT1, 1), :] += total_rows(grad)
        back = norm_back(unit, rate1[here, :1], grad * vec[pl.ds(ROW_GAIN1, 1), :])
        first_grad_ref[here, :] = back
        back_low = back.astype(BF16)
        second_low[here, :] = back_low
        sums[pl.ds(ROW_OUTPUT, 1), :] += total_rows(back_low)
        return carry

    lax.fori_loop(0, bands, first_back, 0)
    context_grad_ref[...] = right_product(second_low[...], output_v[...]).astype(BF16)
    output_g[...] = left_product(context_ref[...], second_low[...]).astype(BF16)
    fold_table(sums, sums_ref, 0, TABLE_ROWS)
    for t in range(tiles - 2, tiles):
        outer_save(t).wait()
        inner_save(t).wait()


def middle(rows, context, cot, lengths, table, output_w, inner_w, outer_w):
    count, width = rows.shape
    hidden = inner_w.shape[1]
    tile = INNER * LANES
    tiles = hidden // tile
    whole = pl.BlockSpec(memory_space=pltpu.VMEM)
    far = pl.BlockSpec(memory_space=pltpu.HBM)

    def space(dtype):
        return pltpu.VMEM((count, width), dtype)

    return pl.pallas_call(
        middle_kernel,
        out_shape=[
            jax.ShapeDtypeStruct((count, width), BF16),
            jax.ShapeDtypeStruct((count, width), F32),
            jax.ShapeDtypeStruct((count, width), BF16),
            jax.ShapeDtypeStruct(table.shape, F32),
            jax.ShapeDtypeStruct(output_w.shape, BF16),
            jax.ShapeDtypeStruct(inner_w.shape, BF16),
            jax.ShapeDtypeStruct(outer_w.shape, BF16),
        ],
        in_specs=[whole] * 3 + [pl.BlockSpec(memory_space=pltpu.SMEM), whole] + [far] * 3,
        out_specs=[whole] * 5 + [far] * 2,
        scratch_shapes=[
            pltpu.VMEM(output_w.shape, BF16),
            pltpu.VMEM((tiles, width, tile), BF16),
            pltpu.VMEM((tiles, tile, width), BF16),
            pltpu.VMEM((TABLE_ROWS, width), F32),
            pltpu.VMEM((TABLE_ROWS, width), F32),
            pltpu.VMEM((tiles, count, tile), BF16),
            pltpu.VMEM((tiles, count, tile), F32),
            space(F32),
            pltpu.VMEM((8, LANES), F32),
            pltpu.VMEM((count, LANES), F32),
            space(F32),
            space(BF16),
            pltpu.VMEM((width, count), BF16),
            space(F32),
            space(BF16),
            pltpu.VMEM((2, width, tile), BF16),
            pltpu.VMEM((2, tile, width), BF16),
            pltpu.SemaphoreType.DMA((3, tiles)),
            pltpu.SemaphoreType.DMA((2, 2)),
        ],
        compiler_params=pltpu.CompilerParams(vmem_limit_bytes=VMEM),
        name="feed_forward",
    )(rows, context, cot, lengths, table, output_w, inner_w, outer_w)


def widen_kernel(splits, lines, *refs):
    count = len(splits)
    many = sum(splits)
    ins, table, outs = refs[:count], refs[count], refs[count + 1 : count + 1 + many]
    vectors = refs[count + 1 + many : count + 1 + many + len(lines)]
    rest = refs[count + 1 + many + len(lines) :]
    narrow, held, wides = rest[:count], rest[count], rest[count + 1 : count + 1 + many]
    load, save = rest[-2:]
    loads = [
        pltpu.make_async_copy(here, there, load.at[k])
        for k, (here, there) in enumerate(zip(ins + (table,), narrow + (held,)))
    ]
    for copy in loads:
        copy.start()
    copies = []
    at = 0
    for k, parts in enumerate(splits):
        loads[k].wait()
        columns = narrow[k].shape[-1] // parts
        for part in range(parts):
            wides[at][...] = narrow[k][..., part * columns : (part + 1) * columns].astype(
                wides[at].dtype
            )
            copies.append(pltpu.make_async_copy(wides[at], outs[at], save.at[at]))
            copies[-1].start()
            at += 1
    loads[count].wait()
    row = 0
    for vector, extent in zip(vectors, lines):
        for line in range(extent):
            copies.append(
                pltpu.make_async_copy(
                    held.at[row], vector.at[pl.ds(line * LANES, LANES)], save.at[many + row]
                )
            )
            copies[-1].start()
            row += 1
    for copy in copies:
        copy.wait()


def widen(arrays, splits, types, table, lines):
    shapes = []
    for array, parts, kind in zip(arrays, splits, types):
        shape = array.shape[:-1] + (array.shape[-1] // parts,)
        shapes += [jax.ShapeDtypeStruct(shape, kind)] * parts
    far = pl.BlockSpec(memory_space=pltpu.HBM)
    return pl.pallas_call(
        functools.partial(widen_kernel, splits, lines),
        out_shape=shapes + [jax.ShapeDtypeStruct((k * LANES,), F32) for k in lines],
        in_specs=[far] * (len(arrays) + 1),
        out_specs=[far] * (len(shapes) + len(lines)),
        scratch_shapes=[pltpu.VMEM(array.shape, array.dtype) for array in arrays + (table,)]
        + [pltpu.VMEM(shape.shape, shape.dtype) for shape in shapes]
        + [
            pltpu.SemaphoreType.DMA((len(arrays) + 1,)),
            pltpu.SemaphoreType.DMA((len(shapes) + sum(lines),)),
        ],
        compiler_params=pltpu.CompilerParams(vmem_limit_bytes=VMEM),
        name="widen_results",
    )(*arrays, table)


def stack_heads(block, lower):
    zero = jnp.zeros_like(block)
    return jnp.concatenate((jnp.where(lower, block, zero), jnp.where(lower, zero, block)), axis=0)


def repeat(first, stop, action):
    def step(i, carry):
        action(i)
        return carry

    lax.fori_loop(first, stop, step, 0)


GROUPS = 4
HALVES = 2


SPAN = 2 * HEAD_DIM


def span_of(section, pair, width):
    return pl.ds(pl.multiple_of(section * width + pair * SPAN, SPAN), SPAN)


class AttentionForward:
    def __init__(self, place, rows, weight, vec, bias, qkv, context, probs, held, away, send, recv, save):
        self.place, self.rows, self.weight, self.vec, self.bias = place, rows, weight, vec, bias
        self.qkv, self.context, self.probs, self.held, self.away = qkv, context, probs, held, away
        self.send, self.recv, self.save = send, recv, save
        self.count, self.width = context.shape
        self.pairs = self.width // SPAN

    def save_probs(self, pair):
        return pltpu.make_async_copy(self.held.at[pair], self.probs.at[pair], self.save.at[pair])

    def fetch(self, which, pair):
        return pltpu.make_async_remote_copy(
            self.qkv.at[:, span_of(which + 1, pair, self.width)],
            self.away.at[:, span_of(which, pair, self.width)],
            self.send.at[which, pair],
            self.recv.at[which, pair],
            device_id=self.place.twin(),
            device_id_type=MESH,
        )

    def project(self, section):
        tile = 512
        rows = self.rows[...].reshape(self.count, self.width)

        def one(t):
            columns = pl.ds(pl.multiple_of(section * self.width + t * tile, tile), tile)
            product = plain_product(rows, self.weight[:, columns])
            if section != 1:
                row = ROW_QUERY if section == 0 else ROW_VALUE
                product = product + self.vec[
                    pl.ds(row, 1), pl.ds(pl.multiple_of(t * tile, tile), tile)
                ]
            self.qkv[:, columns] = product.astype(BF16)

        repeat(0, self.width // tile, one)

    def give(self, which):
        for pair in range(self.pairs):
            self.fetch(which, pair).start()

    def attend(self, pair):
        for which in range(2):
            self.fetch(which, pair).wait_recv()
        count = self.count
        lower = lax.broadcasted_iota(jnp.int32, (count, SPAN), 1) < HEAD_DIM

        def here(section):
            return self.qkv[:, span_of(section, pair, self.width)]

        def there(section):
            return self.away[:, span_of(section - 1, pair, self.width)]

        stacked = stack_heads(here(0) * HEAD_DIM**-0.5, lower)
        keys = jnp.concatenate((here(1), there(1)), axis=0)
        values = jnp.concatenate((here(2), there(2)), axis=0)
        scores = right_product(stacked, keys) + self.bias[:1, :]
        top = jnp.max(scores, axis=1, keepdims=True)
        weights = jnp.exp(scores - top)
        total = jnp.sum(weights, axis=1, keepdims=True)
        probs = (weights * (1.0 / total)).astype(BF16)
        self.held[pair] = probs
        self.save_probs(pair).start()
        mixed = plain_product(probs, values)
        self.context[:, span_of(0, pair, self.width)] = jnp.where(
            lower, mixed[:count], mixed[count:]
        ).astype(BF16)

    def attend_group(self, group):
        each = self.pairs // GROUPS
        repeat(group * each, (group + 1) * each, self.attend)

    def finish(self):
        for pair in range(self.pairs):
            for which in range(2):
                self.fetch(which, pair).wait_send()
            self.save_probs(pair).wait()


TABLE, QUERIES = 0, 1


def start_actions(gather, work, keep, swaps, save, table_ref):
    found = gather.actions()
    others = [k for k in range(len(keep)) if k not in (TABLE, QUERIES)]

    def ready():
        gather.wait_twins((TABLE, QUERIES))
        for k in (TABLE, QUERIES):
            keep[k].wait()
        swaps[0].finish()
        spread_table(table_ref, work.vec)
        save.start()

    def values():
        work.project(2)
        work.give(0)

    def queries():
        work.give(1)
        work.project(0)

    found.append((("ready",), ready))
    found.append((("project", 0), lambda: work.project(1)))
    found.append((("project", 1), values))
    found.append((("project", 2), queries))
    for group in range(GROUPS):
        found.append((("pa", group), lambda group=group: work.attend_group(group)))

    def last():
        gather.finish(others)
        work.finish()
        for k in others:
            keep[k].wait()
        swaps[1].finish()
        save.wait()

    found.append((("last",), last))
    return found


def start_kernel(flows, spots, order, *refs):
    count = max(array for array, _ in spots) + 1
    shares, refs = refs[: len(spots)], refs[len(spots) :]
    (in_block, cot_block, lengths_ref), refs = refs[:3], refs[3:]
    table_ref, refs = refs[0], refs[1:]
    far, refs = refs[: count - 1], refs[count - 1 :]
    rows, cots, qkv, context, probs, away = refs[:6]
    owns, refs = refs[6 : 6 + count], refs[6 + count :]
    weight, held, vec, bias = refs[:4]
    send, recv, local, load, send2, recv2, save2, saveq = refs[4:12]
    fulls = (table_ref, weight) + tuple(far[1:])
    place = Place()
    loads = [
        pltpu.make_async_copy(
            share, owns[array].at[:, pl.ds(column, share.shape[1])], load.at[k]
        )
        for k, (share, (array, column)) in enumerate(zip(shares, spots))
    ]
    for copy in loads:
        copy.start()
    keep = [
        pltpu.make_async_copy(
            own, full.at[pl.ds(pl.multiple_of(place.shard * own.shape[0], 16), own.shape[0]), :], local.at[k]
        )
        for k, (own, full) in enumerate(zip(owns, fulls))
    ]
    greet(place)
    rows_count = context.shape[0]
    length = lengths_ref[place.side, 0]
    row = lax.broadcasted_iota(jnp.int32, (8, rows_count), 1)
    for k, core in enumerate((place.core, 1 - place.core)):
        bias[:, pl.ds(k * rows_count, rows_count)] = jnp.where(
            row_place(row, core, rows_count) < length, 0.0, -1e30
        )
    for copy in loads:
        copy.wait()
    swaps = [
        Swap(place, [in_block], [rows], *refs[12:15]),
        Swap(place, [cot_block], [cots], *refs[15:18]),
    ]
    for swap in swaps:
        swap.start()
    gather = Gather(place, flows, owns, fulls, send, recv)
    for copy in keep:
        copy.start()
    work = AttentionForward(
        place, rows, weight, vec, bias, qkv, context, probs, held, away, send2, recv2, save2
    )
    save = pltpu.make_async_copy(weight, far[0], saveq.at[0])
    for step in in_order(start_actions(gather, work, keep, swaps, save, table_ref), order):
        step()


def start(shares, spots, blocks, lengths, flows, shards, collective_id, order):
    labels = gather_labels(flows)
    count = max(array for array, _ in spots) + 1
    shapes = []
    for array in range(count):
        members = [share for share, spot in zip(shares, spots) if spot[0] == array]
        shapes.append((members[0].shape[0], sum(m.shape[1] for m in members)))
    _, block_len, width = blocks[0].shape
    rows = 2 * block_len
    pairs = width // SPAN
    far = pl.BlockSpec(memory_space=pltpu.HBM)
    whole = pl.BlockSpec(memory_space=pltpu.VMEM)
    probs_shape = (pairs, 2 * rows, 2 * rows)
    return pl.pallas_call(
        functools.partial(start_kernel, flows, spots, order),
        out_shape=[jax.ShapeDtypeStruct((shards * r, c), BF16) for r, c in shapes]
        + [jax.ShapeDtypeStruct(block.shape, BF16) for block in blocks]
        + [
            jax.ShapeDtypeStruct((rows, 3 * width), BF16),
            jax.ShapeDtypeStruct((rows, width), BF16),
            jax.ShapeDtypeStruct(probs_shape, BF16),
            jax.ShapeDtypeStruct((rows, 2 * width), BF16),
        ],
        in_specs=[far] * (len(shares) + 2) + [pl.BlockSpec(memory_space=pltpu.SMEM)],
        out_specs=[whole] + [far] * (count - 1) + [whole, far] + [whole, whole, far, whole],
        scratch_shapes=[pltpu.VMEM(shape, BF16) for shape in shapes]
        + [
            pltpu.VMEM((shards * shapes[QUERIES][0], shapes[QUERIES][1]), BF16),
            pltpu.VMEM(probs_shape, BF16),
            pltpu.VMEM((TABLE_ROWS, width), F32),
            pltpu.VMEM((8, 2 * rows), F32),
            pltpu.SemaphoreType.DMA((len(labels.numbers),)),
            pltpu.SemaphoreType.DMA((len(labels.numbers),)),
            pltpu.SemaphoreType.DMA((count,)),
            pltpu.SemaphoreType.DMA((len(shares),)),
            pltpu.SemaphoreType.DMA((2, pairs)),
            pltpu.SemaphoreType.DMA((2, pairs)),
            pltpu.SemaphoreType.DMA((pairs,)),
            pltpu.SemaphoreType.DMA((1,)),
        ]
        + swap_scratch(1) * 2,
        compiler_params=pltpu.CompilerParams(
            collective_id=collective_id, has_side_effects=True, vmem_limit_bytes=VMEM
        ),
        name="gather_attention_forward",
    )(*shares, *blocks, lengths)


class AttentionBackward:
    def __init__(self, place, qkv, away, grad, out, keep, leave, come, send, recv):
        self.place, self.qkv, self.away, self.grad = place, qkv, away, grad
        self.out, self.keep, self.leave, self.come = out, keep, leave, come
        self.send, self.recv = send, recv
        self.count, self.width = grad.shape
        self.pairs = self.width // SPAN

    def give(self, which, pair):
        return pltpu.make_async_remote_copy(
            self.leave.at[:, span_of(which, pair, self.width)],
            self.come.at[:, span_of(which, pair, self.width)],
            self.send.at[which, pair],
            self.recv.at[which, pair],
            device_id=self.place.twin(),
            device_id_type=MESH,
        )

    def attend(self, pair, probs):
        count = self.count
        lower = lax.broadcasted_iota(jnp.int32, (count, SPAN), 1) < HEAD_DIM
        scale = HEAD_DIM**-0.5

        def here(section):
            return self.qkv[:, span_of(section, pair, self.width)]

        def there(section):
            return self.away[:, span_of(section - 1, pair, self.width)]

        first = span_of(0, pair, self.width)
        second = span_of(1, pair, self.width)
        stacked = stack_heads(here(0) * scale, lower)
        keys = jnp.concatenate((here(1), there(1)), axis=0)
        values = jnp.concatenate((here(2), there(2)), axis=0)
        grad = stack_heads(self.grad[:, first], lower)
        value_part = left_product(probs, grad)
        probs_grad = right_product(grad, values)
        wide = probs.astype(F32)
        inner = jnp.sum(wide * probs_grad, axis=1, keepdims=True)
        scores_grad = (wide * (probs_grad - inner)).astype(BF16)
        key_part = left_product(scores_grad, stacked)
        self.leave[:, first] = key_part[count:].astype(BF16)
        self.leave[:, second] = value_part[count:].astype(BF16)
        self.keep[:, first] = key_part[:count]
        self.keep[:, second] = value_part[:count]
        mixed = plain_product(scores_grad, keys) * scale
        self.out[:, first] = jnp.where(lower, mixed[:count], mixed[count:]).astype(BF16)
        for which in range(2):
            self.give(which, pair).start()

    def settle(self, pair):
        for which in range(2):
            self.give(which, pair).wait_recv()
            here = span_of(which, pair, self.width)
            self.out[:, span_of(which + 1, pair, self.width)] = (
                self.keep[:, here] + self.come[:, here].astype(F32)
            ).astype(BF16)

    def finish(self):
        for pair in range(self.pairs):
            for which in range(2):
                self.give(which, pair).wait_send()


class Finish:
    def __init__(self, work, tiles, weight, rows_ref, rows_t, first_grad, total, block, sums, held, probs, load, sems):
        self.work, self.tiles, self.weight, self.rows_ref, self.rows_t = work, tiles, weight, rows_ref, rows_t
        self.total, self.block, self.sums = total, block, sums
        self.held, self.probs, self.load, self.sems = held, probs, load, sems
        self.grad_load = pltpu.make_async_copy(first_grad, total, sems.at[held.shape[0]])
        self.count, self.width = total.shape
        self.tile = tiles.shape[2]

    def weight_load(self, t):
        columns = pl.ds(pl.multiple_of(t * self.tile, self.tile), self.tile)
        slot = lax.rem(t, self.tiles.shape[0])
        return pltpu.make_async_copy(
            self.weight.at[:, columns], self.tiles.at[slot], self.load.at[slot]
        )

    def probs_load(self, pair):
        slot = lax.rem(pair, self.held.shape[0])
        return pltpu.make_async_copy(
            self.probs.at[pair], self.held.at[slot], self.sems.at[slot]
        )

    def begin(self):
        for pair in range(self.held.shape[0]):
            self.probs_load(pair).start()
        for t in range(self.tiles.shape[0]):
            self.weight_load(t).start()
        self.grad_load.start()

    def attend(self, group):
        each = self.work.pairs // GROUPS

        slots = self.held.shape[0]

        def one(pair):
            self.probs_load(pair).wait()
            self.work.attend(pair, self.held[lax.rem(pair, slots)])
            pl.when(pair + slots < self.work.pairs)(self.probs_load(pair + slots).start)

        repeat(group * each, (group + 1) * each, one)

    def settle(self):
        repeat(0, self.work.pairs, self.work.settle)

    def weigh(self, core, target):
        shards, rows, columns = target.shape
        tile = self.tile

        def one(j):
            start = pl.multiple_of(core * columns + j * tile, tile)
            product = plain_product(self.rows_t[...], self.work.out[:, pl.ds(start, tile)])
            low = product.astype(BF16)
            for shard in range(shards):
                target[shard, :, pl.ds(pl.multiple_of(j * tile, tile), tile)] = low[
                    shard * rows : (shard + 1) * rows
                ]

        repeat(0, columns // tile, one)

    def turn(self):
        self.rows_t[...] = self.rows_ref[...].T

    def bias_sums(self, target):
        self.sums[pl.ds(0, 1), :] = total_rows(self.work.out[:, : self.width])
        self.sums[pl.ds(1, 1), :] = total_rows(self.work.out[:, 2 * self.width :])
        for shard in range(target.shape[0]):
            target[shard, pl.ds(ROW_QUERY, 2), :] = self.sums[
                pl.ds(0, 2), pl.ds(shard * LANES, LANES)
            ]

    def spread(self, half):
        count = self.weight.shape[1] // self.tile
        each = count // HALVES
        slots = self.tiles.shape[0]
        if half == 0:
            self.grad_load.wait()

        def one(t):
            self.weight_load(t).wait()
            columns = pl.ds(pl.multiple_of(t * self.tile, self.tile), self.tile)
            tile = self.tiles[lax.rem(t, slots)]
            self.total[...] += right_product(self.work.out[:, columns], tile)
            pl.when(t + slots < count)(self.weight_load(t + slots).start)

        repeat(half * each, (half + 1) * each, one)
        if half == HALVES - 1:
            rows = self.block.shape[1]
            for part in range(2):
                self.block[part] = self.total[pl.ds(part * rows, rows), :].astype(BF16)


def finish_actions(reduce, finish, swaps):
    queries, vectors = 3, 4
    place = reduce.place
    found = reduce.actions()

    def load():
        finish.begin()
        finish.turn()

    found.append((("load",), load))
    found.append((("swapout",), swaps[0].start))
    for group in range(GROUPS):
        found.append((("att", group), lambda group=group: finish.attend(group)))
    found.append((("settleatt",), finish.settle))
    found.append((("leave",), lambda: finish.weigh(1 - place.core, reduce.grads[queries])))
    found.append((("own",), lambda: finish.weigh(place.core, reduce.own[queries])))
    found.append((("sums",), lambda: finish.bias_sums(reduce.own[vectors])))
    for half in range(HALVES):
        found.append((("dx", half), lambda half=half: finish.spread(half)))
    found.append((("swapin",), swaps[1].start))
    return found


def finish_kernel(parts, order, *refs):
    rows_ref, qkv, away, grad, table_ref, first_grad, probs, weight = refs[:8]
    grads, out_block = list(refs[8:11]), refs[11]
    outs, swapped, refs = refs[12:17], refs[17:19], refs[19:]
    leave_q, tiles, held, out, keep, leave, come, total, sums, rows_t, block = refs[:11]
    send2, recv2, load2, sems = refs[11:15]
    scratch, rest = refs[15:-9], refs[-9:]
    place = Place()
    work = AttentionBackward(place, qkv, away, grad, out, keep, leave, come, send2, recv2)
    finish = Finish(
        work, tiles, weight, rows_ref, rows_t, first_grad, total, block, sums, held, probs, load2, sems
    )
    reduce = Reduce(place, parts, grads + [leave_q, None], outs, scratch, *rest[:3])
    swaps = [
        Swap(place, [out_block], [swapped[0]], *rest[3:6]),
        Swap(place, [block], [swapped[1]], *rest[6:9]),
    ]
    for shard in range(LINE * PAIR):
        reduce.own[4][shard] = table_ref[pl.ds(shard * TABLE_ROWS, TABLE_ROWS), :]
    greet(place)
    for step in in_order(finish_actions(reduce, finish, swaps), order):
        step()
    work.finish()
    for swap in swaps:
        swap.finish()


def finish(rows, saved, grad, first_grad, table, weight, grads, block, parts, collective_id, order):
    qkv, away, probs = saved
    count, width = rows.shape
    pairs = width // SPAN
    tile = 512
    labels = reduce_labels(parts)
    whole = pl.BlockSpec(memory_space=pltpu.VMEM)
    far = pl.BlockSpec(memory_space=pltpu.HBM)
    queries = parts[3]
    return pl.pallas_call(
        functools.partial(finish_kernel, parts, order),
        out_shape=[jax.ShapeDtypeStruct((p.rows, p.columns), p.dtype) for p in parts]
        + [jax.ShapeDtypeStruct(block.shape, BF16)] * 2,
        in_specs=[whole] * 5 + [far] * 7,
        out_specs=[whole] * len(parts) + [far] * 2,
        scratch_shapes=[
            pltpu.VMEM((LINE * PAIR, queries.half_rows, queries.half_columns), BF16),
            pltpu.VMEM((2, width, tile), BF16),
            pltpu.VMEM((pairs // 2,) + probs.shape[1:], BF16),
            pltpu.VMEM((count, 3 * width), BF16),
            pltpu.VMEM((count, 2 * width), F32),
            pltpu.VMEM((count, 2 * width), BF16),
            pltpu.VMEM((count, 2 * width), BF16),
            pltpu.VMEM((count, width), F32),
            pltpu.VMEM((8, width), F32),
            pltpu.VMEM((width, count), BF16),
            pltpu.VMEM(block.shape, BF16),
            pltpu.SemaphoreType.DMA((2, pairs)),
            pltpu.SemaphoreType.DMA((2, pairs)),
            pltpu.SemaphoreType.DMA((2,)),
            pltpu.SemaphoreType.DMA((pairs // 2 + 1,)),
        ]
        + reduce_scratch(parts)
        + [
            pltpu.SemaphoreType.DMA((len(labels.numbers),)),
            pltpu.SemaphoreType.DMA((len(labels.numbers),)),
            pltpu.SemaphoreType.DMA((len(parts) * 2 * len(SPOTS),)),
        ]
        + swap_scratch(1) * 2,
        compiler_params=pltpu.CompilerParams(
            collective_id=collective_id, has_side_effects=True, vmem_limit_bytes=VMEM
        ),
        name="attention_backward_reduce",
    )(rows, qkv, away, grad, table, first_grad, probs, weight, *grads, block)


def exact_gelu(hidden):
    return jax.nn.gelu(hidden, approximate=False)


def plain_product(left, right):
    return jnp.dot(left, right, preferred_element_type=F32)


def left_product(left, right):
    return lax.dot_general(left, right, (((0,), (0,)), ((), ())), preferred_element_type=F32)


def right_product(left, right):
    return lax.dot_general(left, right, (((1,), (1,)), ((), ())), preferred_element_type=F32)


def column_sums(rows):
    return jnp.sum(rows.astype(F32), axis=0)


def norm_parts(total):
    average = jnp.mean(total, axis=-1, keepdims=True)
    centered = total - average
    variance = jnp.mean(centered * centered, axis=-1, keepdims=True)
    rate = lax.rsqrt(variance + EPSILON)
    return centered * rate, rate


def norm_back(unit, rate, grad):
    return rate * (
        grad
        - jnp.mean(grad, axis=-1, keepdims=True)
        - unit * jnp.mean(grad * unit, axis=-1, keepdims=True)
    )


def split_columns(packed, widths):
    pieces = []
    start = 0
    for width in widths:
        pieces.append(packed[..., start : start + width])
        start += width
    return pieces


def native_forward(queries, keys_all, values_all, key_valid, heads):
    shape = queries.shape[:2] + (heads, HEAD_DIM)
    key_shape = keys_all.shape[:2] + (heads, HEAD_DIM)
    scores = jnp.einsum(
        "sqhd,skhd->shqk",
        queries.reshape(shape),
        keys_all.reshape(key_shape),
        preferred_element_type=F32,
    ) * (HEAD_DIM**-0.5)
    scores = jnp.where(key_valid[:, None, None, :], scores, -1e30)
    top = jnp.max(scores, axis=-1, keepdims=True)
    weights = jnp.exp(scores - top)
    probs = (weights / jnp.sum(weights, axis=-1, keepdims=True)).astype(BF16)
    context = jnp.einsum(
        "shqk,skhd->sqhd", probs, values_all.reshape(key_shape), preferred_element_type=F32
    )
    return context.reshape(queries.shape).astype(BF16), probs


def native_backward(queries, keys_all, values_all, probs, context_grad, heads):
    shape = queries.shape[:2] + (heads, HEAD_DIM)
    key_shape = keys_all.shape[:2] + (heads, HEAD_DIM)
    scale = HEAD_DIM**-0.5
    grad_heads = context_grad.reshape(shape)
    wide = probs.astype(F32)
    probs_grad = jnp.einsum(
        "sqhd,skhd->shqk", grad_heads, values_all.reshape(key_shape), preferred_element_type=F32
    )
    inner_total = jnp.sum(wide * probs_grad, axis=-1, keepdims=True)
    scores_grad = (wide * (probs_grad - inner_total)).astype(BF16)
    query_grad = jnp.einsum(
        "shqk,skhd->sqhd", scores_grad, keys_all.reshape(key_shape), preferred_element_type=F32
    )
    key_part = jnp.einsum(
        "shqk,sqhd->skhd", scores_grad, queries.reshape(shape), preferred_element_type=F32
    )
    value_part = jnp.einsum("shqk,sqhd->skhd", probs, grad_heads, preferred_element_type=F32)
    return (
        (query_grad * scale).astype(BF16).reshape(queries.shape),
        (key_part * scale).astype(BF16).reshape(keys_all.shape),
        value_part.astype(BF16).reshape(values_all.shape),
    )


def gather_rows(part):
    return lax.all_gather(part, "fsdp", axis=0, tiled=True)


def reduce_rows(part):
    share = lax.psum_scatter(part.astype(BF16), "fsdp", scatter_dimension=0, tiled=True)
    return lax.psum(share, "ctx").astype(F32)


def layer(flat_rows, cot_rows, row_mask, packed, widths, weights, forward, backward):
    full_qkv, full_output, full_inner, full_outer = weights
    rows, width = flat_rows.shape
    shards = packed.shape[0]
    (
        bias_query,
        bias_value,
        bias_output,
        gain_first,
        shift_first,
        bias_inner,
        bias_outer,
        gain_second,
        shift_second,
    ) = [piece.reshape(-1).astype(F32) for piece in split_columns(packed, widths)]
    bias_qkv = jnp.concatenate((bias_query, jnp.zeros_like(bias_query), bias_value))
    qkv = (plain_product(flat_rows, full_qkv) + bias_qkv).astype(BF16)
    context, saved = forward(qkv)

    first_sum = flat_rows.astype(F32) + plain_product(context, full_output) + bias_output
    first_unit, first_rate = norm_parts(first_sum)
    normed = first_unit * gain_first + shift_first
    normed_low = normed.astype(BF16)
    hidden = plain_product(normed_low, full_inner) + bias_inner
    active, gelu_back = jax.vjp(exact_gelu, hidden)
    active_low = active.astype(BF16)
    second_sum = normed + plain_product(active_low, full_outer) + bias_outer
    second_unit, second_rate = norm_parts(second_sum)
    output = ((second_unit * gain_second + shift_second) * row_mask).astype(BF16)

    out_grad = cot_rows.astype(F32) * row_mask
    second_gain_part = jnp.sum(out_grad * second_unit, axis=0)
    second_shift_part = jnp.sum(out_grad, axis=0)
    second_grad = norm_back(second_unit, second_rate, out_grad * gain_second)
    second_low = second_grad.astype(BF16)
    outer_weight_part = left_product(active_low, second_low).astype(BF16)
    outer_bias_part = column_sums(second_low)
    (hidden_grad,) = gelu_back(right_product(second_low, full_outer))
    hidden_low = hidden_grad.astype(BF16)
    inner_weight_part = left_product(normed_low, hidden_low).astype(BF16)
    inner_bias_part = column_sums(hidden_low)
    normed_grad = second_grad + right_product(hidden_low, full_inner)
    first_gain_part = jnp.sum(normed_grad * first_unit, axis=0)
    first_shift_part = jnp.sum(normed_grad, axis=0)
    first_grad = norm_back(first_unit, first_rate, normed_grad * gain_first)
    branch_low = first_grad.astype(BF16)
    output_weight_part = left_product(context, branch_low).astype(BF16)
    output_bias_part = column_sums(branch_low)
    context_grad = right_product(branch_low, full_output).astype(BF16)
    qkv_grad = backward(saved, context_grad)
    qkv_weight_part = left_product(flat_rows, qkv_grad).astype(BF16)
    query_bias_part = column_sums(qkv_grad[:, :width])
    value_bias_part = column_sums(qkv_grad[:, 2 * width :])
    input_grad = first_grad + right_product(qkv_grad, full_qkv)
    vector_parts = (
        query_bias_part,
        value_bias_part,
        output_bias_part,
        first_gain_part,
        first_shift_part,
        inner_bias_part,
        outer_bias_part,
        second_gain_part,
        second_shift_part,
    )
    packed_parts = jnp.concatenate([part.reshape(shards, -1) for part in vector_parts], axis=1)
    return (
        output,
        input_grad,
        packed_parts,
        (qkv_weight_part, output_weight_part, inner_weight_part, outer_weight_part),
    )


def native_body(inputs, cotangent, lengths, vectors, weights):
    widths = [member.shape[0] for member in vectors]
    packed = lax.all_gather(jnp.concatenate(vectors), "fsdp", axis=0, tiled=False)
    joined = (jnp.concatenate(weights[:3], axis=1),) + weights[3:]
    full = tuple(gather_rows(part) for part in joined)
    micro, seqs, block_len, width = inputs.shape
    heads = width // HEAD_DIM
    total_slots = block_len * lax.axis_size("ctx")
    group = micro * seqs
    rows = group * block_len
    flat_len = lengths.reshape(group)
    local_pos = lax.axis_index("ctx") * block_len + jnp.arange(block_len, dtype=jnp.int32)
    row_mask = (local_pos[None, :] < flat_len[:, None]).astype(F32).reshape(rows, 1)
    key_valid = jnp.arange(total_slots, dtype=jnp.int32)[None, :] < flat_len[:, None]

    def forward(qkv):
        queries = qkv[:, :width].reshape(group, block_len, width)
        keys_values = lax.all_gather(
            qkv[:, width:].reshape(group, block_len, 2 * width), "ctx", axis=1, tiled=True
        )
        keys, values = keys_values[:, :, :width], keys_values[:, :, width:]
        context, probs = native_forward(queries, keys, values, key_valid, heads)
        return context.reshape(rows, width), (queries, keys, values, probs)

    def backward(saved, context_grad):
        query_grad, key_part, value_part = native_backward(
            *saved, context_grad.reshape(group, block_len, width), heads
        )
        keys_values_grad = lax.psum_scatter(
            jnp.concatenate((key_part, value_part), axis=2), "ctx", scatter_dimension=1, tiled=True
        )
        return jnp.concatenate(
            (query_grad.reshape(rows, width), keys_values_grad.reshape(rows, 2 * width)), axis=1
        )

    output, input_grad, packed_parts, parts = layer(
        inputs.reshape(rows, width),
        cotangent.reshape(rows, width),
        row_mask,
        packed,
        widths,
        full,
        forward,
        backward,
    )
    share = lax.psum_scatter(packed_parts, "fsdp", scatter_dimension=0, tiled=True)
    return (
        output.reshape(inputs.shape),
        input_grad.reshape(inputs.shape),
        split_columns(lax.psum(share, "ctx")[0], widths),
        tuple(split_columns(reduce_rows(parts[0]), [width] * 3))
        + tuple(reduce_rows(part) for part in parts[1:]),
    )


def direct_body(inputs, cotangent, lengths, vectors, weights):
    micro, seqs, block_len, width = inputs.shape
    shards = LINE * PAIR
    rows = 2 * block_len
    table = jnp.zeros((TABLE_ROWS, LANES), F32)
    row = 0
    for vector in vectors:
        lines = vector.shape[0] // LANES
        filled = ((row, TABLE_ROWS - row - lines), (0, 0))
        table += jnp.pad(vector.astype(F32).reshape(lines, LANES), filled)
        row += lines
    query_weight, key_weight, value_weight, output_weight, inner_weight, outer_weight = weights
    blocks = (inputs.reshape(micro, block_len, width), cotangent.reshape(micro, block_len, width))
    shard_rows, hidden = inner_weight.shape
    flows = [Flow(0, TABLE_ROWS, lambda core, side: (0, TABLE_ROWS, 0, LANES), cores=False)]
    flows += column_flows(1, shard_rows, 3 * width, *GATHER_SPLIT[0])
    flows += column_flows(2, shard_rows, width, *GATHER_SPLIT[1])
    flows += column_flows(3, shard_rows, hidden, *GATHER_SPLIT[2])
    flows += row_flows(4, hidden // shards, width, *GATHER_SPLIT[3])
    (
        tables,
        full_qkv,
        full_output,
        full_inner,
        full_outer,
        in_rows,
        cot_rows,
        qkv,
        context,
        probs,
        away,
    ) = start(
        (table.astype(BF16),) + weights,
        ((0, 0), (1, 0), (1, width), (1, 2 * width), (2, 0), (3, 0), (4, 0)),
        blocks,
        lengths,
        flows,
        shards,
        1,
        GATHER_ORDER,
    )
    in_rows = in_rows.reshape(rows, width)
    cot_rows = cot_rows.reshape(rows, width)
    output, first_grad, context_grad, table_grad, output_part, inner_part, outer_part = middle(
        in_rows, context, cot_rows, lengths, tables, full_output, full_inner, full_outer
    )
    sums = finish(
        in_rows,
        (qkv, away, probs),
        context_grad,
        first_grad,
        table_grad,
        full_qkv,
        (inner_part, outer_part, output_part),
        output.reshape(micro, block_len, width),
        [
            column_part(shard_rows, hidden, *REDUCE_SPLIT[0]),
            row_part(hidden // shards, width, *REDUCE_SPLIT[1]),
            column_part(shard_rows, width, *REDUCE_SPLIT[2]),
            column_part(shard_rows, 3 * width, *REDUCE_SPLIT[3], inside=True),
            vector_part(TABLE_ROWS, LANES, inside=True),
        ],
        2,
        REDUCE_ORDER,
    )
    inner_share, outer_share, output_share, qkv_share, table_share, outs, grads = sums
    lines = tuple(vector.shape[0] // LANES for vector in vectors)
    wide = widen(
        (qkv_share, output_share, inner_share, outer_share, grads, outs),
        (3, 1, 1, 1, 1, 1),
        (F32,) * 5 + (BF16,),
        table_share,
        lines,
    )
    return (
        wide[7].reshape(inputs.shape),
        wide[6].reshape(inputs.shape),
        tuple(wide[8:]),
        tuple(wide[:6]),
    )


def body(
    inputs,
    cotangent,
    lengths,
    query_weight,
    key_weight,
    value_weight,
    output_weight,
    query_bias,
    value_bias,
    output_bias,
    first_gain,
    first_shift,
    inner_weight,
    inner_bias,
    outer_weight,
    outer_bias,
    second_gain,
    second_shift,
):
    vectors = (
        query_bias,
        value_bias,
        output_bias,
        first_gain,
        first_shift,
        inner_bias,
        outer_bias,
        second_gain,
        second_shift,
    )
    widths = [member.shape[0] for member in vectors]
    weights = (
        query_weight,
        key_weight,
        value_weight,
        output_weight,
        inner_weight,
        outer_weight,
    )
    laid_out = lax.axis_size("fsdp") == LINE * PAIR and lax.axis_size("ctx") == 4
    whole_lines = all(extent % LANES == 0 for extent in widths)
    direct = laid_out and inputs.shape[:2] == (2, 1) and whole_lines
    run = direct_body if direct else native_body
    output, input_grad, shares, weight_shares = run(inputs, cotangent, lengths, vectors, weights)
    query_share, key_share, value_share, output_share, inner_share, outer_share = weight_shares
    return (
        output,
        input_grad,
        query_share,
        key_share,
        value_share,
        output_share,
        shares[0],
        shares[1],
        shares[2],
        shares[3],
        shares[4],
        inner_share,
        shares[5],
        outer_share,
        shares[6],
        shares[7],
        shares[8],
    )


def solution(mesh):
    data = P(None, "fsdp", "ctx", None)
    matrix = P("fsdp", None)
    vector = P("fsdp")
    return jax.shard_map(
        body,
        mesh=mesh,
        in_specs=(data, data, P(None, "fsdp"))
        + (matrix,) * 4
        + (vector,) * 5
        + (matrix, vector, matrix, vector, vector, vector),
        out_specs=(data, data)
        + (matrix,) * 4
        + (vector,) * 5
        + (matrix, vector, matrix, vector, vector, vector),
        check_vma=False,
    )
```

```python
import functools

import jax
import jax.numpy as jnp
from jax import lax
from jax.experimental import pallas as pl
from jax.experimental.pallas import tpu as pltpu
from jax.sharding import PartitionSpec as P

HEAD_DIM = 64
EPSILON = 1e-06
F32 = jnp.float32
BF16 = jnp.bfloat16

GATHER_SPLIT = ((256, 384), (256, 128), (1024, 128), (128, 64))
REDUCE_SPLIT = ((1024, 512), (160, 0), (256, 128), (768, 256))
GATHER_ORDER = (
    3, 4, 7, 10, 0, 2, 32, 66, 1, 38, 17, 100, 8, 29, 63, 5, 68, 30, 64, 106, 35, 62, 98, 97, 168,
    72, 174, 103, 77, 69, 136, 191, 43, 34, 74, 13, 81, 96, 132, 79, 12, 28, 47, 111, 142, 134,
    15, 164, 204, 131, 153, 137, 102, 49, 145, 210, 140, 9, 165, 213, 14, 117, 208, 40, 200, 83,
    46, 76, 166, 99, 42, 31, 171, 18, 70, 78, 179, 170, 135, 221, 175, 183, 101, 217, 118, 185,
    151, 48, 65, 123, 169, 130, 199, 50, 11, 108, 36, 112, 6, 143, 218, 23, 55, 21, 86, 198, 157,
    115, 149, 216, 82, 202, 59, 209, 180, 205, 196, 110, 138, 24, 141, 148, 167, 182, 184, 144,
    152, 52, 37, 162, 150, 128, 25, 188, 197, 91, 71, 41, 133, 33, 214, 219, 154, 116, 186, 230,
    222, 22, 53, 44, 57, 67, 114, 109, 89, 73, 16, 120, 113, 201, 172, 85, 51, 215, 220, 20, 178,
    87, 211, 104, 80, 84, 158, 225, 45, 26, 181, 155, 19, 187, 75, 203, 163, 94, 192, 159, 212,
    147, 232, 233, 39, 231, 161, 206, 90, 124, 119, 223, 234, 60, 92, 121, 93, 105, 235, 146, 139,
    125, 56, 176, 236, 237, 207, 195, 226, 229, 107, 58, 95, 173, 129, 189, 126, 227, 127, 54,
    193, 238, 88, 156, 177, 160, 27, 122, 228, 194, 61, 239, 224, 190, 240,
)
REDUCE_ORDER = (
    7, 8, 10, 3, 198, 14, 68, 9, 0, 67, 200, 70, 69, 85, 86, 12, 199, 11, 201, 2, 1, 74, 28, 5,
    75, 35, 72, 15, 4, 83, 84, 89, 202, 71, 203, 77, 16, 34, 38, 29, 13, 42, 36, 100, 40, 204, 39,
    76, 90, 207, 205, 17, 18, 21, 24, 107, 22, 23, 206, 132, 135, 25, 43, 104, 87, 88, 134, 78,
    37, 133, 91, 93, 94, 6, 136, 164, 30, 165, 33, 32, 139, 45, 185, 148, 182, 208, 26, 79, 102,
    73, 31, 184, 209, 210, 44, 53, 140, 154, 47, 150, 20, 141, 181, 137, 27, 101, 41, 116, 166,
    55, 51, 19, 168, 57, 92, 143, 158, 174, 120, 156, 183, 138, 170, 189, 167, 103, 118, 188, 151,
    152, 54, 95, 155, 109, 172, 80, 81, 142, 46, 176, 186, 96, 61, 108, 149, 191, 52, 59, 122,
    159, 105, 97, 106, 48, 144, 190, 169, 49, 82, 119, 117, 56, 110, 187, 193, 145, 146, 58, 111,
    153, 124, 63, 60, 123, 121, 112, 62, 98, 192, 126, 160, 50, 157, 113, 114, 171, 125, 173, 194,
    195, 99, 64, 65, 175, 128, 127, 161, 162, 177, 178, 129, 130, 115, 196, 147, 179, 66, 131,
    163, 180, 197,
)

MESH = pl.DeviceIdType.MESH
LINE = 4
PAIR = 2


class Place:
    def __init__(self):
        self.ctx = lax.axis_index("ctx")
        self.shard = lax.axis_index("fsdp")
        self.side = lax.div(self.ctx, 2)
        self.core = lax.rem(self.ctx, 2)
        self.line = lax.div(self.shard, PAIR)
        self.pair = lax.rem(self.shard, PAIR)

    def ahead(self, way):
        return (self.ctx, self.shard + way * PAIR)

    def across(self):
        return (self.ctx, self.shard + 1 - 2 * self.pair)

    def beside(self):
        return (self.ctx + 2 - 4 * self.side, self.shard)

    def twin(self):
        return (self.ctx + 1 - 2 * self.core, self.shard)

    def has(self, way, steps):
        if steps == 0:
            return None
        return self.line >= steps if way > 0 else self.line <= LINE - 1 - steps

    def can(self, way):
        return self.line <= LINE - 2 if way > 0 else self.line >= 1

    def shard_of(self, way, steps, other):
        pair = 1 - self.pair if other else self.pair
        return (self.line - way * steps) * PAIR + pair


def when(conditions, action):
    held = [c for c in conditions if c is not None]
    if not held:
        action()
        return
    both = held[0]
    for c in held[1:]:
        both = jnp.logical_and(both, c)
    pl.when(both)(action)


def greet(place):
    barrier = pltpu.get_barrier_semaphore()
    for peer in (place.across(), place.beside(), place.twin()):
        pl.semaphore_signal(barrier, inc=1, device_id=peer, device_id_type=MESH)
    for way in (1, -1):
        when(
            [place.can(way)],
            lambda way=way: pl.semaphore_signal(
                barrier, inc=1, device_id=place.ahead(way), device_id_type=MESH
            ),
        )
    lines = jnp.minimum(place.line, 1) + jnp.minimum(LINE - 1 - place.line, 1)
    pl.semaphore_wait(barrier, 3 + lines)


class Flow:
    def __init__(self, array, shard_rows, region, order="line", sides=False, cores=True):
        self.array = array
        self.shard_rows = shard_rows
        self.region = region
        self.order = order
        self.sides = sides
        self.cores = cores

    def view(self, ref, shard, core, side):
        row, rows, column, columns = self.region(core, side)
        start = row if shard is None else shard * self.shard_rows + row
        if not isinstance(start, int):
            start = pl.multiple_of(start, 16)
        if not isinstance(column, int):
            column = pl.multiple_of(column, 128)
        return ref.at[pl.ds(start, rows), pl.ds(column, columns)]


def positions(order):
    found = []
    if order == "line":
        found.append(("P", 1, 0, True))
        for steps in range(1, LINE):
            for way in (1, -1):
                found.append(("L", way, steps, False))
                found.append(("P", way, steps, True))
    else:
        found.append(("P", 1, 0, True))
        for steps in range(1, LINE):
            for way in (1, -1):
                found.append(("L", way, steps, False))
                found.append(("L", way, steps, True))
    return found


class Labels:
    def __init__(self):
        self.numbers = {}

    def __call__(self, key):
        return self.numbers.setdefault(key, len(self.numbers))


def gather_labels(flows):
    labels = Labels()
    for number, flow in enumerate(flows):
        for spot in positions(flow.order):
            labels((number, "in") + spot)
            if flow.sides:
                labels((number, "side") + spot)
            if flow.cores:
                labels((number, "twin") + spot)
                if flow.sides:
                    labels((number, "twinside") + spot)
    return labels


class Gather:
    def __init__(self, place, flows, owns, fulls, send, recv):
        self.place, self.flows, self.owns, self.fulls = place, flows, owns, fulls
        self.send, self.recv = send, recv
        self.labels = gather_labels(flows)
        self.sent = []

    def copy(self, number, key, spot, peer, core, side, own=False):
        flow = self.flows[number]
        place = self.place
        if own:
            shard = place.shard
            source = flow.view(self.owns[flow.array], None, core, side)
        else:
            shard = place.shard_of(*spot[1:])
            source = flow.view(self.fulls[flow.array], shard, core, side)
        target = flow.view(self.fulls[flow.array], shard, core, side)
        label = self.labels((number,) + key)
        return pltpu.make_async_remote_copy(
            source,
            target,
            self.send.at[label],
            self.recv.at[label],
            device_id=peer,
            device_id_type=MESH,
        )

    def start(self, conditions, copy):
        when(conditions, copy.start)
        self.sent.append((conditions, copy))

    def begin(self, number):
        flow, place = self.flows[number], self.place
        core, side = place.core, place.side
        here = (None, 1, 0, False)
        for way in (1, -1):
            self.start(
                [place.can(way)],
                self.copy(
                    number, ("in", "L", way, 1, False), here, place.ahead(way), core, side, True
                ),
            )
        self.start(
            [],
            self.copy(number, ("in", "P", 1, 0, True), here, place.across(), core, side, True),
        )

    def arrive(self, number, spot):
        flow, place = self.flows[number], self.place
        kind, way, steps, other = spot
        core, side = place.core, place.side
        there = place.has(way, steps)

        def take():
            self.copy(number, ("in",) + spot, spot, place.across(), core, side).wait_recv()

        when([there], take)

        def onward(extra, key, peer):
            self.start(
                [c for c in (there, extra) if c is not None],
                self.copy(number, key, spot, peer, core, side),
            )

        if kind == "L" and steps + 1 < LINE:
            onward(place.can(way), ("in", "L", way, steps + 1, other), place.ahead(way))
        if kind == "L" and flow.order == "line":
            onward(None, ("in", "P", way, steps, True), place.across())
        if kind == "P" and flow.order == "pair":
            for direction in (1, -1):
                onward(
                    place.can(direction), ("in", "L", direction, 1, True), place.ahead(direction)
                )
        if flow.sides:
            onward(None, ("side",) + spot, place.beside())
        if flow.cores:
            onward(None, ("twin",) + spot, place.twin())

    def arrive_side(self, number, spot):
        flow, place = self.flows[number], self.place
        there = place.has(*spot[1:3])
        core, side = place.core, 1 - place.side
        when(
            [there],
            lambda: self.copy(
                number, ("side",) + spot, spot, place.beside(), core, side
            ).wait_recv(),
        )
        if flow.cores:
            self.start(
                [there] if there is not None else [],
                self.copy(number, ("twinside",) + spot, spot, place.twin(), core, side),
            )

    def arrive_twin(self, number, spot):
        flow, place = self.flows[number], self.place
        there = place.has(*spot[1:3])
        core = 1 - place.core
        if flow.cores:
            when(
                [there],
                lambda: self.copy(
                    number, ("twin",) + spot, spot, place.twin(), core, place.side
                ).wait_recv(),
            )
            if flow.sides:
                when(
                    [there],
                    lambda: self.copy(
                        number, ("twinside",) + spot, spot, place.twin(), core, 1 - place.side
                    ).wait_recv(),
                )

    def actions(self):
        found = []
        for n, flow in enumerate(self.flows):
            found.append((("begin", n), lambda n=n: self.begin(n)))
        for index in range(len(positions("line"))):
            for n, flow in enumerate(self.flows):
                spot = positions(flow.order)[index]
                found.append((("in", n, spot), lambda n=n, spot=spot: self.arrive(n, spot)))
                if flow.sides:
                    found.append(
                        (("side", n, spot), lambda n=n, spot=spot: self.arrive_side(n, spot))
                    )
        return found

    def wait_twins(self, arrays):
        for number, flow in enumerate(self.flows):
            if flow.array in arrays:
                for spot in positions(flow.order):
                    self.arrive_twin(number, spot)

    def finish(self, arrays):
        self.wait_twins(arrays)
        for conditions, copy in self.sent:
            when(conditions, copy.wait_send)


class Swap:
    def __init__(self, place, ins, outs, send, recv, local):
        side = place.side
        self.away = [
            pltpu.make_async_remote_copy(
                here.at[1 - side],
                there.at[side],
                send.at[k],
                recv.at[k],
                device_id=place.beside(),
                device_id_type=MESH,
            )
            for k, (here, there) in enumerate(zip(ins, outs))
        ]
        self.stay = [
            pltpu.make_async_copy(here.at[side], there.at[side], local.at[k])
            for k, (here, there) in enumerate(zip(ins, outs))
        ]

    def start(self):
        for copy in self.away + self.stay:
            copy.start()

    def finish(self):
        for copy in self.away + self.stay:
            copy.wait()


def swap_scratch(count):
    return [pltpu.SemaphoreType.DMA((count,))] * 3


def column_flows(array, shard_rows, columns, shared, early):
    half = columns // 2
    part = (half - shared) // 2
    flows = []
    if shared:
        flows.append(
            Flow(array, shard_rows, lambda core, side: (0, shard_rows, core * half, shared))
        )
    if early:
        flows.append(
            Flow(
                array,
                shard_rows,
                lambda core, side: (0, shard_rows, core * half + shared + side * part, early),
                sides=True,
            )
        )
    if part > early:
        flows.append(
            Flow(
                array,
                shard_rows,
                lambda core, side: (
                    0,
                    shard_rows,
                    core * half + shared + side * part + early,
                    part - early,
                ),
                order="pair",
                sides=True,
            )
        )
    return flows


def row_flows(array, shard_rows, columns, shared, early):
    half = shard_rows // 2
    part = (half - shared) // 2
    flows = [
        Flow(array, shard_rows, lambda core, side: (core * half, shared, 0, columns)),
        Flow(
            array,
            shard_rows,
            lambda core, side: (core * half + shared + side * part, early, 0, columns),
            sides=True,
        ),
        Flow(
            array,
            shard_rows,
            lambda core, side: (core * half + shared + side * part + early, part - early, 0, columns),
            order="pair",
            sides=True,
        ),
    ]
    return [flow for flow in flows if flow.region(0, 0)[1]]


class Part:
    def __init__(self, rows, columns, along, flows, dtype=BF16, inside=False):
        self.rows, self.columns, self.along, self.dtype = rows, columns, along, dtype
        self.inside = inside
        self.flows = flows
        self.half_rows = rows // 2 if along == "rows" else rows
        self.half_columns = columns // 2 if along == "columns" else columns

    def half(self, ref, shard, core):
        base = 0 if shard is None else pl.multiple_of(shard * self.rows, 16)
        if self.along == "rows":
            row = core * self.half_rows + (0 if shard is None else shard * self.rows)
            return ref.at[pl.ds(pl.multiple_of(row, 16), self.half_rows), :]
        if self.along == "columns":
            column = pl.multiple_of(core * self.half_columns, 128)
            return ref.at[pl.ds(base, self.rows), pl.ds(column, self.half_columns)]
        return ref.at[pl.ds(base, self.rows), :]

    def inner(self, flow, side):
        first, extent = flow[0](side), flow[1]
        if self.along == "rows":
            start = first if isinstance(first, int) else pl.multiple_of(first, 16)
            return pl.ds(start, extent), slice(None)
        start = first if isinstance(first, int) else pl.multiple_of(first, 128)
        return slice(None), pl.ds(start, extent)

    def outer(self, flow, core, side):
        first, extent = flow[0](side), flow[1]
        if self.along == "rows":
            return pl.ds(pl.multiple_of(core * self.half_rows + first, 16), extent), slice(None)
        if self.along == "columns":
            return slice(None), pl.ds(
                pl.multiple_of(core * self.half_columns + first, 128), extent
            )
        return slice(None), slice(None)

    def extent(self, flow):
        if self.along == "rows":
            return flow[1], self.half_columns
        return self.half_rows, flow[1]


SPOTS = [(1, 3), (-1, 3), (1, 2), (-1, 2), (1, 1), (-1, 1), (1, 0)]


def reduce_scratch(parts):
    shapes = []
    for part in parts:
        half = (LINE * PAIR, part.half_rows, part.half_columns)
        shapes.append(pltpu.VMEM(half, part.dtype))
        shapes.append(pltpu.VMEM(half if part.along else half[1:], part.dtype))
        for flow in part.flows:
            rows, columns = part.extent(flow)
            shapes.append(
                pltpu.VMEM((LINE * PAIR if flow[3] else 1, rows, columns), part.dtype)
            )
            shapes.append(
                pltpu.VMEM((LINE if flow[2] == "line" else 1, rows, columns), part.dtype)
            )
            shapes.append(
                pltpu.VMEM(
                    ((LINE + 1) * (1 if flow[2] == "line" else PAIR), rows, columns), part.dtype
                )
            )
    return shapes


def reduce_labels(parts):
    labels = Labels()
    for n, part in enumerate(parts):
        for way, steps in SPOTS:
            for other in (False, True):
                labels((n, "twin", way, steps, other))
        labels((n, "twinend"))
        for k, flow in enumerate(part.flows):
            for way, steps in SPOTS:
                for other in (False, True):
                    if flow[3]:
                        labels((n, k, "side", way, steps, other))
                    if flow[2] == "pair" or not other:
                        labels((n, k, "line", way, steps, other))
                        if steps == 0:
                            labels((n, k, "line", -way, steps, other))
                if flow[2] == "line" or steps == 0:
                    labels((n, k, "pair", way, steps))
            labels((n, k, "sideend"))
            labels((n, k, "twinend"))
            labels((n, k, "twinsideend"))
    return labels


class Reduce:
    def __init__(self, place, parts, grads, outs, scratch, send, recv, load):
        self.place, self.parts, self.grads, self.outs = place, parts, grads, outs
        self.send, self.recv, self.load = send, recv, load
        self.labels = reduce_labels(parts)
        self.sent = []
        self.own, self.other, self.lanes = [], [], []
        at = 0
        for part in parts:
            self.own.append(scratch[at])
            self.other.append(scratch[at + 1])
            at += 2
            lanes = []
            for _ in part.flows:
                lanes.append(scratch[at : at + 3])
                at += 3
            self.lanes.append(lanes)

    def copy(self, source, target, key, peer):
        label = self.labels(key)
        return pltpu.make_async_remote_copy(
            source,
            target,
            self.send.at[label],
            self.recv.at[label],
            device_id=peer,
            device_id_type=MESH,
        )

    def start(self, conditions, copy):
        when(conditions, copy.start)
        self.sent.append((conditions, copy))

    def there(self, spot):
        return self.place.has(-spot[0], spot[1])

    def shard(self, spot, other):
        return self.place.shard_of(-spot[0], spot[1], other)

    def keep(self, n, spot, other):
        shard = self.shard(spot, other)
        label = SPOTS.index(spot) * 2 + int(other)
        return pltpu.make_async_copy(
            self.parts[n].half(self.grads[n], shard, self.place.core),
            self.own[n].at[shard],
            self.load.at[n * 2 * len(SPOTS) + label],
        )

    def twin(self, n, spot, other, core):
        shard = self.shard(spot, other)
        part = self.parts[n]
        return self.copy(
            self.grads[n].at[shard] if part.inside else part.half(self.grads[n], shard, core),
            self.other[n].at[shard],
            (n, "twin") + spot + (other,),
            self.place.twin(),
        )

    def begin(self, n, spot):
        there = self.there(spot)
        for other in (True, False):
            if not self.parts[n].inside:
                when([there], self.keep(n, spot, other).start)
            if self.parts[n].along:
                self.start([there], self.twin(n, spot, other, 1 - self.place.core))

    def piece(self, n, k, shard, side):
        part = self.parts[n]
        rows, columns = part.inner(part.flows[k], side)
        return self.own[n].at[shard, rows, columns]

    def side_copy(self, n, k, spot, other, side):
        shard = self.shard(spot, other)
        return self.copy(
            self.piece(n, k, shard, side),
            self.lanes[n][k][0].at[shard],
            (n, k, "side") + spot + (other,),
            self.place.beside(),
        )

    def add_cores(self, n, spot):
        there = self.there(spot)
        part = self.parts[n]
        for other in (True, False):

            def add(other=other):
                shard = self.shard(spot, other)
                if not part.inside:
                    self.keep(n, spot, other).wait()
                if part.along:
                    self.twin(n, spot, other, self.place.core).wait_recv()
                    self.own[n][shard] = self.own[n][shard] + self.other[n][shard]

            when([there], add)
        for other in (True, False):
            for k, flow in enumerate(part.flows):
                if flow[3]:
                    self.start([there], self.side_copy(n, k, spot, other, 1 - self.place.side))
                elif other:
                    self.start([there], self.pair_copy(n, k, spot, self.shard(spot, True)))

    def pair_copy(self, n, k, spot, shard):
        flow = self.parts[n].flows[k]
        slot = self.place.line + spot[0] * spot[1] if flow[2] == "line" else 0
        return self.copy(
            self.piece(n, k, shard, self.place.side),
            self.lanes[n][k][1].at[slot],
            (n, k, "pair") + spot,
            self.place.across(),
        )

    def add_sides(self, n, k, spot):
        there = self.there(spot)
        side = self.place.side
        for other in (True, False):

            def add(other=other):
                shard = self.shard(spot, other)
                self.side_copy(n, k, spot, other, side).wait_recv()
                piece = self.piece(n, k, shard, side)
                piece[...] = piece[...] + self.lanes[n][k][0][shard]

            when([there], add)
        if self.parts[n].flows[k][2] == "line":
            self.start([there], self.pair_copy(n, k, spot, self.shard(spot, True)))

    def line_slot(self, flow, way, steps, other, line):
        slot = line if (steps > 0 or way > 0) else LINE
        return slot + (LINE + 1) * int(other) if flow[2] == "pair" else slot

    def line_copy(self, n, k, spot, other, arriving):
        flow = self.parts[n].flows[k]
        way, steps = spot
        shard = self.shard(spot, other)
        line = self.place.line + way * steps
        left = steps if arriving else steps - 1
        return self.copy(
            self.piece(n, k, shard, self.place.side),
            self.lanes[n][k][2].at[self.line_slot(flow, way, left, other, line)],
            (n, k, "line", way, left, other),
            self.place.ahead(way),
        )

    def add_line(self, n, k, spot):
        place = self.place
        there = self.there(spot)
        way, steps = spot
        side = place.side
        flow = self.parts[n].flows[k]
        if flow[2] == "line":

            def add():
                shard = self.shard(spot, False)
                self.pair_copy(n, k, spot, shard).wait_recv()
                piece = self.piece(n, k, shard, side)
                piece[...] = piece[...] + self.lanes[n][k][1][place.line + way * steps]

            when([there], add)
        for other in (True, False) if flow[2] == "pair" else (False,):
            for direction in (1, -1) if steps == 0 else (way,):

                def add_line(other=other, here=(direction, steps)):
                    self.line_copy(n, k, here, other, True).wait_recv()
                    piece = self.piece(n, k, self.shard(here, other), side)
                    line = place.line + here[0] * here[1]
                    slot = self.line_slot(flow, here[0], here[1], other, line)
                    piece[...] = piece[...] + self.lanes[n][k][2][slot]

                when([there, place.can(-direction)], add_line)
            if steps > 0:
                self.start([there], self.line_copy(n, k, spot, other, False))

    def send_pair(self, n, k):
        self.start([], self.pair_copy(n, k, (1, 0), self.shard((1, 0), True)))

    def send_swap(self, n, k):
        self.start([], self.swap(n, k))

    def settle(self, n, k):
        place = self.place
        core, side, here = place.core, place.side, place.shard
        part = self.parts[n]
        flow = part.flows[k]
        piece = self.piece(n, k, here, side)
        out = self.out_view(n, k, core, side)
        if flow[3]:
            if flow[2] == "pair":
                self.pair_copy(n, k, (1, 0), here).wait_recv()
                out[...] = piece[...] + self.lanes[n][k][1][0]
            else:
                out[...] = piece[...]
            self.start([], self.out_copy(n, k, "sideend", place.beside(), core, side))
        else:
            self.swap(n, k).wait_recv()
            out[...] = piece[...] + self.lanes[n][k][0][0]
        if part.along:
            self.start([], self.out_copy(n, k, "twinend", place.twin(), core, side))
        else:
            self.start([], self.whole(n, k))

    def settle_side(self, n, k):
        place = self.place
        core, side = place.core, 1 - place.side
        self.out_copy(n, k, "sideend", place.beside(), core, side).wait_recv()
        self.start([], self.out_copy(n, k, "twinsideend", place.twin(), core, side))

    def swap(self, n, k):
        return self.copy(
            self.piece(n, k, self.place.shard, self.place.side),
            self.lanes[n][k][0].at[0],
            (n, k, "sideend"),
            self.place.beside(),
        )

    def out_view(self, n, k, core, side):
        part = self.parts[n]
        rows, columns = part.outer(part.flows[k], core, side)
        return self.outs[n].at[rows, columns]

    def out_copy(self, n, k, key, peer, core, side):
        view = self.out_view(n, k, core, side)
        return self.copy(view, view, (n, k, key), peer)

    def last(self):
        place = self.place
        core, side = place.core, place.side
        everything = [(n, k) for n, part in enumerate(self.parts) for k in range(len(part.flows))]
        for n, k in everything:
            if self.parts[n].along:
                self.out_copy(n, k, "twinend", place.twin(), 1 - core, side).wait_recv()
                if self.parts[n].flows[k][3]:
                    self.out_copy(
                        n, k, "twinsideend", place.twin(), 1 - core, 1 - side
                    ).wait_recv()
            else:
                self.whole(n, k).wait_recv()
        for conditions, copy in self.sent:
            when(conditions, copy.wait_send)
        for n, k in everything:
            if not self.parts[n].along:
                view = self.out_view(n, k, core, side)
                view[...] = view[...] + self.other[n][...]

    def whole(self, n, k):
        return self.copy(
            self.out_view(n, k, self.place.core, self.place.side),
            self.other[n],
            (n, k, "twinend"),
            self.place.twin(),
        )

    def actions(self):
        found = []
        for n, part in enumerate(self.parts):
            for spot in SPOTS:
                found.append((("begin", n, spot), lambda n=n, s=spot: self.begin(n, s)))
        for n, part in enumerate(self.parts):
            for spot in SPOTS:
                found.append((("cores", n, spot), lambda n=n, s=spot: self.add_cores(n, s)))
            for k, flow in enumerate(part.flows):
                at = (n, k)
                for spot in SPOTS:
                    if flow[3]:
                        found.append(
                            (("sides", n, k, spot), lambda at=at, s=spot: self.add_sides(*at, s))
                        )
                    found.append(
                        (("line", n, k, spot), lambda at=at, s=spot: self.add_line(*at, s))
                    )
                if flow[2] == "pair":
                    found.append((("pair", n, k), lambda at=at: self.send_pair(*at)))
                if not flow[3]:
                    found.append((("swap", n, k), lambda at=at: self.send_swap(*at)))
                found.append((("settle", n, k), lambda at=at: self.settle(*at)))
                if flow[3]:
                    found.append((("after", n, k), lambda at=at: self.settle_side(*at)))
        found.append((("last",), self.last))
        return found


def in_order(actions, order):
    if order is None:
        return [action for _, action in actions]
    assert sorted(order) == list(range(len(actions)))
    return [actions[i][1] for i in order]


def column_part(rows, columns, shared, early, inside=False):
    half = columns // 2
    part = (half - shared) // 2
    flows = []
    if shared:
        flows.append((lambda side: 0, shared, "line", False))
    if early:
        flows.append((lambda side: shared + side * part, early, "line", True))
    if part > early:
        flows.append((lambda side: shared + side * part + early, part - early, "pair", True))
    return Part(rows, columns, "columns", flows, inside=inside)


def row_part(rows, columns, shared, early):
    half = rows // 2
    part = (half - shared) // 2
    flows = [
        (lambda side: 0, shared, "line", False),
        (lambda side: shared + side * part, early, "line", True),
        (lambda side: shared + side * part + early, part - early, "pair", True),
    ]
    return Part(rows, columns, "rows", [flow for flow in flows if flow[1]])


def vector_part(rows, columns, inside=False):
    return Part(rows, columns, None, [(lambda side: 0, columns, "line", False)], F32, inside)


ROW_QUERY, ROW_VALUE, ROW_OUTPUT, ROW_GAIN1, ROW_SHIFT1, ROW_INNER, INNER = 0, 1, 2, 3, 4, 5, 4
ROW_OUTER, ROW_GAIN2, ROW_SHIFT2 = 9, 10, 11
TABLE_ROWS = 16
VMEM = 67043328
LANES = 128
BAND = 128


def spread_table(table_ref, vec):
    for shard in range(table_ref.shape[0] // TABLE_ROWS):
        vec[:, pl.ds(shard * LANES, LANES)] = table_ref[
            pl.ds(shard * TABLE_ROWS, TABLE_ROWS), :
        ].astype(F32)


def fold_table(vec, table_ref, first, count):
    for shard in range(table_ref.shape[0] // TABLE_ROWS):
        table_ref[pl.ds(shard * TABLE_ROWS + first, count), :] = vec[
            pl.ds(first, count), pl.ds(shard * LANES, LANES)
        ]


def row_place(row, core, rows):
    half = rows // 2
    return jnp.where(row < half, row, row + half) + core * half


def total_rows(block):
    return jnp.sum(block.astype(F32), axis=0, keepdims=True)


def middle_kernel(
    rows_far,
    context_far,
    cot_far,
    lengths_ref,
    table_ref,
    output_w,
    inner_w,
    outer_w,
    out_far,
    first_grad_far,
    context_grad_far,
    sums_ref,
    output_far,
    inner_g,
    outer_g,
    rows_ref,
    context_ref,
    cot_ref,
    out_ref,
    first_grad_ref,
    context_grad_ref,
    output_g,
    output_v,
    inner_v,
    outer_v,
    vec,
    sums,
    active,
    slope,
    unit1,
    rate1,
    total,
    low,
    low_t,
    second,
    second_low,
    inner_b,
    outer_b,
    load,
    save,
    few,
):
    rows, width = rows_ref.shape
    tiles, _, tile = inner_v.shape
    ctx = lax.axis_index("ctx")
    side, core = lax.div(ctx, 2), lax.rem(ctx, 2)
    length = lengths_ref[side]
    bands = rows // BAND

    def inner_load(t):
        return pltpu.make_async_copy(
            inner_w.at[:, pl.ds(pl.multiple_of(t * tile, tile), tile)], inner_v.at[t], load.at[0, t]
        )

    def outer_load(t):
        return pltpu.make_async_copy(
            outer_w.at[pl.ds(pl.multiple_of(t * tile, tile), tile), :], outer_v.at[t], load.at[1, t]
        )

    output_load = pltpu.make_async_copy(output_w, output_v, few.at[0])
    context_load = pltpu.make_async_copy(context_far, context_ref, few.at[1])
    rows_load = pltpu.make_async_copy(rows_far, rows_ref, few.at[2])
    cot_load = pltpu.make_async_copy(cot_far, cot_ref, few.at[3])
    out_save = pltpu.make_async_copy(out_ref, out_far, few.at[4])
    first_save = pltpu.make_async_copy(first_grad_ref, first_grad_far, few.at[5])
    context_save = pltpu.make_async_copy(context_grad_ref, context_grad_far, few.at[6])
    output_save = pltpu.make_async_copy(output_g, output_far, few.at[7])
    for copy in (context_load, output_load, rows_load):
        copy.start()
    spread_table(table_ref, vec)
    sums[...] = jnp.zeros_like(sums)
    context_load.wait()
    output_load.wait()
    ahead = 3
    for t in range(ahead):
        inner_load(t).start()
        outer_load(t).start()
    total[...] = plain_product(context_ref[...], output_v[...])
    rows_load.wait()

    def band_of(b):
        return pl.ds(pl.multiple_of(b * BAND, BAND), BAND)

    def first_norm(b, carry):
        here = band_of(b)
        first_sum = (
            rows_ref[here, :].astype(F32) + total[here, :] + vec[pl.ds(ROW_OUTPUT, 1), :]
        )
        unit, rate = norm_parts(first_sum)
        unit1[here, :] = unit
        rate1[here, :] = jnp.broadcast_to(rate, (BAND, LANES))
        normed = unit * vec[pl.ds(ROW_GAIN1, 1), :] + vec[pl.ds(ROW_SHIFT1, 1), :]
        low[here, :] = normed.astype(BF16)
        total[here, :] = normed + vec[pl.ds(ROW_OUTER, 1), :]
        return carry

    lax.fori_loop(0, bands, first_norm, 0)
    low_t[...] = low[...].T

    cot_load.start()

    def forward(t, carry):
        inner_load(t).wait()

        @pl.when(t + ahead < tiles)
        def _():
            inner_load(t + ahead).start()
            outer_load(t + ahead).start()

        bias = jnp.concatenate(
            [
                vec[pl.ds(ROW_INNER + k, 1), pl.ds(pl.multiple_of(t * LANES, LANES), LANES)]
                for k in range(INNER)
            ],
            axis=1,
        )
        hidden = plain_product(low[...], inner_v[t]) + bias
        share = 0.5 + 0.5 * lax.erf(hidden * 0.7071067811865476)
        active[t] = (hidden * share).astype(BF16)
        slope[t] = share + hidden * (jnp.exp(-0.5 * hidden * hidden) * 0.3989422804014327)
        outer_load(t).wait()
        total[...] += plain_product(active[t], outer_v[t])
        return carry

    lax.fori_loop(0, tiles, forward, 0)

    cot_load.wait()

    def second_norm(b, carry):
        here = band_of(b)
        unit, rate = norm_parts(total[here, :])
        row = b * BAND + lax.broadcasted_iota(jnp.int32, (BAND, width), 0)
        mask = (row_place(row, core, rows) < length).astype(F32)
        gain = vec[pl.ds(ROW_GAIN2, 1), :]
        out_ref[here, :] = ((unit * gain + vec[pl.ds(ROW_SHIFT2, 1), :]) * mask).astype(BF16)
        out_grad = cot_ref[here, :].astype(F32) * mask
        grad = norm_back(unit, rate, out_grad * gain)
        second[here, :] = grad
        grad_low = grad.astype(BF16)
        second_low[here, :] = grad_low
        sums[pl.ds(ROW_GAIN2, 1), :] += total_rows(out_grad * unit)
        sums[pl.ds(ROW_SHIFT2, 1), :] += total_rows(out_grad)
        sums[pl.ds(ROW_OUTER, 1), :] += total_rows(grad_low)
        return carry

    lax.fori_loop(0, bands, second_norm, 0)
    out_save.start()

    def inner_save(t):
        slot = lax.rem(t, 2)
        return pltpu.make_async_copy(
            inner_b.at[slot],
            inner_g.at[:, pl.ds(pl.multiple_of(t * tile, tile), tile)],
            save.at[0, slot],
        )

    def outer_save(t):
        slot = lax.rem(t, 2)
        return pltpu.make_async_copy(
            outer_b.at[slot],
            outer_g.at[pl.ds(pl.multiple_of(t * tile, tile), tile), :],
            save.at[1, slot],
        )

    def backward(t, carry):
        slot = lax.rem(t, 2)
        hidden_grad = (right_product(second_low[...], outer_v[t]) * slope[t]).astype(BF16)
        summed = total_rows(hidden_grad)
        for k in range(INNER):
            sums[
                pl.ds(ROW_INNER + k, 1), pl.ds(pl.multiple_of(t * LANES, LANES), LANES)
            ] = summed[:, k * LANES : (k + 1) * LANES]

        @pl.when(t >= 2)
        def _():
            outer_save(t - 2).wait()
            inner_save(t - 2).wait()

        outer_b[slot] = left_product(active[t], second_low[...]).astype(BF16)
        inner_b[slot] = plain_product(low_t[...], hidden_grad).astype(BF16)
        outer_save(t).start()
        second[...] += right_product(hidden_grad, inner_v[t])
        inner_save(t).start()
        return carry

    lax.fori_loop(0, tiles, backward, 0)

    def first_back(b, carry):
        here = band_of(b)
        grad = second[here, :]
        unit = unit1[here, :]
        sums[pl.ds(ROW_GAIN1, 1), :] += total_rows(grad * unit)
        sums[pl.ds(ROW_SHIFT1, 1), :] += total_rows(grad)
        back = norm_back(unit, rate1[here, :1], grad * vec[pl.ds(ROW_GAIN1, 1), :])
        first_grad_ref[here, :] = back
        back_low = back.astype(BF16)
        second_low[here, :] = back_low
        sums[pl.ds(ROW_OUTPUT, 1), :] += total_rows(back_low)
        return carry

    lax.fori_loop(0, bands, first_back, 0)
    output_g[...] = left_product(context_ref[...], second_low[...]).astype(BF16)
    first_save.start()
    context_grad_ref[...] = right_product(second_low[...], output_v[...]).astype(BF16)
    output_save.start()
    fold_table(sums, sums_ref, 0, TABLE_ROWS)
    context_save.start()
    for t in range(tiles - 2, tiles):
        outer_save(t).wait()
        inner_save(t).wait()
    for copy in (out_save, first_save, output_save, context_save):
        copy.wait()


def middle(rows, context, cot, lengths, table, output_w, inner_w, outer_w):
    count, width = rows.shape
    hidden = inner_w.shape[1]
    tile = INNER * LANES
    tiles = hidden // tile
    whole = pl.BlockSpec(memory_space=pltpu.VMEM)
    far = pl.BlockSpec(memory_space=pltpu.HBM)

    def space(dtype):
        return pltpu.VMEM((count, width), dtype)

    return pl.pallas_call(
        middle_kernel,
        out_shape=[
            jax.ShapeDtypeStruct((count, width), BF16),
            jax.ShapeDtypeStruct((count, width), F32),
            jax.ShapeDtypeStruct((count, width), BF16),
            jax.ShapeDtypeStruct(table.shape, F32),
            jax.ShapeDtypeStruct(output_w.shape, BF16),
            jax.ShapeDtypeStruct(inner_w.shape, BF16),
            jax.ShapeDtypeStruct(outer_w.shape, BF16),
        ],
        in_specs=[far] * 3 + [pl.BlockSpec(memory_space=pltpu.SMEM), whole] + [far] * 3,
        out_specs=[far] * 3 + [whole] + [far] * 3,
        scratch_shapes=[
            space(BF16),
            space(BF16),
            space(BF16),
            space(BF16),
            space(F32),
            space(BF16),
            pltpu.VMEM(output_w.shape, BF16),
            pltpu.VMEM(output_w.shape, BF16),
            pltpu.VMEM((tiles, width, tile), BF16),
            pltpu.VMEM((tiles, tile, width), BF16),
            pltpu.VMEM((TABLE_ROWS, width), F32),
            pltpu.VMEM((TABLE_ROWS, width), F32),
            pltpu.VMEM((tiles, count, tile), BF16),
            pltpu.VMEM((tiles, count, tile), F32),
            space(F32),
            pltpu.VMEM((count, LANES), F32),
            space(F32),
            space(BF16),
            pltpu.VMEM((width, count), BF16),
            space(F32),
            space(BF16),
            pltpu.VMEM((2, width, tile), BF16),
            pltpu.VMEM((2, tile, width), BF16),
            pltpu.SemaphoreType.DMA((2, tiles)),
            pltpu.SemaphoreType.DMA((2, 2)),
            pltpu.SemaphoreType.DMA((8,)),
        ],
        compiler_params=pltpu.CompilerParams(vmem_limit_bytes=VMEM),
        name="feed_forward",
    )(rows, context, cot, lengths, table, output_w, inner_w, outer_w)


def widen_kernel(splits, lines, *refs):
    count = len(splits)
    many = sum(splits)
    ins, table, outs = refs[:count], refs[count], refs[count + 1 : count + 1 + many]
    vectors = refs[count + 1 + many : count + 1 + many + len(lines)]
    rest = refs[count + 1 + many + len(lines) :]
    narrow, held, wides = rest[:count], rest[count], rest[count + 1 : count + 1 + many]
    load, save = rest[-2:]
    loads = [
        pltpu.make_async_copy(here, there, load.at[k])
        for k, (here, there) in enumerate(zip(ins + (table,), narrow + (held,)))
    ]
    for copy in loads:
        copy.start()
    copies = []
    at = 0
    for k, parts in enumerate(splits):
        loads[k].wait()
        columns = narrow[k].shape[-1] // parts
        for part in range(parts):
            wides[at][...] = narrow[k][..., part * columns : (part + 1) * columns].astype(
                wides[at].dtype
            )
            copies.append(pltpu.make_async_copy(wides[at], outs[at], save.at[at]))
            copies[-1].start()
            at += 1
    loads[count].wait()
    row = 0
    for vector, extent in zip(vectors, lines):
        for line in range(extent):
            copies.append(
                pltpu.make_async_copy(
                    held.at[row], vector.at[pl.ds(line * LANES, LANES)], save.at[many + row]
                )
            )
            copies[-1].start()
            row += 1
    for copy in copies:
        copy.wait()


def widen(arrays, splits, types, table, lines):
    shapes = []
    for array, parts, kind in zip(arrays, splits, types):
        shape = array.shape[:-1] + (array.shape[-1] // parts,)
        shapes += [jax.ShapeDtypeStruct(shape, kind)] * parts
    far = pl.BlockSpec(memory_space=pltpu.HBM)
    return pl.pallas_call(
        functools.partial(widen_kernel, splits, lines),
        out_shape=shapes + [jax.ShapeDtypeStruct((k * LANES,), F32) for k in lines],
        in_specs=[far] * (len(arrays) + 1),
        out_specs=[far] * (len(shapes) + len(lines)),
        scratch_shapes=[pltpu.VMEM(array.shape, array.dtype) for array in arrays + (table,)]
        + [pltpu.VMEM(shape.shape, shape.dtype) for shape in shapes]
        + [
            pltpu.SemaphoreType.DMA((len(arrays) + 1,)),
            pltpu.SemaphoreType.DMA((len(shapes) + sum(lines),)),
        ],
        compiler_params=pltpu.CompilerParams(vmem_limit_bytes=VMEM),
        name="widen_results",
    )(*arrays, table)


def stack_heads(block, lower):
    zero = jnp.zeros_like(block)
    return jnp.concatenate((jnp.where(lower, block, zero), jnp.where(lower, zero, block)), axis=0)


def repeat(first, stop, action):
    def step(i, carry):
        action(i)
        return carry

    lax.fori_loop(first, stop, step, 0)


GROUPS = 4
HALVES = 2


SPAN = 2 * HEAD_DIM


def span_of(section, pair, width):
    return pl.ds(pl.multiple_of(section * width + pair * SPAN, SPAN), SPAN)


class AttentionForward:
    def __init__(self, place, rows, weight, vec, bias, qkv, context, probs, held, away, send, recv, save):
        self.place, self.rows, self.weight, self.vec, self.bias = place, rows, weight, vec, bias
        self.qkv, self.context, self.probs, self.held, self.away = qkv, context, probs, held, away
        self.send, self.recv, self.save = send, recv, save
        self.count, self.width = context.shape
        self.pairs = self.width // SPAN

    def save_probs(self, pair):
        return pltpu.make_async_copy(self.held.at[pair], self.probs.at[pair], self.save.at[pair])

    def fetch(self, which, pair):
        return pltpu.make_async_remote_copy(
            self.qkv.at[:, span_of(which + 1, pair, self.width)],
            self.away.at[:, span_of(which, pair, self.width)],
            self.send.at[which, pair],
            self.recv.at[which, pair],
            device_id=self.place.twin(),
            device_id_type=MESH,
        )

    def project(self, section):
        tile = 512
        rows = self.rows[...].reshape(self.count, self.width)

        def one(t):
            columns = pl.ds(pl.multiple_of(section * self.width + t * tile, tile), tile)
            product = plain_product(rows, self.weight[:, columns])
            if section != 1:
                row = ROW_QUERY if section == 0 else ROW_VALUE
                product = product + self.vec[
                    pl.ds(row, 1), pl.ds(pl.multiple_of(t * tile, tile), tile)
                ]
            self.qkv[:, columns] = product.astype(BF16)

        repeat(0, self.width // tile, one)

    def give(self, which):
        for pair in range(self.pairs):
            self.fetch(which, pair).start()

    def attend(self, pair):
        for which in range(2):
            self.fetch(which, pair).wait_recv()
        count = self.count
        lower = lax.broadcasted_iota(jnp.int32, (count, SPAN), 1) < HEAD_DIM

        def here(section):
            return self.qkv[:, span_of(section, pair, self.width)]

        def there(section):
            return self.away[:, span_of(section - 1, pair, self.width)]

        stacked = stack_heads(here(0) * HEAD_DIM**-0.5, lower)
        keys = jnp.concatenate((here(1), there(1)), axis=0)
        values = jnp.concatenate((here(2), there(2)), axis=0)
        scores = right_product(stacked, keys) + self.bias[:1, :]
        top = jnp.max(scores, axis=1, keepdims=True)
        weights = jnp.exp(scores - top)
        total = jnp.sum(weights, axis=1, keepdims=True)
        probs = (weights * (1.0 / total)).astype(BF16)
        self.held[pair] = probs
        self.save_probs(pair).start()
        mixed = plain_product(probs, values)
        self.context[:, span_of(0, pair, self.width)] = jnp.where(
            lower, mixed[:count], mixed[count:]
        ).astype(BF16)

    def attend_group(self, group):
        each = self.pairs // GROUPS
        repeat(group * each, (group + 1) * each, self.attend)

    def finish(self):
        for pair in range(self.pairs):
            for which in range(2):
                self.fetch(which, pair).wait_send()
            self.save_probs(pair).wait()


TABLE, QUERIES = 0, 1


def start_actions(gather, work, keep, swaps, save, table_ref):
    found = gather.actions()
    others = [k for k in range(len(keep)) if k not in (TABLE, QUERIES)]

    def ready():
        gather.wait_twins((TABLE, QUERIES))
        for k in (TABLE, QUERIES):
            keep[k].wait()
        swaps[0].finish()
        spread_table(table_ref, work.vec)
        save.start()

    def values():
        work.project(2)
        work.give(0)

    def queries():
        work.give(1)
        work.project(0)

    found.append((("ready",), ready))
    found.append((("project", 0), lambda: work.project(1)))
    found.append((("project", 1), values))
    found.append((("project", 2), queries))
    for group in range(GROUPS):
        found.append((("pa", group), lambda group=group: work.attend_group(group)))

    def last():
        gather.finish(others)
        work.finish()
        for k in others:
            keep[k].wait()
        swaps[1].finish()
        save.wait()

    found.append((("last",), last))
    return found


def start_kernel(flows, spots, order, *refs):
    count = max(array for array, _ in spots) + 1
    shares, refs = refs[: len(spots)], refs[len(spots) :]
    (in_block, cot_block, lengths_ref), refs = refs[:3], refs[3:]
    table_ref, refs = refs[0], refs[1:]
    far, refs = refs[: count - 1], refs[count - 1 :]
    rows, cots, qkv, context, probs, away = refs[:6]
    owns, refs = refs[6 : 6 + count], refs[6 + count :]
    weight, held, vec, bias = refs[:4]
    send, recv, local, load, send2, recv2, save2, saveq = refs[4:12]
    fulls = (table_ref, weight) + tuple(far[1:])
    place = Place()
    loads = [
        pltpu.make_async_copy(
            share, owns[array].at[:, pl.ds(column, share.shape[1])], load.at[k]
        )
        for k, (share, (array, column)) in enumerate(zip(shares, spots))
    ]
    for copy in loads:
        copy.start()
    keep = [
        pltpu.make_async_copy(
            own, full.at[pl.ds(pl.multiple_of(place.shard * own.shape[0], 16), own.shape[0]), :], local.at[k]
        )
        for k, (own, full) in enumerate(zip(owns, fulls))
    ]
    greet(place)
    rows_count = context.shape[0]
    length = lengths_ref[place.side]
    row = lax.broadcasted_iota(jnp.int32, (8, rows_count), 1)
    for k, core in enumerate((place.core, 1 - place.core)):
        bias[:, pl.ds(k * rows_count, rows_count)] = jnp.where(
            row_place(row, core, rows_count) < length, 0.0, -1e30
        )
    for copy in loads:
        copy.wait()
    swaps = [
        Swap(place, [in_block], [rows], *refs[12:15]),
        Swap(place, [cot_block], [cots], *refs[15:18]),
    ]
    for swap in swaps:
        swap.start()
    gather = Gather(place, flows, owns, fulls, send, recv)
    for copy in keep:
        copy.start()
    work = AttentionForward(
        place, rows, weight, vec, bias, qkv, context, probs, held, away, send2, recv2, save2
    )
    save = pltpu.make_async_copy(weight, far[0], saveq.at[0])
    for step in in_order(start_actions(gather, work, keep, swaps, save, table_ref), order):
        step()


def start(shares, spots, blocks, lengths, flows, shards, collective_id, order):
    labels = gather_labels(flows)
    count = max(array for array, _ in spots) + 1
    shapes = []
    for array in range(count):
        members = [share for share, spot in zip(shares, spots) if spot[0] == array]
        shapes.append((members[0].shape[0], sum(m.shape[1] for m in members)))
    _, block_len, width = blocks[0].shape
    rows = 2 * block_len
    pairs = width // SPAN
    far = pl.BlockSpec(memory_space=pltpu.HBM)
    whole = pl.BlockSpec(memory_space=pltpu.VMEM)
    probs_shape = (pairs, 2 * rows, 2 * rows)
    return pl.pallas_call(
        functools.partial(start_kernel, flows, spots, order),
        out_shape=[jax.ShapeDtypeStruct((shards * r, c), BF16) for r, c in shapes]
        + [jax.ShapeDtypeStruct(block.shape, BF16) for block in blocks]
        + [
            jax.ShapeDtypeStruct((rows, 3 * width), BF16),
            jax.ShapeDtypeStruct((rows, width), BF16),
            jax.ShapeDtypeStruct(probs_shape, BF16),
            jax.ShapeDtypeStruct((rows, 2 * width), BF16),
        ],
        in_specs=[far] * (len(shares) + 2) + [pl.BlockSpec(memory_space=pltpu.SMEM)],
        out_specs=[whole] + [far] * (count - 1) + [whole, far] + [whole, whole, far, whole],
        scratch_shapes=[pltpu.VMEM(shape, BF16) for shape in shapes]
        + [
            pltpu.VMEM((shards * shapes[QUERIES][0], shapes[QUERIES][1]), BF16),
            pltpu.VMEM(probs_shape, BF16),
            pltpu.VMEM((TABLE_ROWS, width), F32),
            pltpu.VMEM((8, 2 * rows), F32),
            pltpu.SemaphoreType.DMA((len(labels.numbers),)),
            pltpu.SemaphoreType.DMA((len(labels.numbers),)),
            pltpu.SemaphoreType.DMA((count,)),
            pltpu.SemaphoreType.DMA((len(shares),)),
            pltpu.SemaphoreType.DMA((2, pairs)),
            pltpu.SemaphoreType.DMA((2, pairs)),
            pltpu.SemaphoreType.DMA((pairs,)),
            pltpu.SemaphoreType.DMA((1,)),
        ]
        + swap_scratch(1) * 2,
        compiler_params=pltpu.CompilerParams(
            collective_id=collective_id, has_side_effects=True, vmem_limit_bytes=VMEM
        ),
        name="gather_attention_forward",
    )(*shares, *blocks, lengths)


class AttentionBackward:
    def __init__(self, place, qkv, away, grad, out, keep, leave, come, send, recv):
        self.place, self.qkv, self.away, self.grad = place, qkv, away, grad
        self.out, self.keep, self.leave, self.come = out, keep, leave, come
        self.send, self.recv = send, recv
        self.count, self.width = grad.shape
        self.pairs = self.width // SPAN

    def give(self, which, pair):
        return pltpu.make_async_remote_copy(
            self.leave.at[:, span_of(which, pair, self.width)],
            self.come.at[:, span_of(which, pair, self.width)],
            self.send.at[which, pair],
            self.recv.at[which, pair],
            device_id=self.place.twin(),
            device_id_type=MESH,
        )

    def attend(self, pair, probs):
        count = self.count
        lower = lax.broadcasted_iota(jnp.int32, (count, SPAN), 1) < HEAD_DIM
        scale = HEAD_DIM**-0.5

        def here(section):
            return self.qkv[:, span_of(section, pair, self.width)]

        def there(section):
            return self.away[:, span_of(section - 1, pair, self.width)]

        first = span_of(0, pair, self.width)
        second = span_of(1, pair, self.width)
        stacked = stack_heads(here(0) * scale, lower)
        keys = jnp.concatenate((here(1), there(1)), axis=0)
        values = jnp.concatenate((here(2), there(2)), axis=0)
        grad = stack_heads(self.grad[:, first], lower)
        value_part = left_product(probs, grad)
        probs_grad = right_product(grad, values)
        wide = probs.astype(F32)
        inner = jnp.sum(wide * probs_grad, axis=1, keepdims=True)
        scores_grad = (wide * (probs_grad - inner)).astype(BF16)
        key_part = left_product(scores_grad, stacked)
        self.leave[:, first] = key_part[count:].astype(BF16)
        self.leave[:, second] = value_part[count:].astype(BF16)
        self.keep[:, first] = key_part[:count]
        self.keep[:, second] = value_part[:count]
        mixed = plain_product(scores_grad, keys) * scale
        self.out[:, first] = jnp.where(lower, mixed[:count], mixed[count:]).astype(BF16)
        for which in range(2):
            self.give(which, pair).start()

    def settle(self, pair):
        for which in range(2):
            self.give(which, pair).wait_recv()
            here = span_of(which, pair, self.width)
            self.out[:, span_of(which + 1, pair, self.width)] = (
                self.keep[:, here] + self.come[:, here].astype(F32)
            ).astype(BF16)

    def finish(self):
        for pair in range(self.pairs):
            for which in range(2):
                self.give(which, pair).wait_send()


class Finish:
    def __init__(self, work, tiles, weight, rows_ref, rows_t, first_grad, total, block, sums, held, probs, load, sems):
        self.work, self.tiles, self.weight, self.rows_ref, self.rows_t = work, tiles, weight, rows_ref, rows_t
        self.total, self.block, self.sums = total, block, sums
        self.held, self.probs, self.load, self.sems = held, probs, load, sems
        self.grad_load = pltpu.make_async_copy(first_grad, total, sems.at[held.shape[0]])
        self.count, self.width = total.shape
        self.tile = tiles.shape[2]

    def weight_load(self, t):
        columns = pl.ds(pl.multiple_of(t * self.tile, self.tile), self.tile)
        slot = lax.rem(t, self.tiles.shape[0])
        return pltpu.make_async_copy(
            self.weight.at[:, columns], self.tiles.at[slot], self.load.at[slot]
        )

    def probs_load(self, pair):
        slot = lax.rem(pair, self.held.shape[0])
        return pltpu.make_async_copy(
            self.probs.at[pair], self.held.at[slot], self.sems.at[slot]
        )

    def begin(self):
        for pair in range(self.held.shape[0]):
            self.probs_load(pair).start()
        for t in range(self.tiles.shape[0]):
            self.weight_load(t).start()
        self.grad_load.start()

    def attend(self, group):
        each = self.work.pairs // GROUPS

        slots = self.held.shape[0]

        def one(pair):
            self.probs_load(pair).wait()
            self.work.attend(pair, self.held[lax.rem(pair, slots)])
            pl.when(pair + slots < self.work.pairs)(self.probs_load(pair + slots).start)

        repeat(group * each, (group + 1) * each, one)

    def settle(self):
        repeat(0, self.work.pairs, self.work.settle)

    def weigh(self, core, target):
        shards, rows, columns = target.shape
        tile = self.tile

        def one(j):
            start = pl.multiple_of(core * columns + j * tile, tile)
            product = plain_product(self.rows_t[...], self.work.out[:, pl.ds(start, tile)])
            low = product.astype(BF16)
            for shard in range(shards):
                target[shard, :, pl.ds(pl.multiple_of(j * tile, tile), tile)] = low[
                    shard * rows : (shard + 1) * rows
                ]

        repeat(0, columns // tile, one)

    def turn(self):
        self.rows_t[...] = self.rows_ref[...].T

    def bias_sums(self, target):
        self.sums[pl.ds(0, 1), :] = total_rows(self.work.out[:, : self.width])
        self.sums[pl.ds(1, 1), :] = total_rows(self.work.out[:, 2 * self.width :])
        for shard in range(target.shape[0]):
            target[shard, pl.ds(ROW_QUERY, 2), :] = self.sums[
                pl.ds(0, 2), pl.ds(shard * LANES, LANES)
            ]

    def spread(self, half):
        count = self.weight.shape[1] // self.tile
        each = count // HALVES
        slots = self.tiles.shape[0]
        if half == 0:
            self.grad_load.wait()

        def one(t):
            self.weight_load(t).wait()
            columns = pl.ds(pl.multiple_of(t * self.tile, self.tile), self.tile)
            tile = self.tiles[lax.rem(t, slots)]
            self.total[...] += right_product(self.work.out[:, columns], tile)
            pl.when(t + slots < count)(self.weight_load(t + slots).start)

        repeat(half * each, (half + 1) * each, one)
        if half == HALVES - 1:
            rows = self.block.shape[1]
            for part in range(2):
                self.block[part] = self.total[pl.ds(part * rows, rows), :].astype(BF16)


def finish_actions(reduce, finish, swaps):
    queries, vectors = 3, 4
    place = reduce.place
    found = reduce.actions()

    def load():
        finish.begin()
        finish.turn()

    found.append((("load",), load))
    found.append((("swapout",), swaps[0].start))
    for group in range(GROUPS):
        found.append((("att", group), lambda group=group: finish.attend(group)))
    found.append((("settleatt",), finish.settle))
    found.append((("leave",), lambda: finish.weigh(1 - place.core, reduce.grads[queries])))
    found.append((("own",), lambda: finish.weigh(place.core, reduce.own[queries])))
    found.append((("sums",), lambda: finish.bias_sums(reduce.own[vectors])))
    for half in range(HALVES):
        found.append((("dx", half), lambda half=half: finish.spread(half)))
    found.append((("swapin",), swaps[1].start))
    return found


def finish_kernel(parts, order, *refs):
    rows_ref, qkv, away, grad, table_ref, first_grad, probs, weight = refs[:8]
    grads, out_block = list(refs[8:11]), refs[11]
    outs, swapped, refs = refs[12:17], refs[17:19], refs[19:]
    leave_q, tiles, held, out, keep, leave, come, total, sums, rows_t, block = refs[:11]
    send2, recv2, load2, sems = refs[11:15]
    scratch, rest = refs[15:-9], refs[-9:]
    place = Place()
    work = AttentionBackward(place, qkv, away, grad, out, keep, leave, come, send2, recv2)
    finish = Finish(
        work, tiles, weight, rows_ref, rows_t, first_grad, total, block, sums, held, probs, load2, sems
    )
    reduce = Reduce(place, parts, grads + [leave_q, None], outs, scratch, *rest[:3])
    swaps = [
        Swap(place, [out_block], [swapped[0]], *rest[3:6]),
        Swap(place, [block], [swapped[1]], *rest[6:9]),
    ]
    for shard in range(LINE * PAIR):
        reduce.own[4][shard] = table_ref[pl.ds(shard * TABLE_ROWS, TABLE_ROWS), :]
    greet(place)
    for step in in_order(finish_actions(reduce, finish, swaps), order):
        step()
    work.finish()
    for swap in swaps:
        swap.finish()


def finish(rows, saved, grad, first_grad, table, weight, grads, block, parts, collective_id, order):
    qkv, away, probs = saved
    count, width = rows.shape
    pairs = width // SPAN
    tile = 512
    labels = reduce_labels(parts)
    whole = pl.BlockSpec(memory_space=pltpu.VMEM)
    far = pl.BlockSpec(memory_space=pltpu.HBM)
    queries = parts[3]
    return pl.pallas_call(
        functools.partial(finish_kernel, parts, order),
        out_shape=[jax.ShapeDtypeStruct((p.rows, p.columns), p.dtype) for p in parts]
        + [jax.ShapeDtypeStruct(block.shape, BF16)] * 2,
        in_specs=[whole] * 5 + [far] * 7,
        out_specs=[whole] * len(parts) + [far] * 2,
        scratch_shapes=[
            pltpu.VMEM((LINE * PAIR, queries.half_rows, queries.half_columns), BF16),
            pltpu.VMEM((2, width, tile), BF16),
            pltpu.VMEM((pairs // 2,) + probs.shape[1:], BF16),
            pltpu.VMEM((count, 3 * width), BF16),
            pltpu.VMEM((count, 2 * width), F32),
            pltpu.VMEM((count, 2 * width), BF16),
            pltpu.VMEM((count, 2 * width), BF16),
            pltpu.VMEM((count, width), F32),
            pltpu.VMEM((8, width), F32),
            pltpu.VMEM((width, count), BF16),
            pltpu.VMEM(block.shape, BF16),
            pltpu.SemaphoreType.DMA((2, pairs)),
            pltpu.SemaphoreType.DMA((2, pairs)),
            pltpu.SemaphoreType.DMA((2,)),
            pltpu.SemaphoreType.DMA((pairs // 2 + 1,)),
        ]
        + reduce_scratch(parts)
        + [
            pltpu.SemaphoreType.DMA((len(labels.numbers),)),
            pltpu.SemaphoreType.DMA((len(labels.numbers),)),
            pltpu.SemaphoreType.DMA((len(parts) * 2 * len(SPOTS),)),
        ]
        + swap_scratch(1) * 2,
        compiler_params=pltpu.CompilerParams(
            collective_id=collective_id, has_side_effects=True, vmem_limit_bytes=VMEM
        ),
        name="attention_backward_reduce",
    )(rows, qkv, away, grad, table, first_grad, probs, weight, *grads, block)


def exact_gelu(hidden):
    return jax.nn.gelu(hidden, approximate=False)


def plain_product(left, right):
    return jnp.dot(left, right, preferred_element_type=F32)


def left_product(left, right):
    return lax.dot_general(left, right, (((0,), (0,)), ((), ())), preferred_element_type=F32)


def right_product(left, right):
    return lax.dot_general(left, right, (((1,), (1,)), ((), ())), preferred_element_type=F32)


def column_sums(rows):
    return jnp.sum(rows.astype(F32), axis=0)


def norm_parts(total):
    average = jnp.mean(total, axis=-1, keepdims=True)
    centered = total - average
    variance = jnp.mean(centered * centered, axis=-1, keepdims=True)
    rate = lax.rsqrt(variance + EPSILON)
    return centered * rate, rate


def norm_back(unit, rate, grad):
    return rate * (
        grad
        - jnp.mean(grad, axis=-1, keepdims=True)
        - unit * jnp.mean(grad * unit, axis=-1, keepdims=True)
    )


def split_columns(packed, widths):
    pieces = []
    start = 0
    for width in widths:
        pieces.append(packed[..., start : start + width])
        start += width
    return pieces


def native_forward(queries, keys_all, values_all, key_valid, heads):
    shape = queries.shape[:2] + (heads, HEAD_DIM)
    key_shape = keys_all.shape[:2] + (heads, HEAD_DIM)
    scores = jnp.einsum(
        "sqhd,skhd->shqk",
        queries.reshape(shape),
        keys_all.reshape(key_shape),
        preferred_element_type=F32,
    ) * (HEAD_DIM**-0.5)
    scores = jnp.where(key_valid[:, None, None, :], scores, -1e30)
    top = jnp.max(scores, axis=-1, keepdims=True)
    weights = jnp.exp(scores - top)
    probs = (weights / jnp.sum(weights, axis=-1, keepdims=True)).astype(BF16)
    context = jnp.einsum(
        "shqk,skhd->sqhd", probs, values_all.reshape(key_shape), preferred_element_type=F32
    )
    return context.reshape(queries.shape).astype(BF16), probs


def native_backward(queries, keys_all, values_all, probs, context_grad, heads):
    shape = queries.shape[:2] + (heads, HEAD_DIM)
    key_shape = keys_all.shape[:2] + (heads, HEAD_DIM)
    scale = HEAD_DIM**-0.5
    grad_heads = context_grad.reshape(shape)
    wide = probs.astype(F32)
    probs_grad = jnp.einsum(
        "sqhd,skhd->shqk", grad_heads, values_all.reshape(key_shape), preferred_element_type=F32
    )
    inner_total = jnp.sum(wide * probs_grad, axis=-1, keepdims=True)
    scores_grad = (wide * (probs_grad - inner_total)).astype(BF16)
    query_grad = jnp.einsum(
        "shqk,skhd->sqhd", scores_grad, keys_all.reshape(key_shape), preferred_element_type=F32
    )
    key_part = jnp.einsum(
        "shqk,sqhd->skhd", scores_grad, queries.reshape(shape), preferred_element_type=F32
    )
    value_part = jnp.einsum("shqk,sqhd->skhd", probs, grad_heads, preferred_element_type=F32)
    return (
        (query_grad * scale).astype(BF16).reshape(queries.shape),
        (key_part * scale).astype(BF16).reshape(keys_all.shape),
        value_part.astype(BF16).reshape(values_all.shape),
    )


def gather_rows(part):
    return lax.all_gather(part, "fsdp", axis=0, tiled=True)


def reduce_rows(part):
    share = lax.psum_scatter(part.astype(BF16), "fsdp", scatter_dimension=0, tiled=True)
    return lax.psum(share, "ctx").astype(F32)


def layer(flat_rows, cot_rows, row_mask, packed, widths, weights, forward, backward):
    full_qkv, full_output, full_inner, full_outer = weights
    rows, width = flat_rows.shape
    shards = packed.shape[0]
    (
        bias_query,
        bias_value,
        bias_output,
        gain_first,
        shift_first,
        bias_inner,
        bias_outer,
        gain_second,
        shift_second,
    ) = [piece.reshape(-1).astype(F32) for piece in split_columns(packed, widths)]
    bias_qkv = jnp.concatenate((bias_query, jnp.zeros_like(bias_query), bias_value))
    qkv = (plain_product(flat_rows, full_qkv) + bias_qkv).astype(BF16)
    context, saved = forward(qkv)

    first_sum = flat_rows.astype(F32) + plain_product(context, full_output) + bias_output
    first_unit, first_rate = norm_parts(first_sum)
    normed = first_unit * gain_first + shift_first
    normed_low = normed.astype(BF16)
    hidden = plain_product(normed_low, full_inner) + bias_inner
    active, gelu_back = jax.vjp(exact_gelu, hidden)
    active_low = active.astype(BF16)
    second_sum = normed + plain_product(active_low, full_outer) + bias_outer
    second_unit, second_rate = norm_parts(second_sum)
    output = ((second_unit * gain_second + shift_second) * row_mask).astype(BF16)

    out_grad = cot_rows.astype(F32) * row_mask
    second_gain_part = jnp.sum(out_grad * second_unit, axis=0)
    second_shift_part = jnp.sum(out_grad, axis=0)
    second_grad = norm_back(second_unit, second_rate, out_grad * gain_second)
    second_low = second_grad.astype(BF16)
    outer_weight_part = left_product(active_low, second_low).astype(BF16)
    outer_bias_part = column_sums(second_low)
    (hidden_grad,) = gelu_back(right_product(second_low, full_outer))
    hidden_low = hidden_grad.astype(BF16)
    inner_weight_part = left_product(normed_low, hidden_low).astype(BF16)
    inner_bias_part = column_sums(hidden_low)
    normed_grad = second_grad + right_product(hidden_low, full_inner)
    first_gain_part = jnp.sum(normed_grad * first_unit, axis=0)
    first_shift_part = jnp.sum(normed_grad, axis=0)
    first_grad = norm_back(first_unit, first_rate, normed_grad * gain_first)
    branch_low = first_grad.astype(BF16)
    output_weight_part = left_product(context, branch_low).astype(BF16)
    output_bias_part = column_sums(branch_low)
    context_grad = right_product(branch_low, full_output).astype(BF16)
    qkv_grad = backward(saved, context_grad)
    qkv_weight_part = left_product(flat_rows, qkv_grad).astype(BF16)
    query_bias_part = column_sums(qkv_grad[:, :width])
    value_bias_part = column_sums(qkv_grad[:, 2 * width :])
    input_grad = first_grad + right_product(qkv_grad, full_qkv)
    vector_parts = (
        query_bias_part,
        value_bias_part,
        output_bias_part,
        first_gain_part,
        first_shift_part,
        inner_bias_part,
        outer_bias_part,
        second_gain_part,
        second_shift_part,
    )
    packed_parts = jnp.concatenate([part.reshape(shards, -1) for part in vector_parts], axis=1)
    return (
        output,
        input_grad,
        packed_parts,
        (qkv_weight_part, output_weight_part, inner_weight_part, outer_weight_part),
    )


def native_body(inputs, cotangent, lengths, vectors, weights):
    widths = [member.shape[0] for member in vectors]
    packed = lax.all_gather(jnp.concatenate(vectors), "fsdp", axis=0, tiled=False)
    joined = (jnp.concatenate(weights[:3], axis=1),) + weights[3:]
    full = tuple(gather_rows(part) for part in joined)
    micro, seqs, block_len, width = inputs.shape
    heads = width // HEAD_DIM
    total_slots = block_len * lax.axis_size("ctx")
    group = micro * seqs
    rows = group * block_len
    flat_len = lengths.reshape(group)
    local_pos = lax.axis_index("ctx") * block_len + jnp.arange(block_len, dtype=jnp.int32)
    row_mask = (local_pos[None, :] < flat_len[:, None]).astype(F32).reshape(rows, 1)
    key_valid = jnp.arange(total_slots, dtype=jnp.int32)[None, :] < flat_len[:, None]

    def forward(qkv):
        queries = qkv[:, :width].reshape(group, block_len, width)
        keys_values = lax.all_gather(
            qkv[:, width:].reshape(group, block_len, 2 * width), "ctx", axis=1, tiled=True
        )
        keys, values = keys_values[:, :, :width], keys_values[:, :, width:]
        context, probs = native_forward(queries, keys, values, key_valid, heads)
        return context.reshape(rows, width), (queries, keys, values, probs)

    def backward(saved, context_grad):
        query_grad, key_part, value_part = native_backward(
            *saved, context_grad.reshape(group, block_len, width), heads
        )
        keys_values_grad = lax.psum_scatter(
            jnp.concatenate((key_part, value_part), axis=2), "ctx", scatter_dimension=1, tiled=True
        )
        return jnp.concatenate(
            (query_grad.reshape(rows, width), keys_values_grad.reshape(rows, 2 * width)), axis=1
        )

    output, input_grad, packed_parts, parts = layer(
        inputs.reshape(rows, width),
        cotangent.reshape(rows, width),
        row_mask,
        packed,
        widths,
        full,
        forward,
        backward,
    )
    share = lax.psum_scatter(packed_parts, "fsdp", scatter_dimension=0, tiled=True)
    return (
        output.reshape(inputs.shape),
        input_grad.reshape(inputs.shape),
        split_columns(lax.psum(share, "ctx")[0], widths),
        tuple(split_columns(reduce_rows(parts[0]), [width] * 3))
        + tuple(reduce_rows(part) for part in parts[1:]),
    )


def direct_body(inputs, cotangent, lengths, vectors, weights):
    micro, seqs, block_len, width = inputs.shape
    shards = LINE * PAIR
    lengths = lengths.reshape(micro)
    rows = 2 * block_len
    table = jnp.zeros((TABLE_ROWS, LANES), F32)
    row = 0
    for vector in vectors:
        lines = vector.shape[0] // LANES
        filled = ((row, TABLE_ROWS - row - lines), (0, 0))
        table += jnp.pad(vector.astype(F32).reshape(lines, LANES), filled)
        row += lines
    query_weight, key_weight, value_weight, output_weight, inner_weight, outer_weight = weights
    blocks = (inputs.reshape(micro, block_len, width), cotangent.reshape(micro, block_len, width))
    shard_rows, hidden = inner_weight.shape
    flows = [Flow(0, TABLE_ROWS, lambda core, side: (0, TABLE_ROWS, 0, LANES), cores=False)]
    flows += column_flows(1, shard_rows, 3 * width, *GATHER_SPLIT[0])
    flows += column_flows(2, shard_rows, width, *GATHER_SPLIT[1])
    flows += column_flows(3, shard_rows, hidden, *GATHER_SPLIT[2])
    flows += row_flows(4, hidden // shards, width, *GATHER_SPLIT[3])
    (
        tables,
        full_qkv,
        full_output,
        full_inner,
        full_outer,
        in_rows,
        cot_rows,
        qkv,
        context,
        probs,
        away,
    ) = start(
        (table.astype(BF16),) + weights,
        ((0, 0), (1, 0), (1, width), (1, 2 * width), (2, 0), (3, 0), (4, 0)),
        blocks,
        lengths,
        flows,
        shards,
        1,
        GATHER_ORDER,
    )
    in_rows = in_rows.reshape(rows, width)
    cot_rows = cot_rows.reshape(rows, width)
    output, first_grad, context_grad, table_grad, output_part, inner_part, outer_part = middle(
        in_rows, context, cot_rows, lengths, tables, full_output, full_inner, full_outer
    )
    sums = finish(
        in_rows,
        (qkv, away, probs),
        context_grad,
        first_grad,
        table_grad,
        full_qkv,
        (inner_part, outer_part, output_part),
        output.reshape(micro, block_len, width),
        [
            column_part(shard_rows, hidden, *REDUCE_SPLIT[0]),
            row_part(hidden // shards, width, *REDUCE_SPLIT[1]),
            column_part(shard_rows, width, *REDUCE_SPLIT[2]),
            column_part(shard_rows, 3 * width, *REDUCE_SPLIT[3], inside=True),
            vector_part(TABLE_ROWS, LANES, inside=True),
        ],
        2,
        REDUCE_ORDER,
    )
    inner_share, outer_share, output_share, qkv_share, table_share, outs, grads = sums
    lines = tuple(vector.shape[0] // LANES for vector in vectors)
    wide = widen(
        (qkv_share, output_share, inner_share, outer_share, grads, outs),
        (3, 1, 1, 1, 1, 1),
        (F32,) * 5 + (BF16,),
        table_share,
        lines,
    )
    return (
        wide[7].reshape(inputs.shape),
        wide[6].reshape(inputs.shape),
        tuple(wide[8:]),
        tuple(wide[:6]),
    )


def body(
    inputs,
    cotangent,
    lengths,
    query_weight,
    key_weight,
    value_weight,
    output_weight,
    query_bias,
    value_bias,
    output_bias,
    first_gain,
    first_shift,
    inner_weight,
    inner_bias,
    outer_weight,
    outer_bias,
    second_gain,
    second_shift,
):
    vectors = (
        query_bias,
        value_bias,
        output_bias,
        first_gain,
        first_shift,
        inner_bias,
        outer_bias,
        second_gain,
        second_shift,
    )
    widths = [member.shape[0] for member in vectors]
    weights = (
        query_weight,
        key_weight,
        value_weight,
        output_weight,
        inner_weight,
        outer_weight,
    )
    laid_out = lax.axis_size("fsdp") == LINE * PAIR and lax.axis_size("ctx") == 4
    whole_lines = all(extent % LANES == 0 for extent in widths)
    direct = laid_out and inputs.shape[:2] == (2, 1) and whole_lines
    run = direct_body if direct else native_body
    output, input_grad, shares, weight_shares = run(inputs, cotangent, lengths, vectors, weights)
    query_share, key_share, value_share, output_share, inner_share, outer_share = weight_shares
    return (
        output,
        input_grad,
        query_share,
        key_share,
        value_share,
        output_share,
        shares[0],
        shares[1],
        shares[2],
        shares[3],
        shares[4],
        inner_share,
        shares[5],
        outer_share,
        shares[6],
        shares[7],
        shares[8],
    )


def solution(mesh):
    data = P(None, "fsdp", "ctx", None)
    matrix = P("fsdp", None)
    vector = P("fsdp")
    return jax.shard_map(
        body,
        mesh=mesh,
        in_specs=(data, data, P(None, "fsdp"))
        + (matrix,) * 4
        + (vector,) * 5
        + (matrix, vector, matrix, vector, vector, vector),
        out_specs=(data, data)
        + (matrix,) * 4
        + (vector,) * 5
        + (matrix, vector, matrix, vector, vector, vector),
        check_vma=False,
    )
```

```python
import functools

import jax
import jax.numpy as jnp
from jax import lax
from jax.experimental import pallas as pl
from jax.experimental.pallas import tpu as pltpu
from jax.sharding import PartitionSpec as P

HEAD_DIM = 64
EPSILON = 1e-06
F32 = jnp.float32
BF16 = jnp.bfloat16

GATHER_SPLIT = ((256, 384), (256, 128), (1024, 128), (128, 64))
REDUCE_SPLIT = ((768, 256), (160, 48), (256, 128), (1024, 256))
GATHER_ORDER = (
    10, 3, 2, 7, 4, 0, 8, 66, 64, 30, 5, 28, 1, 38, 43, 77, 72, 132, 15, 134, 98, 47, 111, 35,
    166, 69, 140, 200, 145, 29, 103, 32, 97, 9, 183, 162, 74, 89, 128, 36, 100, 179, 114, 60, 63,
    81, 106, 213, 67, 96, 180, 115, 34, 102, 68, 49, 12, 217, 94, 65, 201, 62, 149, 142, 141, 18,
    164, 13, 208, 184, 99, 146, 31, 40, 168, 137, 76, 129, 78, 131, 16, 42, 83, 50, 136, 6, 61,
    48, 51, 101, 209, 112, 174, 107, 151, 93, 117, 110, 225, 82, 171, 33, 14, 170, 123, 45, 214,
    205, 130, 153, 144, 118, 52, 21, 19, 55, 202, 165, 119, 181, 169, 53, 175, 73, 113, 90, 218,
    185, 152, 135, 116, 198, 133, 124, 199, 196, 150, 23, 120, 46, 85, 219, 59, 172, 167, 204,
    203, 37, 108, 222, 22, 84, 148, 80, 188, 86, 71, 138, 79, 221, 220, 216, 20, 230, 212, 39, 11,
    75, 210, 186, 178, 215, 154, 191, 182, 147, 232, 233, 70, 91, 234, 235, 17, 24, 104, 139, 105,
    26, 121, 157, 236, 155, 176, 195, 163, 109, 143, 57, 226, 54, 159, 161, 92, 95, 211, 27, 25,
    237, 197, 173, 56, 41, 177, 125, 127, 58, 231, 207, 238, 223, 160, 189, 193, 227, 44, 229,
    126, 87, 88, 206, 122, 158, 187, 156, 239, 228, 190, 192, 194, 224, 240,
)
REDUCE_ORDER = (
    14, 8, 4, 7, 0, 116, 5, 10, 197, 9, 2, 1, 85, 39, 84, 198, 40, 123, 12, 35, 3, 15, 86, 87,
    199, 92, 91, 200, 37, 36, 42, 89, 11, 94, 38, 201, 43, 32, 31, 69, 93, 29, 13, 88, 67, 68,
    202, 203, 23, 70, 102, 205, 181, 18, 51, 117, 90, 61, 28, 19, 180, 24, 183, 22, 96, 95, 16,
    132, 44, 100, 134, 118, 204, 104, 121, 17, 21, 148, 33, 110, 45, 124, 71, 72, 120, 34, 125,
    77, 6, 101, 188, 20, 73, 74, 150, 119, 149, 47, 46, 151, 41, 57, 97, 190, 75, 136, 76, 103,
    26, 156, 187, 133, 184, 126, 153, 168, 78, 164, 25, 185, 155, 106, 30, 127, 98, 182, 206, 152,
    207, 105, 208, 158, 128, 79, 157, 122, 165, 189, 55, 53, 27, 52, 48, 108, 166, 80, 81, 154,
    186, 135, 107, 172, 49, 170, 174, 54, 138, 160, 167, 129, 99, 159, 112, 169, 192, 56, 142,
    191, 82, 59, 111, 130, 140, 161, 162, 109, 171, 176, 58, 63, 137, 173, 175, 139, 193, 194,
    113, 114, 144, 62, 60, 131, 143, 177, 178, 141, 83, 50, 64, 65, 163, 145, 146, 115, 66, 179,
    195, 147, 196,
)

MESH = pl.DeviceIdType.MESH
LINE = 4
PAIR = 2


class Place:
    def __init__(self):
        self.ctx = lax.axis_index("ctx")
        self.shard = lax.axis_index("fsdp")
        self.side = lax.div(self.ctx, 2)
        self.core = lax.rem(self.ctx, 2)
        self.line = lax.div(self.shard, PAIR)
        self.pair = lax.rem(self.shard, PAIR)

    def ahead(self, way):
        return (self.ctx, self.shard + way * PAIR)

    def across(self):
        return (self.ctx, self.shard + 1 - 2 * self.pair)

    def beside(self):
        return (self.ctx + 2 - 4 * self.side, self.shard)

    def twin(self):
        return (self.ctx + 1 - 2 * self.core, self.shard)

    def has(self, way, steps):
        if steps == 0:
            return None
        return self.line >= steps if way > 0 else self.line <= LINE - 1 - steps

    def can(self, way):
        return self.line <= LINE - 2 if way > 0 else self.line >= 1

    def shard_of(self, way, steps, other):
        pair = 1 - self.pair if other else self.pair
        return (self.line - way * steps) * PAIR + pair


def when(conditions, action):
    held = [c for c in conditions if c is not None]
    if not held:
        action()
        return
    both = held[0]
    for c in held[1:]:
        both = jnp.logical_and(both, c)
    pl.when(both)(action)


def greet(place):
    barrier = pltpu.get_barrier_semaphore()
    for peer in (place.across(), place.beside(), place.twin()):
        pl.semaphore_signal(barrier, inc=1, device_id=peer, device_id_type=MESH)
    for way in (1, -1):
        when(
            [place.can(way)],
            lambda way=way: pl.semaphore_signal(
                barrier, inc=1, device_id=place.ahead(way), device_id_type=MESH
            ),
        )
    lines = jnp.minimum(place.line, 1) + jnp.minimum(LINE - 1 - place.line, 1)
    pl.semaphore_wait(barrier, 3 + lines)


class Flow:
    def __init__(self, array, shard_rows, region, order="line", sides=False, cores=True):
        self.array = array
        self.shard_rows = shard_rows
        self.region = region
        self.order = order
        self.sides = sides
        self.cores = cores

    def view(self, ref, shard, core, side):
        row, rows, column, columns = self.region(core, side)
        start = row if shard is None else shard * self.shard_rows + row
        if not isinstance(start, int):
            start = pl.multiple_of(start, 16)
        if not isinstance(column, int):
            column = pl.multiple_of(column, 128)
        return ref.at[pl.ds(start, rows), pl.ds(column, columns)]


def positions(order):
    found = []
    if order == "line":
        found.append(("P", 1, 0, True))
        for steps in range(1, LINE):
            for way in (1, -1):
                found.append(("L", way, steps, False))
                found.append(("P", way, steps, True))
    else:
        found.append(("P", 1, 0, True))
        for steps in range(1, LINE):
            for way in (1, -1):
                found.append(("L", way, steps, False))
                found.append(("L", way, steps, True))
    return found


class Labels:
    def __init__(self):
        self.numbers = {}

    def __call__(self, key):
        return self.numbers.setdefault(key, len(self.numbers))


def gather_labels(flows):
    labels = Labels()
    for number, flow in enumerate(flows):
        for spot in positions(flow.order):
            labels((number, "in") + spot)
            if flow.sides:
                labels((number, "side") + spot)
            if flow.cores:
                labels((number, "twin") + spot)
                if flow.sides:
                    labels((number, "twinside") + spot)
    return labels


class Gather:
    def __init__(self, place, flows, owns, fulls, send, recv):
        self.place, self.flows, self.owns, self.fulls = place, flows, owns, fulls
        self.send, self.recv = send, recv
        self.labels = gather_labels(flows)
        self.sent = []

    def copy(self, number, key, spot, peer, core, side, own=False):
        flow = self.flows[number]
        place = self.place
        if own:
            shard = place.shard
            source = flow.view(self.owns[flow.array], None, core, side)
        else:
            shard = place.shard_of(*spot[1:])
            source = flow.view(self.fulls[flow.array], shard, core, side)
        target = flow.view(self.fulls[flow.array], shard, core, side)
        label = self.labels((number,) + key)
        return pltpu.make_async_remote_copy(
            source,
            target,
            self.send.at[label],
            self.recv.at[label],
            device_id=peer,
            device_id_type=MESH,
        )

    def start(self, conditions, copy):
        when(conditions, copy.start)
        self.sent.append((conditions, copy))

    def begin(self, number):
        flow, place = self.flows[number], self.place
        core, side = place.core, place.side
        here = (None, 1, 0, False)
        for way in (1, -1):
            self.start(
                [place.can(way)],
                self.copy(
                    number, ("in", "L", way, 1, False), here, place.ahead(way), core, side, True
                ),
            )
        self.start(
            [],
            self.copy(number, ("in", "P", 1, 0, True), here, place.across(), core, side, True),
        )

    def arrive(self, number, spot):
        flow, place = self.flows[number], self.place
        kind, way, steps, other = spot
        core, side = place.core, place.side
        there = place.has(way, steps)

        def take():
            self.copy(number, ("in",) + spot, spot, place.across(), core, side).wait_recv()

        when([there], take)

        def onward(extra, key, peer):
            self.start(
                [c for c in (there, extra) if c is not None],
                self.copy(number, key, spot, peer, core, side),
            )

        if kind == "L" and steps + 1 < LINE:
            onward(place.can(way), ("in", "L", way, steps + 1, other), place.ahead(way))
        if kind == "L" and flow.order == "line":
            onward(None, ("in", "P", way, steps, True), place.across())
        if kind == "P" and flow.order == "pair":
            for direction in (1, -1):
                onward(
                    place.can(direction), ("in", "L", direction, 1, True), place.ahead(direction)
                )
        if flow.sides:
            onward(None, ("side",) + spot, place.beside())
        if flow.cores:
            onward(None, ("twin",) + spot, place.twin())

    def arrive_side(self, number, spot):
        flow, place = self.flows[number], self.place
        there = place.has(*spot[1:3])
        core, side = place.core, 1 - place.side
        when(
            [there],
            lambda: self.copy(
                number, ("side",) + spot, spot, place.beside(), core, side
            ).wait_recv(),
        )
        if flow.cores:
            self.start(
                [there] if there is not None else [],
                self.copy(number, ("twinside",) + spot, spot, place.twin(), core, side),
            )

    def arrive_twin(self, number, spot):
        flow, place = self.flows[number], self.place
        there = place.has(*spot[1:3])
        core = 1 - place.core
        if flow.cores:
            when(
                [there],
                lambda: self.copy(
                    number, ("twin",) + spot, spot, place.twin(), core, place.side
                ).wait_recv(),
            )
            if flow.sides:
                when(
                    [there],
                    lambda: self.copy(
                        number, ("twinside",) + spot, spot, place.twin(), core, 1 - place.side
                    ).wait_recv(),
                )

    def actions(self):
        found = []
        for n, flow in enumerate(self.flows):
            found.append((("begin", n), lambda n=n: self.begin(n)))
        for index in range(len(positions("line"))):
            for n, flow in enumerate(self.flows):
                spot = positions(flow.order)[index]
                found.append((("in", n, spot), lambda n=n, spot=spot: self.arrive(n, spot)))
                if flow.sides:
                    found.append(
                        (("side", n, spot), lambda n=n, spot=spot: self.arrive_side(n, spot))
                    )
        return found

    def wait_twins(self, arrays):
        for number, flow in enumerate(self.flows):
            if flow.array in arrays:
                for spot in positions(flow.order):
                    self.arrive_twin(number, spot)

    def finish(self, arrays):
        self.wait_twins(arrays)
        for conditions, copy in self.sent:
            when(conditions, copy.wait_send)


class Swap:
    def __init__(self, place, ins, outs, send, recv, local):
        side = place.side
        self.away = [
            pltpu.make_async_remote_copy(
                here.at[1 - side],
                there.at[side],
                send.at[k],
                recv.at[k],
                device_id=place.beside(),
                device_id_type=MESH,
            )
            for k, (here, there) in enumerate(zip(ins, outs))
        ]
        self.stay = [
            pltpu.make_async_copy(here.at[side], there.at[side], local.at[k])
            for k, (here, there) in enumerate(zip(ins, outs))
        ]

    def start(self, k=0):
        self.away[k].start()
        self.stay[k].start()

    def wait_here(self, k):
        self.away[k].wait_recv()
        self.stay[k].wait()
        self.held = k

    held = None

    def finish(self):
        for k, (away, stay) in enumerate(zip(self.away, self.stay)):
            if k == self.held:
                away.wait_send()
            else:
                away.wait()
                stay.wait()


def swap_scratch(count):
    return [pltpu.SemaphoreType.DMA((count,))] * 3


def column_flows(array, shard_rows, columns, shared, early):
    half = columns // 2
    part = (half - shared) // 2
    flows = []
    if shared:
        flows.append(
            Flow(array, shard_rows, lambda core, side: (0, shard_rows, core * half, shared))
        )
    if early:
        flows.append(
            Flow(
                array,
                shard_rows,
                lambda core, side: (0, shard_rows, core * half + shared + side * part, early),
                sides=True,
            )
        )
    if part > early:
        flows.append(
            Flow(
                array,
                shard_rows,
                lambda core, side: (
                    0,
                    shard_rows,
                    core * half + shared + side * part + early,
                    part - early,
                ),
                order="pair",
                sides=True,
            )
        )
    return flows


def row_flows(array, shard_rows, columns, shared, early):
    half = shard_rows // 2
    part = (half - shared) // 2
    flows = [
        Flow(array, shard_rows, lambda core, side: (core * half, shared, 0, columns)),
        Flow(
            array,
            shard_rows,
            lambda core, side: (core * half + shared + side * part, early, 0, columns),
            sides=True,
        ),
        Flow(
            array,
            shard_rows,
            lambda core, side: (core * half + shared + side * part + early, part - early, 0, columns),
            order="pair",
            sides=True,
        ),
    ]
    return [flow for flow in flows if flow.region(0, 0)[1]]


class Part:
    def __init__(self, rows, columns, along, flows, dtype=BF16, inside=False):
        self.rows, self.columns, self.along, self.dtype = rows, columns, along, dtype
        self.inside = inside
        self.flows = flows
        self.half_rows = rows // 2 if along == "rows" else rows
        self.half_columns = columns // 2 if along == "columns" else columns

    def half(self, ref, shard, core):
        base = 0 if shard is None else pl.multiple_of(shard * self.rows, 16)
        if self.along == "rows":
            row = core * self.half_rows + (0 if shard is None else shard * self.rows)
            return ref.at[pl.ds(pl.multiple_of(row, 16), self.half_rows), :]
        if self.along == "columns":
            column = pl.multiple_of(core * self.half_columns, 128)
            return ref.at[pl.ds(base, self.rows), pl.ds(column, self.half_columns)]
        return ref.at[pl.ds(base, self.rows), :]

    def inner(self, flow, side):
        first, extent = flow[0](side), flow[1]
        if self.along == "rows":
            start = first if isinstance(first, int) else pl.multiple_of(first, 16)
            return pl.ds(start, extent), slice(None)
        start = first if isinstance(first, int) else pl.multiple_of(first, 128)
        return slice(None), pl.ds(start, extent)

    def outer(self, flow, core, side):
        first, extent = flow[0](side), flow[1]
        if self.along == "rows":
            return pl.ds(pl.multiple_of(core * self.half_rows + first, 16), extent), slice(None)
        if self.along == "columns":
            return slice(None), pl.ds(
                pl.multiple_of(core * self.half_columns + first, 128), extent
            )
        return slice(None), slice(None)

    def extent(self, flow):
        if self.along == "rows":
            return flow[1], self.half_columns
        return self.half_rows, flow[1]


SPOTS = [(1, 3), (-1, 3), (1, 2), (-1, 2), (1, 1), (-1, 1), (1, 0)]


def reduce_scratch(parts):
    shapes = []
    for part in parts:
        half = (LINE * PAIR, part.half_rows, part.half_columns)
        shapes.append(pltpu.VMEM(half, part.dtype))
        shapes.append(pltpu.VMEM(half if part.along else half[1:], part.dtype))
        for flow in part.flows:
            rows, columns = part.extent(flow)
            shapes.append(
                pltpu.VMEM((LINE * PAIR if flow[3] else 1, rows, columns), part.dtype)
            )
            shapes.append(
                pltpu.VMEM((LINE if flow[2] == "line" else 1, rows, columns), part.dtype)
            )
            shapes.append(
                pltpu.VMEM(
                    ((LINE + 1) * (1 if flow[2] == "line" else PAIR), rows, columns), part.dtype
                )
            )
    return shapes


def reduce_labels(parts):
    labels = Labels()
    for n, part in enumerate(parts):
        for way, steps in SPOTS:
            for other in (False, True):
                labels((n, "twin", way, steps, other))
        labels((n, "twinend"))
        for k, flow in enumerate(part.flows):
            for way, steps in SPOTS:
                for other in (False, True):
                    if flow[3]:
                        labels((n, k, "side", way, steps, other))
                    if flow[2] == "pair" or not other:
                        labels((n, k, "line", way, steps, other))
                        if steps == 0:
                            labels((n, k, "line", -way, steps, other))
                if flow[2] == "line" or steps == 0:
                    labels((n, k, "pair", way, steps))
            labels((n, k, "sideend"))
            labels((n, k, "twinend"))
            labels((n, k, "twinsideend"))
    return labels


class Reduce:
    def __init__(self, place, parts, grads, outs, scratch, send, recv, load):
        self.place, self.parts, self.grads, self.outs = place, parts, grads, outs
        self.send, self.recv, self.load = send, recv, load
        self.labels = reduce_labels(parts)
        self.sent = []
        self.own, self.other, self.lanes = [], [], []
        at = 0
        for part in parts:
            self.own.append(scratch[at])
            self.other.append(scratch[at + 1])
            at += 2
            lanes = []
            for _ in part.flows:
                lanes.append(scratch[at : at + 3])
                at += 3
            self.lanes.append(lanes)

    def copy(self, source, target, key, peer):
        label = self.labels(key)
        return pltpu.make_async_remote_copy(
            source,
            target,
            self.send.at[label],
            self.recv.at[label],
            device_id=peer,
            device_id_type=MESH,
        )

    def start(self, conditions, copy):
        when(conditions, copy.start)
        self.sent.append((conditions, copy))

    def there(self, spot):
        return self.place.has(-spot[0], spot[1])

    def shard(self, spot, other):
        return self.place.shard_of(-spot[0], spot[1], other)

    def keep(self, n, spot, other):
        shard = self.shard(spot, other)
        label = SPOTS.index(spot) * 2 + int(other)
        return pltpu.make_async_copy(
            self.parts[n].half(self.grads[n], shard, self.place.core),
            self.own[n].at[shard],
            self.load.at[n * 2 * len(SPOTS) + label],
        )

    def twin(self, n, spot, other, core):
        shard = self.shard(spot, other)
        part = self.parts[n]
        return self.copy(
            self.grads[n].at[shard] if part.inside else part.half(self.grads[n], shard, core),
            self.other[n].at[shard],
            (n, "twin") + spot + (other,),
            self.place.twin(),
        )

    def begin(self, n, spot):
        there = self.there(spot)
        for other in (True, False):
            if not self.parts[n].inside:
                when([there], self.keep(n, spot, other).start)
            if self.parts[n].along:
                self.start([there], self.twin(n, spot, other, 1 - self.place.core))

    def piece(self, n, k, shard, side):
        part = self.parts[n]
        rows, columns = part.inner(part.flows[k], side)
        return self.own[n].at[shard, rows, columns]

    def side_copy(self, n, k, spot, other, side):
        shard = self.shard(spot, other)
        return self.copy(
            self.piece(n, k, shard, side),
            self.lanes[n][k][0].at[shard],
            (n, k, "side") + spot + (other,),
            self.place.beside(),
        )

    def add_cores(self, n, spot):
        there = self.there(spot)
        part = self.parts[n]
        for other in (True, False):

            def add(other=other):
                shard = self.shard(spot, other)
                if not part.inside:
                    self.keep(n, spot, other).wait()
                if part.along:
                    self.twin(n, spot, other, self.place.core).wait_recv()
                    self.own[n][shard] = self.own[n][shard] + self.other[n][shard]

            when([there], add)
        for other in (True, False):
            for k, flow in enumerate(part.flows):
                if flow[3]:
                    self.start([there], self.side_copy(n, k, spot, other, 1 - self.place.side))
                elif other:
                    self.start([there], self.pair_copy(n, k, spot, self.shard(spot, True)))

    def pair_copy(self, n, k, spot, shard):
        flow = self.parts[n].flows[k]
        slot = self.place.line + spot[0] * spot[1] if flow[2] == "line" else 0
        return self.copy(
            self.piece(n, k, shard, self.place.side),
            self.lanes[n][k][1].at[slot],
            (n, k, "pair") + spot,
            self.place.across(),
        )

    def add_sides(self, n, k, spot):
        there = self.there(spot)
        side = self.place.side
        for other in (True, False):

            def add(other=other):
                shard = self.shard(spot, other)
                self.side_copy(n, k, spot, other, side).wait_recv()
                piece = self.piece(n, k, shard, side)
                piece[...] = piece[...] + self.lanes[n][k][0][shard]

            when([there], add)
        if self.parts[n].flows[k][2] == "line":
            self.start([there], self.pair_copy(n, k, spot, self.shard(spot, True)))

    def line_slot(self, flow, way, steps, other, line):
        slot = line if (steps > 0 or way > 0) else LINE
        return slot + (LINE + 1) * int(other) if flow[2] == "pair" else slot

    def line_copy(self, n, k, spot, other, arriving):
        flow = self.parts[n].flows[k]
        way, steps = spot
        shard = self.shard(spot, other)
        line = self.place.line + way * steps
        left = steps if arriving else steps - 1
        return self.copy(
            self.piece(n, k, shard, self.place.side),
            self.lanes[n][k][2].at[self.line_slot(flow, way, left, other, line)],
            (n, k, "line", way, left, other),
            self.place.ahead(way),
        )

    def add_line(self, n, k, spot):
        place = self.place
        there = self.there(spot)
        way, steps = spot
        side = place.side
        flow = self.parts[n].flows[k]
        if flow[2] == "line":

            def add():
                shard = self.shard(spot, False)
                self.pair_copy(n, k, spot, shard).wait_recv()
                piece = self.piece(n, k, shard, side)
                piece[...] = piece[...] + self.lanes[n][k][1][place.line + way * steps]

            when([there], add)
        for other in (True, False) if flow[2] == "pair" else (False,):
            for direction in (1, -1) if steps == 0 else (way,):

                def add_line(other=other, here=(direction, steps)):
                    self.line_copy(n, k, here, other, True).wait_recv()
                    piece = self.piece(n, k, self.shard(here, other), side)
                    line = place.line + here[0] * here[1]
                    slot = self.line_slot(flow, here[0], here[1], other, line)
                    piece[...] = piece[...] + self.lanes[n][k][2][slot]

                when([there, place.can(-direction)], add_line)
            if steps > 0:
                self.start([there], self.line_copy(n, k, spot, other, False))

    def send_pair(self, n, k):
        self.start([], self.pair_copy(n, k, (1, 0), self.shard((1, 0), True)))

    def send_swap(self, n, k):
        self.start([], self.swap(n, k))

    def settle(self, n, k):
        place = self.place
        core, side, here = place.core, place.side, place.shard
        part = self.parts[n]
        flow = part.flows[k]
        piece = self.piece(n, k, here, side)
        out = self.out_view(n, k, core, side)
        if flow[3]:
            if flow[2] == "pair":
                self.pair_copy(n, k, (1, 0), here).wait_recv()
                out[...] = piece[...] + self.lanes[n][k][1][0]
            else:
                out[...] = piece[...]
            self.start([], self.out_copy(n, k, "sideend", place.beside(), core, side))
        else:
            self.swap(n, k).wait_recv()
            out[...] = piece[...] + self.lanes[n][k][0][0]
        if part.along:
            self.start([], self.out_copy(n, k, "twinend", place.twin(), core, side))
        else:
            self.start([], self.whole(n, k))

    def settle_side(self, n, k):
        place = self.place
        core, side = place.core, 1 - place.side
        self.out_copy(n, k, "sideend", place.beside(), core, side).wait_recv()
        self.start([], self.out_copy(n, k, "twinsideend", place.twin(), core, side))

    def swap(self, n, k):
        return self.copy(
            self.piece(n, k, self.place.shard, self.place.side),
            self.lanes[n][k][0].at[0],
            (n, k, "sideend"),
            self.place.beside(),
        )

    def out_view(self, n, k, core, side):
        part = self.parts[n]
        rows, columns = part.outer(part.flows[k], core, side)
        return self.outs[n].at[rows, columns]

    def out_copy(self, n, k, key, peer, core, side):
        view = self.out_view(n, k, core, side)
        return self.copy(view, view, (n, k, key), peer)

    def last(self):
        place = self.place
        core, side = place.core, place.side
        everything = [(n, k) for n, part in enumerate(self.parts) for k in range(len(part.flows))]
        for n, k in everything:
            if self.parts[n].along:
                self.out_copy(n, k, "twinend", place.twin(), 1 - core, side).wait_recv()
                if self.parts[n].flows[k][3]:
                    self.out_copy(
                        n, k, "twinsideend", place.twin(), 1 - core, 1 - side
                    ).wait_recv()
            else:
                self.whole(n, k).wait_recv()
        for conditions, copy in self.sent:
            when(conditions, copy.wait_send)
        for n, k in everything:
            if not self.parts[n].along:
                view = self.out_view(n, k, core, side)
                view[...] = view[...] + self.other[n][...]

    def whole(self, n, k):
        return self.copy(
            self.out_view(n, k, self.place.core, self.place.side),
            self.other[n],
            (n, k, "twinend"),
            self.place.twin(),
        )

    def actions(self):
        found = []
        for n, part in enumerate(self.parts):
            for spot in SPOTS:
                found.append((("begin", n, spot), lambda n=n, s=spot: self.begin(n, s)))
        for n, part in enumerate(self.parts):
            for spot in SPOTS:
                found.append((("cores", n, spot), lambda n=n, s=spot: self.add_cores(n, s)))
            for k, flow in enumerate(part.flows):
                at = (n, k)
                for spot in SPOTS:
                    if flow[3]:
                        found.append(
                            (("sides", n, k, spot), lambda at=at, s=spot: self.add_sides(*at, s))
                        )
                    found.append(
                        (("line", n, k, spot), lambda at=at, s=spot: self.add_line(*at, s))
                    )
                if flow[2] == "pair":
                    found.append((("pair", n, k), lambda at=at: self.send_pair(*at)))
                if not flow[3]:
                    found.append((("swap", n, k), lambda at=at: self.send_swap(*at)))
                found.append((("settle", n, k), lambda at=at: self.settle(*at)))
                if flow[3]:
                    found.append((("after", n, k), lambda at=at: self.settle_side(*at)))
        found.append((("last",), self.last))
        return found


def in_order(actions, order):
    if order is None:
        return [action for _, action in actions]
    assert sorted(order) == list(range(len(actions)))
    return [actions[i][1] for i in order]


def column_part(rows, columns, shared, early, inside=False):
    half = columns // 2
    part = (half - shared) // 2
    flows = []
    if shared:
        flows.append((lambda side: 0, shared, "line", False))
    if early:
        flows.append((lambda side: shared + side * part, early, "line", True))
    if part > early:
        flows.append((lambda side: shared + side * part + early, part - early, "pair", True))
    return Part(rows, columns, "columns", flows, inside=inside)


def row_part(rows, columns, shared, early):
    half = rows // 2
    part = (half - shared) // 2
    flows = [
        (lambda side: 0, shared, "line", False),
        (lambda side: shared + side * part, early, "line", True),
        (lambda side: shared + side * part + early, part - early, "pair", True),
    ]
    return Part(rows, columns, "rows", [flow for flow in flows if flow[1]])


def vector_part(rows, columns, inside=False):
    return Part(rows, columns, None, [(lambda side: 0, columns, "line", False)], F32, inside)


ROW_QUERY, ROW_VALUE, ROW_OUTPUT, ROW_GAIN1, ROW_SHIFT1, ROW_INNER, INNER = 0, 1, 2, 3, 4, 5, 4
ROW_OUTER, ROW_GAIN2, ROW_SHIFT2 = 9, 10, 11
TABLE_ROWS = 16
VMEM = 67043328
LANES = 128
BAND = 128


def spread_table(table_ref, vec):
    for shard in range(table_ref.shape[0] // TABLE_ROWS):
        vec[:, pl.ds(shard * LANES, LANES)] = table_ref[
            pl.ds(shard * TABLE_ROWS, TABLE_ROWS), :
        ].astype(F32)


def fold_table(vec, table_ref, first, count):
    for shard in range(table_ref.shape[0] // TABLE_ROWS):
        table_ref[pl.ds(shard * TABLE_ROWS + first, count), :] = vec[
            pl.ds(first, count), pl.ds(shard * LANES, LANES)
        ]


def row_place(row, core, rows):
    half = rows // 2
    return jnp.where(row < half, row, row + half) + core * half


def total_rows(block):
    return jnp.sum(block.astype(F32), axis=0, keepdims=True)


def middle_kernel(
    rows_far,
    context_far,
    cot_far,
    lengths_ref,
    table_ref,
    output_w,
    inner_w,
    outer_w,
    out_far,
    first_grad_far,
    context_grad_far,
    sums_ref,
    output_far,
    inner_g,
    outer_g,
    rows_ref,
    context_ref,
    cot_ref,
    out_ref,
    first_grad_ref,
    context_grad_ref,
    output_g,
    output_v,
    inner_v,
    outer_v,
    vec,
    sums,
    active,
    slope,
    unit1,
    rate1,
    total,
    low,
    low_t,
    second,
    second_low,
    inner_b,
    outer_b,
    load,
    save,
    few,
    swap_send,
    swap_recv,
    swap_local,
):
    rows, width = rows_ref.shape
    tiles, _, tile = inner_v.shape
    place = Place()
    side, core = place.side, place.core
    length = lengths_ref[side]
    bands = rows // BAND
    assert BAND == cot_ref.shape[1]
    barrier = pltpu.get_barrier_semaphore()
    pl.semaphore_signal(barrier, inc=1, device_id=place.beside(), device_id_type=MESH)

    def inner_load(t):
        return pltpu.make_async_copy(
            inner_w.at[:, pl.ds(pl.multiple_of(t * tile, tile), tile)], inner_v.at[t], load.at[0, t]
        )

    def outer_load(t):
        return pltpu.make_async_copy(
            outer_w.at[pl.ds(pl.multiple_of(t * tile, tile), tile), :], outer_v.at[t], load.at[1, t]
        )

    output_load = pltpu.make_async_copy(output_w, output_v, few.at[0])
    context_load = pltpu.make_async_copy(context_far, context_ref, few.at[1])
    rows_load = pltpu.make_async_copy(rows_far, rows_ref, few.at[2])
    turn = Swap(
        place, [cot_far, out_ref], [cot_ref, out_far], swap_send, swap_recv, swap_local
    )
    first_save = pltpu.make_async_copy(first_grad_ref, first_grad_far, few.at[5])
    context_save = pltpu.make_async_copy(context_grad_ref, context_grad_far, few.at[6])
    output_save = pltpu.make_async_copy(output_g, output_far, few.at[7])
    for copy in (context_load, output_load, rows_load):
        copy.start()
    spread_table(table_ref, vec)
    sums[...] = jnp.zeros_like(sums)
    context_load.wait()
    output_load.wait()
    pl.semaphore_wait(barrier, 1)
    turn.start(0)
    ahead = 3
    for t in range(ahead):
        inner_load(t).start()
        outer_load(t).start()
    total[...] = plain_product(context_ref[...], output_v[...])
    rows_load.wait()

    def band_of(b):
        return pl.ds(pl.multiple_of(b * BAND, BAND), BAND)

    def first_norm(b, carry):
        here = band_of(b)
        first_sum = (
            rows_ref[here, :].astype(F32) + total[here, :] + vec[pl.ds(ROW_OUTPUT, 1), :]
        )
        unit, rate = norm_parts(first_sum)
        unit1[here, :] = unit
        rate1[here, :] = jnp.broadcast_to(rate, (BAND, LANES))
        normed = unit * vec[pl.ds(ROW_GAIN1, 1), :] + vec[pl.ds(ROW_SHIFT1, 1), :]
        low[here, :] = normed.astype(BF16)
        total[here, :] = normed + vec[pl.ds(ROW_OUTER, 1), :]
        return carry

    lax.fori_loop(0, bands, first_norm, 0)
    low_t[...] = low[...].T


    def forward(t, carry):
        inner_load(t).wait()

        @pl.when(t + ahead < tiles)
        def _():
            inner_load(t + ahead).start()
            outer_load(t + ahead).start()

        bias = jnp.concatenate(
            [
                vec[pl.ds(ROW_INNER + k, 1), pl.ds(pl.multiple_of(t * LANES, LANES), LANES)]
                for k in range(INNER)
            ],
            axis=1,
        )
        hidden = plain_product(low[...], inner_v[t]) + bias
        share = 0.5 + 0.5 * lax.erf(hidden * 0.7071067811865476)
        active[t] = (hidden * share).astype(BF16)
        slope[t] = share + hidden * (jnp.exp(-0.5 * hidden * hidden) * 0.3989422804014327)
        outer_load(t).wait()
        total[...] += plain_product(active[t], outer_v[t])
        return carry

    lax.fori_loop(0, tiles, forward, 0)

    turn.wait_here(0)

    def second_norm(b, carry):
        here = band_of(b)
        unit, rate = norm_parts(total[here, :])
        row = b * BAND + lax.broadcasted_iota(jnp.int32, (BAND, width), 0)
        mask = (row_place(row, core, rows) < length).astype(F32)
        gain = vec[pl.ds(ROW_GAIN2, 1), :]
        out_ref[b] = ((unit * gain + vec[pl.ds(ROW_SHIFT2, 1), :]) * mask).astype(BF16)
        out_grad = cot_ref[b].astype(F32) * mask
        grad = norm_back(unit, rate, out_grad * gain)
        second[here, :] = grad
        grad_low = grad.astype(BF16)
        second_low[here, :] = grad_low
        sums[pl.ds(ROW_GAIN2, 1), :] += total_rows(out_grad * unit)
        sums[pl.ds(ROW_SHIFT2, 1), :] += total_rows(out_grad)
        sums[pl.ds(ROW_OUTER, 1), :] += total_rows(grad_low)
        return carry

    lax.fori_loop(0, bands, second_norm, 0)
    turn.start(1)

    def inner_save(t):
        slot = lax.rem(t, 2)
        return pltpu.make_async_copy(
            inner_b.at[slot],
            inner_g.at[:, pl.ds(pl.multiple_of(t * tile, tile), tile)],
            save.at[0, slot],
        )

    def outer_save(t):
        slot = lax.rem(t, 2)
        return pltpu.make_async_copy(
            outer_b.at[slot],
            outer_g.at[pl.ds(pl.multiple_of(t * tile, tile), tile), :],
            save.at[1, slot],
        )

    def backward(t, carry):
        slot = lax.rem(t, 2)
        hidden_grad = (right_product(second_low[...], outer_v[t]) * slope[t]).astype(BF16)
        summed = total_rows(hidden_grad)
        for k in range(INNER):
            sums[
                pl.ds(ROW_INNER + k, 1), pl.ds(pl.multiple_of(t * LANES, LANES), LANES)
            ] = summed[:, k * LANES : (k + 1) * LANES]

        @pl.when(t >= 2)
        def _():
            outer_save(t - 2).wait()
            inner_save(t - 2).wait()

        outer_b[slot] = left_product(active[t], second_low[...]).astype(BF16)
        inner_b[slot] = plain_product(low_t[...], hidden_grad).astype(BF16)
        outer_save(t).start()
        second[...] += right_product(hidden_grad, inner_v[t])
        inner_save(t).start()
        return carry

    lax.fori_loop(0, tiles, backward, 0)

    def first_back(b, carry):
        here = band_of(b)
        grad = second[here, :]
        unit = unit1[here, :]
        sums[pl.ds(ROW_GAIN1, 1), :] += total_rows(grad * unit)
        sums[pl.ds(ROW_SHIFT1, 1), :] += total_rows(grad)
        back = norm_back(unit, rate1[here, :1], grad * vec[pl.ds(ROW_GAIN1, 1), :])
        first_grad_ref[here, :] = back
        back_low = back.astype(BF16)
        second_low[here, :] = back_low
        sums[pl.ds(ROW_OUTPUT, 1), :] += total_rows(back_low)
        return carry

    lax.fori_loop(0, bands, first_back, 0)
    output_g[...] = left_product(context_ref[...], second_low[...]).astype(BF16)
    first_save.start()
    context_grad_ref[...] = right_product(second_low[...], output_v[...]).astype(BF16)
    output_save.start()
    fold_table(sums, sums_ref, 0, TABLE_ROWS)
    context_save.start()
    for t in range(tiles - 2, tiles):
        outer_save(t).wait()
        inner_save(t).wait()
    for copy in (first_save, output_save, context_save):
        copy.wait()
    turn.finish()


def middle(collective_id, rows, context, cot, lengths, table, output_w, inner_w, outer_w):
    count, width = rows.shape
    hidden = inner_w.shape[1]
    tile = INNER * LANES
    tiles = hidden // tile
    whole = pl.BlockSpec(memory_space=pltpu.VMEM)
    far = pl.BlockSpec(memory_space=pltpu.HBM)

    def space(dtype):
        return pltpu.VMEM((count, width), dtype)

    return pl.pallas_call(
        middle_kernel,
        out_shape=[
            jax.ShapeDtypeStruct(cot.shape, BF16),
            jax.ShapeDtypeStruct((count, width), F32),
            jax.ShapeDtypeStruct((count, width), BF16),
            jax.ShapeDtypeStruct(table.shape, F32),
            jax.ShapeDtypeStruct(output_w.shape, BF16),
            jax.ShapeDtypeStruct(inner_w.shape, BF16),
            jax.ShapeDtypeStruct(outer_w.shape, BF16),
        ],
        in_specs=[far] * 3 + [pl.BlockSpec(memory_space=pltpu.SMEM), whole] + [far] * 3,
        out_specs=[far] * 3 + [whole] + [far] * 3,
        scratch_shapes=[
            space(BF16),
            space(BF16),
            pltpu.VMEM(cot.shape, BF16),
            pltpu.VMEM(cot.shape, BF16),
            space(F32),
            space(BF16),
            pltpu.VMEM(output_w.shape, BF16),
            pltpu.VMEM(output_w.shape, BF16),
            pltpu.VMEM((tiles, width, tile), BF16),
            pltpu.VMEM((tiles, tile, width), BF16),
            pltpu.VMEM((TABLE_ROWS, width), F32),
            pltpu.VMEM((TABLE_ROWS, width), F32),
            pltpu.VMEM((tiles, count, tile), BF16),
            pltpu.VMEM((tiles, count, tile), F32),
            space(F32),
            pltpu.VMEM((count, LANES), F32),
            space(F32),
            space(BF16),
            pltpu.VMEM((width, count), BF16),
            space(F32),
            space(BF16),
            pltpu.VMEM((2, width, tile), BF16),
            pltpu.VMEM((2, tile, width), BF16),
            pltpu.SemaphoreType.DMA((2, tiles)),
            pltpu.SemaphoreType.DMA((2, 2)),
            pltpu.SemaphoreType.DMA((8,)),
        ]
        + swap_scratch(2),
        compiler_params=pltpu.CompilerParams(
            collective_id=collective_id, has_side_effects=True, vmem_limit_bytes=VMEM
        ),
        name="feed_forward",
    )(rows, context, cot, lengths, table, output_w, inner_w, outer_w)


def widen_kernel(splits, lines, *refs):
    count = len(splits)
    many = sum(splits)
    ins, table, outs = refs[:count], refs[count], refs[count + 1 : count + 1 + many]
    vectors = refs[count + 1 + many : count + 1 + many + len(lines)]
    rest = refs[count + 1 + many + len(lines) :]
    narrow, held, wides = rest[:count], rest[count], rest[count + 1 : count + 1 + many]
    load, save = rest[-2:]
    loads = [
        pltpu.make_async_copy(here, there, load.at[k])
        for k, (here, there) in enumerate(zip(ins + (table,), narrow + (held,)))
    ]
    for copy in loads:
        copy.start()
    copies = []
    at = 0
    for k, parts in enumerate(splits):
        loads[k].wait()
        columns = narrow[k].shape[-1] // parts
        for part in range(parts):
            wides[at][...] = narrow[k][..., part * columns : (part + 1) * columns].astype(
                wides[at].dtype
            )
            copies.append(pltpu.make_async_copy(wides[at], outs[at], save.at[at]))
            copies[-1].start()
            at += 1
    loads[count].wait()
    row = 0
    for vector, extent in zip(vectors, lines):
        for line in range(extent):
            copies.append(
                pltpu.make_async_copy(
                    held.at[row], vector.at[pl.ds(line * LANES, LANES)], save.at[many + row]
                )
            )
            copies[-1].start()
            row += 1
    for copy in copies:
        copy.wait()


def widen(arrays, splits, types, table, lines):
    shapes = []
    for array, parts, kind in zip(arrays, splits, types):
        shape = array.shape[:-1] + (array.shape[-1] // parts,)
        shapes += [jax.ShapeDtypeStruct(shape, kind)] * parts
    far = pl.BlockSpec(memory_space=pltpu.HBM)
    return pl.pallas_call(
        functools.partial(widen_kernel, splits, lines),
        out_shape=shapes + [jax.ShapeDtypeStruct((k * LANES,), F32) for k in lines],
        in_specs=[far] * (len(arrays) + 1),
        out_specs=[far] * (len(shapes) + len(lines)),
        scratch_shapes=[pltpu.VMEM(array.shape, array.dtype) for array in arrays + (table,)]
        + [pltpu.VMEM(shape.shape, shape.dtype) for shape in shapes]
        + [
            pltpu.SemaphoreType.DMA((len(arrays) + 1,)),
            pltpu.SemaphoreType.DMA((len(shapes) + sum(lines),)),
        ],
        compiler_params=pltpu.CompilerParams(vmem_limit_bytes=VMEM),
        name="widen_results",
    )(*arrays, table)


def stack_heads(block, lower):
    zero = jnp.zeros_like(block)
    return jnp.concatenate((jnp.where(lower, block, zero), jnp.where(lower, zero, block)), axis=0)


def repeat(first, stop, action):
    def step(i, carry):
        action(i)
        return carry

    lax.fori_loop(first, stop, step, 0)


GROUPS = 4
HALVES = 2


SPAN = 2 * HEAD_DIM


def span_of(section, pair, width):
    return pl.ds(pl.multiple_of(section * width + pair * SPAN, SPAN), SPAN)


class AttentionForward:
    def __init__(self, place, rows, weight, vec, bias, qkv, context, probs, held, away, send, recv, save):
        self.place, self.rows, self.weight, self.vec, self.bias = place, rows, weight, vec, bias
        self.qkv, self.context, self.probs, self.held, self.away = qkv, context, probs, held, away
        self.send, self.recv, self.save = send, recv, save
        self.count, self.width = context.shape
        self.pairs = self.width // SPAN

    def save_probs(self, pair):
        return pltpu.make_async_copy(self.held.at[pair], self.probs.at[pair], self.save.at[pair])

    def fetch(self, which, pair):
        return pltpu.make_async_remote_copy(
            self.qkv.at[:, span_of(which + 1, pair, self.width)],
            self.away.at[:, span_of(which, pair, self.width)],
            self.send.at[which, pair],
            self.recv.at[which, pair],
            device_id=self.place.twin(),
            device_id_type=MESH,
        )

    def project(self, section):
        tile = 512
        rows = self.rows[...].reshape(self.count, self.width)

        def one(t):
            columns = pl.ds(pl.multiple_of(section * self.width + t * tile, tile), tile)
            product = plain_product(rows, self.weight[:, columns])
            if section != 1:
                row = ROW_QUERY if section == 0 else ROW_VALUE
                product = product + self.vec[
                    pl.ds(row, 1), pl.ds(pl.multiple_of(t * tile, tile), tile)
                ]
            self.qkv[:, columns] = product.astype(BF16)

        repeat(0, self.width // tile, one)

    def give(self, which):
        for pair in range(self.pairs):
            self.fetch(which, pair).start()

    def attend(self, pair):
        for which in range(2):
            self.fetch(which, pair).wait_recv()
        count = self.count
        lower = lax.broadcasted_iota(jnp.int32, (count, SPAN), 1) < HEAD_DIM

        def here(section):
            return self.qkv[:, span_of(section, pair, self.width)]

        def there(section):
            return self.away[:, span_of(section - 1, pair, self.width)]

        stacked = stack_heads(here(0) * HEAD_DIM**-0.5, lower)
        keys = jnp.concatenate((here(1), there(1)), axis=0)
        values = jnp.concatenate((here(2), there(2)), axis=0)
        scores = right_product(stacked, keys) + self.bias[:1, :]
        top = jnp.max(scores, axis=1, keepdims=True)
        weights = jnp.exp(scores - top)
        total = jnp.sum(weights, axis=1, keepdims=True)
        probs = (weights * (1.0 / total)).astype(BF16)
        self.held[pair] = probs
        self.save_probs(pair).start()
        mixed = plain_product(probs, values)
        self.context[:, span_of(0, pair, self.width)] = jnp.where(
            lower, mixed[:count], mixed[count:]
        ).astype(BF16)

    def attend_group(self, group):
        each = self.pairs // GROUPS
        repeat(group * each, (group + 1) * each, self.attend)

    def finish(self):
        for pair in range(self.pairs):
            for which in range(2):
                self.fetch(which, pair).wait_send()
            self.save_probs(pair).wait()


TABLE, QUERIES = 0, 1


def start_actions(gather, work, keep, swap, save, table_ref):
    found = gather.actions()
    others = [k for k in range(len(keep)) if k not in (TABLE, QUERIES)]

    def ready():
        gather.wait_twins((TABLE, QUERIES))
        for k in (TABLE, QUERIES):
            keep[k].wait()
        swap.finish()
        spread_table(table_ref, work.vec)
        save.start()

    def values():
        work.project(2)
        work.give(0)

    def queries():
        work.give(1)
        work.project(0)

    found.append((("ready",), ready))
    found.append((("project", 0), lambda: work.project(1)))
    found.append((("project", 1), values))
    found.append((("project", 2), queries))
    for group in range(GROUPS):
        found.append((("pa", group), lambda group=group: work.attend_group(group)))

    def last():
        gather.finish(others)
        work.finish()
        for k in others:
            keep[k].wait()
        save.wait()

    found.append((("last",), last))
    return found


def start_kernel(flows, spots, order, *refs):
    count = max(array for array, _ in spots) + 1
    shares, refs = refs[: len(spots)], refs[len(spots) :]
    (in_block, lengths_ref), refs = refs[:2], refs[2:]
    table_ref, refs = refs[0], refs[1:]
    far, refs = refs[: count - 1], refs[count - 1 :]
    rows, qkv, context, probs, away = refs[:5]
    owns, refs = refs[5 : 5 + count], refs[5 + count :]
    weight, held, vec, bias = refs[:4]
    send, recv, local, load, send2, recv2, save2, saveq = refs[4:12]
    fulls = (table_ref, weight) + tuple(far[1:])
    place = Place()
    loads = [
        pltpu.make_async_copy(
            share, owns[array].at[:, pl.ds(column, share.shape[1])], load.at[k]
        )
        for k, (share, (array, column)) in enumerate(zip(shares, spots))
    ]
    for copy in loads:
        copy.start()
    keep = [
        pltpu.make_async_copy(
            own, full.at[pl.ds(pl.multiple_of(place.shard * own.shape[0], 16), own.shape[0]), :], local.at[k]
        )
        for k, (own, full) in enumerate(zip(owns, fulls))
    ]
    greet(place)
    rows_count = context.shape[0]
    length = lengths_ref[place.side]
    row = lax.broadcasted_iota(jnp.int32, (8, rows_count), 1)
    for k, core in enumerate((place.core, 1 - place.core)):
        bias[:, pl.ds(k * rows_count, rows_count)] = jnp.where(
            row_place(row, core, rows_count) < length, 0.0, -1e30
        )
    for copy in loads:
        copy.wait()
    swap = Swap(place, [in_block], [rows], *refs[12:15])
    swap.start()
    gather = Gather(place, flows, owns, fulls, send, recv)
    for copy in keep:
        copy.start()
    work = AttentionForward(
        place, rows, weight, vec, bias, qkv, context, probs, held, away, send2, recv2, save2
    )
    save = pltpu.make_async_copy(weight, far[0], saveq.at[0])
    for step in in_order(start_actions(gather, work, keep, swap, save, table_ref), order):
        step()


def start(shares, spots, block, lengths, flows, shards, collective_id, order):
    labels = gather_labels(flows)
    count = max(array for array, _ in spots) + 1
    shapes = []
    for array in range(count):
        members = [share for share, spot in zip(shares, spots) if spot[0] == array]
        shapes.append((members[0].shape[0], sum(m.shape[1] for m in members)))
    _, block_len, width = block.shape
    rows = 2 * block_len
    pairs = width // SPAN
    far = pl.BlockSpec(memory_space=pltpu.HBM)
    whole = pl.BlockSpec(memory_space=pltpu.VMEM)
    probs_shape = (pairs, 2 * rows, 2 * rows)
    return pl.pallas_call(
        functools.partial(start_kernel, flows, spots, order),
        out_shape=[jax.ShapeDtypeStruct((shards * r, c), BF16) for r, c in shapes]
        + [
            jax.ShapeDtypeStruct(block.shape, BF16),
            jax.ShapeDtypeStruct((rows, 3 * width), BF16),
            jax.ShapeDtypeStruct((rows, width), BF16),
            jax.ShapeDtypeStruct(probs_shape, BF16),
            jax.ShapeDtypeStruct((rows, 2 * width), BF16),
        ],
        in_specs=[far] * (len(shares) + 1) + [pl.BlockSpec(memory_space=pltpu.SMEM)],
        out_specs=[whole] + [far] * (count - 1) + [whole, whole, whole, far, whole],
        scratch_shapes=[pltpu.VMEM(shape, BF16) for shape in shapes]
        + [
            pltpu.VMEM((shards * shapes[QUERIES][0], shapes[QUERIES][1]), BF16),
            pltpu.VMEM(probs_shape, BF16),
            pltpu.VMEM((TABLE_ROWS, width), F32),
            pltpu.VMEM((8, 2 * rows), F32),
            pltpu.SemaphoreType.DMA((len(labels.numbers),)),
            pltpu.SemaphoreType.DMA((len(labels.numbers),)),
            pltpu.SemaphoreType.DMA((count,)),
            pltpu.SemaphoreType.DMA((len(shares),)),
            pltpu.SemaphoreType.DMA((2, pairs)),
            pltpu.SemaphoreType.DMA((2, pairs)),
            pltpu.SemaphoreType.DMA((pairs,)),
            pltpu.SemaphoreType.DMA((1,)),
        ]
        + swap_scratch(1),
        compiler_params=pltpu.CompilerParams(
            collective_id=collective_id, has_side_effects=True, vmem_limit_bytes=VMEM
        ),
        name="gather_attention_forward",
    )(*shares, block, lengths)


class AttentionBackward:
    def __init__(self, place, qkv, away, grad, out, keep, leave, come, send, recv):
        self.place, self.qkv, self.away, self.grad = place, qkv, away, grad
        self.out, self.keep, self.leave, self.come = out, keep, leave, come
        self.send, self.recv = send, recv
        self.count, self.width = grad.shape
        self.pairs = self.width // SPAN

    def give(self, which, pair):
        return pltpu.make_async_remote_copy(
            self.leave.at[:, span_of(which, pair, self.width)],
            self.come.at[:, span_of(which, pair, self.width)],
            self.send.at[which, pair],
            self.recv.at[which, pair],
            device_id=self.place.twin(),
            device_id_type=MESH,
        )

    def attend(self, pair, probs):
        count = self.count
        lower = lax.broadcasted_iota(jnp.int32, (count, SPAN), 1) < HEAD_DIM
        scale = HEAD_DIM**-0.5

        def here(section):
            return self.qkv[:, span_of(section, pair, self.width)]

        def there(section):
            return self.away[:, span_of(section - 1, pair, self.width)]

        first = span_of(0, pair, self.width)
        second = span_of(1, pair, self.width)
        stacked = stack_heads(here(0) * scale, lower)
        keys = jnp.concatenate((here(1), there(1)), axis=0)
        values = jnp.concatenate((here(2), there(2)), axis=0)
        grad = stack_heads(self.grad[:, first], lower)
        value_part = left_product(probs, grad)
        probs_grad = right_product(grad, values)
        wide = probs.astype(F32)
        inner = jnp.sum(wide * probs_grad, axis=1, keepdims=True)
        scores_grad = (wide * (probs_grad - inner)).astype(BF16)
        key_part = left_product(scores_grad, stacked)
        self.leave[:, first] = key_part[count:].astype(BF16)
        self.leave[:, second] = value_part[count:].astype(BF16)
        self.keep[:, first] = key_part[:count]
        self.keep[:, second] = value_part[:count]
        mixed = plain_product(scores_grad, keys) * scale
        self.out[:, first] = jnp.where(lower, mixed[:count], mixed[count:]).astype(BF16)
        for which in range(2):
            self.give(which, pair).start()

    def settle(self, pair):
        for which in range(2):
            self.give(which, pair).wait_recv()
            here = span_of(which, pair, self.width)
            self.out[:, span_of(which + 1, pair, self.width)] = (
                self.keep[:, here] + self.come[:, here].astype(F32)
            ).astype(BF16)

    def finish(self):
        for pair in range(self.pairs):
            for which in range(2):
                self.give(which, pair).wait_send()


class Finish:
    def __init__(self, work, tiles, weight, rows_ref, rows_t, first_grad, total, block, sums, held, probs, load, sems):
        self.work, self.tiles, self.weight, self.rows_ref, self.rows_t = work, tiles, weight, rows_ref, rows_t
        self.total, self.block, self.sums = total, block, sums
        self.held, self.probs, self.load, self.sems = held, probs, load, sems
        self.grad_load = pltpu.make_async_copy(first_grad, total, sems.at[held.shape[0]])
        self.count, self.width = total.shape
        self.tile = tiles.shape[2]

    def weight_load(self, t):
        columns = pl.ds(pl.multiple_of(t * self.tile, self.tile), self.tile)
        slot = lax.rem(t, self.tiles.shape[0])
        return pltpu.make_async_copy(
            self.weight.at[:, columns], self.tiles.at[slot], self.load.at[slot]
        )

    def probs_load(self, pair):
        slot = lax.rem(pair, self.held.shape[0])
        return pltpu.make_async_copy(
            self.probs.at[pair], self.held.at[slot], self.sems.at[slot]
        )

    def begin(self):
        for pair in range(self.held.shape[0]):
            self.probs_load(pair).start()
        for t in range(self.tiles.shape[0]):
            self.weight_load(t).start()
        self.grad_load.start()

    def attend(self, group):
        each = self.work.pairs // GROUPS

        slots = self.held.shape[0]

        def one(pair):
            self.probs_load(pair).wait()
            self.work.attend(pair, self.held[lax.rem(pair, slots)])
            pl.when(pair + slots < self.work.pairs)(self.probs_load(pair + slots).start)

        repeat(group * each, (group + 1) * each, one)

    def settle(self):
        repeat(0, self.work.pairs, self.work.settle)

    def weigh(self, core, target):
        shards, rows, columns = target.shape
        tile = self.tile

        def one(j):
            start = pl.multiple_of(core * columns + j * tile, tile)
            product = plain_product(self.rows_t[...], self.work.out[:, pl.ds(start, tile)])
            low = product.astype(BF16)
            for shard in range(shards):
                target[shard, :, pl.ds(pl.multiple_of(j * tile, tile), tile)] = low[
                    shard * rows : (shard + 1) * rows
                ]

        repeat(0, columns // tile, one)

    def turn(self):
        self.rows_t[...] = self.rows_ref[...].T

    def bias_sums(self, target):
        self.sums[pl.ds(0, 1), :] = total_rows(self.work.out[:, : self.width])
        self.sums[pl.ds(1, 1), :] = total_rows(self.work.out[:, 2 * self.width :])
        for shard in range(target.shape[0]):
            target[shard, pl.ds(ROW_QUERY, 2), :] = self.sums[
                pl.ds(0, 2), pl.ds(shard * LANES, LANES)
            ]

    def spread(self, half):
        count = self.weight.shape[1] // self.tile
        each = count // HALVES
        slots = self.tiles.shape[0]
        if half == 0:
            self.grad_load.wait()

        def one(t):
            self.weight_load(t).wait()
            columns = pl.ds(pl.multiple_of(t * self.tile, self.tile), self.tile)
            tile = self.tiles[lax.rem(t, slots)]
            self.total[...] += right_product(self.work.out[:, columns], tile)
            pl.when(t + slots < count)(self.weight_load(t + slots).start)

        repeat(half * each, (half + 1) * each, one)
        if half == HALVES - 1:
            rows = self.block.shape[1]
            for part in range(2):
                self.block[part] = self.total[pl.ds(part * rows, rows), :].astype(BF16)


def finish_actions(reduce, finish, swap):
    queries, vectors = 3, 4
    place = reduce.place
    found = reduce.actions()

    def load():
        finish.begin()
        finish.turn()

    found.append((("load",), load))
    for group in range(GROUPS):
        found.append((("att", group), lambda group=group: finish.attend(group)))
    found.append((("settleatt",), finish.settle))
    found.append((("leave",), lambda: finish.weigh(1 - place.core, reduce.grads[queries])))
    found.append((("own",), lambda: finish.weigh(place.core, reduce.own[queries])))
    found.append((("sums",), lambda: finish.bias_sums(reduce.own[vectors])))
    for half in range(HALVES):
        found.append((("dx", half), lambda half=half: finish.spread(half)))
    found.append((("swapin",), swap.start))
    return found


def finish_kernel(parts, order, *refs):
    rows_ref, qkv, away, grad, table_ref, first_grad, probs, weight = refs[:8]
    grads = list(refs[8:11])
    outs, swapped, refs = refs[11:16], refs[16], refs[17:]
    leave_q, tiles, held, out, keep, leave, come, total, sums, rows_t, block = refs[:11]
    send2, recv2, load2, sems = refs[11:15]
    scratch, rest = refs[15:-6], refs[-6:]
    place = Place()
    work = AttentionBackward(place, qkv, away, grad, out, keep, leave, come, send2, recv2)
    finish = Finish(
        work, tiles, weight, rows_ref, rows_t, first_grad, total, block, sums, held, probs, load2, sems
    )
    reduce = Reduce(place, parts, grads + [leave_q, None], outs, scratch, *rest[:3])
    swap = Swap(place, [block], [swapped], *rest[3:6])
    for shard in range(LINE * PAIR):
        reduce.own[4][shard] = table_ref[pl.ds(shard * TABLE_ROWS, TABLE_ROWS), :]
    greet(place)
    for step in in_order(finish_actions(reduce, finish, swap), order):
        step()
    work.finish()
    swap.finish()


def finish(rows, saved, grad, first_grad, table, weight, grads, parts, collective_id, order):
    qkv, away, probs = saved
    count, width = rows.shape
    pairs = width // SPAN
    tile = 512
    labels = reduce_labels(parts)
    whole = pl.BlockSpec(memory_space=pltpu.VMEM)
    far = pl.BlockSpec(memory_space=pltpu.HBM)
    queries = parts[3]
    return pl.pallas_call(
        functools.partial(finish_kernel, parts, order),
        out_shape=[jax.ShapeDtypeStruct((p.rows, p.columns), p.dtype) for p in parts]
        + [jax.ShapeDtypeStruct((2, count // 2, width), BF16)],
        in_specs=[whole] * 5 + [far] * 6,
        out_specs=[whole] * len(parts) + [far],
        scratch_shapes=[
            pltpu.VMEM((LINE * PAIR, queries.half_rows, queries.half_columns), BF16),
            pltpu.VMEM((2, width, tile), BF16),
            pltpu.VMEM((pairs // 2,) + probs.shape[1:], BF16),
            pltpu.VMEM((count, 3 * width), BF16),
            pltpu.VMEM((count, 2 * width), F32),
            pltpu.VMEM((count, 2 * width), BF16),
            pltpu.VMEM((count, 2 * width), BF16),
            pltpu.VMEM((count, width), F32),
            pltpu.VMEM((8, width), F32),
            pltpu.VMEM((width, count), BF16),
            pltpu.VMEM((2, count // 2, width), BF16),
            pltpu.SemaphoreType.DMA((2, pairs)),
            pltpu.SemaphoreType.DMA((2, pairs)),
            pltpu.SemaphoreType.DMA((2,)),
            pltpu.SemaphoreType.DMA((pairs // 2 + 1,)),
        ]
        + reduce_scratch(parts)
        + [
            pltpu.SemaphoreType.DMA((len(labels.numbers),)),
            pltpu.SemaphoreType.DMA((len(labels.numbers),)),
            pltpu.SemaphoreType.DMA((len(parts) * 2 * len(SPOTS),)),
        ]
        + swap_scratch(1),
        compiler_params=pltpu.CompilerParams(
            collective_id=collective_id, has_side_effects=True, vmem_limit_bytes=VMEM
        ),
        name="attention_backward_reduce",
    )(rows, qkv, away, grad, table, first_grad, probs, weight, *grads)


def exact_gelu(hidden):
    return jax.nn.gelu(hidden, approximate=False)


def plain_product(left, right):
    return jnp.dot(left, right, preferred_element_type=F32)


def left_product(left, right):
    return lax.dot_general(left, right, (((0,), (0,)), ((), ())), preferred_element_type=F32)


def right_product(left, right):
    return lax.dot_general(left, right, (((1,), (1,)), ((), ())), preferred_element_type=F32)


def column_sums(rows):
    return jnp.sum(rows.astype(F32), axis=0)


def norm_parts(total):
    average = jnp.mean(total, axis=-1, keepdims=True)
    centered = total - average
    variance = jnp.mean(centered * centered, axis=-1, keepdims=True)
    rate = lax.rsqrt(variance + EPSILON)
    return centered * rate, rate


def norm_back(unit, rate, grad):
    return rate * (
        grad
        - jnp.mean(grad, axis=-1, keepdims=True)
        - unit * jnp.mean(grad * unit, axis=-1, keepdims=True)
    )


def split_columns(packed, widths):
    pieces = []
    start = 0
    for width in widths:
        pieces.append(packed[..., start : start + width])
        start += width
    return pieces


def native_forward(queries, keys_all, values_all, key_valid, heads):
    shape = queries.shape[:2] + (heads, HEAD_DIM)
    key_shape = keys_all.shape[:2] + (heads, HEAD_DIM)
    scores = jnp.einsum(
        "sqhd,skhd->shqk",
        queries.reshape(shape),
        keys_all.reshape(key_shape),
        preferred_element_type=F32,
    ) * (HEAD_DIM**-0.5)
    scores = jnp.where(key_valid[:, None, None, :], scores, -1e30)
    top = jnp.max(scores, axis=-1, keepdims=True)
    weights = jnp.exp(scores - top)
    probs = (weights / jnp.sum(weights, axis=-1, keepdims=True)).astype(BF16)
    context = jnp.einsum(
        "shqk,skhd->sqhd", probs, values_all.reshape(key_shape), preferred_element_type=F32
    )
    return context.reshape(queries.shape).astype(BF16), probs


def native_backward(queries, keys_all, values_all, probs, context_grad, heads):
    shape = queries.shape[:2] + (heads, HEAD_DIM)
    key_shape = keys_all.shape[:2] + (heads, HEAD_DIM)
    scale = HEAD_DIM**-0.5
    grad_heads = context_grad.reshape(shape)
    wide = probs.astype(F32)
    probs_grad = jnp.einsum(
        "sqhd,skhd->shqk", grad_heads, values_all.reshape(key_shape), preferred_element_type=F32
    )
    inner_total = jnp.sum(wide * probs_grad, axis=-1, keepdims=True)
    scores_grad = (wide * (probs_grad - inner_total)).astype(BF16)
    query_grad = jnp.einsum(
        "shqk,skhd->sqhd", scores_grad, keys_all.reshape(key_shape), preferred_element_type=F32
    )
    key_part = jnp.einsum(
        "shqk,sqhd->skhd", scores_grad, queries.reshape(shape), preferred_element_type=F32
    )
    value_part = jnp.einsum("shqk,sqhd->skhd", probs, grad_heads, preferred_element_type=F32)
    return (
        (query_grad * scale).astype(BF16).reshape(queries.shape),
        (key_part * scale).astype(BF16).reshape(keys_all.shape),
        value_part.astype(BF16).reshape(values_all.shape),
    )


def gather_rows(part):
    return lax.all_gather(part, "fsdp", axis=0, tiled=True)


def reduce_rows(part):
    share = lax.psum_scatter(part.astype(BF16), "fsdp", scatter_dimension=0, tiled=True)
    return lax.psum(share, "ctx").astype(F32)


def layer(flat_rows, cot_rows, row_mask, packed, widths, weights, forward, backward):
    full_qkv, full_output, full_inner, full_outer = weights
    rows, width = flat_rows.shape
    shards = packed.shape[0]
    (
        bias_query,
        bias_value,
        bias_output,
        gain_first,
        shift_first,
        bias_inner,
        bias_outer,
        gain_second,
        shift_second,
    ) = [piece.reshape(-1).astype(F32) for piece in split_columns(packed, widths)]
    bias_qkv = jnp.concatenate((bias_query, jnp.zeros_like(bias_query), bias_value))
    qkv = (plain_product(flat_rows, full_qkv) + bias_qkv).astype(BF16)
    context, saved = forward(qkv)

    first_sum = flat_rows.astype(F32) + plain_product(context, full_output) + bias_output
    first_unit, first_rate = norm_parts(first_sum)
    normed = first_unit * gain_first + shift_first
    normed_low = normed.astype(BF16)
    hidden = plain_product(normed_low, full_inner) + bias_inner
    active, gelu_back = jax.vjp(exact_gelu, hidden)
    active_low = active.astype(BF16)
    second_sum = normed + plain_product(active_low, full_outer) + bias_outer
    second_unit, second_rate = norm_parts(second_sum)
    output = ((second_unit * gain_second + shift_second) * row_mask).astype(BF16)

    out_grad = cot_rows.astype(F32) * row_mask
    second_gain_part = jnp.sum(out_grad * second_unit, axis=0)
    second_shift_part = jnp.sum(out_grad, axis=0)
    second_grad = norm_back(second_unit, second_rate, out_grad * gain_second)
    second_low = second_grad.astype(BF16)
    outer_weight_part = left_product(active_low, second_low).astype(BF16)
    outer_bias_part = column_sums(second_low)
    (hidden_grad,) = gelu_back(right_product(second_low, full_outer))
    hidden_low = hidden_grad.astype(BF16)
    inner_weight_part = left_product(normed_low, hidden_low).astype(BF16)
    inner_bias_part = column_sums(hidden_low)
    normed_grad = second_grad + right_product(hidden_low, full_inner)
    first_gain_part = jnp.sum(normed_grad * first_unit, axis=0)
    first_shift_part = jnp.sum(normed_grad, axis=0)
    first_grad = norm_back(first_unit, first_rate, normed_grad * gain_first)
    branch_low = first_grad.astype(BF16)
    output_weight_part = left_product(context, branch_low).astype(BF16)
    output_bias_part = column_sums(branch_low)
    context_grad = right_product(branch_low, full_output).astype(BF16)
    qkv_grad = backward(saved, context_grad)
    qkv_weight_part = left_product(flat_rows, qkv_grad).astype(BF16)
    query_bias_part = column_sums(qkv_grad[:, :width])
    value_bias_part = column_sums(qkv_grad[:, 2 * width :])
    input_grad = first_grad + right_product(qkv_grad, full_qkv)
    vector_parts = (
        query_bias_part,
        value_bias_part,
        output_bias_part,
        first_gain_part,
        first_shift_part,
        inner_bias_part,
        outer_bias_part,
        second_gain_part,
        second_shift_part,
    )
    packed_parts = jnp.concatenate([part.reshape(shards, -1) for part in vector_parts], axis=1)
    return (
        output,
        input_grad,
        packed_parts,
        (qkv_weight_part, output_weight_part, inner_weight_part, outer_weight_part),
    )


def native_body(inputs, cotangent, lengths, vectors, weights):
    widths = [member.shape[0] for member in vectors]
    packed = lax.all_gather(jnp.concatenate(vectors), "fsdp", axis=0, tiled=False)
    joined = (jnp.concatenate(weights[:3], axis=1),) + weights[3:]
    full = tuple(gather_rows(part) for part in joined)
    micro, seqs, block_len, width = inputs.shape
    heads = width // HEAD_DIM
    total_slots = block_len * lax.axis_size("ctx")
    group = micro * seqs
    rows = group * block_len
    flat_len = lengths.reshape(group)
    local_pos = lax.axis_index("ctx") * block_len + jnp.arange(block_len, dtype=jnp.int32)
    row_mask = (local_pos[None, :] < flat_len[:, None]).astype(F32).reshape(rows, 1)
    key_valid = jnp.arange(total_slots, dtype=jnp.int32)[None, :] < flat_len[:, None]

    def forward(qkv):
        queries = qkv[:, :width].reshape(group, block_len, width)
        keys_values = lax.all_gather(
            qkv[:, width:].reshape(group, block_len, 2 * width), "ctx", axis=1, tiled=True
        )
        keys, values = keys_values[:, :, :width], keys_values[:, :, width:]
        context, probs = native_forward(queries, keys, values, key_valid, heads)
        return context.reshape(rows, width), (queries, keys, values, probs)

    def backward(saved, context_grad):
        query_grad, key_part, value_part = native_backward(
            *saved, context_grad.reshape(group, block_len, width), heads
        )
        keys_values_grad = lax.psum_scatter(
            jnp.concatenate((key_part, value_part), axis=2), "ctx", scatter_dimension=1, tiled=True
        )
        return jnp.concatenate(
            (query_grad.reshape(rows, width), keys_values_grad.reshape(rows, 2 * width)), axis=1
        )

    output, input_grad, packed_parts, parts = layer(
        inputs.reshape(rows, width),
        cotangent.reshape(rows, width),
        row_mask,
        packed,
        widths,
        full,
        forward,
        backward,
    )
    share = lax.psum_scatter(packed_parts, "fsdp", scatter_dimension=0, tiled=True)
    return (
        output.reshape(inputs.shape),
        input_grad.reshape(inputs.shape),
        split_columns(lax.psum(share, "ctx")[0], widths),
        tuple(split_columns(reduce_rows(parts[0]), [width] * 3))
        + tuple(reduce_rows(part) for part in parts[1:]),
    )


def direct_body(inputs, cotangent, lengths, vectors, weights):
    micro, seqs, block_len, width = inputs.shape
    shards = LINE * PAIR
    lengths = lengths.reshape(micro)
    rows = 2 * block_len
    table = jnp.zeros((TABLE_ROWS, LANES), F32)
    row = 0
    for vector in vectors:
        lines = vector.shape[0] // LANES
        filled = ((row, TABLE_ROWS - row - lines), (0, 0))
        table += jnp.pad(vector.astype(F32).reshape(lines, LANES), filled)
        row += lines
    query_weight, key_weight, value_weight, output_weight, inner_weight, outer_weight = weights
    shard_rows, hidden = inner_weight.shape
    flows = [Flow(0, TABLE_ROWS, lambda core, side: (0, TABLE_ROWS, 0, LANES), cores=False)]
    flows += column_flows(1, shard_rows, 3 * width, *GATHER_SPLIT[0])
    flows += column_flows(2, shard_rows, width, *GATHER_SPLIT[1])
    flows += column_flows(3, shard_rows, hidden, *GATHER_SPLIT[2])
    flows += row_flows(4, hidden // shards, width, *GATHER_SPLIT[3])
    (
        tables,
        full_qkv,
        full_output,
        full_inner,
        full_outer,
        in_rows,
        qkv,
        context,
        probs,
        away,
    ) = start(
        (table.astype(BF16),) + weights,
        ((0, 0), (1, 0), (1, width), (1, 2 * width), (2, 0), (3, 0), (4, 0)),
        inputs.reshape(micro, block_len, width),
        lengths,
        flows,
        shards,
        1,
        GATHER_ORDER,
    )
    in_rows = in_rows.reshape(rows, width)
    output, first_grad, context_grad, table_grad, output_part, inner_part, outer_part = middle(
        3,
        in_rows,
        context,
        cotangent.reshape(micro, block_len, width),
        lengths,
        tables,
        full_output,
        full_inner,
        full_outer,
    )
    sums = finish(
        in_rows,
        (qkv, away, probs),
        context_grad,
        first_grad,
        table_grad,
        full_qkv,
        (inner_part, outer_part, output_part),
        [
            column_part(shard_rows, hidden, *REDUCE_SPLIT[0]),
            row_part(hidden // shards, width, *REDUCE_SPLIT[1]),
            column_part(shard_rows, width, *REDUCE_SPLIT[2]),
            column_part(shard_rows, 3 * width, *REDUCE_SPLIT[3], inside=True),
            vector_part(TABLE_ROWS, LANES, inside=True),
        ],
        2,
        REDUCE_ORDER,
    )
    inner_share, outer_share, output_share, qkv_share, table_share, grads = sums
    lines = tuple(vector.shape[0] // LANES for vector in vectors)
    wide = widen(
        (qkv_share, output_share, inner_share, outer_share, grads, output),
        (3, 1, 1, 1, 1, 1),
        (F32,) * 5 + (BF16,),
        table_share,
        lines,
    )
    return (
        wide[7].reshape(inputs.shape),
        wide[6].reshape(inputs.shape),
        tuple(wide[8:]),
        tuple(wide[:6]),
    )


def body(
    inputs,
    cotangent,
    lengths,
    query_weight,
    key_weight,
    value_weight,
    output_weight,
    query_bias,
    value_bias,
    output_bias,
    first_gain,
    first_shift,
    inner_weight,
    inner_bias,
    outer_weight,
    outer_bias,
    second_gain,
    second_shift,
):
    vectors = (
        query_bias,
        value_bias,
        output_bias,
        first_gain,
        first_shift,
        inner_bias,
        outer_bias,
        second_gain,
        second_shift,
    )
    widths = [member.shape[0] for member in vectors]
    weights = (
        query_weight,
        key_weight,
        value_weight,
        output_weight,
        inner_weight,
        outer_weight,
    )
    laid_out = lax.axis_size("fsdp") == LINE * PAIR and lax.axis_size("ctx") == 4
    whole_lines = all(extent % LANES == 0 for extent in widths)
    direct = laid_out and inputs.shape[:2] == (2, 1) and whole_lines
    run = direct_body if direct else native_body
    output, input_grad, shares, weight_shares = run(inputs, cotangent, lengths, vectors, weights)
    query_share, key_share, value_share, output_share, inner_share, outer_share = weight_shares
    return (
        output,
        input_grad,
        query_share,
        key_share,
        value_share,
        output_share,
        shares[0],
        shares[1],
        shares[2],
        shares[3],
        shares[4],
        inner_share,
        shares[5],
        outer_share,
        shares[6],
        shares[7],
        shares[8],
    )


def solution(mesh):
    data = P(None, "fsdp", "ctx", None)
    matrix = P("fsdp", None)
    vector = P("fsdp")
    return jax.shard_map(
        body,
        mesh=mesh,
        in_specs=(data, data, P(None, "fsdp"))
        + (matrix,) * 4
        + (vector,) * 5
        + (matrix, vector, matrix, vector, vector, vector),
        out_specs=(data, data)
        + (matrix,) * 4
        + (vector,) * 5
        + (matrix, vector, matrix, vector, vector, vector),
        check_vma=False,
    )
```

```python
import functools

import jax
import jax.numpy as jnp
from jax import lax
from jax.experimental import pallas as pl
from jax.experimental.pallas import tpu as pltpu
from jax.sharding import PartitionSpec as P

HEAD_DIM = 64
EPSILON = 1e-06
F32 = jnp.float32
BF16 = jnp.bfloat16

GATHER_SPLIT = ((256, 384), (256, 128), (1024, 128), (128, 64))
REDUCE_SPLIT = ((1024, 384), (160, 0), (256, 128), (768, 256))
GATHER_ORDER = (
    2, 3, 7, 64, 0, 10, 30, 72, 132, 1, 5, 38, 28, 200, 140, 43, 29, 77, 62, 15, 111, 98, 96, 8,
    179, 32, 63, 180, 217, 69, 66, 164, 166, 81, 208, 40, 97, 134, 137, 99, 131, 4, 55, 145, 74,
    100, 149, 39, 47, 183, 202, 83, 68, 9, 108, 34, 31, 213, 205, 148, 49, 12, 115, 106, 114, 45,
    142, 136, 13, 151, 35, 46, 16, 48, 76, 204, 162, 230, 219, 203, 42, 130, 41, 117, 85, 17, 82,
    102, 6, 184, 168, 174, 138, 101, 84, 116, 167, 201, 123, 152, 103, 143, 89, 144, 118, 94, 198,
    165, 78, 222, 185, 169, 153, 14, 220, 70, 33, 128, 86, 50, 175, 23, 110, 107, 75, 199, 181,
    65, 79, 25, 171, 67, 225, 147, 37, 218, 135, 71, 133, 150, 90, 191, 157, 176, 21, 196, 154,
    52, 20, 18, 209, 120, 80, 206, 216, 192, 26, 60, 36, 170, 113, 231, 24, 182, 163, 141, 11,
    186, 56, 215, 232, 22, 95, 59, 233, 178, 93, 214, 212, 51, 210, 91, 234, 223, 235, 197, 105,
    158, 161, 226, 19, 127, 57, 53, 139, 236, 73, 119, 159, 195, 221, 27, 188, 211, 146, 44, 87,
    237, 173, 121, 229, 124, 58, 112, 109, 54, 160, 177, 88, 129, 92, 61, 125, 155, 207, 172, 238,
    122, 227, 104, 126, 156, 193, 189, 187, 239, 228, 190, 194, 224, 240,
)
REDUCE_ORDER = (
    33, 7, 9, 0, 8, 215, 84, 10, 85, 216, 1, 87, 86, 12, 5, 100, 29, 4, 102, 103, 101, 2, 217, 16,
    91, 92, 89, 11, 35, 218, 36, 3, 40, 106, 107, 93, 37, 18, 94, 39, 219, 88, 42, 31, 38, 220,
    221, 43, 24, 22, 25, 23, 110, 15, 17, 28, 26, 96, 44, 222, 153, 67, 68, 150, 151, 53, 57, 21,
    13, 6, 14, 104, 105, 154, 30, 152, 69, 189, 45, 108, 149, 19, 118, 95, 109, 71, 72, 223, 90,
    203, 198, 77, 201, 122, 167, 111, 120, 117, 183, 199, 41, 184, 181, 20, 119, 182, 165, 121,
    169, 156, 200, 47, 51, 73, 27, 157, 191, 54, 185, 46, 32, 155, 224, 225, 159, 226, 158, 171,
    97, 98, 55, 133, 124, 70, 79, 205, 141, 143, 75, 76, 74, 160, 186, 59, 161, 187, 139, 58, 61,
    135, 188, 112, 113, 48, 137, 49, 202, 52, 173, 206, 126, 114, 125, 193, 168, 166, 208, 34,
    123, 175, 162, 163, 190, 127, 99, 78, 192, 134, 172, 207, 56, 50, 128, 209, 210, 129, 170,
    136, 80, 81, 138, 194, 60, 195, 115, 62, 63, 204, 130, 140, 131, 82, 177, 145, 196, 174, 176,
    64, 65, 144, 132, 116, 142, 178, 179, 164, 146, 147, 211, 212, 83, 180, 197, 66, 148, 213,
    214,
)

MESH = pl.DeviceIdType.MESH
LINE = 4
PAIR = 2


class Place:
    def __init__(self):
        self.ctx = lax.axis_index("ctx")
        self.shard = lax.axis_index("fsdp")
        self.side = lax.div(self.ctx, 2)
        self.core = lax.rem(self.ctx, 2)
        self.line = lax.div(self.shard, PAIR)
        self.pair = lax.rem(self.shard, PAIR)

    def ahead(self, way):
        return (self.ctx, self.shard + way * PAIR)

    def across(self):
        return (self.ctx, self.shard + 1 - 2 * self.pair)

    def beside(self):
        return (self.ctx + 2 - 4 * self.side, self.shard)

    def twin(self):
        return (self.ctx + 1 - 2 * self.core, self.shard)

    def has(self, way, steps):
        if steps == 0:
            return None
        return self.line >= steps if way > 0 else self.line <= LINE - 1 - steps

    def can(self, way):
        return self.line <= LINE - 2 if way > 0 else self.line >= 1

    def shard_of(self, way, steps, other):
        pair = 1 - self.pair if other else self.pair
        return (self.line - way * steps) * PAIR + pair


def when(conditions, action):
    held = [c for c in conditions if c is not None]
    if not held:
        action()
        return
    both = held[0]
    for c in held[1:]:
        both = jnp.logical_and(both, c)
    pl.when(both)(action)


def greet(place):
    barrier = pltpu.get_barrier_semaphore()
    for peer in (place.across(), place.beside(), place.twin()):
        pl.semaphore_signal(barrier, inc=1, device_id=peer, device_id_type=MESH)
    for way in (1, -1):
        when(
            [place.can(way)],
            lambda way=way: pl.semaphore_signal(
                barrier, inc=1, device_id=place.ahead(way), device_id_type=MESH
            ),
        )
    lines = jnp.minimum(place.line, 1) + jnp.minimum(LINE - 1 - place.line, 1)
    pl.semaphore_wait(barrier, 3 + lines)


class Flow:
    def __init__(self, array, shard_rows, region, order="line", sides=False, cores=True):
        self.array = array
        self.shard_rows = shard_rows
        self.region = region
        self.order = order
        self.sides = sides
        self.cores = cores

    def view(self, ref, shard, core, side):
        row, rows, column, columns = self.region(core, side)
        start = row if shard is None else shard * self.shard_rows + row
        if not isinstance(start, int):
            start = pl.multiple_of(start, 16)
        if not isinstance(column, int):
            column = pl.multiple_of(column, 128)
        return ref.at[pl.ds(start, rows), pl.ds(column, columns)]


def positions(order):
    found = []
    if order == "line":
        found.append(("P", 1, 0, True))
        for steps in range(1, LINE):
            for way in (1, -1):
                found.append(("L", way, steps, False))
                found.append(("P", way, steps, True))
    else:
        found.append(("P", 1, 0, True))
        for steps in range(1, LINE):
            for way in (1, -1):
                found.append(("L", way, steps, False))
                found.append(("L", way, steps, True))
    return found


class Labels:
    def __init__(self):
        self.numbers = {}

    def __call__(self, key):
        return self.numbers.setdefault(key, len(self.numbers))


def gather_labels(flows):
    labels = Labels()
    for number, flow in enumerate(flows):
        for spot in positions(flow.order):
            labels((number, "in") + spot)
            if flow.sides:
                labels((number, "side") + spot)
            if flow.cores:
                labels((number, "twin") + spot)
                if flow.sides:
                    labels((number, "twinside") + spot)
    return labels


class Gather:
    def __init__(self, place, flows, owns, fulls, send, recv):
        self.place, self.flows, self.owns, self.fulls = place, flows, owns, fulls
        self.send, self.recv = send, recv
        self.labels = gather_labels(flows)
        self.sent = []

    def copy(self, number, key, spot, peer, core, side, own=False):
        flow = self.flows[number]
        place = self.place
        if own:
            shard = place.shard
            source = flow.view(self.owns[flow.array], None, core, side)
        else:
            shard = place.shard_of(*spot[1:])
            source = flow.view(self.fulls[flow.array], shard, core, side)
        target = flow.view(self.fulls[flow.array], shard, core, side)
        label = self.labels((number,) + key)
        return pltpu.make_async_remote_copy(
            source,
            target,
            self.send.at[label],
            self.recv.at[label],
            device_id=peer,
            device_id_type=MESH,
        )

    def start(self, conditions, copy):
        when(conditions, copy.start)
        self.sent.append((conditions, copy))

    def begin(self, number):
        flow, place = self.flows[number], self.place
        core, side = place.core, place.side
        here = (None, 1, 0, False)
        for way in (1, -1):
            self.start(
                [place.can(way)],
                self.copy(
                    number, ("in", "L", way, 1, False), here, place.ahead(way), core, side, True
                ),
            )
        self.start(
            [],
            self.copy(number, ("in", "P", 1, 0, True), here, place.across(), core, side, True),
        )

    def arrive(self, number, spot):
        flow, place = self.flows[number], self.place
        kind, way, steps, other = spot
        core, side = place.core, place.side
        there = place.has(way, steps)

        def take():
            self.copy(number, ("in",) + spot, spot, place.across(), core, side).wait_recv()

        when([there], take)

        def onward(extra, key, peer):
            self.start(
                [c for c in (there, extra) if c is not None],
                self.copy(number, key, spot, peer, core, side),
            )

        if kind == "L" and steps + 1 < LINE:
            onward(place.can(way), ("in", "L", way, steps + 1, other), place.ahead(way))
        if kind == "L" and flow.order == "line":
            onward(None, ("in", "P", way, steps, True), place.across())
        if kind == "P" and flow.order == "pair":
            for direction in (1, -1):
                onward(
                    place.can(direction), ("in", "L", direction, 1, True), place.ahead(direction)
                )
        if flow.sides:
            onward(None, ("side",) + spot, place.beside())
        if flow.cores:
            onward(None, ("twin",) + spot, place.twin())

    def arrive_side(self, number, spot):
        flow, place = self.flows[number], self.place
        there = place.has(*spot[1:3])
        core, side = place.core, 1 - place.side
        when(
            [there],
            lambda: self.copy(
                number, ("side",) + spot, spot, place.beside(), core, side
            ).wait_recv(),
        )
        if flow.cores:
            self.start(
                [there] if there is not None else [],
                self.copy(number, ("twinside",) + spot, spot, place.twin(), core, side),
            )

    def arrive_twin(self, number, spot):
        flow, place = self.flows[number], self.place
        there = place.has(*spot[1:3])
        core = 1 - place.core
        if flow.cores:
            when(
                [there],
                lambda: self.copy(
                    number, ("twin",) + spot, spot, place.twin(), core, place.side
                ).wait_recv(),
            )
            if flow.sides:
                when(
                    [there],
                    lambda: self.copy(
                        number, ("twinside",) + spot, spot, place.twin(), core, 1 - place.side
                    ).wait_recv(),
                )

    def actions(self):
        found = []
        for n, flow in enumerate(self.flows):
            found.append((("begin", n), lambda n=n: self.begin(n)))
        for index in range(len(positions("line"))):
            for n, flow in enumerate(self.flows):
                spot = positions(flow.order)[index]
                found.append((("in", n, spot), lambda n=n, spot=spot: self.arrive(n, spot)))
                if flow.sides:
                    found.append(
                        (("side", n, spot), lambda n=n, spot=spot: self.arrive_side(n, spot))
                    )
        return found

    def wait_twins(self, arrays):
        for number, flow in enumerate(self.flows):
            if flow.array in arrays:
                for spot in positions(flow.order):
                    self.arrive_twin(number, spot)

    def finish(self, arrays):
        self.wait_twins(arrays)
        for conditions, copy in self.sent:
            when(conditions, copy.wait_send)


class Swap:
    def __init__(self, place, ins, outs, send, recv, local):
        side = place.side
        self.away = [
            pltpu.make_async_remote_copy(
                here.at[1 - side],
                there.at[side],
                send.at[k],
                recv.at[k],
                device_id=place.beside(),
                device_id_type=MESH,
            )
            for k, (here, there) in enumerate(zip(ins, outs))
        ]
        self.stay = [
            pltpu.make_async_copy(here.at[side], there.at[side], local.at[k])
            for k, (here, there) in enumerate(zip(ins, outs))
        ]

    def start(self, k=0):
        self.away[k].start()
        self.stay[k].start()

    def wait_here(self, k):
        self.away[k].wait_recv()
        self.stay[k].wait()
        self.held = k

    held = None

    def finish(self):
        for k, (away, stay) in enumerate(zip(self.away, self.stay)):
            if k == self.held:
                away.wait_send()
            else:
                away.wait()
                stay.wait()


def swap_scratch(count):
    return [pltpu.SemaphoreType.DMA((count,))] * 3


def column_flows(array, shard_rows, columns, shared, early):
    half = columns // 2
    part = (half - shared) // 2
    flows = []
    if shared:
        flows.append(
            Flow(array, shard_rows, lambda core, side: (0, shard_rows, core * half, shared))
        )
    if early:
        flows.append(
            Flow(
                array,
                shard_rows,
                lambda core, side: (0, shard_rows, core * half + shared + side * part, early),
                sides=True,
            )
        )
    if part > early:
        flows.append(
            Flow(
                array,
                shard_rows,
                lambda core, side: (
                    0,
                    shard_rows,
                    core * half + shared + side * part + early,
                    part - early,
                ),
                order="pair",
                sides=True,
            )
        )
    return flows


def row_flows(array, shard_rows, columns, shared, early):
    half = shard_rows // 2
    part = (half - shared) // 2
    flows = [
        Flow(array, shard_rows, lambda core, side: (core * half, shared, 0, columns)),
        Flow(
            array,
            shard_rows,
            lambda core, side: (core * half + shared + side * part, early, 0, columns),
            sides=True,
        ),
        Flow(
            array,
            shard_rows,
            lambda core, side: (core * half + shared + side * part + early, part - early, 0, columns),
            order="pair",
            sides=True,
        ),
    ]
    return [flow for flow in flows if flow.region(0, 0)[1]]


class Part:
    def __init__(self, rows, columns, along, flows, dtype=BF16, inside=False):
        self.rows, self.columns, self.along, self.dtype = rows, columns, along, dtype
        self.inside = inside
        self.flows = flows
        self.half_rows = rows // 2 if along == "rows" else rows
        self.half_columns = columns // 2 if along == "columns" else columns

    def half(self, ref, shard, core):
        base = 0 if shard is None else pl.multiple_of(shard * self.rows, 16)
        if self.along == "rows":
            row = core * self.half_rows + (0 if shard is None else shard * self.rows)
            return ref.at[pl.ds(pl.multiple_of(row, 16), self.half_rows), :]
        if self.along == "columns":
            column = pl.multiple_of(core * self.half_columns, 128)
            return ref.at[pl.ds(base, self.rows), pl.ds(column, self.half_columns)]
        return ref.at[pl.ds(base, self.rows), :]

    def inner(self, flow, side):
        first, extent = flow[0](side), flow[1]
        if self.along == "rows":
            start = first if isinstance(first, int) else pl.multiple_of(first, 16)
            return pl.ds(start, extent), slice(None)
        start = first if isinstance(first, int) else pl.multiple_of(first, 128)
        return slice(None), pl.ds(start, extent)

    def outer(self, flow, core, side):
        first, extent = flow[0](side), flow[1]
        if self.along == "rows":
            return pl.ds(pl.multiple_of(core * self.half_rows + first, 16), extent), slice(None)
        if self.along == "columns":
            return slice(None), pl.ds(
                pl.multiple_of(core * self.half_columns + first, 128), extent
            )
        return slice(None), slice(None)

    def extent(self, flow):
        if self.along == "rows":
            return flow[1], self.half_columns
        return self.half_rows, flow[1]


SPOTS = [(1, 3), (-1, 3), (1, 2), (-1, 2), (1, 1), (-1, 1), (1, 0)]


def reduce_scratch(parts):
    shapes = []
    for part in parts:
        half = (LINE * PAIR, part.half_rows, part.half_columns)
        shapes.append(pltpu.VMEM(half, part.dtype))
        shapes.append(pltpu.VMEM(half if part.along else half[1:], part.dtype))
        for flow in part.flows:
            rows, columns = part.extent(flow)
            shapes.append(
                pltpu.VMEM((LINE * PAIR if flow[3] else 1, rows, columns), part.dtype)
            )
            shapes.append(
                pltpu.VMEM((LINE if flow[2] == "line" else 1, rows, columns), part.dtype)
            )
            shapes.append(
                pltpu.VMEM(
                    ((LINE + 1) * (1 if flow[2] == "line" else PAIR), rows, columns), part.dtype
                )
            )
    return shapes


def reduce_labels(parts):
    labels = Labels()
    for n, part in enumerate(parts):
        for way, steps in SPOTS:
            for other in (False, True):
                labels((n, "twin", way, steps, other))
        labels((n, "twinend"))
        for k, flow in enumerate(part.flows):
            for way, steps in SPOTS:
                for other in (False, True):
                    if flow[3]:
                        labels((n, k, "side", way, steps, other))
                    if flow[2] == "pair" or not other:
                        labels((n, k, "line", way, steps, other))
                        if steps == 0:
                            labels((n, k, "line", -way, steps, other))
                if flow[2] == "line" or steps == 0:
                    labels((n, k, "pair", way, steps))
            labels((n, k, "sideend"))
            labels((n, k, "twinend"))
            labels((n, k, "twinsideend"))
    return labels


class Reduce:
    def __init__(self, place, parts, grads, outs, scratch, send, recv, load):
        self.place, self.parts, self.grads, self.outs = place, parts, grads, outs
        self.send, self.recv, self.load = send, recv, load
        self.labels = reduce_labels(parts)
        self.sent = []
        self.own, self.other, self.lanes = [], [], []
        at = 0
        for part in parts:
            self.own.append(scratch[at])
            self.other.append(scratch[at + 1])
            at += 2
            lanes = []
            for _ in part.flows:
                lanes.append(scratch[at : at + 3])
                at += 3
            self.lanes.append(lanes)

    def copy(self, source, target, key, peer):
        label = self.labels(key)
        return pltpu.make_async_remote_copy(
            source,
            target,
            self.send.at[label],
            self.recv.at[label],
            device_id=peer,
            device_id_type=MESH,
        )

    def start(self, conditions, copy):
        when(conditions, copy.start)
        self.sent.append((conditions, copy))

    def there(self, spot):
        return self.place.has(-spot[0], spot[1])

    def shard(self, spot, other):
        return self.place.shard_of(-spot[0], spot[1], other)

    def keep(self, n, spot, other):
        shard = self.shard(spot, other)
        label = SPOTS.index(spot) * 2 + int(other)
        return pltpu.make_async_copy(
            self.parts[n].half(self.grads[n], shard, self.place.core),
            self.own[n].at[shard],
            self.load.at[n * 2 * len(SPOTS) + label],
        )

    def twin(self, n, spot, other, core):
        shard = self.shard(spot, other)
        part = self.parts[n]
        return self.copy(
            self.grads[n].at[shard] if part.inside else part.half(self.grads[n], shard, core),
            self.other[n].at[shard],
            (n, "twin") + spot + (other,),
            self.place.twin(),
        )

    def begin(self, n, spot):
        there = self.there(spot)
        for other in (True, False):
            if not self.parts[n].inside:
                when([there], self.keep(n, spot, other).start)
            if self.parts[n].along:
                self.start([there], self.twin(n, spot, other, 1 - self.place.core))

    def piece(self, n, k, shard, side):
        part = self.parts[n]
        rows, columns = part.inner(part.flows[k], side)
        return self.own[n].at[shard, rows, columns]

    def side_copy(self, n, k, spot, other, side):
        shard = self.shard(spot, other)
        return self.copy(
            self.piece(n, k, shard, side),
            self.lanes[n][k][0].at[shard],
            (n, k, "side") + spot + (other,),
            self.place.beside(),
        )

    def add_cores(self, n, spot):
        there = self.there(spot)
        part = self.parts[n]
        for other in (True, False):

            def add(other=other):
                shard = self.shard(spot, other)
                if not part.inside:
                    self.keep(n, spot, other).wait()
                if part.along:
                    self.twin(n, spot, other, self.place.core).wait_recv()
                    self.own[n][shard] = self.own[n][shard] + self.other[n][shard]

            when([there], add)
        for other in (True, False):
            for k, flow in enumerate(part.flows):
                if flow[3]:
                    self.start([there], self.side_copy(n, k, spot, other, 1 - self.place.side))
                elif other:
                    self.start([there], self.pair_copy(n, k, spot, self.shard(spot, True)))

    def pair_copy(self, n, k, spot, shard):
        flow = self.parts[n].flows[k]
        slot = self.place.line + spot[0] * spot[1] if flow[2] == "line" else 0
        return self.copy(
            self.piece(n, k, shard, self.place.side),
            self.lanes[n][k][1].at[slot],
            (n, k, "pair") + spot,
            self.place.across(),
        )

    def add_sides(self, n, k, spot):
        there = self.there(spot)
        side = self.place.side
        for other in (True, False):

            def add(other=other):
                shard = self.shard(spot, other)
                self.side_copy(n, k, spot, other, side).wait_recv()
                piece = self.piece(n, k, shard, side)
                piece[...] = piece[...] + self.lanes[n][k][0][shard]

            when([there], add)
        if self.parts[n].flows[k][2] == "line":
            self.start([there], self.pair_copy(n, k, spot, self.shard(spot, True)))

    def line_slot(self, flow, way, steps, other, line):
        slot = line if (steps > 0 or way > 0) else LINE
        return slot + (LINE + 1) * int(other) if flow[2] == "pair" else slot

    def line_copy(self, n, k, spot, other, arriving):
        flow = self.parts[n].flows[k]
        way, steps = spot
        shard = self.shard(spot, other)
        line = self.place.line + way * steps
        left = steps if arriving else steps - 1
        return self.copy(
            self.piece(n, k, shard, self.place.side),
            self.lanes[n][k][2].at[self.line_slot(flow, way, left, other, line)],
            (n, k, "line", way, left, other),
            self.place.ahead(way),
        )

    def add_line(self, n, k, spot):
        place = self.place
        there = self.there(spot)
        way, steps = spot
        side = place.side
        flow = self.parts[n].flows[k]
        if flow[2] == "line":

            def add():
                shard = self.shard(spot, False)
                self.pair_copy(n, k, spot, shard).wait_recv()
                piece = self.piece(n, k, shard, side)
                piece[...] = piece[...] + self.lanes[n][k][1][place.line + way * steps]

            when([there], add)
        for other in (True, False) if flow[2] == "pair" else (False,):
            for direction in (1, -1) if steps == 0 else (way,):

                def add_line(other=other, here=(direction, steps)):
                    self.line_copy(n, k, here, other, True).wait_recv()
                    piece = self.piece(n, k, self.shard(here, other), side)
                    line = place.line + here[0] * here[1]
                    slot = self.line_slot(flow, here[0], here[1], other, line)
                    piece[...] = piece[...] + self.lanes[n][k][2][slot]

                when([there, place.can(-direction)], add_line)
            if steps > 0:
                self.start([there], self.line_copy(n, k, spot, other, False))

    def send_pair(self, n, k):
        self.start([], self.pair_copy(n, k, (1, 0), self.shard((1, 0), True)))

    def send_swap(self, n, k):
        self.start([], self.swap(n, k))

    def settle(self, n, k):
        place = self.place
        core, side, here = place.core, place.side, place.shard
        part = self.parts[n]
        flow = part.flows[k]
        piece = self.piece(n, k, here, side)
        out = self.out_view(n, k, core, side)
        if flow[3]:
            if flow[2] == "pair":
                self.pair_copy(n, k, (1, 0), here).wait_recv()
                out[...] = piece[...] + self.lanes[n][k][1][0]
            else:
                out[...] = piece[...]
            self.start([], self.out_copy(n, k, "sideend", place.beside(), core, side))
        else:
            self.swap(n, k).wait_recv()
            out[...] = piece[...] + self.lanes[n][k][0][0]
        if part.along:
            self.start([], self.out_copy(n, k, "twinend", place.twin(), core, side))
        else:
            self.start([], self.whole(n, k))

    def settle_side(self, n, k):
        place = self.place
        core, side = place.core, 1 - place.side
        self.out_copy(n, k, "sideend", place.beside(), core, side).wait_recv()
        self.start([], self.out_copy(n, k, "twinsideend", place.twin(), core, side))

    def swap(self, n, k):
        return self.copy(
            self.piece(n, k, self.place.shard, self.place.side),
            self.lanes[n][k][0].at[0],
            (n, k, "sideend"),
            self.place.beside(),
        )

    def out_view(self, n, k, core, side):
        part = self.parts[n]
        rows, columns = part.outer(part.flows[k], core, side)
        return self.outs[n].at[rows, columns]

    def out_copy(self, n, k, key, peer, core, side):
        view = self.out_view(n, k, core, side)
        return self.copy(view, view, (n, k, key), peer)

    def last(self):
        place = self.place
        core, side = place.core, place.side
        everything = [(n, k) for n, part in enumerate(self.parts) for k in range(len(part.flows))]
        for n, k in everything:
            if self.parts[n].along:
                self.out_copy(n, k, "twinend", place.twin(), 1 - core, side).wait_recv()
                if self.parts[n].flows[k][3]:
                    self.out_copy(
                        n, k, "twinsideend", place.twin(), 1 - core, 1 - side
                    ).wait_recv()
            else:
                self.whole(n, k).wait_recv()
        for conditions, copy in self.sent:
            when(conditions, copy.wait_send)
        for n, k in everything:
            if not self.parts[n].along:
                view = self.out_view(n, k, core, side)
                view[...] = view[...] + self.other[n][...]

    def whole(self, n, k):
        return self.copy(
            self.out_view(n, k, self.place.core, self.place.side),
            self.other[n],
            (n, k, "twinend"),
            self.place.twin(),
        )

    def actions(self):
        found = []
        for n, part in enumerate(self.parts):
            for spot in SPOTS:
                found.append((("begin", n, spot), lambda n=n, s=spot: self.begin(n, s)))
        for n, part in enumerate(self.parts):
            for spot in SPOTS:
                found.append((("cores", n, spot), lambda n=n, s=spot: self.add_cores(n, s)))
            for k, flow in enumerate(part.flows):
                at = (n, k)
                for spot in SPOTS:
                    if flow[3]:
                        found.append(
                            (("sides", n, k, spot), lambda at=at, s=spot: self.add_sides(*at, s))
                        )
                    found.append(
                        (("line", n, k, spot), lambda at=at, s=spot: self.add_line(*at, s))
                    )
                if flow[2] == "pair":
                    found.append((("pair", n, k), lambda at=at: self.send_pair(*at)))
                if not flow[3]:
                    found.append((("swap", n, k), lambda at=at: self.send_swap(*at)))
                found.append((("settle", n, k), lambda at=at: self.settle(*at)))
                if flow[3]:
                    found.append((("after", n, k), lambda at=at: self.settle_side(*at)))
        found.append((("last",), self.last))
        return found


def in_order(actions, order):
    if order is None:
        return [action for _, action in actions]
    assert sorted(order) == list(range(len(actions)))
    return [actions[i][1] for i in order]


def column_part(rows, columns, shared, early, inside=False):
    half = columns // 2
    part = (half - shared) // 2
    flows = []
    if shared:
        flows.append((lambda side: 0, shared, "line", False))
    if early:
        flows.append((lambda side: shared + side * part, early, "line", True))
    if part > early:
        flows.append((lambda side: shared + side * part + early, part - early, "pair", True))
    return Part(rows, columns, "columns", flows, inside=inside)


def row_part(rows, columns, shared, early):
    half = rows // 2
    part = (half - shared) // 2
    flows = [
        (lambda side: 0, shared, "line", False),
        (lambda side: shared + side * part, early, "line", True),
        (lambda side: shared + side * part + early, part - early, "pair", True),
    ]
    return Part(rows, columns, "rows", [flow for flow in flows if flow[1]])


def vector_part(rows, columns, inside=False):
    return Part(rows, columns, None, [(lambda side: 0, columns, "line", False)], F32, inside)


ROW_QUERY, ROW_VALUE, ROW_OUTPUT, ROW_GAIN1, ROW_SHIFT1, ROW_INNER, INNER = 0, 1, 2, 3, 4, 5, 4
ROW_OUTER, ROW_GAIN2, ROW_SHIFT2 = 9, 10, 11
TABLE_ROWS = 16
VMEM = 67043328
LANES = 128
BAND = 128


def spread_table(table_ref, vec):
    for shard in range(table_ref.shape[0] // TABLE_ROWS):
        vec[:, pl.ds(shard * LANES, LANES)] = table_ref[
            pl.ds(shard * TABLE_ROWS, TABLE_ROWS), :
        ].astype(F32)


def fold_table(vec, table_ref, first, count):
    for shard in range(table_ref.shape[0] // TABLE_ROWS):
        table_ref[pl.ds(shard * TABLE_ROWS + first, count), :] = vec[
            pl.ds(first, count), pl.ds(shard * LANES, LANES)
        ]


def row_place(row, core, rows):
    half = rows // 2
    return jnp.where(row < half, row, row + half) + core * half


def total_rows(block):
    return jnp.sum(block.astype(F32), axis=0, keepdims=True)


def middle_kernel(
    rows_far,
    context_far,
    cot_far,
    lengths_ref,
    table_ref,
    output_w,
    inner_w,
    outer_w,
    out_far,
    first_grad_far,
    context_grad_far,
    sums_ref,
    output_far,
    inner_g,
    outer_g,
    rows_ref,
    context_ref,
    cot_ref,
    out_ref,
    first_grad_ref,
    context_grad_ref,
    output_g,
    output_v,
    inner_v,
    outer_v,
    vec,
    sums,
    active,
    slope,
    unit1,
    rate1,
    total,
    low,
    low_t,
    second,
    second_low,
    inner_b,
    outer_b,
    load,
    save,
    few,
    swap_send,
    swap_recv,
    swap_local,
):
    rows, width = rows_ref.shape
    tiles, _, tile = inner_v.shape
    place = Place()
    side, core = place.side, place.core
    length = lengths_ref[side]
    bands = rows // BAND
    assert BAND == cot_ref.shape[1]
    barrier = pltpu.get_barrier_semaphore()
    pl.semaphore_signal(barrier, inc=1, device_id=place.beside(), device_id_type=MESH)

    def inner_load(t):
        return pltpu.make_async_copy(
            inner_w.at[:, pl.ds(pl.multiple_of(t * tile, tile), tile)], inner_v.at[t], load.at[0, t]
        )

    def outer_load(t):
        return pltpu.make_async_copy(
            outer_w.at[pl.ds(pl.multiple_of(t * tile, tile), tile), :], outer_v.at[t], load.at[1, t]
        )

    output_load = pltpu.make_async_copy(output_w, output_v, few.at[0])
    context_load = pltpu.make_async_copy(context_far, context_ref, few.at[1])
    rows_load = pltpu.make_async_copy(rows_far, rows_ref, few.at[2])
    turn = Swap(
        place, [cot_far, out_ref], [cot_ref, out_far], swap_send, swap_recv, swap_local
    )
    first_save = pltpu.make_async_copy(first_grad_ref, first_grad_far, few.at[5])
    context_save = pltpu.make_async_copy(context_grad_ref, context_grad_far, few.at[6])
    output_save = pltpu.make_async_copy(output_g, output_far, few.at[7])
    for copy in (context_load, output_load, rows_load):
        copy.start()
    spread_table(table_ref, vec)
    sums[...] = jnp.zeros_like(sums)
    context_load.wait()
    output_load.wait()
    pl.semaphore_wait(barrier, 1)
    turn.start(0)
    ahead = 3
    for t in range(ahead):
        inner_load(t).start()
        outer_load(t).start()
    total[...] = plain_product(context_ref[...], output_v[...])
    rows_load.wait()

    def band_of(b):
        return pl.ds(pl.multiple_of(b * BAND, BAND), BAND)

    def first_norm(b, carry):
        here = band_of(b)
        first_sum = (
            rows_ref[here, :].astype(F32) + total[here, :] + vec[pl.ds(ROW_OUTPUT, 1), :]
        )
        unit, rate = norm_parts(first_sum)
        unit1[here, :] = unit
        rate1[here, :] = jnp.broadcast_to(rate, (BAND, LANES))
        normed = unit * vec[pl.ds(ROW_GAIN1, 1), :] + vec[pl.ds(ROW_SHIFT1, 1), :]
        low[here, :] = normed.astype(BF16)
        total[here, :] = normed + vec[pl.ds(ROW_OUTER, 1), :]
        return carry

    lax.fori_loop(0, bands, first_norm, 0)
    low_t[...] = low[...].T


    def forward(t, carry):
        inner_load(t).wait()

        @pl.when(t + ahead < tiles)
        def _():
            inner_load(t + ahead).start()
            outer_load(t + ahead).start()

        bias = jnp.concatenate(
            [
                vec[pl.ds(ROW_INNER + k, 1), pl.ds(pl.multiple_of(t * LANES, LANES), LANES)]
                for k in range(INNER)
            ],
            axis=1,
        )
        hidden = plain_product(low[...], inner_v[t]) + bias
        share = 0.5 + 0.5 * lax.erf(hidden * 0.7071067811865476)
        active[t] = (hidden * share).astype(BF16)
        slope[t] = share + hidden * (jnp.exp(-0.5 * hidden * hidden) * 0.3989422804014327)
        outer_load(t).wait()
        total[...] += plain_product(active[t], outer_v[t])
        return carry

    lax.fori_loop(0, tiles, forward, 0)

    turn.wait_here(0)

    def second_norm(b, carry):
        here = band_of(b)
        unit, rate = norm_parts(total[here, :])
        row = b * BAND + lax.broadcasted_iota(jnp.int32, (BAND, width), 0)
        mask = (row_place(row, core, rows) < length).astype(F32)
        gain = vec[pl.ds(ROW_GAIN2, 1), :]
        out_ref[b] = ((unit * gain + vec[pl.ds(ROW_SHIFT2, 1), :]) * mask).astype(BF16)
        out_grad = cot_ref[b].astype(F32) * mask
        grad = norm_back(unit, rate, out_grad * gain)
        second[here, :] = grad
        grad_low = grad.astype(BF16)
        second_low[here, :] = grad_low
        sums[pl.ds(ROW_GAIN2, 1), :] += total_rows(out_grad * unit)
        sums[pl.ds(ROW_SHIFT2, 1), :] += total_rows(out_grad)
        sums[pl.ds(ROW_OUTER, 1), :] += total_rows(grad_low)
        return carry

    lax.fori_loop(0, bands, second_norm, 0)
    turn.start(1)

    def inner_save(t):
        slot = lax.rem(t, 2)
        return pltpu.make_async_copy(
            inner_b.at[slot],
            inner_g.at[:, pl.ds(pl.multiple_of(t * tile, tile), tile)],
            save.at[0, slot],
        )

    def outer_save(t):
        slot = lax.rem(t, 2)
        return pltpu.make_async_copy(
            outer_b.at[slot],
            outer_g.at[pl.ds(pl.multiple_of(t * tile, tile), tile), :],
            save.at[1, slot],
        )

    def backward(t, carry):
        slot = lax.rem(t, 2)
        hidden_grad = (right_product(second_low[...], outer_v[t]) * slope[t]).astype(BF16)
        summed = total_rows(hidden_grad)
        for k in range(INNER):
            sums[
                pl.ds(ROW_INNER + k, 1), pl.ds(pl.multiple_of(t * LANES, LANES), LANES)
            ] = summed[:, k * LANES : (k + 1) * LANES]

        @pl.when(t >= 2)
        def _():
            outer_save(t - 2).wait()
            inner_save(t - 2).wait()

        outer_b[slot] = left_product(active[t], second_low[...]).astype(BF16)
        inner_b[slot] = plain_product(low_t[...], hidden_grad).astype(BF16)
        outer_save(t).start()
        second[...] += right_product(hidden_grad, inner_v[t])
        inner_save(t).start()
        return carry

    lax.fori_loop(0, tiles, backward, 0)

    def first_back(b, carry):
        here = band_of(b)
        grad = second[here, :]
        unit = unit1[here, :]
        sums[pl.ds(ROW_GAIN1, 1), :] += total_rows(grad * unit)
        sums[pl.ds(ROW_SHIFT1, 1), :] += total_rows(grad)
        back = norm_back(unit, rate1[here, :1], grad * vec[pl.ds(ROW_GAIN1, 1), :])
        first_grad_ref[here, :] = back
        back_low = back.astype(BF16)
        second_low[here, :] = back_low
        sums[pl.ds(ROW_OUTPUT, 1), :] += total_rows(back_low)
        return carry

    lax.fori_loop(0, bands, first_back, 0)
    output_g[...] = left_product(context_ref[...], second_low[...]).astype(BF16)
    first_save.start()
    context_grad_ref[...] = right_product(second_low[...], output_v[...]).astype(BF16)
    output_save.start()
    fold_table(sums, sums_ref, 0, TABLE_ROWS)
    context_save.start()
    for t in range(tiles - 2, tiles):
        outer_save(t).wait()
        inner_save(t).wait()
    for copy in (first_save, output_save, context_save):
        copy.wait()
    turn.finish()


def middle(collective_id, rows, context, cot, lengths, table, output_w, inner_w, outer_w):
    count, width = rows.shape
    hidden = inner_w.shape[1]
    tile = INNER * LANES
    tiles = hidden // tile
    whole = pl.BlockSpec(memory_space=pltpu.VMEM)
    far = pl.BlockSpec(memory_space=pltpu.HBM)

    def space(dtype):
        return pltpu.VMEM((count, width), dtype)

    return pl.pallas_call(
        middle_kernel,
        out_shape=[
            jax.ShapeDtypeStruct(cot.shape, BF16),
            jax.ShapeDtypeStruct((count, width), F32),
            jax.ShapeDtypeStruct((count, width), BF16),
            jax.ShapeDtypeStruct(table.shape, F32),
            jax.ShapeDtypeStruct(output_w.shape, BF16),
            jax.ShapeDtypeStruct(inner_w.shape, BF16),
            jax.ShapeDtypeStruct(outer_w.shape, BF16),
        ],
        in_specs=[far] * 3 + [pl.BlockSpec(memory_space=pltpu.SMEM), whole] + [far] * 3,
        out_specs=[far] * 3 + [whole] + [far] * 3,
        scratch_shapes=[
            space(BF16),
            space(BF16),
            pltpu.VMEM(cot.shape, BF16),
            pltpu.VMEM(cot.shape, BF16),
            space(F32),
            space(BF16),
            pltpu.VMEM(output_w.shape, BF16),
            pltpu.VMEM(output_w.shape, BF16),
            pltpu.VMEM((tiles, width, tile), BF16),
            pltpu.VMEM((tiles, tile, width), BF16),
            pltpu.VMEM((TABLE_ROWS, width), F32),
            pltpu.VMEM((TABLE_ROWS, width), F32),
            pltpu.VMEM((tiles, count, tile), BF16),
            pltpu.VMEM((tiles, count, tile), F32),
            space(F32),
            pltpu.VMEM((count, LANES), F32),
            space(F32),
            space(BF16),
            pltpu.VMEM((width, count), BF16),
            space(F32),
            space(BF16),
            pltpu.VMEM((2, width, tile), BF16),
            pltpu.VMEM((2, tile, width), BF16),
            pltpu.SemaphoreType.DMA((2, tiles)),
            pltpu.SemaphoreType.DMA((2, 2)),
            pltpu.SemaphoreType.DMA((8,)),
        ]
        + swap_scratch(2),
        compiler_params=pltpu.CompilerParams(
            collective_id=collective_id, has_side_effects=True, vmem_limit_bytes=VMEM
        ),
        name="feed_forward",
    )(rows, context, cot, lengths, table, output_w, inner_w, outer_w)


def widen_kernel(splits, lines, *refs):
    count = len(splits)
    many = sum(splits)
    ins, table, outs = refs[:count], refs[count], refs[count + 1 : count + 1 + many]
    vectors = refs[count + 1 + many : count + 1 + many + len(lines)]
    rest = refs[count + 1 + many + len(lines) :]
    narrow, held, wides = rest[:count], rest[count], rest[count + 1 : count + 1 + many]
    load, save = rest[-2:]
    loads = [
        pltpu.make_async_copy(here, there, load.at[k])
        for k, (here, there) in enumerate(zip(ins + (table,), narrow + (held,)))
    ]
    for copy in loads:
        copy.start()
    copies = []
    at = 0
    for k, parts in enumerate(splits):
        loads[k].wait()
        columns = narrow[k].shape[-1] // parts
        for part in range(parts):
            wides[at][...] = narrow[k][..., part * columns : (part + 1) * columns].astype(
                wides[at].dtype
            )
            copies.append(pltpu.make_async_copy(wides[at], outs[at], save.at[at]))
            copies[-1].start()
            at += 1
    loads[count].wait()
    row = 0
    for vector, extent in zip(vectors, lines):
        for line in range(extent):
            copies.append(
                pltpu.make_async_copy(
                    held.at[row], vector.at[pl.ds(line * LANES, LANES)], save.at[many + row]
                )
            )
            copies[-1].start()
            row += 1
    for copy in copies:
        copy.wait()


def widen(arrays, splits, types, table, lines):
    shapes = []
    for array, parts, kind in zip(arrays, splits, types):
        shape = array.shape[:-1] + (array.shape[-1] // parts,)
        shapes += [jax.ShapeDtypeStruct(shape, kind)] * parts
    far = pl.BlockSpec(memory_space=pltpu.HBM)
    return pl.pallas_call(
        functools.partial(widen_kernel, splits, lines),
        out_shape=shapes + [jax.ShapeDtypeStruct((k * LANES,), F32) for k in lines],
        in_specs=[far] * (len(arrays) + 1),
        out_specs=[far] * (len(shapes) + len(lines)),
        scratch_shapes=[pltpu.VMEM(array.shape, array.dtype) for array in arrays + (table,)]
        + [pltpu.VMEM(shape.shape, shape.dtype) for shape in shapes]
        + [
            pltpu.SemaphoreType.DMA((len(arrays) + 1,)),
            pltpu.SemaphoreType.DMA((len(shapes) + sum(lines),)),
        ],
        compiler_params=pltpu.CompilerParams(vmem_limit_bytes=VMEM),
        name="widen_results",
    )(*arrays, table)


def stack_heads(block, lower):
    zero = jnp.zeros_like(block)
    return jnp.concatenate((jnp.where(lower, block, zero), jnp.where(lower, zero, block)), axis=0)


def repeat(first, stop, action):
    def step(i, carry):
        action(i)
        return carry

    lax.fori_loop(first, stop, step, 0)


GROUPS = 4
HALVES = 2


SPAN = 2 * HEAD_DIM


def span_of(section, pair, width):
    return pl.ds(pl.multiple_of(section * width + pair * SPAN, SPAN), SPAN)


class AttentionForward:
    def __init__(self, place, rows, weight, vec, bias, qkv, context, probs, held, away, send, recv, save):
        self.place, self.rows, self.weight, self.vec, self.bias = place, rows, weight, vec, bias
        self.qkv, self.context, self.probs, self.held, self.away = qkv, context, probs, held, away
        self.send, self.recv, self.save = send, recv, save
        self.count, self.width = context.shape
        self.pairs = self.width // SPAN

    def save_probs(self, pair):
        return pltpu.make_async_copy(self.held.at[pair], self.probs.at[pair], self.save.at[pair])

    def fetch(self, which, pair):
        return pltpu.make_async_remote_copy(
            self.qkv.at[:, span_of(which + 1, pair, self.width)],
            self.away.at[:, span_of(which, pair, self.width)],
            self.send.at[which, pair],
            self.recv.at[which, pair],
            device_id=self.place.twin(),
            device_id_type=MESH,
        )

    def project(self, section):
        tile = 512
        rows = self.rows[...].reshape(self.count, self.width)

        def one(t):
            columns = pl.ds(pl.multiple_of(section * self.width + t * tile, tile), tile)
            product = plain_product(rows, self.weight[:, columns])
            if section != 1:
                row = ROW_QUERY if section == 0 else ROW_VALUE
                product = product + self.vec[
                    pl.ds(row, 1), pl.ds(pl.multiple_of(t * tile, tile), tile)
                ]
            self.qkv[:, columns] = product.astype(BF16)

        repeat(0, self.width // tile, one)

    def give(self, which):
        for pair in range(self.pairs):
            self.fetch(which, pair).start()

    def attend(self, pair):
        for which in range(2):
            self.fetch(which, pair).wait_recv()
        count = self.count
        lower = lax.broadcasted_iota(jnp.int32, (count, SPAN), 1) < HEAD_DIM

        def here(section):
            return self.qkv[:, span_of(section, pair, self.width)]

        def there(section):
            return self.away[:, span_of(section - 1, pair, self.width)]

        stacked = stack_heads(here(0) * HEAD_DIM**-0.5, lower)
        keys = jnp.concatenate((here(1), there(1)), axis=0)
        values = jnp.concatenate((here(2), there(2)), axis=0)
        scores = right_product(stacked, keys) + self.bias[:1, :]
        top = jnp.max(scores, axis=1, keepdims=True)
        weights = jnp.exp(scores - top)
        total = jnp.sum(weights, axis=1, keepdims=True)
        probs = (weights * (1.0 / total)).astype(BF16)
        self.held[pair] = probs
        self.save_probs(pair).start()
        mixed = plain_product(probs, values)
        self.context[:, span_of(0, pair, self.width)] = jnp.where(
            lower, mixed[:count], mixed[count:]
        ).astype(BF16)

    def attend_group(self, group):
        each = self.pairs // GROUPS
        repeat(group * each, (group + 1) * each, self.attend)

    def finish(self):
        for pair in range(self.pairs):
            for which in range(2):
                self.fetch(which, pair).wait_send()
            self.save_probs(pair).wait()


TABLE, QUERIES = 0, 1


def start_actions(gather, work, keep, swap, save, table_ref):
    found = gather.actions()
    others = [k for k in range(len(keep)) if k not in (TABLE, QUERIES)]

    def ready():
        gather.wait_twins((TABLE, QUERIES))
        for k in (TABLE, QUERIES):
            keep[k].wait()
        swap.finish()
        spread_table(table_ref, work.vec)
        save.start()

    def values():
        work.project(2)
        work.give(0)

    def queries():
        work.give(1)
        work.project(0)

    found.append((("ready",), ready))
    found.append((("project", 0), lambda: work.project(1)))
    found.append((("project", 1), values))
    found.append((("project", 2), queries))
    for group in range(GROUPS):
        found.append((("pa", group), lambda group=group: work.attend_group(group)))

    def last():
        gather.finish(others)
        work.finish()
        for k in others:
            keep[k].wait()
        save.wait()

    found.append((("last",), last))
    return found


def start_kernel(flows, spots, order, *refs):
    count = max(array for array, _ in spots) + 1
    shares, refs = refs[: len(spots)], refs[len(spots) :]
    (in_block, lengths_ref), refs = refs[:2], refs[2:]
    table_ref, refs = refs[0], refs[1:]
    far, refs = refs[: count - 1], refs[count - 1 :]
    rows, qkv, context, probs, away = refs[:5]
    owns, refs = refs[5 : 5 + count], refs[5 + count :]
    weight, held, vec, bias = refs[:4]
    send, recv, local, load, send2, recv2, save2, saveq = refs[4:12]
    fulls = (table_ref, weight) + tuple(far[1:])
    place = Place()
    loads = [
        pltpu.make_async_copy(
            share, owns[array].at[:, pl.ds(column, share.shape[1])], load.at[k]
        )
        for k, (share, (array, column)) in enumerate(zip(shares, spots))
    ]
    for copy in loads:
        copy.start()
    keep = [
        pltpu.make_async_copy(
            own, full.at[pl.ds(pl.multiple_of(place.shard * own.shape[0], 16), own.shape[0]), :], local.at[k]
        )
        for k, (own, full) in enumerate(zip(owns, fulls))
    ]
    greet(place)
    rows_count = context.shape[0]
    length = lengths_ref[place.side]
    row = lax.broadcasted_iota(jnp.int32, (8, rows_count), 1)
    for k, core in enumerate((place.core, 1 - place.core)):
        bias[:, pl.ds(k * rows_count, rows_count)] = jnp.where(
            row_place(row, core, rows_count) < length, 0.0, -1e30
        )
    for copy in loads:
        copy.wait()
    swap = Swap(place, [in_block], [rows], *refs[12:15])
    swap.start()
    gather = Gather(place, flows, owns, fulls, send, recv)
    for copy in keep:
        copy.start()
    work = AttentionForward(
        place, rows, weight, vec, bias, qkv, context, probs, held, away, send2, recv2, save2
    )
    save = pltpu.make_async_copy(weight, far[0], saveq.at[0])
    for step in in_order(start_actions(gather, work, keep, swap, save, table_ref), order):
        step()


def start(shares, spots, block, lengths, flows, shards, collective_id, order):
    labels = gather_labels(flows)
    count = max(array for array, _ in spots) + 1
    shapes = []
    for array in range(count):
        members = [share for share, spot in zip(shares, spots) if spot[0] == array]
        shapes.append((members[0].shape[0], sum(m.shape[1] for m in members)))
    _, block_len, width = block.shape
    rows = 2 * block_len
    pairs = width // SPAN
    far = pl.BlockSpec(memory_space=pltpu.HBM)
    whole = pl.BlockSpec(memory_space=pltpu.VMEM)
    probs_shape = (pairs, 2 * rows, 2 * rows)
    return pl.pallas_call(
        functools.partial(start_kernel, flows, spots, order),
        out_shape=[jax.ShapeDtypeStruct((shards * r, c), BF16) for r, c in shapes]
        + [
            jax.ShapeDtypeStruct(block.shape, BF16),
            jax.ShapeDtypeStruct((rows, 3 * width), BF16),
            jax.ShapeDtypeStruct((rows, width), BF16),
            jax.ShapeDtypeStruct(probs_shape, BF16),
            jax.ShapeDtypeStruct((rows, 2 * width), BF16),
        ],
        in_specs=[far] * (len(shares) + 1) + [pl.BlockSpec(memory_space=pltpu.SMEM)],
        out_specs=[whole] + [far] * (count - 1) + [whole, whole, whole, far, whole],
        scratch_shapes=[pltpu.VMEM(shape, BF16) for shape in shapes]
        + [
            pltpu.VMEM((shards * shapes[QUERIES][0], shapes[QUERIES][1]), BF16),
            pltpu.VMEM(probs_shape, BF16),
            pltpu.VMEM((TABLE_ROWS, width), F32),
            pltpu.VMEM((8, 2 * rows), F32),
            pltpu.SemaphoreType.DMA((len(labels.numbers),)),
            pltpu.SemaphoreType.DMA((len(labels.numbers),)),
            pltpu.SemaphoreType.DMA((count,)),
            pltpu.SemaphoreType.DMA((len(shares),)),
            pltpu.SemaphoreType.DMA((2, pairs)),
            pltpu.SemaphoreType.DMA((2, pairs)),
            pltpu.SemaphoreType.DMA((pairs,)),
            pltpu.SemaphoreType.DMA((1,)),
        ]
        + swap_scratch(1),
        compiler_params=pltpu.CompilerParams(
            collective_id=collective_id, has_side_effects=True, vmem_limit_bytes=VMEM
        ),
        name="gather_attention_forward",
    )(*shares, block, lengths)


class AttentionBackward:
    def __init__(self, place, qkv, away, grad, out, keep, leave, come, send, recv):
        self.place, self.qkv, self.away, self.grad = place, qkv, away, grad
        self.out, self.keep, self.leave, self.come = out, keep, leave, come
        self.send, self.recv = send, recv
        self.count, self.width = grad.shape
        self.pairs = self.width // SPAN

    def give(self, which, pair):
        return pltpu.make_async_remote_copy(
            self.leave.at[:, span_of(which, pair, self.width)],
            self.come.at[:, span_of(which, pair, self.width)],
            self.send.at[which, pair],
            self.recv.at[which, pair],
            device_id=self.place.twin(),
            device_id_type=MESH,
        )

    def attend(self, pair, probs):
        count = self.count
        lower = lax.broadcasted_iota(jnp.int32, (count, SPAN), 1) < HEAD_DIM
        scale = HEAD_DIM**-0.5

        def here(section):
            return self.qkv[:, span_of(section, pair, self.width)]

        def there(section):
            return self.away[:, span_of(section - 1, pair, self.width)]

        first = span_of(0, pair, self.width)
        second = span_of(1, pair, self.width)
        stacked = stack_heads(here(0) * scale, lower)
        keys = jnp.concatenate((here(1), there(1)), axis=0)
        values = jnp.concatenate((here(2), there(2)), axis=0)
        grad = stack_heads(self.grad[:, first], lower)
        value_part = left_product(probs, grad)
        probs_grad = right_product(grad, values)
        wide = probs.astype(F32)
        inner = jnp.sum(wide * probs_grad, axis=1, keepdims=True)
        scores_grad = (wide * (probs_grad - inner)).astype(BF16)
        key_part = left_product(scores_grad, stacked)
        self.leave[:, first] = key_part[count:].astype(BF16)
        self.leave[:, second] = value_part[count:].astype(BF16)
        self.keep[:, first] = key_part[:count]
        self.keep[:, second] = value_part[:count]
        mixed = plain_product(scores_grad, keys) * scale
        self.out[:, first] = jnp.where(lower, mixed[:count], mixed[count:]).astype(BF16)
        for which in range(2):
            self.give(which, pair).start()

    def settle(self, pair):
        for which in range(2):
            self.give(which, pair).wait_recv()
            here = span_of(which, pair, self.width)
            self.out[:, span_of(which + 1, pair, self.width)] = (
                self.keep[:, here] + self.come[:, here].astype(F32)
            ).astype(BF16)

    def finish(self):
        for pair in range(self.pairs):
            for which in range(2):
                self.give(which, pair).wait_send()


class Finish:
    def __init__(self, work, tiles, weight, rows_ref, rows_t, first_grad, total, block, sums, held, probs, load, sems):
        self.work, self.tiles, self.weight, self.rows_ref, self.rows_t = work, tiles, weight, rows_ref, rows_t
        self.total, self.block, self.sums = total, block, sums
        self.held, self.probs, self.load, self.sems = held, probs, load, sems
        self.grad_load = pltpu.make_async_copy(first_grad, total, sems.at[held.shape[0]])
        self.count, self.width = total.shape
        self.tile = tiles.shape[2]

    def weight_load(self, t):
        columns = pl.ds(pl.multiple_of(t * self.tile, self.tile), self.tile)
        slot = lax.rem(t, self.tiles.shape[0])
        return pltpu.make_async_copy(
            self.weight.at[:, columns], self.tiles.at[slot], self.load.at[slot]
        )

    def probs_load(self, pair):
        slot = lax.rem(pair, self.held.shape[0])
        return pltpu.make_async_copy(
            self.probs.at[pair], self.held.at[slot], self.sems.at[slot]
        )

    def begin(self):
        for pair in range(self.held.shape[0]):
            self.probs_load(pair).start()
        for t in range(self.tiles.shape[0]):
            self.weight_load(t).start()
        self.grad_load.start()

    def attend(self, group):
        each = self.work.pairs // GROUPS

        slots = self.held.shape[0]

        def one(pair):
            self.probs_load(pair).wait()
            self.work.attend(pair, self.held[lax.rem(pair, slots)])
            pl.when(pair + slots < self.work.pairs)(self.probs_load(pair + slots).start)

        repeat(group * each, (group + 1) * each, one)

    def settle(self):
        repeat(0, self.work.pairs, self.work.settle)

    def weigh(self, core, target):
        shards, rows, columns = target.shape
        tile = self.tile

        def one(j):
            start = pl.multiple_of(core * columns + j * tile, tile)
            product = plain_product(self.rows_t[...], self.work.out[:, pl.ds(start, tile)])
            low = product.astype(BF16)
            for shard in range(shards):
                target[shard, :, pl.ds(pl.multiple_of(j * tile, tile), tile)] = low[
                    shard * rows : (shard + 1) * rows
                ]

        repeat(0, columns // tile, one)

    def turn(self):
        self.rows_t[...] = self.rows_ref[...].T

    def bias_sums(self, target):
        self.sums[pl.ds(0, 1), :] = total_rows(self.work.out[:, : self.width])
        self.sums[pl.ds(1, 1), :] = total_rows(self.work.out[:, 2 * self.width :])
        for shard in range(target.shape[0]):
            target[shard, pl.ds(ROW_QUERY, 2), :] = self.sums[
                pl.ds(0, 2), pl.ds(shard * LANES, LANES)
            ]

    def spread(self, half):
        count = self.weight.shape[1] // self.tile
        each = count // HALVES
        slots = self.tiles.shape[0]
        if half == 0:
            self.grad_load.wait()

        def one(t):
            self.weight_load(t).wait()
            columns = pl.ds(pl.multiple_of(t * self.tile, self.tile), self.tile)
            tile = self.tiles[lax.rem(t, slots)]
            self.total[...] += right_product(self.work.out[:, columns], tile)
            pl.when(t + slots < count)(self.weight_load(t + slots).start)

        repeat(half * each, (half + 1) * each, one)
        if half == HALVES - 1:
            rows = self.block.shape[1]
            for part in range(2):
                self.block[part] = self.total[pl.ds(part * rows, rows), :].astype(BF16)


def finish_actions(reduce, finish, swap):
    queries, vectors = 3, 4
    place = reduce.place
    found = reduce.actions()

    def load():
        finish.begin()
        finish.turn()

    found.append((("load",), load))
    for group in range(GROUPS):
        found.append((("att", group), lambda group=group: finish.attend(group)))
    found.append((("settleatt",), finish.settle))
    found.append((("leave",), lambda: finish.weigh(1 - place.core, reduce.grads[queries])))
    found.append((("own",), lambda: finish.weigh(place.core, reduce.own[queries])))
    found.append((("sums",), lambda: finish.bias_sums(reduce.own[vectors])))
    for half in range(HALVES):
        found.append((("dx", half), lambda half=half: finish.spread(half)))
    found.append((("swapin",), swap.start))
    return found


def finish_kernel(parts, order, *refs):
    rows_ref, qkv, away, grad, table_ref, first_grad, probs, weight = refs[:8]
    grads = list(refs[8:11])
    outs, swapped, refs = refs[11:16], refs[16], refs[17:]
    leave_q, tiles, held, out, keep, leave, come, total, sums, rows_t, block = refs[:11]
    send2, recv2, load2, sems = refs[11:15]
    scratch, rest = refs[15:-6], refs[-6:]
    place = Place()
    work = AttentionBackward(place, qkv, away, grad, out, keep, leave, come, send2, recv2)
    finish = Finish(
        work, tiles, weight, rows_ref, rows_t, first_grad, total, block, sums, held, probs, load2, sems
    )
    reduce = Reduce(place, parts, grads + [leave_q, None], outs, scratch, *rest[:3])
    swap = Swap(place, [block], [swapped], *rest[3:6])
    for shard in range(LINE * PAIR):
        reduce.own[4][shard] = table_ref[pl.ds(shard * TABLE_ROWS, TABLE_ROWS), :]
    greet(place)
    for step in in_order(finish_actions(reduce, finish, swap), order):
        step()
    work.finish()
    swap.finish()


def finish(rows, saved, grad, first_grad, table, weight, grads, parts, collective_id, order):
    qkv, away, probs = saved
    count, width = rows.shape
    pairs = width // SPAN
    tile = 512
    labels = reduce_labels(parts)
    whole = pl.BlockSpec(memory_space=pltpu.VMEM)
    far = pl.BlockSpec(memory_space=pltpu.HBM)
    queries = parts[3]
    return pl.pallas_call(
        functools.partial(finish_kernel, parts, order),
        out_shape=[jax.ShapeDtypeStruct((p.rows, p.columns), p.dtype) for p in parts]
        + [jax.ShapeDtypeStruct((2, count // 2, width), BF16)],
        in_specs=[whole] * 5 + [far] * 6,
        out_specs=[whole] * len(parts) + [far],
        scratch_shapes=[
            pltpu.VMEM((LINE * PAIR, queries.half_rows, queries.half_columns), BF16),
            pltpu.VMEM((2, width, tile), BF16),
            pltpu.VMEM((pairs // 2,) + probs.shape[1:], BF16),
            pltpu.VMEM((count, 3 * width), BF16),
            pltpu.VMEM((count, 2 * width), F32),
            pltpu.VMEM((count, 2 * width), BF16),
            pltpu.VMEM((count, 2 * width), BF16),
            pltpu.VMEM((count, width), F32),
            pltpu.VMEM((8, width), F32),
            pltpu.VMEM((width, count), BF16),
            pltpu.VMEM((2, count // 2, width), BF16),
            pltpu.SemaphoreType.DMA((2, pairs)),
            pltpu.SemaphoreType.DMA((2, pairs)),
            pltpu.SemaphoreType.DMA((2,)),
            pltpu.SemaphoreType.DMA((pairs // 2 + 1,)),
        ]
        + reduce_scratch(parts)
        + [
            pltpu.SemaphoreType.DMA((len(labels.numbers),)),
            pltpu.SemaphoreType.DMA((len(labels.numbers),)),
            pltpu.SemaphoreType.DMA((len(parts) * 2 * len(SPOTS),)),
        ]
        + swap_scratch(1),
        compiler_params=pltpu.CompilerParams(
            collective_id=collective_id, has_side_effects=True, vmem_limit_bytes=VMEM
        ),
        name="attention_backward_reduce",
    )(rows, qkv, away, grad, table, first_grad, probs, weight, *grads)


def exact_gelu(hidden):
    return jax.nn.gelu(hidden, approximate=False)


def plain_product(left, right):
    return jnp.dot(left, right, preferred_element_type=F32)


def left_product(left, right):
    return lax.dot_general(left, right, (((0,), (0,)), ((), ())), preferred_element_type=F32)


def right_product(left, right):
    return lax.dot_general(left, right, (((1,), (1,)), ((), ())), preferred_element_type=F32)


def column_sums(rows):
    return jnp.sum(rows.astype(F32), axis=0)


def norm_parts(total):
    average = jnp.mean(total, axis=-1, keepdims=True)
    centered = total - average
    variance = jnp.mean(centered * centered, axis=-1, keepdims=True)
    rate = lax.rsqrt(variance + EPSILON)
    return centered * rate, rate


def norm_back(unit, rate, grad):
    return rate * (
        grad
        - jnp.mean(grad, axis=-1, keepdims=True)
        - unit * jnp.mean(grad * unit, axis=-1, keepdims=True)
    )


def split_columns(packed, widths):
    pieces = []
    start = 0
    for width in widths:
        pieces.append(packed[..., start : start + width])
        start += width
    return pieces


def native_forward(queries, keys_all, values_all, key_valid, heads):
    shape = queries.shape[:2] + (heads, HEAD_DIM)
    key_shape = keys_all.shape[:2] + (heads, HEAD_DIM)
    scores = jnp.einsum(
        "sqhd,skhd->shqk",
        queries.reshape(shape),
        keys_all.reshape(key_shape),
        preferred_element_type=F32,
    ) * (HEAD_DIM**-0.5)
    scores = jnp.where(key_valid[:, None, None, :], scores, -1e30)
    top = jnp.max(scores, axis=-1, keepdims=True)
    weights = jnp.exp(scores - top)
    probs = (weights / jnp.sum(weights, axis=-1, keepdims=True)).astype(BF16)
    context = jnp.einsum(
        "shqk,skhd->sqhd", probs, values_all.reshape(key_shape), preferred_element_type=F32
    )
    return context.reshape(queries.shape).astype(BF16), probs


def native_backward(queries, keys_all, values_all, probs, context_grad, heads):
    shape = queries.shape[:2] + (heads, HEAD_DIM)
    key_shape = keys_all.shape[:2] + (heads, HEAD_DIM)
    scale = HEAD_DIM**-0.5
    grad_heads = context_grad.reshape(shape)
    wide = probs.astype(F32)
    probs_grad = jnp.einsum(
        "sqhd,skhd->shqk", grad_heads, values_all.reshape(key_shape), preferred_element_type=F32
    )
    inner_total = jnp.sum(wide * probs_grad, axis=-1, keepdims=True)
    scores_grad = (wide * (probs_grad - inner_total)).astype(BF16)
    query_grad = jnp.einsum(
        "shqk,skhd->sqhd", scores_grad, keys_all.reshape(key_shape), preferred_element_type=F32
    )
    key_part = jnp.einsum(
        "shqk,sqhd->skhd", scores_grad, queries.reshape(shape), preferred_element_type=F32
    )
    value_part = jnp.einsum("shqk,sqhd->skhd", probs, grad_heads, preferred_element_type=F32)
    return (
        (query_grad * scale).astype(BF16).reshape(queries.shape),
        (key_part * scale).astype(BF16).reshape(keys_all.shape),
        value_part.astype(BF16).reshape(values_all.shape),
    )


def gather_rows(part):
    return lax.all_gather(part, "fsdp", axis=0, tiled=True)


def reduce_rows(part):
    share = lax.psum_scatter(part.astype(BF16), "fsdp", scatter_dimension=0, tiled=True)
    return lax.psum(share, "ctx").astype(F32)


def layer(flat_rows, cot_rows, row_mask, packed, widths, weights, forward, backward):
    full_qkv, full_output, full_inner, full_outer = weights
    rows, width = flat_rows.shape
    shards = packed.shape[0]
    (
        bias_query,
        bias_value,
        bias_output,
        gain_first,
        shift_first,
        bias_inner,
        bias_outer,
        gain_second,
        shift_second,
    ) = [piece.reshape(-1).astype(F32) for piece in split_columns(packed, widths)]
    bias_qkv = jnp.concatenate((bias_query, jnp.zeros_like(bias_query), bias_value))
    qkv = (plain_product(flat_rows, full_qkv) + bias_qkv).astype(BF16)
    context, saved = forward(qkv)

    first_sum = flat_rows.astype(F32) + plain_product(context, full_output) + bias_output
    first_unit, first_rate = norm_parts(first_sum)
    normed = first_unit * gain_first + shift_first
    normed_low = normed.astype(BF16)
    hidden = plain_product(normed_low, full_inner) + bias_inner
    active, gelu_back = jax.vjp(exact_gelu, hidden)
    active_low = active.astype(BF16)
    second_sum = normed + plain_product(active_low, full_outer) + bias_outer
    second_unit, second_rate = norm_parts(second_sum)
    output = ((second_unit * gain_second + shift_second) * row_mask).astype(BF16)

    out_grad = cot_rows.astype(F32) * row_mask
    second_gain_part = jnp.sum(out_grad * second_unit, axis=0)
    second_shift_part = jnp.sum(out_grad, axis=0)
    second_grad = norm_back(second_unit, second_rate, out_grad * gain_second)
    second_low = second_grad.astype(BF16)
    outer_weight_part = left_product(active_low, second_low).astype(BF16)
    outer_bias_part = column_sums(second_low)
    (hidden_grad,) = gelu_back(right_product(second_low, full_outer))
    hidden_low = hidden_grad.astype(BF16)
    inner_weight_part = left_product(normed_low, hidden_low).astype(BF16)
    inner_bias_part = column_sums(hidden_low)
    normed_grad = second_grad + right_product(hidden_low, full_inner)
    first_gain_part = jnp.sum(normed_grad * first_unit, axis=0)
    first_shift_part = jnp.sum(normed_grad, axis=0)
    first_grad = norm_back(first_unit, first_rate, normed_grad * gain_first)
    branch_low = first_grad.astype(BF16)
    output_weight_part = left_product(context, branch_low).astype(BF16)
    output_bias_part = column_sums(branch_low)
    context_grad = right_product(branch_low, full_output).astype(BF16)
    qkv_grad = backward(saved, context_grad)
    qkv_weight_part = left_product(flat_rows, qkv_grad).astype(BF16)
    query_bias_part = column_sums(qkv_grad[:, :width])
    value_bias_part = column_sums(qkv_grad[:, 2 * width :])
    input_grad = first_grad + right_product(qkv_grad, full_qkv)
    vector_parts = (
        query_bias_part,
        value_bias_part,
        output_bias_part,
        first_gain_part,
        first_shift_part,
        inner_bias_part,
        outer_bias_part,
        second_gain_part,
        second_shift_part,
    )
    packed_parts = jnp.concatenate([part.reshape(shards, -1) for part in vector_parts], axis=1)
    return (
        output,
        input_grad,
        packed_parts,
        (qkv_weight_part, output_weight_part, inner_weight_part, outer_weight_part),
    )


def native_body(inputs, cotangent, lengths, vectors, weights):
    widths = [member.shape[0] for member in vectors]
    packed = lax.all_gather(jnp.concatenate(vectors), "fsdp", axis=0, tiled=False)
    joined = (jnp.concatenate(weights[:3], axis=1),) + weights[3:]
    full = tuple(gather_rows(part) for part in joined)
    micro, seqs, block_len, width = inputs.shape
    heads = width // HEAD_DIM
    total_slots = block_len * lax.axis_size("ctx")
    group = micro * seqs
    rows = group * block_len
    flat_len = lengths.reshape(group)
    local_pos = lax.axis_index("ctx") * block_len + jnp.arange(block_len, dtype=jnp.int32)
    row_mask = (local_pos[None, :] < flat_len[:, None]).astype(F32).reshape(rows, 1)
    key_valid = jnp.arange(total_slots, dtype=jnp.int32)[None, :] < flat_len[:, None]

    def forward(qkv):
        queries = qkv[:, :width].reshape(group, block_len, width)
        keys_values = lax.all_gather(
            qkv[:, width:].reshape(group, block_len, 2 * width), "ctx", axis=1, tiled=True
        )
        keys, values = keys_values[:, :, :width], keys_values[:, :, width:]
        context, probs = native_forward(queries, keys, values, key_valid, heads)
        return context.reshape(rows, width), (queries, keys, values, probs)

    def backward(saved, context_grad):
        query_grad, key_part, value_part = native_backward(
            *saved, context_grad.reshape(group, block_len, width), heads
        )
        keys_values_grad = lax.psum_scatter(
            jnp.concatenate((key_part, value_part), axis=2), "ctx", scatter_dimension=1, tiled=True
        )
        return jnp.concatenate(
            (query_grad.reshape(rows, width), keys_values_grad.reshape(rows, 2 * width)), axis=1
        )

    output, input_grad, packed_parts, parts = layer(
        inputs.reshape(rows, width),
        cotangent.reshape(rows, width),
        row_mask,
        packed,
        widths,
        full,
        forward,
        backward,
    )
    share = lax.psum_scatter(packed_parts, "fsdp", scatter_dimension=0, tiled=True)
    return (
        output.reshape(inputs.shape),
        input_grad.reshape(inputs.shape),
        split_columns(lax.psum(share, "ctx")[0], widths),
        tuple(split_columns(reduce_rows(parts[0]), [width] * 3))
        + tuple(reduce_rows(part) for part in parts[1:]),
    )


def direct_body(inputs, cotangent, lengths, vectors, weights):
    micro, seqs, block_len, width = inputs.shape
    shards = LINE * PAIR
    lengths = lengths.reshape(micro)
    rows = 2 * block_len
    table = jnp.zeros((TABLE_ROWS, LANES), F32)
    row = 0
    for vector in vectors:
        lines = vector.shape[0] // LANES
        filled = ((row, TABLE_ROWS - row - lines), (0, 0))
        table += jnp.pad(vector.astype(F32).reshape(lines, LANES), filled)
        row += lines
    query_weight, key_weight, value_weight, output_weight, inner_weight, outer_weight = weights
    shard_rows, hidden = inner_weight.shape
    flows = [Flow(0, TABLE_ROWS, lambda core, side: (0, TABLE_ROWS, 0, LANES), cores=False)]
    flows += column_flows(1, shard_rows, 3 * width, *GATHER_SPLIT[0])
    flows += column_flows(2, shard_rows, width, *GATHER_SPLIT[1])
    flows += column_flows(3, shard_rows, hidden, *GATHER_SPLIT[2])
    flows += row_flows(4, hidden // shards, width, *GATHER_SPLIT[3])
    (
        tables,
        full_qkv,
        full_output,
        full_inner,
        full_outer,
        in_rows,
        qkv,
        context,
        probs,
        away,
    ) = start(
        (table.astype(BF16),) + weights,
        ((0, 0), (1, 0), (1, width), (1, 2 * width), (2, 0), (3, 0), (4, 0)),
        inputs.reshape(micro, block_len, width),
        lengths,
        flows,
        shards,
        1,
        GATHER_ORDER,
    )
    in_rows = in_rows.reshape(rows, width)
    output, first_grad, context_grad, table_grad, output_part, inner_part, outer_part = middle(
        3,
        in_rows,
        context,
        cotangent.reshape(micro, block_len, width),
        lengths,
        tables,
        full_output,
        full_inner,
        full_outer,
    )
    sums = finish(
        in_rows,
        (qkv, away, probs),
        context_grad,
        first_grad,
        table_grad,
        full_qkv,
        (inner_part, outer_part, output_part),
        [
            column_part(shard_rows, hidden, *REDUCE_SPLIT[0]),
            row_part(hidden // shards, width, *REDUCE_SPLIT[1]),
            column_part(shard_rows, width, *REDUCE_SPLIT[2]),
            column_part(shard_rows, 3 * width, *REDUCE_SPLIT[3], inside=True),
            vector_part(TABLE_ROWS, LANES, inside=True),
        ],
        2,
        REDUCE_ORDER,
    )
    inner_share, outer_share, output_share, qkv_share, table_share, grads = sums
    lines = tuple(vector.shape[0] // LANES for vector in vectors)
    wide = widen(
        (qkv_share, output_share, inner_share, outer_share, grads, output),
        (3, 1, 1, 1, 1, 1),
        (F32,) * 5 + (BF16,),
        table_share,
        lines,
    )
    return (
        wide[7].reshape(inputs.shape),
        wide[6].reshape(inputs.shape),
        tuple(wide[8:]),
        tuple(wide[:6]),
    )


def body(
    inputs,
    cotangent,
    lengths,
    query_weight,
    key_weight,
    value_weight,
    output_weight,
    query_bias,
    value_bias,
    output_bias,
    first_gain,
    first_shift,
    inner_weight,
    inner_bias,
    outer_weight,
    outer_bias,
    second_gain,
    second_shift,
):
    vectors = (
        query_bias,
        value_bias,
        output_bias,
        first_gain,
        first_shift,
        inner_bias,
        outer_bias,
        second_gain,
        second_shift,
    )
    widths = [member.shape[0] for member in vectors]
    weights = (
        query_weight,
        key_weight,
        value_weight,
        output_weight,
        inner_weight,
        outer_weight,
    )
    laid_out = lax.axis_size("fsdp") == LINE * PAIR and lax.axis_size("ctx") == 4
    whole_lines = all(extent % LANES == 0 for extent in widths)
    direct = laid_out and inputs.shape[:2] == (2, 1) and whole_lines
    run = direct_body if direct else native_body
    output, input_grad, shares, weight_shares = run(inputs, cotangent, lengths, vectors, weights)
    query_share, key_share, value_share, output_share, inner_share, outer_share = weight_shares
    return (
        output,
        input_grad,
        query_share,
        key_share,
        value_share,
        output_share,
        shares[0],
        shares[1],
        shares[2],
        shares[3],
        shares[4],
        inner_share,
        shares[5],
        outer_share,
        shares[6],
        shares[7],
        shares[8],
    )


def solution(mesh):
    data = P(None, "fsdp", "ctx", None)
    matrix = P("fsdp", None)
    vector = P("fsdp")
    return jax.shard_map(
        body,
        mesh=mesh,
        in_specs=(data, data, P(None, "fsdp"))
        + (matrix,) * 4
        + (vector,) * 5
        + (matrix, vector, matrix, vector, vector, vector),
        out_specs=(data, data)
        + (matrix,) * 4
        + (vector,) * 5
        + (matrix, vector, matrix, vector, vector, vector),
        check_vma=False,
    )
```

```python
import functools

import jax
import jax.numpy as jnp
from jax import lax
from jax.experimental import pallas as pl
from jax.experimental.pallas import tpu as pltpu
from jax.sharding import PartitionSpec as P

HEAD_DIM = 64
EPSILON = 1e-06
F32 = jnp.float32
BF16 = jnp.bfloat16

GATHER_SPLIT = ((256, 384), (256, 128), (1024, 128), (128, 64))
REDUCE_SPLIT = ((1024, 384), (160, 0), (256, 128), (768, 256))
GATHER_ORDER = (
    2, 3, 7, 64, 0, 10, 30, 72, 132, 1, 5, 38, 28, 200, 140, 43, 29, 77, 62, 15, 111, 98, 96, 8,
    179, 32, 63, 180, 217, 69, 66, 164, 166, 81, 208, 40, 97, 134, 137, 99, 131, 4, 55, 145, 74,
    100, 149, 39, 47, 183, 202, 83, 68, 9, 108, 34, 31, 213, 205, 148, 49, 12, 115, 106, 114, 45,
    142, 136, 13, 151, 35, 46, 16, 48, 76, 204, 162, 230, 219, 203, 42, 130, 41, 117, 85, 17, 82,
    102, 6, 184, 168, 174, 138, 101, 84, 116, 167, 201, 123, 152, 103, 143, 89, 144, 118, 94, 198,
    165, 78, 222, 185, 169, 153, 14, 220, 70, 33, 128, 86, 50, 175, 23, 110, 107, 75, 199, 181,
    65, 79, 25, 171, 67, 225, 147, 37, 218, 135, 71, 133, 150, 90, 191, 157, 176, 21, 196, 154,
    52, 20, 18, 209, 120, 80, 206, 216, 192, 26, 60, 36, 170, 113, 231, 24, 182, 163, 141, 11,
    186, 56, 215, 232, 22, 95, 59, 233, 178, 93, 214, 212, 51, 210, 91, 234, 223, 235, 197, 105,
    158, 161, 226, 19, 127, 57, 53, 139, 236, 73, 119, 159, 195, 221, 27, 188, 211, 146, 44, 87,
    237, 173, 121, 229, 124, 58, 112, 109, 54, 160, 177, 88, 129, 92, 61, 125, 155, 207, 172, 238,
    122, 227, 104, 126, 156, 193, 189, 187, 239, 228, 190, 194, 224, 240,
)
REDUCE_ORDER = (
    33, 7, 9, 0, 8, 215, 84, 10, 85, 216, 1, 87, 86, 12, 5, 100, 29, 4, 102, 103, 101, 2, 217, 16,
    91, 92, 89, 11, 35, 218, 36, 3, 40, 106, 107, 93, 37, 18, 94, 39, 219, 88, 42, 31, 38, 220,
    221, 43, 24, 22, 25, 23, 110, 15, 17, 28, 26, 96, 44, 222, 153, 67, 68, 150, 151, 53, 57, 21,
    13, 6, 14, 104, 105, 154, 30, 152, 69, 189, 45, 108, 149, 19, 118, 95, 109, 71, 72, 223, 90,
    203, 198, 77, 201, 122, 167, 111, 120, 117, 183, 199, 41, 184, 181, 20, 119, 182, 165, 121,
    169, 156, 200, 47, 51, 73, 27, 157, 191, 54, 185, 46, 32, 155, 224, 225, 159, 226, 158, 171,
    97, 98, 55, 133, 124, 70, 79, 205, 141, 143, 75, 76, 74, 160, 186, 59, 161, 187, 139, 58, 61,
    135, 188, 112, 113, 48, 137, 49, 202, 52, 173, 206, 126, 114, 125, 193, 168, 166, 208, 34,
    123, 175, 162, 163, 190, 127, 99, 78, 192, 134, 172, 207, 56, 50, 128, 209, 210, 129, 170,
    136, 80, 81, 138, 194, 60, 195, 115, 62, 63, 204, 130, 140, 131, 82, 177, 145, 196, 174, 176,
    64, 65, 144, 132, 116, 142, 178, 179, 164, 146, 147, 211, 212, 83, 180, 197, 66, 148, 213,
    214,
)

MESH = pl.DeviceIdType.MESH
LINE = 4
PAIR = 2


class Place:
    def __init__(self):
        self.ctx = lax.axis_index("ctx")
        self.shard = lax.axis_index("fsdp")
        self.side = lax.div(self.ctx, 2)
        self.core = lax.rem(self.ctx, 2)
        self.line = lax.div(self.shard, PAIR)
        self.pair = lax.rem(self.shard, PAIR)

    def ahead(self, way):
        return (self.ctx, self.shard + way * PAIR)

    def across(self):
        return (self.ctx, self.shard + 1 - 2 * self.pair)

    def beside(self):
        return (self.ctx + 2 - 4 * self.side, self.shard)

    def twin(self):
        return (self.ctx + 1 - 2 * self.core, self.shard)

    def has(self, way, steps):
        if steps == 0:
            return None
        return self.line >= steps if way > 0 else self.line <= LINE - 1 - steps

    def can(self, way):
        return self.line <= LINE - 2 if way > 0 else self.line >= 1

    def shard_of(self, way, steps, other):
        pair = 1 - self.pair if other else self.pair
        return (self.line - way * steps) * PAIR + pair


def when(conditions, action):
    held = [c for c in conditions if c is not None]
    if not held:
        action()
        return
    both = held[0]
    for c in held[1:]:
        both = jnp.logical_and(both, c)
    pl.when(both)(action)


def greet(place):
    barrier = pltpu.get_barrier_semaphore()
    for peer in (place.across(), place.beside(), place.twin()):
        pl.semaphore_signal(barrier, inc=1, device_id=peer, device_id_type=MESH)
    for way in (1, -1):
        when(
            [place.can(way)],
            lambda way=way: pl.semaphore_signal(
                barrier, inc=1, device_id=place.ahead(way), device_id_type=MESH
            ),
        )
    lines = jnp.minimum(place.line, 1) + jnp.minimum(LINE - 1 - place.line, 1)
    pl.semaphore_wait(barrier, 3 + lines)


class Flow:
    def __init__(self, array, shard_rows, region, order="line", sides=False, cores=True):
        self.array = array
        self.shard_rows = shard_rows
        self.region = region
        self.order = order
        self.sides = sides
        self.cores = cores

    def view(self, ref, shard, core, side):
        row, rows, column, columns = self.region(core, side)
        start = row if shard is None else shard * self.shard_rows + row
        if not isinstance(start, int):
            start = pl.multiple_of(start, 16)
        if not isinstance(column, int):
            column = pl.multiple_of(column, 128)
        return ref.at[pl.ds(start, rows), pl.ds(column, columns)]


def positions(order):
    found = []
    if order == "line":
        found.append(("P", 1, 0, True))
        for steps in range(1, LINE):
            for way in (1, -1):
                found.append(("L", way, steps, False))
                found.append(("P", way, steps, True))
    else:
        found.append(("P", 1, 0, True))
        for steps in range(1, LINE):
            for way in (1, -1):
                found.append(("L", way, steps, False))
                found.append(("L", way, steps, True))
    return found


class Labels:
    def __init__(self):
        self.numbers = {}

    def __call__(self, key):
        return self.numbers.setdefault(key, len(self.numbers))


def gather_labels(flows):
    labels = Labels()
    for number, flow in enumerate(flows):
        for spot in positions(flow.order):
            labels((number, "in") + spot)
            if flow.sides:
                labels((number, "side") + spot)
            if flow.cores:
                labels((number, "twin") + spot)
                if flow.sides:
                    labels((number, "twinside") + spot)
    return labels


class Gather:
    def __init__(self, place, flows, owns, fulls, send, recv):
        self.place, self.flows, self.owns, self.fulls = place, flows, owns, fulls
        self.send, self.recv = send, recv
        self.labels = gather_labels(flows)
        self.sent = []

    def copy(self, number, key, spot, peer, core, side, own=False):
        flow = self.flows[number]
        place = self.place
        if own:
            shard = place.shard
            source = flow.view(self.owns[flow.array], None, core, side)
        else:
            shard = place.shard_of(*spot[1:])
            source = flow.view(self.fulls[flow.array], shard, core, side)
        target = flow.view(self.fulls[flow.array], shard, core, side)
        label = self.labels((number,) + key)
        return pltpu.make_async_remote_copy(
            source,
            target,
            self.send.at[label],
            self.recv.at[label],
            device_id=peer,
            device_id_type=MESH,
        )

    def start(self, conditions, copy):
        when(conditions, copy.start)
        self.sent.append((conditions, copy))

    def begin(self, number):
        flow, place = self.flows[number], self.place
        core, side = place.core, place.side
        here = (None, 1, 0, False)
        for way in (1, -1):
            self.start(
                [place.can(way)],
                self.copy(
                    number, ("in", "L", way, 1, False), here, place.ahead(way), core, side, True
                ),
            )
        self.start(
            [],
            self.copy(number, ("in", "P", 1, 0, True), here, place.across(), core, side, True),
        )

    def arrive(self, number, spot):
        flow, place = self.flows[number], self.place
        kind, way, steps, other = spot
        core, side = place.core, place.side
        there = place.has(way, steps)

        def take():
            self.copy(number, ("in",) + spot, spot, place.across(), core, side).wait_recv()

        when([there], take)

        def onward(extra, key, peer):
            self.start(
                [c for c in (there, extra) if c is not None],
                self.copy(number, key, spot, peer, core, side),
            )

        if kind == "L" and steps + 1 < LINE:
            onward(place.can(way), ("in", "L", way, steps + 1, other), place.ahead(way))
        if kind == "L" and flow.order == "line":
            onward(None, ("in", "P", way, steps, True), place.across())
        if kind == "P" and flow.order == "pair":
            for direction in (1, -1):
                onward(
                    place.can(direction), ("in", "L", direction, 1, True), place.ahead(direction)
                )
        if flow.sides:
            onward(None, ("side",) + spot, place.beside())
        if flow.cores:
            onward(None, ("twin",) + spot, place.twin())

    def arrive_side(self, number, spot):
        flow, place = self.flows[number], self.place
        there = place.has(*spot[1:3])
        core, side = place.core, 1 - place.side
        when(
            [there],
            lambda: self.copy(
                number, ("side",) + spot, spot, place.beside(), core, side
            ).wait_recv(),
        )
        if flow.cores:
            self.start(
                [there] if there is not None else [],
                self.copy(number, ("twinside",) + spot, spot, place.twin(), core, side),
            )

    def arrive_twin(self, number, spot):
        flow, place = self.flows[number], self.place
        there = place.has(*spot[1:3])
        core = 1 - place.core
        if flow.cores:
            when(
                [there],
                lambda: self.copy(
                    number, ("twin",) + spot, spot, place.twin(), core, place.side
                ).wait_recv(),
            )
            if flow.sides:
                when(
                    [there],
                    lambda: self.copy(
                        number, ("twinside",) + spot, spot, place.twin(), core, 1 - place.side
                    ).wait_recv(),
                )

    def actions(self):
        found = []
        for n, flow in enumerate(self.flows):
            found.append((("begin", n), lambda n=n: self.begin(n)))
        for index in range(len(positions("line"))):
            for n, flow in enumerate(self.flows):
                spot = positions(flow.order)[index]
                found.append((("in", n, spot), lambda n=n, spot=spot: self.arrive(n, spot)))
                if flow.sides:
                    found.append(
                        (("side", n, spot), lambda n=n, spot=spot: self.arrive_side(n, spot))
                    )
        return found

    def wait_twins(self, arrays):
        for number, flow in enumerate(self.flows):
            if flow.array in arrays:
                for spot in positions(flow.order):
                    self.arrive_twin(number, spot)

    def finish(self, arrays):
        self.wait_twins(arrays)
        for conditions, copy in self.sent:
            when(conditions, copy.wait_send)


class Swap:
    def __init__(self, place, ins, outs, send, recv, local):
        side = place.side
        self.away = [
            pltpu.make_async_remote_copy(
                here.at[1 - side],
                there.at[side],
                send.at[k],
                recv.at[k],
                device_id=place.beside(),
                device_id_type=MESH,
            )
            for k, (here, there) in enumerate(zip(ins, outs))
        ]
        self.stay = [
            pltpu.make_async_copy(here.at[side], there.at[side], local.at[k])
            for k, (here, there) in enumerate(zip(ins, outs))
        ]

    def start(self, k=0):
        self.away[k].start()
        self.stay[k].start()

    def wait_here(self, k):
        self.away[k].wait_recv()
        self.stay[k].wait()
        self.held = k

    held = None

    def finish(self):
        for k, (away, stay) in enumerate(zip(self.away, self.stay)):
            if k == self.held:
                away.wait_send()
            else:
                away.wait()
                stay.wait()


def swap_scratch(count):
    return [pltpu.SemaphoreType.DMA((count,))] * 3


def column_flows(array, shard_rows, columns, shared, early):
    half = columns // 2
    part = (half - shared) // 2
    flows = []
    if shared:
        flows.append(
            Flow(array, shard_rows, lambda core, side: (0, shard_rows, core * half, shared))
        )
    if early:
        flows.append(
            Flow(
                array,
                shard_rows,
                lambda core, side: (0, shard_rows, core * half + shared + side * part, early),
                sides=True,
            )
        )
    if part > early:
        flows.append(
            Flow(
                array,
                shard_rows,
                lambda core, side: (
                    0,
                    shard_rows,
                    core * half + shared + side * part + early,
                    part - early,
                ),
                order="pair",
                sides=True,
            )
        )
    return flows


def row_flows(array, shard_rows, columns, shared, early):
    half = shard_rows // 2
    part = (half - shared) // 2
    flows = [
        Flow(array, shard_rows, lambda core, side: (core * half, shared, 0, columns)),
        Flow(
            array,
            shard_rows,
            lambda core, side: (core * half + shared + side * part, early, 0, columns),
            sides=True,
        ),
        Flow(
            array,
            shard_rows,
            lambda core, side: (core * half + shared + side * part + early, part - early, 0, columns),
            order="pair",
            sides=True,
        ),
    ]
    return [flow for flow in flows if flow.region(0, 0)[1]]


class Part:
    def __init__(self, rows, columns, along, flows, dtype=BF16, inside=False):
        self.rows, self.columns, self.along, self.dtype = rows, columns, along, dtype
        self.inside = inside
        self.flows = flows
        self.half_rows = rows // 2 if along == "rows" else rows
        self.half_columns = columns // 2 if along == "columns" else columns

    def half(self, ref, shard, core):
        base = 0 if shard is None else pl.multiple_of(shard * self.rows, 16)
        if self.along == "rows":
            row = core * self.half_rows + (0 if shard is None else shard * self.rows)
            return ref.at[pl.ds(pl.multiple_of(row, 16), self.half_rows), :]
        if self.along == "columns":
            column = pl.multiple_of(core * self.half_columns, 128)
            return ref.at[pl.ds(base, self.rows), pl.ds(column, self.half_columns)]
        return ref.at[pl.ds(base, self.rows), :]

    def inner(self, flow, side):
        first, extent = flow[0](side), flow[1]
        if self.along == "rows":
            start = first if isinstance(first, int) else pl.multiple_of(first, 16)
            return pl.ds(start, extent), slice(None)
        start = first if isinstance(first, int) else pl.multiple_of(first, 128)
        return slice(None), pl.ds(start, extent)

    def outer(self, flow, core, side):
        first, extent = flow[0](side), flow[1]
        if self.along == "rows":
            return pl.ds(pl.multiple_of(core * self.half_rows + first, 16), extent), slice(None)
        if self.along == "columns":
            return slice(None), pl.ds(
                pl.multiple_of(core * self.half_columns + first, 128), extent
            )
        return slice(None), slice(None)

    def extent(self, flow):
        if self.along == "rows":
            return flow[1], self.half_columns
        return self.half_rows, flow[1]


SPOTS = [(1, 3), (-1, 3), (1, 2), (-1, 2), (1, 1), (-1, 1), (1, 0)]


def reduce_scratch(parts):
    shapes = []
    for part in parts:
        half = (LINE * PAIR, part.half_rows, part.half_columns)
        shapes.append(pltpu.VMEM(half, part.dtype))
        shapes.append(pltpu.VMEM(half if part.along else half[1:], part.dtype))
        for flow in part.flows:
            rows, columns = part.extent(flow)
            shapes.append(
                pltpu.VMEM((LINE * PAIR if flow[3] else 1, rows, columns), part.dtype)
            )
            shapes.append(
                pltpu.VMEM((LINE if flow[2] == "line" else 1, rows, columns), part.dtype)
            )
            shapes.append(
                pltpu.VMEM(
                    ((LINE + 1) * (1 if flow[2] == "line" else PAIR), rows, columns), part.dtype
                )
            )
    return shapes


def reduce_labels(parts):
    labels = Labels()
    for n, part in enumerate(parts):
        for way, steps in SPOTS:
            for other in (False, True):
                labels((n, "twin", way, steps, other))
        labels((n, "twinend"))
        for k, flow in enumerate(part.flows):
            for way, steps in SPOTS:
                for other in (False, True):
                    if flow[3]:
                        labels((n, k, "side", way, steps, other))
                    if flow[2] == "pair" or not other:
                        labels((n, k, "line", way, steps, other))
                        if steps == 0:
                            labels((n, k, "line", -way, steps, other))
                if flow[2] == "line" or steps == 0:
                    labels((n, k, "pair", way, steps))
            labels((n, k, "sideend"))
            labels((n, k, "twinend"))
            labels((n, k, "twinsideend"))
    return labels


class Reduce:
    def __init__(self, place, parts, grads, outs, scratch, send, recv, load):
        self.place, self.parts, self.grads, self.outs = place, parts, grads, outs
        self.send, self.recv, self.load = send, recv, load
        self.labels = reduce_labels(parts)
        self.sent = []
        self.own, self.other, self.lanes = [], [], []
        at = 0
        for part in parts:
            self.own.append(scratch[at])
            self.other.append(scratch[at + 1])
            at += 2
            lanes = []
            for _ in part.flows:
                lanes.append(scratch[at : at + 3])
                at += 3
            self.lanes.append(lanes)

    def copy(self, source, target, key, peer):
        label = self.labels(key)
        return pltpu.make_async_remote_copy(
            source,
            target,
            self.send.at[label],
            self.recv.at[label],
            device_id=peer,
            device_id_type=MESH,
        )

    def start(self, conditions, copy):
        when(conditions, copy.start)
        self.sent.append((conditions, copy))

    def there(self, spot):
        return self.place.has(-spot[0], spot[1])

    def shard(self, spot, other):
        return self.place.shard_of(-spot[0], spot[1], other)

    def keep(self, n, spot, other):
        shard = self.shard(spot, other)
        label = SPOTS.index(spot) * 2 + int(other)
        return pltpu.make_async_copy(
            self.parts[n].half(self.grads[n], shard, self.place.core),
            self.own[n].at[shard],
            self.load.at[n * 2 * len(SPOTS) + label],
        )

    def twin(self, n, spot, other, core):
        shard = self.shard(spot, other)
        part = self.parts[n]
        return self.copy(
            self.grads[n].at[shard] if part.inside else part.half(self.grads[n], shard, core),
            self.other[n].at[shard],
            (n, "twin") + spot + (other,),
            self.place.twin(),
        )

    def begin(self, n, spot):
        there = self.there(spot)
        for other in (True, False):
            if not self.parts[n].inside:
                when([there], self.keep(n, spot, other).start)
            if self.parts[n].along:
                self.start([there], self.twin(n, spot, other, 1 - self.place.core))

    def piece(self, n, k, shard, side):
        part = self.parts[n]
        rows, columns = part.inner(part.flows[k], side)
        return self.own[n].at[shard, rows, columns]

    def side_copy(self, n, k, spot, other, side):
        shard = self.shard(spot, other)
        return self.copy(
            self.piece(n, k, shard, side),
            self.lanes[n][k][0].at[shard],
            (n, k, "side") + spot + (other,),
            self.place.beside(),
        )

    def add_cores(self, n, spot):
        there = self.there(spot)
        part = self.parts[n]
        for other in (True, False):

            def add(other=other):
                shard = self.shard(spot, other)
                if not part.inside:
                    self.keep(n, spot, other).wait()
                if part.along:
                    self.twin(n, spot, other, self.place.core).wait_recv()
                    self.own[n][shard] = self.own[n][shard] + self.other[n][shard]

            when([there], add)
        for other in (True, False):
            for k, flow in enumerate(part.flows):
                if flow[3]:
                    self.start([there], self.side_copy(n, k, spot, other, 1 - self.place.side))
                elif other:
                    self.start([there], self.pair_copy(n, k, spot, self.shard(spot, True)))

    def pair_copy(self, n, k, spot, shard):
        flow = self.parts[n].flows[k]
        slot = self.place.line + spot[0] * spot[1] if flow[2] == "line" else 0
        return self.copy(
            self.piece(n, k, shard, self.place.side),
            self.lanes[n][k][1].at[slot],
            (n, k, "pair") + spot,
            self.place.across(),
        )

    def add_sides(self, n, k, spot):
        there = self.there(spot)
        side = self.place.side
        for other in (True, False):

            def add(other=other):
                shard = self.shard(spot, other)
                self.side_copy(n, k, spot, other, side).wait_recv()
                piece = self.piece(n, k, shard, side)
                piece[...] = piece[...] + self.lanes[n][k][0][shard]

            when([there], add)
        if self.parts[n].flows[k][2] == "line":
            self.start([there], self.pair_copy(n, k, spot, self.shard(spot, True)))

    def line_slot(self, flow, way, steps, other, line):
        slot = line if (steps > 0 or way > 0) else LINE
        return slot + (LINE + 1) * int(other) if flow[2] == "pair" else slot

    def line_copy(self, n, k, spot, other, arriving):
        flow = self.parts[n].flows[k]
        way, steps = spot
        shard = self.shard(spot, other)
        line = self.place.line + way * steps
        left = steps if arriving else steps - 1
        return self.copy(
            self.piece(n, k, shard, self.place.side),
            self.lanes[n][k][2].at[self.line_slot(flow, way, left, other, line)],
            (n, k, "line", way, left, other),
            self.place.ahead(way),
        )

    def add_line(self, n, k, spot):
        place = self.place
        there = self.there(spot)
        way, steps = spot
        side = place.side
        flow = self.parts[n].flows[k]
        if flow[2] == "line":

            def add():
                shard = self.shard(spot, False)
                self.pair_copy(n, k, spot, shard).wait_recv()
                piece = self.piece(n, k, shard, side)
                piece[...] = piece[...] + self.lanes[n][k][1][place.line + way * steps]

            when([there], add)
        for other in (True, False) if flow[2] == "pair" else (False,):
            for direction in (1, -1) if steps == 0 else (way,):

                def add_line(other=other, here=(direction, steps)):
                    self.line_copy(n, k, here, other, True).wait_recv()
                    piece = self.piece(n, k, self.shard(here, other), side)
                    line = place.line + here[0] * here[1]
                    slot = self.line_slot(flow, here[0], here[1], other, line)
                    piece[...] = piece[...] + self.lanes[n][k][2][slot]

                when([there, place.can(-direction)], add_line)
            if steps > 0:
                self.start([there], self.line_copy(n, k, spot, other, False))

    def send_pair(self, n, k):
        self.start([], self.pair_copy(n, k, (1, 0), self.shard((1, 0), True)))

    def send_swap(self, n, k):
        self.start([], self.swap(n, k))

    def settle(self, n, k):
        place = self.place
        core, side, here = place.core, place.side, place.shard
        part = self.parts[n]
        flow = part.flows[k]
        piece = self.piece(n, k, here, side)
        out = self.out_view(n, k, core, side)
        if flow[3]:
            if flow[2] == "pair":
                self.pair_copy(n, k, (1, 0), here).wait_recv()
                out[...] = piece[...] + self.lanes[n][k][1][0]
            else:
                out[...] = piece[...]
            self.start([], self.out_copy(n, k, "sideend", place.beside(), core, side))
        else:
            self.swap(n, k).wait_recv()
            out[...] = piece[...] + self.lanes[n][k][0][0]
        if part.along:
            self.start([], self.out_copy(n, k, "twinend", place.twin(), core, side))
        else:
            self.start([], self.whole(n, k))

    def settle_side(self, n, k):
        place = self.place
        core, side = place.core, 1 - place.side
        self.out_copy(n, k, "sideend", place.beside(), core, side).wait_recv()
        self.start([], self.out_copy(n, k, "twinsideend", place.twin(), core, side))

    def swap(self, n, k):
        return self.copy(
            self.piece(n, k, self.place.shard, self.place.side),
            self.lanes[n][k][0].at[0],
            (n, k, "sideend"),
            self.place.beside(),
        )

    def out_view(self, n, k, core, side):
        part = self.parts[n]
        rows, columns = part.outer(part.flows[k], core, side)
        return self.outs[n].at[rows, columns]

    def out_copy(self, n, k, key, peer, core, side):
        view = self.out_view(n, k, core, side)
        return self.copy(view, view, (n, k, key), peer)

    def last(self):
        place = self.place
        core, side = place.core, place.side
        everything = [(n, k) for n, part in enumerate(self.parts) for k in range(len(part.flows))]
        for n, k in everything:
            if self.parts[n].along:
                self.out_copy(n, k, "twinend", place.twin(), 1 - core, side).wait_recv()
                if self.parts[n].flows[k][3]:
                    self.out_copy(
                        n, k, "twinsideend", place.twin(), 1 - core, 1 - side
                    ).wait_recv()
            else:
                self.whole(n, k).wait_recv()
        for conditions, copy in self.sent:
            when(conditions, copy.wait_send)
        for n, k in everything:
            if not self.parts[n].along:
                view = self.out_view(n, k, core, side)
                view[...] = view[...] + self.other[n][...]

    def whole(self, n, k):
        return self.copy(
            self.out_view(n, k, self.place.core, self.place.side),
            self.other[n],
            (n, k, "twinend"),
            self.place.twin(),
        )

    def actions(self):
        found = []
        for n, part in enumerate(self.parts):
            for spot in SPOTS:
                found.append((("begin", n, spot), lambda n=n, s=spot: self.begin(n, s)))
        for n, part in enumerate(self.parts):
            for spot in SPOTS:
                found.append((("cores", n, spot), lambda n=n, s=spot: self.add_cores(n, s)))
            for k, flow in enumerate(part.flows):
                at = (n, k)
                for spot in SPOTS:
                    if flow[3]:
                        found.append(
                            (("sides", n, k, spot), lambda at=at, s=spot: self.add_sides(*at, s))
                        )
                    found.append(
                        (("line", n, k, spot), lambda at=at, s=spot: self.add_line(*at, s))
                    )
                if flow[2] == "pair":
                    found.append((("pair", n, k), lambda at=at: self.send_pair(*at)))
                if not flow[3]:
                    found.append((("swap", n, k), lambda at=at: self.send_swap(*at)))
                found.append((("settle", n, k), lambda at=at: self.settle(*at)))
                if flow[3]:
                    found.append((("after", n, k), lambda at=at: self.settle_side(*at)))
        found.append((("last",), self.last))
        return found


def in_order(actions, order):
    if order is None:
        return [action for _, action in actions]
    assert sorted(order) == list(range(len(actions)))
    return [actions[i][1] for i in order]


def column_part(rows, columns, shared, early, inside=False):
    half = columns // 2
    part = (half - shared) // 2
    flows = []
    if shared:
        flows.append((lambda side: 0, shared, "line", False))
    if early:
        flows.append((lambda side: shared + side * part, early, "line", True))
    if part > early:
        flows.append((lambda side: shared + side * part + early, part - early, "pair", True))
    return Part(rows, columns, "columns", flows, inside=inside)


def row_part(rows, columns, shared, early):
    half = rows // 2
    part = (half - shared) // 2
    flows = [
        (lambda side: 0, shared, "line", False),
        (lambda side: shared + side * part, early, "line", True),
        (lambda side: shared + side * part + early, part - early, "pair", True),
    ]
    return Part(rows, columns, "rows", [flow for flow in flows if flow[1]])


def vector_part(rows, columns, inside=False):
    return Part(rows, columns, None, [(lambda side: 0, columns, "line", False)], F32, inside)


ROW_QUERY, ROW_VALUE, ROW_OUTPUT, ROW_GAIN1, ROW_SHIFT1, ROW_INNER, INNER = 0, 1, 2, 3, 4, 5, 4
ROW_OUTER, ROW_GAIN2, ROW_SHIFT2 = 9, 10, 11
TABLE_ROWS = 16
VMEM = 67043328
LANES = 128
BAND = 128


def spread_table(table_ref, vec):
    for shard in range(table_ref.shape[0] // TABLE_ROWS):
        vec[:, pl.ds(shard * LANES, LANES)] = table_ref[
            pl.ds(shard * TABLE_ROWS, TABLE_ROWS), :
        ].astype(F32)


def fold_table(vec, table_ref, first, count):
    for shard in range(table_ref.shape[0] // TABLE_ROWS):
        table_ref[pl.ds(shard * TABLE_ROWS + first, count), :] = vec[
            pl.ds(first, count), pl.ds(shard * LANES, LANES)
        ]


def row_place(row, core, rows):
    half = rows // 2
    return jnp.where(row < half, row, row + half) + core * half


def total_rows(block):
    return jnp.sum(block.astype(F32), axis=0, keepdims=True)


def middle_kernel(
    rows_far,
    context_far,
    cot_far,
    lengths_ref,
    table_ref,
    output_w,
    inner_w,
    outer_w,
    out_far,
    first_grad_far,
    context_grad_far,
    sums_ref,
    output_far,
    inner_g,
    outer_g,
    rows_ref,
    context_ref,
    cot_ref,
    out_ref,
    first_grad_ref,
    context_grad_ref,
    output_g,
    output_v,
    inner_v,
    outer_v,
    vec,
    sums,
    active,
    slope,
    unit1,
    rate1,
    total,
    low,
    low_t,
    second,
    second_low,
    inner_b,
    outer_b,
    load,
    save,
    few,
    swap_send,
    swap_recv,
    swap_local,
):
    rows, width = rows_ref.shape
    tiles, _, tile = inner_v.shape
    place = Place()
    side, core = place.side, place.core
    length = lengths_ref[side]
    bands = rows // BAND
    assert BAND == cot_ref.shape[1]
    barrier = pltpu.get_barrier_semaphore()
    pl.semaphore_signal(barrier, inc=1, device_id=place.beside(), device_id_type=MESH)

    def inner_load(t):
        return pltpu.make_async_copy(
            inner_w.at[:, pl.ds(pl.multiple_of(t * tile, tile), tile)], inner_v.at[t], load.at[0, t]
        )

    def outer_load(t):
        return pltpu.make_async_copy(
            outer_w.at[pl.ds(pl.multiple_of(t * tile, tile), tile), :], outer_v.at[t], load.at[1, t]
        )

    output_load = pltpu.make_async_copy(output_w, output_v, few.at[0])
    context_load = pltpu.make_async_copy(context_far, context_ref, few.at[1])
    rows_load = pltpu.make_async_copy(rows_far, rows_ref, few.at[2])
    turn = Swap(
        place, [cot_far, out_ref], [cot_ref, out_far], swap_send, swap_recv, swap_local
    )
    first_save = pltpu.make_async_copy(first_grad_ref, first_grad_far, few.at[5])
    context_save = pltpu.make_async_copy(context_grad_ref, context_grad_far, few.at[6])
    output_save = pltpu.make_async_copy(output_g, output_far, few.at[7])
    for copy in (context_load, output_load, rows_load):
        copy.start()
    spread_table(table_ref, vec)
    sums[...] = jnp.zeros_like(sums)
    context_load.wait()
    output_load.wait()
    pl.semaphore_wait(barrier, 1)
    turn.start(0)
    ahead = 3
    for t in range(ahead):
        inner_load(t).start()
        outer_load(t).start()
    total[...] = plain_product(context_ref[...], output_v[...])
    rows_load.wait()

    def band_of(b):
        return pl.ds(pl.multiple_of(b * BAND, BAND), BAND)

    def first_norm(b, carry):
        here = band_of(b)
        first_sum = (
            rows_ref[here, :].astype(F32) + total[here, :] + vec[pl.ds(ROW_OUTPUT, 1), :]
        )
        unit, rate = norm_parts(first_sum)
        unit1[here, :] = unit
        rate1[here, :] = jnp.broadcast_to(rate, (BAND, LANES))
        normed = unit * vec[pl.ds(ROW_GAIN1, 1), :] + vec[pl.ds(ROW_SHIFT1, 1), :]
        low[here, :] = normed.astype(BF16)
        total[here, :] = normed + vec[pl.ds(ROW_OUTER, 1), :]
        return carry

    lax.fori_loop(0, bands, first_norm, 0)
    low_t[...] = low[...].T


    def forward(t, carry):
        inner_load(t).wait()

        @pl.when(t + ahead < tiles)
        def _():
            inner_load(t + ahead).start()
            outer_load(t + ahead).start()

        bias = jnp.concatenate(
            [
                vec[pl.ds(ROW_INNER + k, 1), pl.ds(pl.multiple_of(t * LANES, LANES), LANES)]
                for k in range(INNER)
            ],
            axis=1,
        )
        hidden = plain_product(low[...], inner_v[t]) + bias
        share = 0.5 + 0.5 * lax.erf(hidden * 0.7071067811865476)
        active[t] = (hidden * share).astype(BF16)
        slope[t] = share + hidden * (jnp.exp(-0.5 * hidden * hidden) * 0.3989422804014327)
        outer_load(t).wait()
        total[...] += plain_product(active[t], outer_v[t])
        return carry

    lax.fori_loop(0, tiles, forward, 0)

    turn.wait_here(0)

    def second_norm(b, carry):
        here = band_of(b)
        unit, rate = norm_parts(total[here, :])
        row = b * BAND + lax.broadcasted_iota(jnp.int32, (BAND, width), 0)
        mask = (row_place(row, core, rows) < length).astype(F32)
        gain = vec[pl.ds(ROW_GAIN2, 1), :]
        out_ref[b] = ((unit * gain + vec[pl.ds(ROW_SHIFT2, 1), :]) * mask).astype(BF16)
        out_grad = cot_ref[b].astype(F32) * mask
        grad = norm_back(unit, rate, out_grad * gain)
        second[here, :] = grad
        grad_low = grad.astype(BF16)
        second_low[here, :] = grad_low
        sums[pl.ds(ROW_GAIN2, 1), :] += total_rows(out_grad * unit)
        sums[pl.ds(ROW_SHIFT2, 1), :] += total_rows(out_grad)
        sums[pl.ds(ROW_OUTER, 1), :] += total_rows(grad_low)
        return carry

    lax.fori_loop(0, bands, second_norm, 0)
    turn.start(1)

    def inner_save(t):
        slot = lax.rem(t, 2)
        return pltpu.make_async_copy(
            inner_b.at[slot],
            inner_g.at[:, pl.ds(pl.multiple_of(t * tile, tile), tile)],
            save.at[0, slot],
        )

    def outer_save(t):
        slot = lax.rem(t, 2)
        return pltpu.make_async_copy(
            outer_b.at[slot],
            outer_g.at[pl.ds(pl.multiple_of(t * tile, tile), tile), :],
            save.at[1, slot],
        )

    def backward(t, carry):
        slot = lax.rem(t, 2)
        hidden_grad = (right_product(second_low[...], outer_v[t]) * slope[t]).astype(BF16)
        summed = total_rows(hidden_grad)
        for k in range(INNER):
            sums[
                pl.ds(ROW_INNER + k, 1), pl.ds(pl.multiple_of(t * LANES, LANES), LANES)
            ] = summed[:, k * LANES : (k + 1) * LANES]

        @pl.when(t >= 2)
        def _():
            outer_save(t - 2).wait()
            inner_save(t - 2).wait()

        outer_b[slot] = left_product(active[t], second_low[...]).astype(BF16)
        inner_b[slot] = plain_product(low_t[...], hidden_grad).astype(BF16)
        outer_save(t).start()
        second[...] += right_product(hidden_grad, inner_v[t])
        inner_save(t).start()
        return carry

    lax.fori_loop(0, tiles, backward, 0)

    def first_back(b, carry):
        here = band_of(b)
        grad = second[here, :]
        unit = unit1[here, :]
        sums[pl.ds(ROW_GAIN1, 1), :] += total_rows(grad * unit)
        sums[pl.ds(ROW_SHIFT1, 1), :] += total_rows(grad)
        back = norm_back(unit, rate1[here, :1], grad * vec[pl.ds(ROW_GAIN1, 1), :])
        first_grad_ref[here, :] = back
        back_low = back.astype(BF16)
        second_low[here, :] = back_low
        sums[pl.ds(ROW_OUTPUT, 1), :] += total_rows(back_low)
        return carry

    lax.fori_loop(0, bands, first_back, 0)
    output_g[...] = left_product(context_ref[...], second_low[...]).astype(BF16)
    first_save.start()
    context_grad_ref[...] = right_product(second_low[...], output_v[...]).astype(BF16)
    output_save.start()
    fold_table(sums, sums_ref, 0, TABLE_ROWS)
    context_save.start()
    for t in range(tiles - 2, tiles):
        outer_save(t).wait()
        inner_save(t).wait()
    for copy in (first_save, output_save, context_save):
        copy.wait()
    turn.finish()


def middle(collective_id, rows, context, cot, lengths, table, output_w, inner_w, outer_w):
    count, width = rows.shape
    hidden = inner_w.shape[1]
    tile = INNER * LANES
    tiles = hidden // tile
    whole = pl.BlockSpec(memory_space=pltpu.VMEM)
    far = pl.BlockSpec(memory_space=pltpu.HBM)

    def space(dtype):
        return pltpu.VMEM((count, width), dtype)

    return pl.pallas_call(
        middle_kernel,
        out_shape=[
            jax.ShapeDtypeStruct(cot.shape, BF16),
            jax.ShapeDtypeStruct((count, width), F32),
            jax.ShapeDtypeStruct((count, width), BF16),
            jax.ShapeDtypeStruct(table.shape, F32),
            jax.ShapeDtypeStruct(output_w.shape, BF16),
            jax.ShapeDtypeStruct(inner_w.shape, BF16),
            jax.ShapeDtypeStruct(outer_w.shape, BF16),
        ],
        in_specs=[far] * 3 + [pl.BlockSpec(memory_space=pltpu.SMEM), whole] + [far] * 3,
        out_specs=[far] * 3 + [whole] + [far] * 3,
        scratch_shapes=[
            space(BF16),
            space(BF16),
            pltpu.VMEM(cot.shape, BF16),
            pltpu.VMEM(cot.shape, BF16),
            space(F32),
            space(BF16),
            pltpu.VMEM(output_w.shape, BF16),
            pltpu.VMEM(output_w.shape, BF16),
            pltpu.VMEM((tiles, width, tile), BF16),
            pltpu.VMEM((tiles, tile, width), BF16),
            pltpu.VMEM((TABLE_ROWS, width), F32),
            pltpu.VMEM((TABLE_ROWS, width), F32),
            pltpu.VMEM((tiles, count, tile), BF16),
            pltpu.VMEM((tiles, count, tile), F32),
            space(F32),
            pltpu.VMEM((count, LANES), F32),
            space(F32),
            space(BF16),
            pltpu.VMEM((width, count), BF16),
            space(F32),
            space(BF16),
            pltpu.VMEM((2, width, tile), BF16),
            pltpu.VMEM((2, tile, width), BF16),
            pltpu.SemaphoreType.DMA((2, tiles)),
            pltpu.SemaphoreType.DMA((2, 2)),
            pltpu.SemaphoreType.DMA((8,)),
        ]
        + swap_scratch(2),
        compiler_params=pltpu.CompilerParams(
            collective_id=collective_id, has_side_effects=True, vmem_limit_bytes=VMEM
        ),
        name="feed_forward",
    )(rows, context, cot, lengths, table, output_w, inner_w, outer_w)


def widen_kernel(splits, lines, *refs):
    count = len(splits)
    many = sum(splits)
    ins, table, outs = refs[:count], refs[count], refs[count + 1 : count + 1 + many]
    vectors = refs[count + 1 + many : count + 1 + many + len(lines)]
    rest = refs[count + 1 + many + len(lines) :]
    narrow, held, wides = rest[:count], rest[count], rest[count + 1 : count + 1 + many]
    load, save = rest[-2:]
    loads = [
        pltpu.make_async_copy(here, there, load.at[k])
        for k, (here, there) in enumerate(zip(ins + (table,), narrow + (held,)))
    ]
    for k in (0, 1, count):
        loads[k].start()
    copies = []
    at = 0
    for k, parts in enumerate(splits):
        loads[k].wait()
        if k + 2 < count:
            loads[k + 2].start()
        columns = narrow[k].shape[-1] // parts
        for part in range(parts):
            wides[at][...] = narrow[k][..., part * columns : (part + 1) * columns].astype(
                wides[at].dtype
            )
            copies.append(pltpu.make_async_copy(wides[at], outs[at], save.at[at]))
            copies[-1].start()
            at += 1
    loads[count].wait()
    row = 0
    for vector, extent in zip(vectors, lines):
        for line in range(extent):
            copies.append(
                pltpu.make_async_copy(
                    held.at[row], vector.at[pl.ds(line * LANES, LANES)], save.at[many + row]
                )
            )
            copies[-1].start()
            row += 1
    for copy in copies:
        copy.wait()


def widen(arrays, splits, types, table, lines):
    shapes = []
    for array, parts, kind in zip(arrays, splits, types):
        shape = array.shape[:-1] + (array.shape[-1] // parts,)
        shapes += [jax.ShapeDtypeStruct(shape, kind)] * parts
    far = pl.BlockSpec(memory_space=pltpu.HBM)
    return pl.pallas_call(
        functools.partial(widen_kernel, splits, lines),
        out_shape=shapes + [jax.ShapeDtypeStruct((k * LANES,), F32) for k in lines],
        in_specs=[far] * (len(arrays) + 1),
        out_specs=[far] * (len(shapes) + len(lines)),
        scratch_shapes=[pltpu.VMEM(array.shape, array.dtype) for array in arrays + (table,)]
        + [pltpu.VMEM(shape.shape, shape.dtype) for shape in shapes]
        + [
            pltpu.SemaphoreType.DMA((len(arrays) + 1,)),
            pltpu.SemaphoreType.DMA((len(shapes) + sum(lines),)),
        ],
        compiler_params=pltpu.CompilerParams(vmem_limit_bytes=VMEM),
        name="widen_results",
    )(*arrays, table)


def stack_heads(block, lower):
    zero = jnp.zeros_like(block)
    return jnp.concatenate((jnp.where(lower, block, zero), jnp.where(lower, zero, block)), axis=0)


def repeat(first, stop, action):
    def step(i, carry):
        action(i)
        return carry

    lax.fori_loop(first, stop, step, 0)


GROUPS = 4
HALVES = 2


SPAN = 2 * HEAD_DIM


def span_of(section, pair, width):
    return pl.ds(pl.multiple_of(section * width + pair * SPAN, SPAN), SPAN)


class AttentionForward:
    def __init__(self, place, rows, weight, vec, bias, qkv, context, probs, held, away, send, recv, save):
        self.place, self.rows, self.weight, self.vec, self.bias = place, rows, weight, vec, bias
        self.qkv, self.context, self.probs, self.held, self.away = qkv, context, probs, held, away
        self.send, self.recv, self.save = send, recv, save
        self.count, self.width = context.shape
        self.pairs = self.width // SPAN

    def save_probs(self, pair):
        return pltpu.make_async_copy(self.held.at[pair], self.probs.at[pair], self.save.at[pair])

    def fetch(self, which, pair):
        return pltpu.make_async_remote_copy(
            self.qkv.at[:, span_of(which + 1, pair, self.width)],
            self.away.at[:, span_of(which, pair, self.width)],
            self.send.at[which, pair],
            self.recv.at[which, pair],
            device_id=self.place.twin(),
            device_id_type=MESH,
        )

    def project(self, section):
        tile = 512
        rows = self.rows[...].reshape(self.count, self.width)

        def one(t):
            columns = pl.ds(pl.multiple_of(section * self.width + t * tile, tile), tile)
            product = plain_product(rows, self.weight[:, columns])
            if section != 1:
                row = ROW_QUERY if section == 0 else ROW_VALUE
                product = product + self.vec[
                    pl.ds(row, 1), pl.ds(pl.multiple_of(t * tile, tile), tile)
                ]
            self.qkv[:, columns] = product.astype(BF16)

        repeat(0, self.width // tile, one)

    def give(self, which):
        for pair in range(self.pairs):
            self.fetch(which, pair).start()

    def attend(self, pair):
        for which in range(2):
            self.fetch(which, pair).wait_recv()
        count = self.count
        lower = lax.broadcasted_iota(jnp.int32, (count, SPAN), 1) < HEAD_DIM

        def here(section):
            return self.qkv[:, span_of(section, pair, self.width)]

        def there(section):
            return self.away[:, span_of(section - 1, pair, self.width)]

        stacked = stack_heads(here(0) * HEAD_DIM**-0.5, lower)
        keys = jnp.concatenate((here(1), there(1)), axis=0)
        values = jnp.concatenate((here(2), there(2)), axis=0)
        scores = right_product(stacked, keys) + self.bias[:1, :]
        top = jnp.max(scores, axis=1, keepdims=True)
        weights = jnp.exp(scores - top)
        total = jnp.sum(weights, axis=1, keepdims=True)
        probs = (weights * (1.0 / total)).astype(BF16)
        self.held[pair] = probs
        self.save_probs(pair).start()
        mixed = plain_product(probs, values)
        self.context[:, span_of(0, pair, self.width)] = jnp.where(
            lower, mixed[:count], mixed[count:]
        ).astype(BF16)

    def attend_group(self, group):
        each = self.pairs // GROUPS
        repeat(group * each, (group + 1) * each, self.attend)

    def finish(self):
        for pair in range(self.pairs):
            for which in range(2):
                self.fetch(which, pair).wait_send()
            self.save_probs(pair).wait()


TABLE, QUERIES = 0, 1


def start_actions(gather, work, keep, swap, save, table_ref):
    found = gather.actions()
    others = [k for k in range(len(keep)) if k not in (TABLE, QUERIES)]

    def ready():
        gather.wait_twins((TABLE, QUERIES))
        for k in (TABLE, QUERIES):
            keep[k].wait()
        swap.finish()
        spread_table(table_ref, work.vec)
        save.start()

    def values():
        work.project(2)
        work.give(0)

    def queries():
        work.give(1)
        work.project(0)

    found.append((("ready",), ready))
    found.append((("project", 0), lambda: work.project(1)))
    found.append((("project", 1), values))
    found.append((("project", 2), queries))
    for group in range(GROUPS):
        found.append((("pa", group), lambda group=group: work.attend_group(group)))

    def last():
        gather.finish(others)
        work.finish()
        for k in others:
            keep[k].wait()
        save.wait()

    found.append((("last",), last))
    return found


def start_kernel(flows, spots, order, *refs):
    count = max(array for array, _ in spots) + 1
    shares, refs = refs[: len(spots)], refs[len(spots) :]
    (in_block, lengths_ref), refs = refs[:2], refs[2:]
    table_ref, refs = refs[0], refs[1:]
    far, refs = refs[: count - 1], refs[count - 1 :]
    rows, qkv, context, probs, away = refs[:5]
    owns, refs = refs[5 : 5 + count], refs[5 + count :]
    weight, held, vec, bias = refs[:4]
    send, recv, local, load, send2, recv2, save2, saveq = refs[4:12]
    fulls = (table_ref, weight) + tuple(far[1:])
    place = Place()
    loads = [
        pltpu.make_async_copy(
            share, owns[array].at[:, pl.ds(column, share.shape[1])], load.at[k]
        )
        for k, (share, (array, column)) in enumerate(zip(shares, spots))
    ]
    for copy in loads:
        copy.start()
    keep = [
        pltpu.make_async_copy(
            own, full.at[pl.ds(pl.multiple_of(place.shard * own.shape[0], 16), own.shape[0]), :], local.at[k]
        )
        for k, (own, full) in enumerate(zip(owns, fulls))
    ]
    greet(place)
    rows_count = context.shape[0]
    length = lengths_ref[place.side]
    row = lax.broadcasted_iota(jnp.int32, (8, rows_count), 1)
    for k, core in enumerate((place.core, 1 - place.core)):
        bias[:, pl.ds(k * rows_count, rows_count)] = jnp.where(
            row_place(row, core, rows_count) < length, 0.0, -1e30
        )
    for copy in loads:
        copy.wait()
    swap = Swap(place, [in_block], [rows], *refs[12:15])
    swap.start()
    gather = Gather(place, flows, owns, fulls, send, recv)
    for copy in keep:
        copy.start()
    work = AttentionForward(
        place, rows, weight, vec, bias, qkv, context, probs, held, away, send2, recv2, save2
    )
    save = pltpu.make_async_copy(weight, far[0], saveq.at[0])
    for step in in_order(start_actions(gather, work, keep, swap, save, table_ref), order):
        step()


def start(shares, spots, block, lengths, flows, shards, collective_id, order):
    labels = gather_labels(flows)
    count = max(array for array, _ in spots) + 1
    shapes = []
    for array in range(count):
        members = [share for share, spot in zip(shares, spots) if spot[0] == array]
        shapes.append((members[0].shape[0], sum(m.shape[1] for m in members)))
    _, block_len, width = block.shape
    rows = 2 * block_len
    pairs = width // SPAN
    far = pl.BlockSpec(memory_space=pltpu.HBM)
    whole = pl.BlockSpec(memory_space=pltpu.VMEM)
    probs_shape = (pairs, 2 * rows, 2 * rows)
    return pl.pallas_call(
        functools.partial(start_kernel, flows, spots, order),
        out_shape=[jax.ShapeDtypeStruct((shards * r, c), BF16) for r, c in shapes]
        + [
            jax.ShapeDtypeStruct(block.shape, BF16),
            jax.ShapeDtypeStruct((rows, 3 * width), BF16),
            jax.ShapeDtypeStruct((rows, width), BF16),
            jax.ShapeDtypeStruct(probs_shape, BF16),
            jax.ShapeDtypeStruct((rows, 2 * width), BF16),
        ],
        in_specs=[far] * (len(shares) + 1) + [pl.BlockSpec(memory_space=pltpu.SMEM)],
        out_specs=[whole] + [far] * (count - 1) + [whole, whole, whole, far, whole],
        scratch_shapes=[pltpu.VMEM(shape, BF16) for shape in shapes]
        + [
            pltpu.VMEM((shards * shapes[QUERIES][0], shapes[QUERIES][1]), BF16),
            pltpu.VMEM(probs_shape, BF16),
            pltpu.VMEM((TABLE_ROWS, width), F32),
            pltpu.VMEM((8, 2 * rows), F32),
            pltpu.SemaphoreType.DMA((len(labels.numbers),)),
            pltpu.SemaphoreType.DMA((len(labels.numbers),)),
            pltpu.SemaphoreType.DMA((count,)),
            pltpu.SemaphoreType.DMA((len(shares),)),
            pltpu.SemaphoreType.DMA((2, pairs)),
            pltpu.SemaphoreType.DMA((2, pairs)),
            pltpu.SemaphoreType.DMA((pairs,)),
            pltpu.SemaphoreType.DMA((1,)),
        ]
        + swap_scratch(1),
        compiler_params=pltpu.CompilerParams(
            collective_id=collective_id, has_side_effects=True, vmem_limit_bytes=VMEM
        ),
        name="gather_attention_forward",
    )(*shares, block, lengths)


class AttentionBackward:
    def __init__(self, place, qkv, away, grad, out, keep, leave, come, send, recv):
        self.place, self.qkv, self.away, self.grad = place, qkv, away, grad
        self.out, self.keep, self.leave, self.come = out, keep, leave, come
        self.send, self.recv = send, recv
        self.count, self.width = grad.shape
        self.pairs = self.width // SPAN

    def give(self, which, pair):
        return pltpu.make_async_remote_copy(
            self.leave.at[:, span_of(which, pair, self.width)],
            self.come.at[:, span_of(which, pair, self.width)],
            self.send.at[which, pair],
            self.recv.at[which, pair],
            device_id=self.place.twin(),
            device_id_type=MESH,
        )

    def attend(self, pair, probs):
        count = self.count
        lower = lax.broadcasted_iota(jnp.int32, (count, SPAN), 1) < HEAD_DIM
        scale = HEAD_DIM**-0.5

        def here(section):
            return self.qkv[:, span_of(section, pair, self.width)]

        def there(section):
            return self.away[:, span_of(section - 1, pair, self.width)]

        first = span_of(0, pair, self.width)
        second = span_of(1, pair, self.width)
        stacked = stack_heads(here(0) * scale, lower)
        keys = jnp.concatenate((here(1), there(1)), axis=0)
        values = jnp.concatenate((here(2), there(2)), axis=0)
        grad = stack_heads(self.grad[:, first], lower)
        value_part = left_product(probs, grad)
        probs_grad = right_product(grad, values)
        wide = probs.astype(F32)
        inner = jnp.sum(wide * probs_grad, axis=1, keepdims=True)
        scores_grad = (wide * (probs_grad - inner)).astype(BF16)
        key_part = left_product(scores_grad, stacked)
        self.leave[:, first] = key_part[count:].astype(BF16)
        self.leave[:, second] = value_part[count:].astype(BF16)
        self.keep[:, first] = key_part[:count]
        self.keep[:, second] = value_part[:count]
        mixed = plain_product(scores_grad, keys) * scale
        self.out[:, first] = jnp.where(lower, mixed[:count], mixed[count:]).astype(BF16)
        for which in range(2):
            self.give(which, pair).start()

    def settle(self, pair):
        for which in range(2):
            self.give(which, pair).wait_recv()
            here = span_of(which, pair, self.width)
            self.out[:, span_of(which + 1, pair, self.width)] = (
                self.keep[:, here] + self.come[:, here].astype(F32)
            ).astype(BF16)

    def finish(self):
        for pair in range(self.pairs):
            for which in range(2):
                self.give(which, pair).wait_send()


class Finish:
    def __init__(self, work, tiles, weight, rows_ref, rows_t, first_grad, total, block, sums, held, probs, load, sems):
        self.work, self.tiles, self.weight, self.rows_ref, self.rows_t = work, tiles, weight, rows_ref, rows_t
        self.total, self.block, self.sums = total, block, sums
        self.held, self.probs, self.load, self.sems = held, probs, load, sems
        self.grad_load = pltpu.make_async_copy(first_grad, total, sems.at[held.shape[0]])
        self.count, self.width = total.shape
        self.tile = tiles.shape[2]

    def weight_load(self, t):
        columns = pl.ds(pl.multiple_of(t * self.tile, self.tile), self.tile)
        slot = lax.rem(t, self.tiles.shape[0])
        return pltpu.make_async_copy(
            self.weight.at[:, columns], self.tiles.at[slot], self.load.at[slot]
        )

    def probs_load(self, pair):
        slot = lax.rem(pair, self.held.shape[0])
        return pltpu.make_async_copy(
            self.probs.at[pair], self.held.at[slot], self.sems.at[slot]
        )

    def begin(self):
        for pair in range(self.held.shape[0]):
            self.probs_load(pair).start()
        for t in range(self.tiles.shape[0]):
            self.weight_load(t).start()
        self.grad_load.start()

    def attend(self, group):
        each = self.work.pairs // GROUPS

        slots = self.held.shape[0]

        def one(pair):
            self.probs_load(pair).wait()
            self.work.attend(pair, self.held[lax.rem(pair, slots)])
            pl.when(pair + slots < self.work.pairs)(self.probs_load(pair + slots).start)

        repeat(group * each, (group + 1) * each, one)

    def settle(self):
        repeat(0, self.work.pairs, self.work.settle)

    def weigh(self, core, target):
        shards, rows, columns = target.shape
        tile = self.tile

        def one(j):
            start = pl.multiple_of(core * columns + j * tile, tile)
            product = plain_product(self.rows_t[...], self.work.out[:, pl.ds(start, tile)])
            low = product.astype(BF16)
            for shard in range(shards):
                target[shard, :, pl.ds(pl.multiple_of(j * tile, tile), tile)] = low[
                    shard * rows : (shard + 1) * rows
                ]

        repeat(0, columns // tile, one)

    def turn(self):
        self.rows_t[...] = self.rows_ref[...].T

    def bias_sums(self, target):
        self.sums[pl.ds(0, 1), :] = total_rows(self.work.out[:, : self.width])
        self.sums[pl.ds(1, 1), :] = total_rows(self.work.out[:, 2 * self.width :])
        for shard in range(target.shape[0]):
            target[shard, pl.ds(ROW_QUERY, 2), :] = self.sums[
                pl.ds(0, 2), pl.ds(shard * LANES, LANES)
            ]

    def spread(self, half):
        count = self.weight.shape[1] // self.tile
        each = count // HALVES
        slots = self.tiles.shape[0]
        if half == 0:
            self.grad_load.wait()

        def one(t):
            self.weight_load(t).wait()
            columns = pl.ds(pl.multiple_of(t * self.tile, self.tile), self.tile)
            tile = self.tiles[lax.rem(t, slots)]
            self.total[...] += right_product(self.work.out[:, columns], tile)
            pl.when(t + slots < count)(self.weight_load(t + slots).start)

        repeat(half * each, (half + 1) * each, one)
        if half == HALVES - 1:
            rows = self.block.shape[1]
            for part in range(2):
                self.block[part] = self.total[pl.ds(part * rows, rows), :].astype(BF16)


def finish_actions(reduce, finish, swap):
    queries, vectors = 3, 4
    place = reduce.place
    found = reduce.actions()

    def load():
        finish.begin()
        finish.turn()

    found.append((("load",), load))
    for group in range(GROUPS):
        found.append((("att", group), lambda group=group: finish.attend(group)))
    found.append((("settleatt",), finish.settle))
    found.append((("leave",), lambda: finish.weigh(1 - place.core, reduce.grads[queries])))
    found.append((("own",), lambda: finish.weigh(place.core, reduce.own[queries])))
    found.append((("sums",), lambda: finish.bias_sums(reduce.own[vectors])))
    for half in range(HALVES):
        found.append((("dx", half), lambda half=half: finish.spread(half)))
    found.append((("swapin",), swap.start))
    return found


def finish_kernel(parts, order, *refs):
    rows_ref, qkv, away, grad, table_ref, first_grad, probs, weight = refs[:8]
    grads = list(refs[8:11])
    outs, swapped, refs = refs[11:16], refs[16], refs[17:]
    leave_q, tiles, held, out, keep, leave, come, total, sums, rows_t, block = refs[:11]
    send2, recv2, load2, sems = refs[11:15]
    scratch, rest = refs[15:-6], refs[-6:]
    place = Place()
    work = AttentionBackward(place, qkv, away, grad, out, keep, leave, come, send2, recv2)
    finish = Finish(
        work, tiles, weight, rows_ref, rows_t, first_grad, total, block, sums, held, probs, load2, sems
    )
    reduce = Reduce(place, parts, grads + [leave_q, None], outs, scratch, *rest[:3])
    swap = Swap(place, [block], [swapped], *rest[3:6])
    for shard in range(LINE * PAIR):
        reduce.own[4][shard] = table_ref[pl.ds(shard * TABLE_ROWS, TABLE_ROWS), :]
    greet(place)
    for step in in_order(finish_actions(reduce, finish, swap), order):
        step()
    work.finish()
    swap.finish()


def finish(rows, saved, grad, first_grad, table, weight, grads, parts, collective_id, order):
    qkv, away, probs = saved
    count, width = rows.shape
    pairs = width // SPAN
    tile = 512
    labels = reduce_labels(parts)
    whole = pl.BlockSpec(memory_space=pltpu.VMEM)
    far = pl.BlockSpec(memory_space=pltpu.HBM)
    queries = parts[3]
    return pl.pallas_call(
        functools.partial(finish_kernel, parts, order),
        out_shape=[jax.ShapeDtypeStruct((p.rows, p.columns), p.dtype) for p in parts]
        + [jax.ShapeDtypeStruct((2, count // 2, width), BF16)],
        in_specs=[whole] * 5 + [far] * 6,
        out_specs=[whole] * len(parts) + [far],
        scratch_shapes=[
            pltpu.VMEM((LINE * PAIR, queries.half_rows, queries.half_columns), BF16),
            pltpu.VMEM((2, width, tile), BF16),
            pltpu.VMEM((pairs // 2,) + probs.shape[1:], BF16),
            pltpu.VMEM((count, 3 * width), BF16),
            pltpu.VMEM((count, 2 * width), F32),
            pltpu.VMEM((count, 2 * width), BF16),
            pltpu.VMEM((count, 2 * width), BF16),
            pltpu.VMEM((count, width), F32),
            pltpu.VMEM((8, width), F32),
            pltpu.VMEM((width, count), BF16),
            pltpu.VMEM((2, count // 2, width), BF16),
            pltpu.SemaphoreType.DMA((2, pairs)),
            pltpu.SemaphoreType.DMA((2, pairs)),
            pltpu.SemaphoreType.DMA((2,)),
            pltpu.SemaphoreType.DMA((pairs // 2 + 1,)),
        ]
        + reduce_scratch(parts)
        + [
            pltpu.SemaphoreType.DMA((len(labels.numbers),)),
            pltpu.SemaphoreType.DMA((len(labels.numbers),)),
            pltpu.SemaphoreType.DMA((len(parts) * 2 * len(SPOTS),)),
        ]
        + swap_scratch(1),
        compiler_params=pltpu.CompilerParams(
            collective_id=collective_id, has_side_effects=True, vmem_limit_bytes=VMEM
        ),
        name="attention_backward_reduce",
    )(rows, qkv, away, grad, table, first_grad, probs, weight, *grads)


def exact_gelu(hidden):
    return jax.nn.gelu(hidden, approximate=False)


def plain_product(left, right):
    return jnp.dot(left, right, preferred_element_type=F32)


def left_product(left, right):
    return lax.dot_general(left, right, (((0,), (0,)), ((), ())), preferred_element_type=F32)


def right_product(left, right):
    return lax.dot_general(left, right, (((1,), (1,)), ((), ())), preferred_element_type=F32)


def column_sums(rows):
    return jnp.sum(rows.astype(F32), axis=0)


def norm_parts(total):
    average = jnp.mean(total, axis=-1, keepdims=True)
    centered = total - average
    variance = jnp.mean(centered * centered, axis=-1, keepdims=True)
    rate = lax.rsqrt(variance + EPSILON)
    return centered * rate, rate


def norm_back(unit, rate, grad):
    return rate * (
        grad
        - jnp.mean(grad, axis=-1, keepdims=True)
        - unit * jnp.mean(grad * unit, axis=-1, keepdims=True)
    )


def split_columns(packed, widths):
    pieces = []
    start = 0
    for width in widths:
        pieces.append(packed[..., start : start + width])
        start += width
    return pieces


def native_forward(queries, keys_all, values_all, key_valid, heads):
    shape = queries.shape[:2] + (heads, HEAD_DIM)
    key_shape = keys_all.shape[:2] + (heads, HEAD_DIM)
    scores = jnp.einsum(
        "sqhd,skhd->shqk",
        queries.reshape(shape),
        keys_all.reshape(key_shape),
        preferred_element_type=F32,
    ) * (HEAD_DIM**-0.5)
    scores = jnp.where(key_valid[:, None, None, :], scores, -1e30)
    top = jnp.max(scores, axis=-1, keepdims=True)
    weights = jnp.exp(scores - top)
    probs = (weights / jnp.sum(weights, axis=-1, keepdims=True)).astype(BF16)
    context = jnp.einsum(
        "shqk,skhd->sqhd", probs, values_all.reshape(key_shape), preferred_element_type=F32
    )
    return context.reshape(queries.shape).astype(BF16), probs


def native_backward(queries, keys_all, values_all, probs, context_grad, heads):
    shape = queries.shape[:2] + (heads, HEAD_DIM)
    key_shape = keys_all.shape[:2] + (heads, HEAD_DIM)
    scale = HEAD_DIM**-0.5
    grad_heads = context_grad.reshape(shape)
    wide = probs.astype(F32)
    probs_grad = jnp.einsum(
        "sqhd,skhd->shqk", grad_heads, values_all.reshape(key_shape), preferred_element_type=F32
    )
    inner_total = jnp.sum(wide * probs_grad, axis=-1, keepdims=True)
    scores_grad = (wide * (probs_grad - inner_total)).astype(BF16)
    query_grad = jnp.einsum(
        "shqk,skhd->sqhd", scores_grad, keys_all.reshape(key_shape), preferred_element_type=F32
    )
    key_part = jnp.einsum(
        "shqk,sqhd->skhd", scores_grad, queries.reshape(shape), preferred_element_type=F32
    )
    value_part = jnp.einsum("shqk,sqhd->skhd", probs, grad_heads, preferred_element_type=F32)
    return (
        (query_grad * scale).astype(BF16).reshape(queries.shape),
        (key_part * scale).astype(BF16).reshape(keys_all.shape),
        value_part.astype(BF16).reshape(values_all.shape),
    )


def gather_rows(part):
    return lax.all_gather(part, "fsdp", axis=0, tiled=True)


def reduce_rows(part):
    share = lax.psum_scatter(part.astype(BF16), "fsdp", scatter_dimension=0, tiled=True)
    return lax.psum(share, "ctx").astype(F32)


def layer(flat_rows, cot_rows, row_mask, packed, widths, weights, forward, backward):
    full_qkv, full_output, full_inner, full_outer = weights
    rows, width = flat_rows.shape
    shards = packed.shape[0]
    (
        bias_query,
        bias_value,
        bias_output,
        gain_first,
        shift_first,
        bias_inner,
        bias_outer,
        gain_second,
        shift_second,
    ) = [piece.reshape(-1).astype(F32) for piece in split_columns(packed, widths)]
    bias_qkv = jnp.concatenate((bias_query, jnp.zeros_like(bias_query), bias_value))
    qkv = (plain_product(flat_rows, full_qkv) + bias_qkv).astype(BF16)
    context, saved = forward(qkv)

    first_sum = flat_rows.astype(F32) + plain_product(context, full_output) + bias_output
    first_unit, first_rate = norm_parts(first_sum)
    normed = first_unit * gain_first + shift_first
    normed_low = normed.astype(BF16)
    hidden = plain_product(normed_low, full_inner) + bias_inner
    active, gelu_back = jax.vjp(exact_gelu, hidden)
    active_low = active.astype(BF16)
    second_sum = normed + plain_product(active_low, full_outer) + bias_outer
    second_unit, second_rate = norm_parts(second_sum)
    output = ((second_unit * gain_second + shift_second) * row_mask).astype(BF16)

    out_grad = cot_rows.astype(F32) * row_mask
    second_gain_part = jnp.sum(out_grad * second_unit, axis=0)
    second_shift_part = jnp.sum(out_grad, axis=0)
    second_grad = norm_back(second_unit, second_rate, out_grad * gain_second)
    second_low = second_grad.astype(BF16)
    outer_weight_part = left_product(active_low, second_low).astype(BF16)
    outer_bias_part = column_sums(second_low)
    (hidden_grad,) = gelu_back(right_product(second_low, full_outer))
    hidden_low = hidden_grad.astype(BF16)
    inner_weight_part = left_product(normed_low, hidden_low).astype(BF16)
    inner_bias_part = column_sums(hidden_low)
    normed_grad = second_grad + right_product(hidden_low, full_inner)
    first_gain_part = jnp.sum(normed_grad * first_unit, axis=0)
    first_shift_part = jnp.sum(normed_grad, axis=0)
    first_grad = norm_back(first_unit, first_rate, normed_grad * gain_first)
    branch_low = first_grad.astype(BF16)
    output_weight_part = left_product(context, branch_low).astype(BF16)
    output_bias_part = column_sums(branch_low)
    context_grad = right_product(branch_low, full_output).astype(BF16)
    qkv_grad = backward(saved, context_grad)
    qkv_weight_part = left_product(flat_rows, qkv_grad).astype(BF16)
    query_bias_part = column_sums(qkv_grad[:, :width])
    value_bias_part = column_sums(qkv_grad[:, 2 * width :])
    input_grad = first_grad + right_product(qkv_grad, full_qkv)
    vector_parts = (
        query_bias_part,
        value_bias_part,
        output_bias_part,
        first_gain_part,
        first_shift_part,
        inner_bias_part,
        outer_bias_part,
        second_gain_part,
        second_shift_part,
    )
    packed_parts = jnp.concatenate([part.reshape(shards, -1) for part in vector_parts], axis=1)
    return (
        output,
        input_grad,
        packed_parts,
        (qkv_weight_part, output_weight_part, inner_weight_part, outer_weight_part),
    )


def native_body(inputs, cotangent, lengths, vectors, weights):
    widths = [member.shape[0] for member in vectors]
    packed = lax.all_gather(jnp.concatenate(vectors), "fsdp", axis=0, tiled=False)
    joined = (jnp.concatenate(weights[:3], axis=1),) + weights[3:]
    full = tuple(gather_rows(part) for part in joined)
    micro, seqs, block_len, width = inputs.shape
    heads = width // HEAD_DIM
    total_slots = block_len * lax.axis_size("ctx")
    group = micro * seqs
    rows = group * block_len
    flat_len = lengths.reshape(group)
    local_pos = lax.axis_index("ctx") * block_len + jnp.arange(block_len, dtype=jnp.int32)
    row_mask = (local_pos[None, :] < flat_len[:, None]).astype(F32).reshape(rows, 1)
    key_valid = jnp.arange(total_slots, dtype=jnp.int32)[None, :] < flat_len[:, None]

    def forward(qkv):
        queries = qkv[:, :width].reshape(group, block_len, width)
        keys_values = lax.all_gather(
            qkv[:, width:].reshape(group, block_len, 2 * width), "ctx", axis=1, tiled=True
        )
        keys, values = keys_values[:, :, :width], keys_values[:, :, width:]
        context, probs = native_forward(queries, keys, values, key_valid, heads)
        return context.reshape(rows, width), (queries, keys, values, probs)

    def backward(saved, context_grad):
        query_grad, key_part, value_part = native_backward(
            *saved, context_grad.reshape(group, block_len, width), heads
        )
        keys_values_grad = lax.psum_scatter(
            jnp.concatenate((key_part, value_part), axis=2), "ctx", scatter_dimension=1, tiled=True
        )
        return jnp.concatenate(
            (query_grad.reshape(rows, width), keys_values_grad.reshape(rows, 2 * width)), axis=1
        )

    output, input_grad, packed_parts, parts = layer(
        inputs.reshape(rows, width),
        cotangent.reshape(rows, width),
        row_mask,
        packed,
        widths,
        full,
        forward,
        backward,
    )
    share = lax.psum_scatter(packed_parts, "fsdp", scatter_dimension=0, tiled=True)
    return (
        output.reshape(inputs.shape),
        input_grad.reshape(inputs.shape),
        split_columns(lax.psum(share, "ctx")[0], widths),
        tuple(split_columns(reduce_rows(parts[0]), [width] * 3))
        + tuple(reduce_rows(part) for part in parts[1:]),
    )


def direct_body(inputs, cotangent, lengths, vectors, weights):
    micro, seqs, block_len, width = inputs.shape
    shards = LINE * PAIR
    lengths = lengths.reshape(micro)
    rows = 2 * block_len
    table = jnp.zeros((TABLE_ROWS, LANES), F32)
    row = 0
    for vector in vectors:
        lines = vector.shape[0] // LANES
        filled = ((row, TABLE_ROWS - row - lines), (0, 0))
        table += jnp.pad(vector.astype(F32).reshape(lines, LANES), filled)
        row += lines
    query_weight, key_weight, value_weight, output_weight, inner_weight, outer_weight = weights
    shard_rows, hidden = inner_weight.shape
    flows = [Flow(0, TABLE_ROWS, lambda core, side: (0, TABLE_ROWS, 0, LANES), cores=False)]
    flows += column_flows(1, shard_rows, 3 * width, *GATHER_SPLIT[0])
    flows += column_flows(2, shard_rows, width, *GATHER_SPLIT[1])
    flows += column_flows(3, shard_rows, hidden, *GATHER_SPLIT[2])
    flows += row_flows(4, hidden // shards, width, *GATHER_SPLIT[3])
    (
        tables,
        full_qkv,
        full_output,
        full_inner,
        full_outer,
        in_rows,
        qkv,
        context,
        probs,
        away,
    ) = start(
        (table.astype(BF16),) + weights,
        ((0, 0), (1, 0), (1, width), (1, 2 * width), (2, 0), (3, 0), (4, 0)),
        inputs.reshape(micro, block_len, width),
        lengths,
        flows,
        shards,
        1,
        GATHER_ORDER,
    )
    in_rows = in_rows.reshape(rows, width)
    output, first_grad, context_grad, table_grad, output_part, inner_part, outer_part = middle(
        3,
        in_rows,
        context,
        cotangent.reshape(micro, block_len, width),
        lengths,
        tables,
        full_output,
        full_inner,
        full_outer,
    )
    sums = finish(
        in_rows,
        (qkv, away, probs),
        context_grad,
        first_grad,
        table_grad,
        full_qkv,
        (inner_part, outer_part, output_part),
        [
            column_part(shard_rows, hidden, *REDUCE_SPLIT[0]),
            row_part(hidden // shards, width, *REDUCE_SPLIT[1]),
            column_part(shard_rows, width, *REDUCE_SPLIT[2]),
            column_part(shard_rows, 3 * width, *REDUCE_SPLIT[3], inside=True),
            vector_part(TABLE_ROWS, LANES, inside=True),
        ],
        2,
        REDUCE_ORDER,
    )
    inner_share, outer_share, output_share, qkv_share, table_share, grads = sums
    lines = tuple(vector.shape[0] // LANES for vector in vectors)
    wide = widen(
        (qkv_share, output_share, inner_share, outer_share, grads, output),
        (3, 1, 1, 1, 1, 1),
        (F32,) * 5 + (BF16,),
        table_share,
        lines,
    )
    return (
        wide[7].reshape(inputs.shape),
        wide[6].reshape(inputs.shape),
        tuple(wide[8:]),
        tuple(wide[:6]),
    )


def body(
    inputs,
    cotangent,
    lengths,
    query_weight,
    key_weight,
    value_weight,
    output_weight,
    query_bias,
    value_bias,
    output_bias,
    first_gain,
    first_shift,
    inner_weight,
    inner_bias,
    outer_weight,
    outer_bias,
    second_gain,
    second_shift,
):
    vectors = (
        query_bias,
        value_bias,
        output_bias,
        first_gain,
        first_shift,
        inner_bias,
        outer_bias,
        second_gain,
        second_shift,
    )
    widths = [member.shape[0] for member in vectors]
    weights = (
        query_weight,
        key_weight,
        value_weight,
        output_weight,
        inner_weight,
        outer_weight,
    )
    laid_out = lax.axis_size("fsdp") == LINE * PAIR and lax.axis_size("ctx") == 4
    whole_lines = all(extent % LANES == 0 for extent in widths)
    direct = laid_out and inputs.shape[:2] == (2, 1) and whole_lines
    run = direct_body if direct else native_body
    output, input_grad, shares, weight_shares = run(inputs, cotangent, lengths, vectors, weights)
    query_share, key_share, value_share, output_share, inner_share, outer_share = weight_shares
    return (
        output,
        input_grad,
        query_share,
        key_share,
        value_share,
        output_share,
        shares[0],
        shares[1],
        shares[2],
        shares[3],
        shares[4],
        inner_share,
        shares[5],
        outer_share,
        shares[6],
        shares[7],
        shares[8],
    )


def solution(mesh):
    data = P(None, "fsdp", "ctx", None)
    matrix = P("fsdp", None)
    vector = P("fsdp")
    return jax.shard_map(
        body,
        mesh=mesh,
        in_specs=(data, data, P(None, "fsdp"))
        + (matrix,) * 4
        + (vector,) * 5
        + (matrix, vector, matrix, vector, vector, vector),
        out_specs=(data, data)
        + (matrix,) * 4
        + (vector,) * 5
        + (matrix, vector, matrix, vector, vector, vector),
        check_vma=False,
    )
```
